32 devices in a mesh: dp: 4 (over y, core), mp: 8 (over z, x).
Axes of the slice: x: 2, y: 2, z: 4, core: 2. Of those that a mesh axis runs over, the one named last changes fastest.
Arguments:
- inputs: bfloat16 [8192, 2048], P('dp', 'mp'), may hold values from -6 to 6
- segments: int32 [4, 2048], P('dp'), may hold values from 0 to 7, never falling along the last dimension, each value on 1 to 1024 neighbouring positions
- gain_attn: float32 [2048], P('mp'), may hold values from 0.5 to 1.5
- gain_ffn: float32 [2048], P('mp'), may hold values from 0.5 to 1.5
- w_qkv: bfloat16 [3, 2048, 2048], P(None, 'mp'), may hold values from -0.125 to 0.125
- a_qkv: float32 [3, 2048, 16], P(None, 'mp'), may hold values from -0.125 to 0.125
- query_key_value_factor: float32 [3, 16, 2048], replicated, may hold values from -0.3 to 0.3
- m_qkv: float32 [3, 2048], P(None, 'mp'), may hold values from 1 to 1.6
- w_out: bfloat16 [2048, 2048], P('mp'), may hold values from -0.125 to 0.125
- a_out: float32 [2048, 16], P('mp'), may hold values from -0.125 to 0.125
- b_out: float32 [16, 2048], replicated, may hold values from -0.3 to 0.3
- m_out: float32 [2048], P('mp'), may hold values from 3 to 6
- w_gu: bfloat16 [2, 2048, 5632], P(None, 'mp'), may hold values from -0.125 to 0.125
- a_gu: float32 [2, 2048, 16], P(None, 'mp'), may hold values from -0.125 to 0.125
- gate_up_factor: float32 [2, 16, 5632], replicated, may hold values from -0.3 to 0.3
- m_gu: float32 [2, 5632], P(None, 'mp'), may hold values from 1 to 1.6
- w_down: bfloat16 [5632, 2048], P('mp'), may hold values from -0.078125 to 0.078125
- a_down: float32 [5632, 16], P('mp'), may hold values from -0.078125 to 0.078125
- b_down: float32 [16, 2048], replicated, may hold values from -0.3 to 0.3
- m_down: float32 [2048], P('mp'), may hold values from 1.5 to 3
- cotangent: bfloat16 [8192, 2048], P('dp', 'mp'), may hold values from -6 to 6
Outputs:
- block_out: bfloat16 [8192, 2048], P('dp', 'mp')
- grad_input: float32 [8192, 2048], P('dp', 'mp')
- grad_a_qkv: float32 [3, 2048, 16], P(None, 'mp')
- grad_b_qkv: float32 [3, 16, 2048], P(None, None, 'mp')
- grad_m_qkv: float32 [3, 2048], P(None, 'mp')
- grad_a_out: float32 [2048, 16], P('mp')
- grad_b_out: float32 [16, 2048], P(None, 'mp')
- grad_m_out: float32 [2048], P('mp')
- grad_a_gu: float32 [2, 2048, 16], P(None, 'mp')
- grad_b_gu: float32 [2, 16, 5632], P(None, None, 'mp')
- grad_m_gu: float32 [2, 5632], P(None, 'mp')
- grad_a_down: float32 [5632, 16], P('mp')
- grad_b_down: float32 [16, 2048], P(None, 'mp')
- grad_m_down: float32 [2048], P('mp')
The draws below stay inside these ranges and needn't reach their ends.
Inputs may be any that keep to these rules, and one draw needn't show every extreme that they name: Within each packed row the segment numbers never fall; each of the 8 segments holds 1 to 1024 tokens, and one holds exactly 1024.
All inputs are finite; a program needn't handle non-finite values.
Results may differ from the reference program's by a relative error of at most 0.019.
Values may be sent and summed in bfloat16 or wider, within the bound.
A program may use at most 320 MiB of HBM per device.

```python
import math
import jax
import jax.numpy as jnp
import numpy as np
from jax import lax

D = 2048
HEADS = 16
HD = 128
FF = 5632
ADAPTER_RANK = 16
ADAPTER_ALPHA = 32
SEQ = 2048
SEGS = 8
MOST = 1024
ROWS = 4
TOKENS = 8192


def level_of(stream_key, shape, split, smallest, top_value):
    loudness = 1.0
    for position, blocks in split:
        heights = jax.random.uniform(jax.random.fold_in(jax.random.fold_in(stream_key, 6), position), (blocks,), jnp.float32, smallest / len(split), top_value / len(split))
        loudness = loudness * jnp.repeat(jnp.exp(heights), shape[position] // blocks).reshape((-1,) + (1,) * (len(shape) - 1 - position))
    return loudness


def length_profile(count, total, reach, skew):
    loads = [(1 << 20) // math.isqrt(standing ** skew) + 1 for standing in range(2, count + 1)]
    surplus, given = total - reach - (count - 1), [1] * (count - 1)
    while surplus > 0:
        movable = [i for i in range(count - 1) if given[i] < reach]
        pool, left = sum([loads[i] for i in movable]), surplus
        for i in movable:
            extra = min(reach - given[i], max(1, left * loads[i] // pool), surplus)
            given[i] = given[i] + extra
            surplus = surplus - extra
    return np.array([reach] + given)


def ragged_sizes(key, amount, total, most, lean):
    if amount == 2:
        one = jax.random.randint(key, (), max(1, total - most), min(most, total - 1) + 1)
        return jnp.stack([one, total - one])
    sizes = jnp.asarray(length_profile(amount, total, most, lean), jnp.int32)
    twos = (amount - 1) // 2
    giver, receiver = sizes[1:1 + 2 * twos:2], sizes[2:2 + 2 * twos:2]
    room = jnp.minimum(giver - 1, most - receiver)
    shifted = jax.random.randint(jax.random.fold_in(key, 1), (twos,), 0, 1 << 20) % (room + 1)
    sizes = sizes.at[1:1 + 2 * twos:2].set(giver - shifted).at[2:2 + 2 * twos:2].set(receiver + shifted)
    return sizes[jax.random.permutation(jax.random.fold_in(key, 2), amount)]


def centred(rng, shape, width, reach, cuts=(), kind=jnp.bfloat16):
    entries = jax.random.normal(rng, shape, jnp.float32) * width
    if len(cuts) > 0:
        entries = level_of(rng, shape, cuts, -0.22, 0.18) * entries
    return jnp.clip(entries, min=-reach, max=reach).astype(kind)


def setup_inputs(seed: int = 0) -> dict:
    arg_keys = jax.random.split(jax.random.key(seed), 22)
    inputs = centred(arg_keys[0], (TOKENS, D), 1.0, 6.0, ((0, 4), (1, 8)))
    segments = jax.vmap(lambda own: jnp.searchsorted(jnp.cumsum(ragged_sizes(own, SEGS, SEQ, MOST, 1)), jnp.arange(SEQ), side="right"))(jax.random.split(arg_keys[1], ROWS)).reshape((ROWS, SEQ)).astype(jnp.int32)
    gain_attn = jnp.clip(1.0 + 0.1 * jax.random.normal(arg_keys[2], (D,), jnp.float32), 0.5, 1.5)
    gain_ffn = jnp.clip(1.0 + 0.1 * jax.random.normal(arg_keys[3], (D,), jnp.float32), 0.5, 1.5)
    w_qkv = centred(arg_keys[4], (3, D, D), D ** -0.5, 0.125, ((1, 8),))
    a_qkv = centred(arg_keys[5], (3, D, ADAPTER_RANK), D ** -0.5, 0.125, ((1, 8),), jnp.float32)
    query_key_value_factor = centred(arg_keys[6], (3, ADAPTER_RANK, D), 0.05, 0.3, (), jnp.float32)
    m_qkv = jnp.clip(1.0 + 0.6 * jax.random.uniform(arg_keys[7], (3, D), jnp.float32) ** level_of(arg_keys[7], (3, D), ((1, 8),), -0.2, 0.2), 1.0, 1.6)
    w_out = centred(arg_keys[8], (D, D), D ** -0.5, 0.125, ((0, 8),))
    a_out = centred(arg_keys[9], (D, ADAPTER_RANK), D ** -0.5, 0.125, ((0, 8),), jnp.float32)
    b_out = centred(arg_keys[10], (ADAPTER_RANK, D), 0.05, 0.3, (), jnp.float32)
    m_out = jnp.clip(3.0 + 3.0 * jax.random.uniform(arg_keys[11], (D,), jnp.float32) ** level_of(arg_keys[11], (D,), ((0, 8),), -0.2, 0.2), 3.0, 6.0)
    w_gu = centred(arg_keys[12], (2, D, FF), D ** -0.5, 0.125, ((1, 8),))
    a_gu = centred(arg_keys[13], (2, D, ADAPTER_RANK), D ** -0.5, 0.125, ((1, 8),), jnp.float32)
    gate_up_factor = centred(arg_keys[14], (2, ADAPTER_RANK, FF), 0.05, 0.3, (), jnp.float32)
    m_gu = jnp.clip(1.0 + 0.6 * jax.random.uniform(arg_keys[15], (2, FF), jnp.float32) ** level_of(arg_keys[15], (2, FF), ((1, 8),), -0.2, 0.2), 1.0, 1.6)
    w_down = centred(arg_keys[16], (FF, D), FF ** -0.5, 0.078125, ((0, 8),))
    a_down = centred(arg_keys[17], (FF, ADAPTER_RANK), FF ** -0.5, 0.078125, ((0, 8),), jnp.float32)
    b_down = centred(arg_keys[18], (ADAPTER_RANK, D), 0.05, 0.3, (), jnp.float32)
    m_down = jnp.clip(1.5 + 1.5 * jax.random.uniform(arg_keys[19], (D,), jnp.float32) ** level_of(arg_keys[19], (D,), ((0, 8),), -0.2, 0.2), 1.5, 3.0)
    cotangent = centred(arg_keys[20], (TOKENS, D), 1.0, 6.0, ((0, 4), (1, 8)))
    return {"inputs": inputs, "segments": segments, "gain_attn": gain_attn, "gain_ffn": gain_ffn, "w_qkv": w_qkv, "a_qkv": a_qkv, "query_key_value_factor": query_key_value_factor, "m_qkv": m_qkv, "w_out": w_out, "a_out": a_out, "b_out": b_out, "m_out": m_out, "w_gu": w_gu, "a_gu": a_gu, "gate_up_factor": gate_up_factor, "m_gu": m_gu, "w_down": w_down, "a_down": a_down, "b_down": b_down, "m_down": m_down, "cotangent": cotangent}


highest_precision = lax.Precision.HIGHEST
epsilon = 1e-05
masked_score = -1e+30

@jax.custom_vjp
def low(v):
    return lax.optimization_barrier(v.astype(jnp.bfloat16)).astype(jnp.float32)

@jax.custom_vjp
def low_back(v):
    return v

def low_keep(v):
    return (low(v), None)

def low_pass(kept, grad):
    return (grad,)

def back_keep(v):
    return (v, None)

def back_low(kept, grad):
    return (low(grad),)
low.defvjp(low_keep, low_pass)
low_back.defvjp(back_keep, back_low)

def positions_of(segment_rows):
    index_row = jnp.arange(segment_rows.shape[1], dtype=jnp.int32)
    starts = jnp.concatenate([jnp.ones((segment_rows.shape[0], 1), jnp.bool_), segment_rows[:, 1:] != segment_rows[:, :-1]], axis=1)
    begin_at = lax.cummax(jnp.where(starts, index_row[None, :], 0), axis=1)
    return index_row[None, :] - begin_at

def rotary_tables(positions):
    freq_rows = jnp.exp(jnp.arange(HD // 2, dtype=jnp.float32) * (-2.0 * math.log(10000.0) / HD))
    angles = positions.astype(jnp.float32)[:, None] * freq_rows[None, :]
    return (jnp.cos(angles), jnp.sin(angles))

def rotate(head_values, cosine, sine_table):
    first_half = head_values[..., :HD // 2]
    second_half = head_values[..., HD // 2:]
    cosine = cosine[:, None, :]
    sine_table = sine_table[:, None, :]
    return jnp.concatenate([first_half * cosine - second_half * sine_table, second_half * cosine + first_half * sine_table], axis=-1)

def rms_norm(values_in, gain_row):
    return low(values_in * lax.rsqrt(lax.optimization_barrier(jnp.mean(values_in * values_in, axis=-1, keepdims=True)) + epsilon) * gain_row)

def apply_projection(input_portion, frozen_weight, adapter_down_factor, adapter_up_factor, magnitude_vector):
    adapter_scale = ADAPTER_ALPHA / ADAPTER_RANK
    adapter_input = jnp.dot(input_portion, adapter_down_factor, precision=highest_precision)
    sharded_output = jnp.dot(input_portion, frozen_weight, precision=highest_precision) + adapter_scale * jnp.dot(adapter_input, adapter_up_factor, precision=highest_precision)
    merged_weight = frozen_weight + adapter_scale * jnp.dot(adapter_down_factor, adapter_up_factor, precision=highest_precision)
    column_slice = jnp.sqrt(lax.optimization_barrier(jnp.sum(merged_weight * merged_weight, axis=0)))
    return low_back(sharded_output) * (magnitude_vector / column_slice)

def attend_row(query_rows, key_rows, value_rows, segment_row):
    scores = low_back(jnp.einsum('qhd,khd->hqk', query_rows, key_rows, precision=highest_precision) * HD ** (-0.5))
    index_row = jnp.arange(SEQ, dtype=jnp.int32)
    allowed = (segment_row[:, None] == segment_row[None, :]) & (index_row[None, :] <= index_row[:, None])
    scores = jnp.where(allowed[None], scores, masked_score)
    weights = jax.nn.softmax(scores, axis=-1)
    return jnp.einsum('hqk,khd->qhd', low(weights), value_rows, precision=highest_precision)

def reference(inputs, segments, gain_attn, gain_ffn, w_qkv, a_qkv, query_key_value_factor, m_qkv, w_out, a_out, b_out, m_out, w_gu, a_gu, gate_up_factor, m_gu, w_down, a_down, b_down, m_down, cotangent):
    frozen_qkv = w_qkv.astype(jnp.float32)
    frozen_out = w_out.astype(jnp.float32)
    frozen_gu = w_gu.astype(jnp.float32)
    frozen_down = w_down.astype(jnp.float32)
    positions = positions_of(segments).reshape(TOKENS)
    cosine, sine_table = rotary_tables(positions)

    def shaped(tensor):
        return tensor.reshape(ROWS, SEQ, HEADS, HD)

    def block_forward(block_in, a_qkv, query_key_value_factor, m_qkv, a_out, b_out, m_out, a_gu, gate_up_factor, m_gu, a_down, b_down, m_down):
        normed = rms_norm(block_in, gain_attn)
        query_proj = apply_projection(normed, frozen_qkv[0], a_qkv[0], query_key_value_factor[0], m_qkv[0])
        key_proj = apply_projection(normed, frozen_qkv[1], a_qkv[1], query_key_value_factor[1], m_qkv[1])
        value_proj = apply_projection(normed, frozen_qkv[2], a_qkv[2], query_key_value_factor[2], m_qkv[2])
        query_rows = low(rotate(query_proj.reshape(TOKENS, HEADS, HD), cosine, sine_table))
        key_rows = low(rotate(key_proj.reshape(TOKENS, HEADS, HD), cosine, sine_table))
        value_rows = low(value_proj.reshape(TOKENS, HEADS, HD))
        attended = lax.map(jax.checkpoint(lambda packed: attend_row(packed[0], packed[1], packed[2], packed[3])), (shaped(query_rows), shaped(key_rows), shaped(value_rows), segments))
        attended = low(low_back(attended.reshape(TOKENS, D)))
        middle = block_in + apply_projection(attended, frozen_out, a_out, b_out, m_out)
        normed_ffn = rms_norm(middle, gain_ffn)
        gate_proj = apply_projection(normed_ffn, frozen_gu[0], a_gu[0], gate_up_factor[0], m_gu[0])
        up_proj = apply_projection(normed_ffn, frozen_gu[1], a_gu[1], gate_up_factor[1], m_gu[1])
        hidden = low(jax.nn.silu(gate_proj) * up_proj)
        return middle + apply_projection(hidden, frozen_down, a_down, b_down, m_down)
    result, pullback = jax.vjp(block_forward, inputs.astype(jnp.float32), a_qkv, query_key_value_factor, m_qkv, a_out, b_out, m_out, a_gu, gate_up_factor, m_gu, a_down, b_down, m_down)
    grads = pullback(cotangent.astype(jnp.float32))
    return (result.astype(jnp.bfloat16), grads[0], grads[1], grads[2], grads[3], grads[4], grads[5], grads[6], grads[7], grads[8], grads[9], grads[10], grads[11], grads[12])
```

```python
import math

import jax
import jax.numpy as jnp
from jax import lax
from jax.experimental import pallas as pl
from jax.experimental.pallas import tpu as pltpu
from jax.sharding import Mesh
from jax.sharding import PartitionSpec as P

HD = 128
RANK = 16
SCALE = 2.0
EPS = 1e-05
MASKED = -1e30
HIGHEST = lax.Precision.HIGHEST
MESH = pl.DeviceIdType.MESH
F32 = jnp.float32
BF16 = jnp.bfloat16
LANES = 128
VMEM_LIMIT = 60 * 1024 * 1024


def nt(a, b, precision=None):
    return lax.dot_general(
        a, b, (((1,), (1,)), ((), ())), precision=precision, preferred_element_type=F32
    )


def tn(a, b, precision=None):
    return lax.dot_general(
        a, b, (((0,), (0,)), ((), ())), precision=precision, preferred_element_type=F32
    )


def nn(a, b, precision=None):
    return lax.dot_general(
        a, b, (((1,), (0,)), ((), ())), precision=precision, preferred_element_type=F32
    )


WINDOW = 3


class Comm:
    def __init__(self, nl, nc, tc, fw, out_by_one=0.5, back_by_two=0.5):
        self.nl, self.nc, self.tc, self.fw = nl, nc, tc, fw
        self.square = nl == 4
        self.cut = int(tc * out_by_one) // 16 * 16
        self.back = int(tc * back_by_two) // 16 * 16
        self.c = lax.axis_index("c")
        self.g = lax.axis_index("g")

    def rows(self, i):
        return pl.ds(pl.multiple_of(i * self.tc, self.tc), self.tc)

    def after(self, m):
        return lax.rem(self.g + m, self.nl)

    def before(self, m):
        return lax.rem(self.g + self.nl - m, self.nl)

    def columns(self, c, g):
        return pl.ds(pl.multiple_of((c * self.nl + g) * self.fw, self.fw), self.fw)

    def copy(self, src, dst, send, recv, c, g):
        return pltpu.make_async_remote_copy(
            src_ref=src,
            dst_ref=dst,
            send_sem=send,
            recv_sem=recv,
            device_id={"c": c, "g": g},
            device_id_type=MESH,
        )

    def barrier(self, others=(), one_more=None):
        sem = pltpu.get_barrier_semaphore()
        everyone = [
            {"c": 1 - self.c if other else self.c, "g": self.after(m)}
            for other in (0, 1)
            for m in range(self.nl)
            if (other, m) != (0, 0)
        ] + list(others)
        for device in everyone:
            pl.semaphore_signal(sem, inc=1, device_id=device, device_id_type=MESH)
        if one_more is None:
            pl.semaphore_wait(sem, len(everyone))
        else:
            apart = self.c - lax.axis_index("h")

            @pl.when(apart != 0)
            def _():
                for device in one_more:
                    pl.semaphore_signal(sem, inc=1, device_id=device, device_id_type=MESH)

            pl.semaphore_wait(sem, len(everyone) + len(one_more) * apart * apart)

    def other(self, m):
        if m == 1:
            return self.g + 1 - 2 * lax.rem(self.g, 2)
        return lax.rem(self.g + 2, 4) if m == 2 else 3 - self.g

    def comes_from(self, m):
        if m == 0:
            return self.g
        return self.other(m) if self.square else self.before(m)

    def goes_to(self, m):
        return self.other(m) if self.square else self.after(m)

    def some(self, i, way):
        cut = self.cut
        start, size = (0, cut) if way == 0 else (cut, self.tc - cut)
        return pl.ds(pl.multiple_of(i * self.tc + start, 16), size)

    def ag_refs(self, x, full, own, sd, rd, sc, rc):
        self.x, self.full, self.own = x, full, own
        self.sd, self.rd, self.sc, self.rc = sd, rd, sc, rc

    def ag_steps(self):
        return (1, 2) if self.square else range(1, self.nl)

    def ag_direct(self, i, m):
        rows = self.rows(i)
        return self.copy(
            self.x.at[rows],
            self.full.at[rows, self.columns(self.c, self.g)],
            self.sd.at[i, m],
            self.rd.at[i, m],
            self.c,
            self.goes_to(m),
        )

    def ag_relay(self, i, way):
        rows = self.some(i, way)
        columns = self.columns(self.c, self.other(2 - way))
        return self.copy(
            self.full.at[rows, columns],
            self.full.at[rows, columns],
            self.sd.at[i, 3 * way],
            self.rd.at[i, 3 * way],
            self.c,
            self.other(1 + way),
        )

    def ag_across(self, i, m):
        rows = self.rows(i)
        columns = self.columns(self.c, self.comes_from(m))
        src = self.x.at[rows] if m == 0 else self.full.at[rows, columns]
        return self.copy(
            src,
            self.full.at[rows, columns],
            self.sc.at[i, m],
            self.rc.at[i, m],
            1 - self.c,
            self.g,
        )

    def ag_own(self, i):
        rows = self.rows(i)
        return pltpu.make_async_copy(
            self.x.at[rows],
            self.full.at[rows, self.columns(self.c, self.g)],
            self.own.at[i],
        )

    def ag_send(self, i):
        for m in self.ag_steps():
            self.ag_direct(i, m).start()
        self.ag_across(i, 0).start()
        self.ag_own(i).start()

    def ag_start(self):
        for i in range(min(WINDOW, self.nc)):
            self.ag_send(jnp.int32(i))

    def ag_forward(self, i):
        for m in self.ag_steps():
            self.ag_direct(i, m).wait_recv()
        if self.square:
            for way in (0, 1):
                self.ag_relay(i, way).start()
        for m in self.ag_steps():
            self.ag_across(i, m).start()

    def ag_corner(self, i):
        if self.square:
            for way in (0, 1):
                self.ag_relay(i, way).wait_recv()
            self.ag_across(i, 3).start()

    def ag_step(self, i, more=True):
        @pl.when(i < self.nc)
        def _():
            self.ag_forward(i)

        if more:

            @pl.when(i + WINDOW < self.nc)
            def _():
                self.ag_send(i + WINDOW)

        @pl.when((i >= 1) & (i <= self.nc))
        def _():
            self.ag_corner(i - 1)

    def ag_ahead(self):
        self.ag_step(jnp.int32(0))
        self.ag_step(jnp.int32(1))

    def ag_wait(self, i):
        self.ag_own(i).wait()
        for m in range(self.nl):
            self.ag_across(i, m).wait_recv()

    def ag_drain(self, i):
        for m in self.ag_steps():
            self.ag_direct(i, m).wait_send()
        if self.square:
            for way in (0, 1):
                self.ag_relay(i, way).wait_send()
        for m in range(self.nl):
            self.ag_across(i, m).wait_send()

    def rs_refs(self, sb, cb, gb, s1, r1, s2, r2):
        self.sb, self.cb, self.gb = sb, cb, gb
        self.s1, self.r1, self.s2, self.r2 = s1, r1, s2, r2

    def rs_across(self, i):
        return self.copy(
            self.sb.at[i, 1 - self.c],
            self.cb.at[i],
            self.s1.at[i],
            self.r1.at[i],
            1 - self.c,
            self.g,
        )

    def rs_direct(self, i, m):
        to = self.goes_to(m)
        return self.copy(
            self.sb.at[i, self.c, to],
            self.gb.at[i, m - 1],
            self.s2.at[i, m],
            self.r2.at[i, m],
            self.c,
            to,
        )

    def rs_corner(self, i, way):
        rows = pl.ds(0, self.back) if way == 0 else pl.ds(self.back, self.tc - self.back)
        return self.copy(
            self.sb.at[i, self.c, self.other(3), rows],
            self.gb.at[i, 2, rows],
            self.s2.at[i, 3 * way],
            self.r2.at[i, 3 * way],
            self.c,
            self.other(2 - way),
        )

    def rs_middle(self, i):
        self.rs_across(i).wait_recv()
        for gp in range(self.nl):
            mine = self.sb[i, self.c, gp].astype(F32) + self.cb[i, gp].astype(F32)
            self.sb[i, self.c, gp] = mine.astype(BF16)
        if self.square:
            for way in (0, 1):
                self.rs_corner(i, way).start()
        else:
            for m in range(1, self.nl):
                self.rs_direct(i, m).start()

    def rs_second(self, i):
        if not self.square:
            return
        for way in (0, 1):
            self.rs_corner(i, way).wait_recv()
            rows = pl.ds(0, self.back) if way == 0 else pl.ds(self.back, self.tc - self.back)
            to = self.other(1 + way)
            both = self.sb[i, self.c, to, rows].astype(F32) + self.gb[i, 2, rows].astype(F32)
            self.sb[i, self.c, to, rows] = both.astype(BF16)
        for m in (1, 2):
            self.rs_direct(i, m).start()

    def rs_total(self, i):
        steps = (1, 2) if self.square else range(1, self.nl)
        for m in steps:
            self.rs_direct(i, m).wait_recv()
        total = self.sb[i, self.c, self.g].astype(F32)
        for m in steps:
            total = total + self.gb[i, m - 1].astype(F32)
        return total

    def rs_drain(self, i):
        self.rs_across(i).wait_send()
        if self.square:
            for way in (0, 1):
                self.rs_corner(i, way).wait_send()
        for m in (1, 2) if self.square else range(1, self.nl):
            self.rs_direct(i, m).wait_send()

    def rs_steps(self, i):
        @pl.when((i >= 1) & (i <= self.nc))
        def _():
            self.rs_middle(i - 1)

        @pl.when((i >= 2) & (i <= self.nc + 1))
        def _():
            self.rs_second(i - 2)

    def st_refs(self, st, sa, ss, sr):
        self.st, self.sa, self.ss, self.sr = st, sa, ss, sr

    def st_copy(self, i, other, m):
        rows = self.rows(i)
        place = pl.ds(pl.multiple_of((self.c * self.nl + self.g) * 8, 8), 8)
        return self.copy(
            self.st.at[:, rows],
            self.sa.at[place, rows],
            self.ss.at[i, other * self.nl + m],
            self.sr.at[i, other * self.nl + m],
            1 - self.c if other else self.c,
            self.after(m),
        )

    def st_peers(self):
        return [(o, m) for o in (0, 1) for m in range(self.nl) if (o, m) != (0, 0)]

    def st_send(self, i):
        for o, m in self.st_peers():
            self.st_copy(i, o, m).start()
        place = pl.ds(pl.multiple_of((self.c * self.nl + self.g) * 8, 8), 8)
        self.sa[place, self.rows(i)] = self.st[:, self.rows(i)]

    def st_wait(self, i):
        for o, m in self.st_peers():
            self.st_copy(i, o, m).wait_recv()

    def st_sum(self, i):
        held = self.sa[:, self.rows(i)]
        return tn(held, jnp.full((held.shape[0], LANES), 0.125, F32), HIGHEST)

    def st_drain(self, i):
        for o, m in self.st_peers():
            self.st_copy(i, o, m).wait_send()

    def cs_refs(self, part, held, ss, sr):
        self.part, self.held, self.cs, self.cr = part, held, ss, sr

    def cs_copy(self, other, m):
        c, g = 1 - self.c if other else self.c, self.after(m)
        place = pl.ds(pl.multiple_of((self.c * self.nl + self.g) * 8, 8), 8)
        k = other * self.nl + m
        return self.copy(
            self.part.at[:, self.columns(c, g)], self.held.at[place], self.cs.at[k], self.cr.at[k], c, g
        )

    def cs_start(self, w_ref):
        for role in range(2 * self.nl):
            at = slice(role * self.fw, (role + 1) * self.fw)
            value = w_ref[:, at].astype(F32)
            self.part[:, at] = jnp.broadcast_to(row_sum(value * value), (8, self.fw))
        for o, m in self.st_peers():
            self.cs_copy(o, m).start()
        place = pl.ds(pl.multiple_of((self.c * self.nl + self.g) * 8, 8), 8)
        self.held[place, :] = self.part[:, self.columns(self.c, self.g)]

    def cs_total(self):
        for o, m in self.st_peers():
            self.cs_copy(o, m).wait_recv()
        return row_sum(self.held[...]) * 0.125

    def cs_drain(self):
        for o, m in self.st_peers():
            self.cs_copy(o, m).wait_send()


class Swap:
    def __init__(self, cm):
        self.cm = cm
        self.h = lax.axis_index("h")
        self.moves = cm.c != self.h
        self.partner = {"c": self.h, "h": cm.c}

    def far(self, src, dst, send, recv):
        return pltpu.make_async_remote_copy(
            src_ref=src, dst_ref=dst, send_sem=send, recv_sem=recv, device_id=self.partner, device_id_type=MESH
        )

    def start(self, src, dst, sems):
        @pl.when(self.moves)
        def _():
            self.far(src, dst, sems[0], sems[1]).start()

        @pl.when(jnp.logical_not(self.moves))
        def _():
            pltpu.make_async_copy(src, dst, sems[2]).start()

    def wait(self, src, dst, sems):
        @pl.when(self.moves)
        def _():
            self.far(src, dst, sems[0], sems[1]).wait_recv()

        @pl.when(jnp.logical_not(self.moves))
        def _():
            pltpu.make_async_copy(src, dst, sems[2]).wait()

    def drain(self, src, dst, sems):
        @pl.when(self.moves)
        def _():
            self.far(src, dst, sems[0], sems[1]).wait_send()


PIECES = 2


class RowMove:
    def __init__(self, swap, ny, part, e_ref, w_ref, ws, wr, wl, ys, yr):
        self.swap, self.ny, self.part, self.size = swap, ny, part, part // PIECES
        self.e, self.w = e_ref, w_ref
        self.ws, self.wr, self.wl, self.ys, self.yr = ws, wr, wl, ys, yr
        self.y = lax.axis_index("y")

    def rows(self, y, p):
        return pl.ds(pl.multiple_of(y * self.part + p * self.size, 16), self.size)

    def far(self, p):
        mine = self.rows(self.y, p)
        return self.swap.far(self.e.at[mine], self.w.at[mine], self.ws.at[p], self.wr.at[p])

    def near(self):
        every = pl.ds(0, self.part * self.ny)
        return pltpu.make_async_copy(self.e.at[every], self.w.at[every], self.wl)

    def shared(self, k, p, y):
        where = self.rows(y, p)
        return pltpu.make_async_remote_copy(
            src_ref=self.w.at[where], dst_ref=self.w.at[where],
            send_sem=self.ys.at[k - 1, p], recv_sem=self.yr.at[k - 1, p],
            device_id={"y": lax.rem(self.y + k, self.ny)}, device_id_type=MESH,
        )

    def start(self):
        @pl.when(self.swap.moves)
        def _():
            for p in range(PIECES):
                self.far(p).start()

        @pl.when(jnp.logical_not(self.swap.moves))
        def _():
            self.near().start()

    def pass_on(self):
        @pl.when(self.swap.moves)
        def _():
            for p in range(PIECES):
                self.far(p).wait_recv()
                for k in range(1, self.ny):
                    self.shared(k, p, self.y).start()

    def wait(self):
        @pl.when(self.swap.moves)
        def _():
            for k in range(1, self.ny):
                for p in range(PIECES):
                    self.shared(k, p, lax.rem(self.y + self.ny - k, self.ny)).wait_recv()

        @pl.when(jnp.logical_not(self.swap.moves))
        def _():
            self.near().wait()

    def drain(self):
        @pl.when(self.swap.moves)
        def _():
            for p in range(PIECES):
                self.far(p).wait_send()
                for k in range(1, self.ny):
                    self.shared(k, p, self.y).wait_send()


def row_move_scratch(ny):
    dma = pltpu.SemaphoreType.DMA
    between = dma((max(ny - 1, 1), PIECES))
    return [dma((PIECES,)), dma((PIECES,)), dma, between, between]


class Spread:
    def __init__(self, cm, ny, e_ref, w_ref, hs, hr, ps, pr, pn, ys, yr):
        self.cm, self.ny, self.e, self.w = cm, ny, e_ref, w_ref
        self.hs, self.hr, self.ps, self.pr, self.pn, self.ys, self.yr = hs, hr, ps, pr, pn, ys, yr
        self.y, self.h = lax.axis_index("y"), lax.axis_index("h")
        self.part = cm.fw // ny

    def place(self, hh, gg, yy):
        return self.w.at[
            pl.ds(pl.multiple_of((hh * self.cm.nl + gg) * self.cm.fw + yy * self.part, self.part), self.part)
        ]

    def piece(self, m):
        cm, to = self.cm, self.cm.after(m)
        return cm.copy(
            self.e.at[to], self.place(self.h, cm.g, self.y), self.ps.at[m], self.pr.at[m], cm.c, to
        )

    def here(self):
        return pltpu.make_async_copy(
            self.e.at[self.cm.g], self.place(self.h, self.cm.g, self.y), self.pn
        )

    def crossed(self, m, hh):
        where = self.place(hh, self.cm.before(m), self.y)
        return pltpu.make_async_remote_copy(
            src_ref=where, dst_ref=where, send_sem=self.hs.at[m], recv_sem=self.hr.at[m],
            device_id={"h": 1 - self.h}, device_id_type=MESH,
        )

    def shared(self, side, m, k, yy):
        where = self.place(self.h if side == 0 else 1 - self.h, self.cm.before(m), yy)
        return pltpu.make_async_remote_copy(
            src_ref=where, dst_ref=where,
            send_sem=self.ys.at[side, m, k - 1], recv_sem=self.yr.at[side, m, k - 1],
            device_id={"y": lax.rem(self.y + k, self.ny)}, device_id_type=MESH,
        )

    def start(self):
        self.here().start()
        for m in range(1, self.cm.nl):
            self.piece(m).start()

    def pass_own(self, m):
        if m == 0:
            self.here().wait()
        else:
            self.piece(m).wait_recv()
        if m < 2:
            self.crossed(m, self.h).start()
        for k in range(1, self.ny):
            self.shared(0, m, k, self.y).start()

    def pass_crossed(self, m):
        self.crossed(m, 1 - self.h).wait_recv()
        if m + 2 < self.cm.nl:
            self.crossed(m + 2, self.h).start()
        for k in range(1, self.ny):
            self.shared(1, m, k, self.y).start()

    def wait(self):
        for side in (0, 1):
            for m in range(self.cm.nl):
                for k in range(1, self.ny):
                    self.shared(side, m, k, lax.rem(self.y + self.ny - k, self.ny)).wait_recv()

    def drain(self):
        for m in range(self.cm.nl):
            self.crossed(m, self.h).wait_send()
            if m > 0:
                self.piece(m).wait_send()
            for side in (0, 1):
                for k in range(1, self.ny):
                    self.shared(side, m, k, self.y).wait_send()


def spread_scratch(ny, nl):
    dma = pltpu.SemaphoreType.DMA
    return [
        dma((nl,)),
        dma((nl,)),
        dma((nl,)),
        dma((nl,)),
        dma,
        dma((2, nl, max(ny - 1, 1))),
        dma((2, nl, max(ny - 1, 1))),
    ]


def movers(ny):
    y, h = lax.axis_index("y"), lax.axis_index("h")
    return [{"y": lax.rem(y + k, ny)} for k in range(1, ny)] + [{"h": 1 - h}]


def ag_scratch(nl, nc, t, d):
    return [
        pltpu.VMEM((t, d), BF16),
        pltpu.SemaphoreType.DMA((nc,)),
        pltpu.SemaphoreType.DMA((nc, nl)),
        pltpu.SemaphoreType.DMA((nc, nl)),
        pltpu.SemaphoreType.DMA((nc, nl)),
        pltpu.SemaphoreType.DMA((nc, nl)),
    ]


def rs_scratch(nl, nc, tc, fw):
    return [
        pltpu.VMEM((nc, 2, nl, tc, fw), BF16),
        pltpu.VMEM((nc, nl, tc, fw), BF16),
        pltpu.VMEM((nc, nl - 1, tc, fw), BF16),
        pltpu.SemaphoreType.DMA((nc,)),
        pltpu.SemaphoreType.DMA((nc,)),
        pltpu.SemaphoreType.DMA((nc, nl)),
        pltpu.SemaphoreType.DMA((nc, nl)),
    ]


def st_scratch(nl, nc, t):
    return [
        pltpu.VMEM((2 * nl * 8, t), F32),
        pltpu.SemaphoreType.DMA((nc, 2 * nl)),
        pltpu.SemaphoreType.DMA((nc, 2 * nl)),
    ]


def cs_scratch(nl, d, fw):
    return [
        pltpu.VMEM((8, d), F32),
        pltpu.VMEM((2 * nl * 8, fw), F32),
        pltpu.SemaphoreType.DMA((2 * nl,)),
        pltpu.SemaphoreType.DMA((2 * nl,)),
    ]


VM = pl.BlockSpec(memory_space=pltpu.VMEM)
SM = pl.BlockSpec(memory_space=pltpu.SMEM)
ANY = pl.BlockSpec(memory_space=pl.ANY)


class Background:
    def __init__(self, loads, stores, step):
        self.loads, self.stores, self.step = loads, stores, step
        for copy in loads:
            copy.start()

    def ready(self):
        for copy in self.loads:
            copy.wait()

    def copy(self, k, i):
        held, out, sems = self.stores[k]
        rows = pl.ds(pl.multiple_of(i * self.step, self.step), self.step)
        return pltpu.make_async_copy(held.at[rows], out.at[rows], sems.at[i])

    def store(self, i, *which):
        for k in which:
            self.copy(k, i).start()

    def stored(self, i):
        for k in self.stores:
            self.copy(k, i).wait()


def call(kernel, name, outs, in_specs, out_specs, scratch, collective, us, args, late=(), flow=(), step=1):
    extra = {}
    if collective is not None:
        extra = {"collective_id": collective, "has_side_effects": True}
    single = not isinstance(outs, tuple)
    results = (outs,) if single else outs
    in_specs, out_specs = list(in_specs), [out_specs] if single else list(out_specs)
    n_in, n_out, n_scratch = len(args), len(results), len(scratch)
    dma = pltpu.SemaphoreType.DMA
    more = []
    for k in late:
        in_specs[k] = ANY
        more += [pltpu.VMEM(args[k].shape, args[k].dtype), dma]
    for k in flow:
        out_specs[k] = ANY
        more += [pltpu.VMEM(results[k].shape, results[k].dtype), dma((results[k].shape[0] // step,))]

    def whole(*refs):
        ins, results_here = list(refs[:n_in]), list(refs[n_in : n_in + n_out])
        own = refs[n_in + n_out : n_in + n_out + n_scratch]
        extras = list(refs[n_in + n_out + n_scratch :])
        loads, stores = [], {}
        for k in late:
            held, sem = extras.pop(0), extras.pop(0)
            loads.append(pltpu.make_async_copy(ins[k], held, sem))
            ins[k] = held
        for k in flow:
            held, sems = extras.pop(0), extras.pop(0)
            stores[k] = (held, results_here[k], sems)
            results_here[k] = held
        kernel(Background(loads, stores, step), *ins, *results_here, *own)

    return pl.pallas_call(
        whole,
        name=name,
        out_shape=outs,
        in_specs=in_specs,
        out_specs=out_specs[0] if single else tuple(out_specs),
        scratch_shapes=scratch + more,
        compiler_params=pltpu.CompilerParams(vmem_limit_bytes=VMEM_LIMIT, **extra),
        cost_estimate=pl.CostEstimate(
            flops=int(us * 5e8), bytes_accessed=int(us * 3e6), transcendentals=0
        ),
    )(*args)


def shape(s, dtype):
    return jax.ShapeDtypeStruct(s, dtype)


def ones_rows(values):
    folded = values[:, :LANES]
    for k in range(1, values.shape[1] // LANES):
        folded = folded + values[:, k * LANES : (k + 1) * LANES]
    return nt(jnp.ones((8, LANES), F32), folded, HIGHEST)


def row_sum(values):
    return jnp.sum(values, axis=0, keepdims=True)


def merged_tile(frozen, down, up):
    return frozen.astype(F32) + SCALE * nn(down, up, HIGHEST)


def qkv_forward(
    cfg, ny, npad, nf, x_in, w_qkv, a_qkv, b_qkv, tail_qkv, gains, rows_out, small, small_gu, cosine, sine,
    w_gu, a_gu, b_gu, tail_gu,
):
    t, fw, d, nl, nc, tc = cfg
    width = 3 * fw
    wide = width + LANES
    part = fw // ny
    ff_half = w_gu.shape[2] // 2

    def kernel(
        io, x_ref, wq_hbm, aq_ref, bq_ref, tq_ref, gain_ref, eo_ref, m_ref, mg_ref, cos_ref, sin_ref,
        wg_hbm, ag_ref, bg_ref, tg_ref,
        xs_ref, w_ref, wo_ref, ms_ref, mgs_ref, sc_ref, sq_ref, qkv_ref, lora_ref, rate_ref, eg_ref, out_ref,
        full, own, sd, rd, sc, rc, keep, xs_s, xs_r, xs_l, small_sems,
        hs, hr, ps, pr, pn, ys, yr, os, orr, ol, oys, oyr,
        e_ref, wq, wg, wload,
    ):
        cm = Comm(nl, nc, tc, fw, out_by_one=0.9375)
        cm.ag_refs(xs_ref, full, own, sd, rd, sc, rc)
        swap = Swap(cm)
        weights = Spread(cm, ny, e_ref, w_ref, hs, hr, ps, pr, pn, ys, yr)
        mine = pl.ds(pl.multiple_of(weights.y * part, part), part)
        load_q = pltpu.make_async_copy(
            wq_hbm.at[:, mine, pl.ds(pl.multiple_of(cm.c * (d // 2), LANES), d // 2)], wq, wload.at[0]
        )
        load_g = pltpu.make_async_copy(
            wg_hbm.at[:, mine, pl.ds(pl.multiple_of(cm.c * ff_half, LANES), ff_half)], wg, wload.at[1]
        )
        load_q.start()
        load_g.start()
        output = RowMove(swap, ny, fw // ny, eo_ref, wo_ref, os, orr, ol, oys, oyr)
        cm.barrier(movers(ny), [swap.partner])

        def token_swap(i):
            rows = cm.rows(i)
            return x_ref.at[rows], xs_ref.at[rows], (xs_s.at[i], xs_r.at[i], xs_l.at[i])

        m_swap = (m_ref, ms_ref, tuple(small_sems.at[k] for k in range(3)))
        mg_swap = (mg_ref, mgs_ref, tuple(small_sems.at[k] for k in range(3, 6)))

        def start_swap(i, carry_on):
            swap.start(*token_swap(i))
            return carry_on

        lax.fori_loop(0, min(WINDOW, nc), start_swap, 0)
        swap.start(*m_swap)
        swap.start(*mg_swap)
        load_q.wait()
        gain_attn, gain_ffn = gain_ref[mine, 0:1], gain_ref[mine, 1:2]
        for gg in range(nl):
            columns = pl.ds(pl.multiple_of((cm.c * nl + gg) * fw, fw), fw)
            for k in range(3):
                tile = merged_tile(wq[k, :, gg * fw : (gg + 1) * fw], aq_ref[k, mine, :], bq_ref[k, :, columns])
                e_ref[gg, :, k * fw : (k + 1) * fw] = (tile * gain_attn).astype(BF16)
            e_ref[gg, :, width:] = tq_ref[mine, :]
        weights.start()

        def gate_up(gg):
            off = gg * nf % LANES
            window = -(-(off + nf) // LANES) * LANES
            for k in range(2):
                raw = wg[k, :, gg * nf - off : gg * nf - off + window].astype(F32)
                if off:
                    raw = pltpu.roll(raw, window - off, 1)
                tile = merged_tile(raw[:, :npad], ag_ref[k, mine, :], bg_ref[k, cm.c * nl + gg]) * gain_ffn
                lane = lax.broadcasted_iota(jnp.int32, tile.shape, 1)
                eg_ref[gg, :, k * npad : (k + 1) * npad] = jnp.where(
                    lane < nf, tile, tg_ref[k, mine, :].astype(F32)
                ).astype(BF16)

        def gather(i, carry_on):
            swap.wait(*token_swap(i))

            @pl.when(i + WINDOW < nc)
            def _():
                swap.start(*token_swap(i + WINDOW))

            cm.ag_send(i)
            return carry_on

        def forward(i, carry_on):
            cm.ag_step(i, more=False)
            return carry_on

        weights.pass_own(0)
        half = nc // 2
        lax.fori_loop(0, half, gather, 0)
        weights.pass_own(1)
        lax.fori_loop(half, nc, gather, 0)
        for m in range(2, nl):
            weights.pass_own(m)
        load_g.wait()
        io.ready()
        for m in range(nl):
            lax.fori_loop(nc * m // nl, nc * (m + 1) // nl, forward, 0)
            gate_up(m)
            weights.pass_crossed(m)
        output.start()
        cm.ag_step(jnp.int32(nc), more=False)

        def stored(i):
            rows = cm.rows(i)
            return pltpu.make_async_copy(full.at[rows], out_ref.at[rows], keep.at[i])

        def rates(i, carry_on):
            cm.ag_wait(i)
            stored(i).start()
            wide_block = full[cm.rows(i), :].astype(F32)
            rate = lax.rsqrt(jnp.sum(wide_block * wide_block, axis=1, keepdims=True) / d + EPS)
            rate_ref[cm.rows(i), :] = jnp.broadcast_to(rate, (tc, LANES))
            return carry_on

        lax.fori_loop(0, nc, rates, 0)
        weights.wait()
        output.pass_on()

        def squares(i, total):
            rows = pl.ds(pl.multiple_of(i * fw, fw), fw)
            tail = w_ref[rows, width:].astype(F32)
            gain = tail[:, 3 * RANK : 3 * RANK + 1] + tail[:, 3 * RANK + 1 : 3 * RANK + 2]
            value = w_ref[rows, :width].astype(F32) * (1.0 / gain)
            return total + row_sum(value * value)

        square = lax.fori_loop(0, 2 * nl, squares, jnp.zeros((1, width), F32))
        swap.wait(*m_swap)
        sq_ref[...] = jnp.broadcast_to(square, (8, width))
        for k in range(3):
            at = slice(k * fw, (k + 1) * fw)
            sc_ref[:, at] = jnp.broadcast_to(ms_ref[k : k + 1, :] * lax.rsqrt(square[:, at]), (8, fw))
        sc_ref[:, width:] = jnp.ones((8, LANES), F32)

        big = 2 * tc if nc % 2 == 0 else tc

        def body(i, carry_on):
            rows = pl.ds(pl.multiple_of(i * big, big), big)
            out = nn(full[rows, :], w_ref[...]) * rate_ref[rows, 0:1] * sc_ref[0:1, :]
            cosine_here, sine_here = cos_ref[rows, :], sin_ref[rows, :]
            for k in range(3):
                for hd in range(fw // HD):
                    at = k * fw + hd * HD
                    value = out[:, at : at + HD]
                    if k < 2:
                        value = value * cosine_here + pltpu.roll(value, HD // 2, 1) * sine_here
                    qkv_ref[rows, at : at + HD] = value.astype(BF16)
            lora_ref[rows, :] = out[:, width:].astype(BF16)
            for k in range(big // tc):
                io.store(i * (big // tc) + k, 7, 8, 9)
            return carry_on

        lax.fori_loop(0, t // big, body, 0)
        output.wait()
        swap.wait(*mg_swap)

        def drain(i, carry_on):
            cm.ag_drain(i)
            stored(i).wait()
            io.stored(i)
            swap.drain(*token_swap(i))
            return carry_on

        lax.fori_loop(0, nc, drain, 0)
        swap.drain(*m_swap)
        swap.drain(*mg_swap)
        weights.drain()
        output.drain()

    dma = pltpu.SemaphoreType.DMA
    return call(
        kernel,
        "qkv_forward",
        (
            shape((t, fw), BF16),
            shape((d, wide), BF16),
            shape(rows_out.shape, BF16),
            shape(small.shape, F32),
            shape(small_gu.shape, F32),
            shape((8, wide), F32),
            shape((8, width), F32),
            shape((t, width), BF16),
            shape((t, LANES), BF16),
            shape((t, LANES), F32),
            shape((nl, part, 2 * npad), BF16),
            shape((t, d), BF16),
        ),
        [VM, ANY, VM, VM, VM, VM, ANY, VM, VM, VM, VM, ANY, VM, VM, VM],
        (VM,) * 11 + (ANY,),
        ag_scratch(nl, nc, t, d)
        + [dma((nc,))] * 4
        + [dma((6,))]
        + spread_scratch(ny, nl)
        + row_move_scratch(ny)
        + [
            pltpu.VMEM((nl, part, wide), BF16),
            pltpu.VMEM((3, part, d // 2), BF16),
            pltpu.VMEM((2, part, ff_half), BF16),
            dma((2,)),
        ],
        1,
        90,
        (
            x_in, w_qkv, a_qkv, b_qkv, tail_qkv, gains, rows_out, small, small_gu, cosine, sine,
            w_gu, a_gu, b_gu, tail_gu,
        ),
        late=(9, 10, 12, 13, 14),
        flow=(7, 8, 9),
        step=tc,
    )


def allowed_of(key_segment, query_segment, j, i, block):
    key_at = j * block + lax.broadcasted_iota(jnp.int32, (block, block), 0)
    query_at = i * block + lax.broadcasted_iota(jnp.int32, (block, block), 1)
    return (key_segment == query_segment) & (key_at <= query_at)


def attention_forward(cfg, qkv, seg_column, seg_row, first_block, block):
    t, fw = cfg[0], cfg[1]
    heads = fw // HD

    def kernel(io, qkv_ref, sc_ref, sr_ref, first_ref, out_ref, lse_ref):
        def at(i):
            return pl.ds(pl.multiple_of(i * block, block), block)

        def columns(k, hd):
            return slice(k * fw + hd * HD, k * fw + (hd + 1) * HD)

        def one_query(i, carry_on):
            queries = [qkv_ref[at(i), columns(0, hd)] for hd in range(heads)]
            query_segment = sr_ref[0:1, at(i)]

            def one_key(j, carry):
                allowed = allowed_of(sc_ref[at(j), 0:1], query_segment, j, i, block)
                out = []
                for hd in range(heads):
                    top, total, acc = carry[hd]
                    s = nt(qkv_ref[at(j), columns(1, hd)], queries[hd]) * (HD**-0.5)
                    s = jnp.where(allowed, s, MASKED)
                    new = jnp.maximum(top, jnp.max(s, axis=0, keepdims=True))
                    p = jnp.exp(s - new)
                    shrink = jnp.exp(top - new)
                    total = total * shrink + jnp.sum(p, axis=0, keepdims=True)
                    acc = acc * shrink + tn(qkv_ref[at(j), columns(2, hd)], p.astype(BF16))
                    out.append((new, total, acc))
                return tuple(out)

            first = (
                jnp.full((1, block), MASKED, F32),
                jnp.zeros((1, block), F32),
                jnp.zeros((HD, block), F32),
            )
            out = lax.fori_loop(first_ref[i], i + 1, one_key, (first,) * heads)
            for hd in range(heads):
                top, total, acc = out[hd]
                out_ref[at(i), hd * HD : (hd + 1) * HD] = (acc / total).T.astype(BF16)
                lse_ref[hd * 8 : hd * 8 + 8, at(i)] = jnp.broadcast_to(
                    top + jnp.log(total), (8, block)
                )
            return carry_on

        lax.fori_loop(0, t // block, one_query, 0)

    return call(
        kernel,
        "attention_forward",
        (shape((t, fw), BF16), shape((heads * 8, t), F32)),
        [VM, VM, VM, SM],
        (VM, VM),
        [],
        None,
        15,
        (qkv, seg_column, seg_row, first_block),
    )


def out_forward(cfg, ny, npad, attended, weights, x, magnitude, blocks, w_down, a_down, b_down):
    t, fw, d, nl, nc, tc = cfg
    wide = blocks.shape[2]
    nf = w_down.shape[0]
    part = -(-(-(-nf // ny)) // (16 * PIECES)) * 16 * PIECES
    tiles = 2 * nl

    def kernel(
        io, a_ref, w_ref, x_ref, m_ref, e_ref, wdown_ref, ad_ref, bd_ref,
        mid_ref, u_ref, st_ref, sc_ref, sq_ref, lora_ref, wg_ref, wd_ref,
        sb, cb, gb, s1, r1, s2, r2, cpart, cheld, css, csr,
        hs, hr, ps, pr, pn, ys, yr, dws, dwr, dwl, dys, dyr, ed_ref,
    ):
        cm = Comm(nl, nc, tc, fw, back_by_two=0.0625)
        cm.rs_refs(sb, cb, gb, s1, r1, s2, r2)
        cm.cs_refs(cpart, cheld, css, csr)
        columns = Spread(cm, ny, e_ref, wg_ref, hs, hr, ps, pr, pn, ys, yr)
        swap = Swap(cm)
        down_rows = RowMove(swap, ny, part, ed_ref, wd_ref, dws, dwr, dwl, dys, dyr)
        cm.barrier(movers(ny), [swap.partner])
        columns.start()
        cm.cs_start(w_ref)
        columns.pass_own(0)
        if part * ny > nf:
            ed_ref[nf:, :] = jnp.zeros((part * ny - nf, ed_ref.shape[1]), BF16)
        if part * ny < npad:
            wd_ref[part * ny :, :] = jnp.zeros((npad - part * ny, wd_ref.shape[1]), BF16)
        io.ready()
        ed_ref[:nf, d:] = jnp.zeros((nf, LANES), BF16)
        ed_ref[:nf, d : d + RANK] = ad_ref[...].astype(BF16)

        def down_tile(k):
            at = pl.ds(pl.multiple_of(k * fw, fw), fw)
            ed_ref[:nf, at] = merged_tile(wdown_ref[:, at], ad_ref[...], bd_ref[:, at]).astype(BF16)

        def body(i, carry_on):
            @pl.when(i < nc)
            def _():
                block = a_ref[cm.rows(i), :]
                for role in range(2 * nl):
                    sb[i, role // nl, role % nl] = nn(
                        block, w_ref[:, role * fw : (role + 1) * fw]
                    ).astype(BF16)
                cm.rs_across(i).start()
                lora_ref[cm.rows(i), :] = nn(block, w_ref[:, d:]).astype(BF16)
                io.store(i, 5)

            cm.rs_steps(i)

            @pl.when(i == 3)
            def _():
                total = cm.cs_total()
                sq_ref[...] = jnp.broadcast_to(total, (8, fw))
                sc_ref[...] = jnp.broadcast_to(m_ref[3:4, :] * lax.rsqrt(total), (8, fw))
                for m in range(2, nl):
                    columns.pass_own(m)

            @pl.when(i == 1)
            def _():
                columns.pass_own(1)

            @pl.when((i >= 1) & (i <= tiles))
            def _():
                down_tile(i - 1)

            @pl.when(i == min(6, nc + 1))
            def _():
                columns.pass_crossed(0)

            @pl.when(i == nc + 2)
            def _():
                columns.pass_crossed(1)

            @pl.when((i >= 3) & (i <= nc + 2))
            def _():
                rows = cm.rows(i - 3)
                middle = x_ref[rows, :].astype(F32) + cm.rs_total(i - 3) * sc_ref[0:1, :]
                mid_ref[rows, :] = middle
                u_ref[rows, :] = middle.astype(BF16)
                st_ref[:, rows] = ones_rows(middle * middle)
                io.store(i - 3, 0, 1)

            return carry_on

        lax.fori_loop(0, max(nc + 3, tiles + 1), body, 0)

        def drain(i, carry_on):
            cm.rs_drain(i)
            io.stored(i)
            return carry_on

        down_rows.start()
        for m in range(2, nl):
            columns.pass_crossed(m)
        down_rows.pass_on()
        columns.wait()
        down_rows.wait()
        lax.fori_loop(0, nc, drain, 0)
        cm.cs_drain()
        columns.drain()
        down_rows.drain()

    return call(
        kernel,
        "out_forward",
        (
            shape((t, fw), F32),
            shape((t, fw), BF16),
            shape((8, t), F32),
            shape((8, fw), F32),
            shape((8, fw), F32),
            shape((t, LANES), BF16),
            shape((d, wide), BF16),
            shape((npad, d + LANES), BF16),
        ),
        [VM] * 4 + [ANY, VM, VM, VM],
        (VM,) * 6 + (ANY, VM),
        rs_scratch(nl, nc, tc, fw)
        + cs_scratch(nl, d, fw)
        + spread_scratch(ny, nl)
        + row_move_scratch(ny)
        + [pltpu.VMEM((part * ny, d + LANES), BF16)],
        2,
        90,
        (attended, weights, x, magnitude, blocks, w_down, a_down, b_down),
        late=(5, 6, 7),
        flow=(0, 1, 5),
        step=tc,
    )


def ffn_forward(cfg, npad, nf, u, stats, w_gu, m_gu, w_down, small, middle, cotangent):
    t, fw, d, nl, nc, tc = cfg

    def kernel(
        io, u_ref, st_ref, wg_ref, mg_ref, wd_ref, m_ref, mid_ref, cin_ref,
        gu_ref, hid_ref, out_ref, gm_ref, rate_ref, gp_ref, sg_ref, qg_ref, sd_ref, qd_ref, lora_ref, cot_ref, uf_ref,
        full, own, sd, rd, sc, rc, sb, cb, gb, s1, r1, s2, r2, sa, ss, sr, cpart, cheld, css, csr, keep,
        stage, cs_s, cs_r, cs_l, bs_s, bs_r, bs_l,
    ):
        cm = Comm(nl, nc, tc, fw, out_by_one=0.75, back_by_two=0.25)
        cm.ag_refs(u_ref, full, own, sd, rd, sc, rc)
        cm.rs_refs(sb, cb, gb, s1, r1, s2, r2)
        cm.st_refs(st_ref, sa, ss, sr)
        cm.cs_refs(cpart, cheld, css, csr)
        swap = Swap(cm)
        cm.barrier((), [swap.partner])

        def cot_swap(i):
            rows = cm.rows(i)
            return cin_ref.at[rows], cot_ref.at[rows], (cs_s.at[i], cs_r.at[i], cs_l.at[i])

        def out_swap(i):
            rows = cm.rows(i)
            return stage.at[rows], out_ref.at[rows], (bs_s.at[i], bs_r.at[i], bs_l.at[i])

        def stats_out(i, carry_on):
            cm.st_send(i)
            return carry_on

        lax.fori_loop(0, nc, stats_out, 0)
        cm.ag_start()
        io.ready()

        def cot_out(i, carry_on):
            swap.start(*cot_swap(i))
            return carry_on


        def squares(i, total):
            rows = pl.ds(pl.multiple_of(i * fw, fw), fw)
            gain = (
                wg_ref[rows, nf + RANK : nf + RANK + 1].astype(F32)
                + wg_ref[rows, nf + RANK + 1 : nf + RANK + 2].astype(F32)
            )
            value = wg_ref[rows, :].astype(F32) * (1.0 / gain)
            return total + row_sum(value * value)

        square = lax.fori_loop(0, 2 * nl, squares, jnp.zeros((1, 2 * npad), F32))
        column = lax.rem(lax.broadcasted_iota(jnp.int32, (1, 2 * npad), 1), npad)
        square = jnp.where(column < nf, square, 1.0)
        qg_ref[...] = jnp.broadcast_to(square, (8, 2 * npad))
        sg_ref[...] = jnp.broadcast_to(mg_ref[...] * lax.rsqrt(square), (8, 2 * npad))
        cm.ag_ahead()
        gm_ref[...] = jnp.zeros_like(gm_ref)

        def stored(i):
            rows = cm.rows(i)
            return pltpu.make_async_copy(full.at[rows], uf_ref.at[rows], keep.at[i])

        cm.cs_start(wd_ref)
        lax.fori_loop(0, nc, cot_out, 0)

        def body(i, carry_on):
            @pl.when(i < nc)
            def _():
                cm.ag_step(i + 2)
                cm.ag_wait(i)
                cm.st_wait(i)
                stored(i).start()
                rows = cm.rows(i)
                rate = lax.rsqrt(cm.st_sum(i) / d + EPS)
                rate_ref[rows, :] = rate
                out = nn(full[rows, :], wg_ref[...]) * rate[:, 0:1] * sg_ref[0:1, :]
                gu_ref[rows, :] = out.astype(BF16)
                gate, up = out[:, :npad], out[:, npad:]
                hidden = (gate / (1.0 + jnp.exp(-gate)) * up).astype(BF16)
                hid_ref[rows, :] = hidden
                for role in range(2 * nl):
                    sb[i, role // nl, role % nl] = nn(
                        hidden, wd_ref[:, role * fw : (role + 1) * fw]
                    ).astype(BF16)
                cm.rs_across(i).start()
                lora_ref[rows, :] = nn(hidden, wd_ref[:, d:]).astype(BF16)
                io.store(i, 0, 1, 4, 10)

            cm.rs_steps(i)

            @pl.when(i == 3)
            def _():
                total = cm.cs_total()
                qd_ref[...] = jnp.broadcast_to(total, (8, fw))
                sd_ref[...] = jnp.broadcast_to(m_ref[4:5, :] * lax.rsqrt(total), (8, fw))

            @pl.when(i >= 3)
            def _():
                rows = cm.rows(i - 3)
                down = cm.rs_total(i - 3) * sd_ref[0:1, :]
                stage[rows, :] = (mid_ref[rows, :] + down).astype(BF16)
                swap.start(*out_swap(i - 3))
                swap.wait(*cot_swap(i - 3))
                seed = cot_ref[rows, :].astype(F32)
                gm_ref[0:1, :] += row_sum(seed * down)
                gp_ref[rows, :] = (seed * sd_ref[0:1, :]).astype(BF16)
                io.store(i - 3, 5)

            return carry_on

        lax.fori_loop(0, nc + 3, body, 0)

        def drain(i, carry_on):
            cm.ag_drain(i)
            cm.rs_drain(i)
            cm.st_drain(i)
            stored(i).wait()
            io.stored(i)
            swap.wait(*out_swap(i))
            swap.drain(*out_swap(i))
            swap.drain(*cot_swap(i))
            return carry_on

        lax.fori_loop(0, nc, drain, 0)
        cm.cs_drain()

    dma = pltpu.SemaphoreType.DMA
    return call(
        kernel,
        "ffn_forward",
        (
            shape((t, 2 * npad), BF16),
            shape((t, npad), BF16),
            shape((t, fw), BF16),
            shape((8, fw), F32),
            shape((t, LANES), F32),
            shape((t, fw), BF16),
            shape((8, 2 * npad), F32),
            shape((8, 2 * npad), F32),
            shape((8, fw), F32),
            shape((8, fw), F32),
            shape((t, LANES), BF16),
            shape((t, fw), BF16),
            shape((t, d), BF16),
        ),
        [VM] * 8,
        (VM,) * 12 + (ANY,),
        ag_scratch(nl, nc, t, d)
        + rs_scratch(nl, nc, tc, fw)
        + st_scratch(nl, nc, t)
        + cs_scratch(nl, d, fw)
        + [dma((nc,)), pltpu.VMEM((t, fw), BF16)]
        + [dma((nc,))] * 6,
        3,
        110,
        (u, stats, w_gu, m_gu, w_down, small, middle, cotangent),
        late=(2, 4, 6),
        flow=(0, 1, 4, 5, 10),
        step=tc,
    )


def ffn_backward(cfg, npad, gp, gu, w_gu, sc_gu, b_gu, w_down, b_down, rate, cotangent, middle, x, sc_out):
    t, fw, d, nl, nc, tc = cfg

    def kernel(
        io, gp_ref, gu_hbm, wg_ref, sg_ref, bg_ref, wd_ref, bd_ref, rate_ref, cot_ref, mid_ref, x_ref, so_ref,
        dm_ref, go_ref, gmo_ref, gm_ref, lg_ref, ld_ref, dp_hbm, gf_ref,
        full, own, sd, rd, sc, rc, sb, cb, gb, s1, r1, s2, r2, sa, ss, sr, st, gu_s, keep, load, save,
    ):
        cm = Comm(nl, nc, tc, fw)
        cm.ag_refs(gp_ref, full, own, sd, rd, sc, rc)
        cm.rs_refs(sb, cb, gb, s1, r1, s2, r2)
        cm.st_refs(st, sa, ss, sr)

        def loaded(i):
            rows = cm.rows(i)
            return pltpu.make_async_copy(gu_hbm.at[rows], gu_s.at[rows], load.at[i])

        def saved(i):
            rows = cm.rows(i)
            return pltpu.make_async_copy(gu_s.at[rows], dp_hbm.at[rows], save.at[i])

        def stored(i):
            rows = cm.rows(i)
            return pltpu.make_async_copy(full.at[rows], gf_ref.at[rows], keep.at[i])

        cm.barrier()
        cm.ag_start()

        def start_loads(i, carry_on):
            loaded(i).start()
            return carry_on

        lax.fori_loop(0, nc, start_loads, 0)
        cm.ag_ahead()
        io.ready()
        gm_ref[...] = jnp.zeros_like(gm_ref)
        gmo_ref[...] = jnp.zeros_like(gmo_ref)

        def body(i, carry_on):
            @pl.when(i < nc)
            def _():
                cm.ag_step(i + 2)
                cm.ag_wait(i)
                stored(i).start()
                loaded(i).wait()
                rows = cm.rows(i)
                block = full[rows, :]
                dh = nt(block, wd_ref[:, :d])
                ld_ref[rows, :] = nt(block, bd_ref[...]).astype(BF16)
                gate = gu_s[rows, :npad].astype(F32)
                up = gu_s[rows, npad:].astype(F32)
                sig = 1.0 / (1.0 + jnp.exp(-gate))
                dgate = dh * up * (sig * (1.0 + gate * (1.0 - sig)))
                dup = dh * (gate * sig)
                pg, pu = dgate * gate, dup * up
                gm_ref[0:1, :npad] += jnp.sum(pg, axis=0, keepdims=True)
                gm_ref[0:1, npad:] += jnp.sum(pu, axis=0, keepdims=True)
                st[:, rows] = ones_rows(pg + pu)
                cm.st_send(i)
                gu_s[rows, :npad] = (dgate * sg_ref[0:1, :npad]).astype(BF16)
                gu_s[rows, npad:] = (dup * sg_ref[0:1, npad:]).astype(BF16)
                saved(i).start()
                dp = gu_s[rows, :]
                lg_ref[rows, :] = (nt(dp, bg_ref[...].astype(BF16)) * rate_ref[rows, :]).astype(BF16)
                io.store(i, 4, 5)
                for role in range(2 * nl):
                    sb[i, role // nl, role % nl] = nt(
                        dp, wg_ref[role * fw : (role + 1) * fw, :]
                    ).astype(BF16)
                cm.rs_across(i).start()

            cm.rs_steps(i)

            @pl.when(i >= 3)
            def _():
                k = i - 3
                rows = cm.rows(k)
                cm.st_wait(k)
                r = rate_ref[rows, 0:1]
                inner = cm.st_sum(k)[:, 0:1]
                mid = mid_ref[rows, :]
                dm = (
                    cot_ref[rows, :].astype(F32)
                    + r * cm.rs_total(k)
                    - mid * (r * r * inner / d)
                )
                dm_ref[rows, :] = dm
                go_ref[rows, :] = (dm * so_ref[0:1, :]).astype(BF16)
                io.store(k, 0, 1)
                gmo_ref[0:1, :] += jnp.sum(
                    dm * (mid - x_ref[rows, :].astype(F32)), axis=0, keepdims=True
                )

            return carry_on

        lax.fori_loop(0, nc + 3, body, 0)

        def drain(i, carry_on):
            cm.ag_drain(i)
            cm.rs_drain(i)
            cm.st_drain(i)
            stored(i).wait()
            saved(i).wait()
            io.stored(i)
            return carry_on

        lax.fori_loop(0, nc, drain, 0)

    return call(
        kernel,
        "ffn_backward",
        (
            shape((t, fw), F32),
            shape((t, fw), BF16),
            shape((8, fw), F32),
            shape((8, 2 * npad), F32),
            shape((t, LANES), BF16),
            shape((t, LANES), BF16),
            shape((t, 2 * npad), BF16),
            shape((t, d), BF16),
        ),
        [VM, ANY] + [VM] * 10,
        (VM,) * 6 + (ANY, ANY),
        ag_scratch(nl, nc, t, d)
        + rs_scratch(nl, nc, tc, fw)
        + st_scratch(nl, nc, t)
        + [
            pltpu.VMEM((8, t), F32),
            pltpu.VMEM((t, 2 * npad), BF16),
            pltpu.SemaphoreType.DMA((nc,)),
            pltpu.SemaphoreType.DMA((nc,)),
            pltpu.SemaphoreType.DMA((nc,)),
        ],
        4,
        120,
        (gp, gu, w_gu, sc_gu, b_gu, w_down, b_down, rate, cotangent, middle, x, sc_out),
        late=(2, 4, 5, 6, 7, 8, 9, 10),
        flow=(0, 1, 4, 5),
        step=tc,
    )


def gain_rows(tail, at):
    lane = lax.broadcasted_iota(jnp.int32, (8, LANES), 1)
    pick = jnp.where((lane == at) | (lane == at + 1), 1.0, 0.0).astype(BF16)
    column = tail[:, at : at + 1].astype(F32) + tail[:, at + 1 : at + 2].astype(F32)
    return nt(pick, tail)[0:1, :], column


class Stream:
    def __init__(self, sources, slots, sems, step):
        self.sources, self.slots, self.sems, self.step = sources, slots, sems, step

    def copies(self, i):
        rows = pl.ds(pl.multiple_of(i * self.step, self.step), self.step)
        slot = lax.rem(i, 2)
        return [
            pltpu.make_async_copy(src.at[rows, columns], held.at[slot], self.sems.at[k, slot])
            for k, ((src, columns), held) in enumerate(zip(self.sources, self.slots))
        ]

    def start(self, i):
        for copy in self.copies(i):
            copy.start()

    def wait(self, i):
        for copy in self.copies(i):
            copy.wait()
        return [held[lax.rem(i, 2)] for held in self.slots]


def stream_scratch(step, widths):
    return [pltpu.VMEM((2, step, n), BF16) for n in widths] + [pltpu.SemaphoreType.DMA((len(widths), 2))]


def out_backward(
    cfg, npad, nf, go, weights, b_out, ratios, w_gu, w_down, up_gu, b_down, gm_gu, square_gu, m_gu,
    u_full, lg_gu, gu, dp_gu, hidden, lg_down, lora_down, gp_full,
):
    t, fw, d, nl, nc, tc = cfg
    off = nf - (npad - LANES)
    widths = (d, LANES, LANES, LANES, 2 * npad, npad, LANES, LANES, d)

    def kernel(
        io, go_ref, w_ref, b_ref, q_ref, wg_ref, wd_ref, up_ref, bd_ref, gm_ref, sq_ref, m_ref,
        uf_hbm, lg_hbm, gu_hbm, dp_hbm, hid_hbm, ld_hbm, lo2_hbm, gp_hbm,
        da_ref, lo_ref, qs_ref, sh_ref, lc_ref, gf_ref,
        full, own, sd, rd, sc, rc, keep, qss, qsr, acc_a, acc_g, acc_u, acc_d, acc_p, *streams,
    ):
        cm = Comm(nl, nc, tc, fw)
        cm.ag_refs(go_ref, full, own, sd, rd, sc, rc)
        every = lambda n: pl.ds(0, n)
        stream = Stream(
            [
                (uf_hbm, every(d)),
                (lg_hbm, every(LANES)),
                (gu_hbm, pl.ds(npad - LANES, LANES)),
                (gu_hbm, pl.ds(2 * npad - LANES, LANES)),
                (dp_hbm, every(2 * npad)),
                (hid_hbm, every(npad)),
                (ld_hbm, every(LANES)),
                (lo2_hbm, every(LANES)),
                (gp_hbm, every(d)),
            ],
            streams[:-1],
            streams[-1],
            tc,
        )
        stream.start(jnp.int32(0))
        cm.barrier()

        def ratio_copy(o, m):
            k = o * nl + m
            return cm.copy(
                q_ref, qs_ref.at[:, cm.columns(cm.c, cm.g)], qss.at[k], qsr.at[k], 1 - cm.c if o else cm.c, cm.after(m)
            )

        cm.ag_start()
        for o, m in cm.st_peers():
            ratio_copy(o, m).start()
        qs_ref[:, cm.columns(cm.c, cm.g)] = q_ref[...]
        for acc in (acc_a, acc_g, acc_u, acc_d, acc_p):
            acc[...] = jnp.zeros_like(acc)
        cm.ag_ahead()
        io.ready()

        def stored(i):
            rows = cm.rows(i)
            return pltpu.make_async_copy(full.at[rows], gf_ref.at[rows], keep.at[i])

        def body(i, carry_on):
            cm.ag_step(i + 2)

            @pl.when(i + 1 < nc)
            def _():
                stream.start(i + 1)

            u, lg, low_g, low_u, dp, hid, ld, low_d, gp = stream.wait(i)
            acc_a[...] += tn(lg, u)
            acc_g[...] += tn(low_g, dp[:, :npad])
            acc_u[...] += tn(low_u, dp[:, npad:])
            acc_d[...] += tn(ld, hid)
            acc_p[...] += tn(low_d, gp)
            cm.ag_wait(i)
            stored(i).start()
            rows = cm.rows(i)
            block = full[rows, :]
            da_ref[rows, :] = nt(block, w_ref[:, :d]).astype(BF16)
            lo_ref[rows, :] = nt(block, b_ref[...]).astype(BF16)
            return carry_on

        lax.fori_loop(0, nc, body, 0)

        ratio = -gm_ref[0:1, :] / sq_ref[0:1, :]
        term = nt((up_ref[...] * ratio).astype(BF16), wg_ref[...])
        tail_g, tail_u = wg_ref[:, npad - LANES : npad], wg_ref[:, 2 * npad - LANES :]
        gain_row, gain_column = gain_rows(tail_g, off + RANK)
        inverse = 1.0 / (gain_column * gain_column)
        sh_ref[: 2 * RANK, :] = (
            SCALE * (acc_a[: 2 * RANK, :] * gain_row + term[: 2 * RANK, :] / gain_row)
        ).astype(BF16)
        for k, (acc, tail) in enumerate(((acc_g, tail_g), (acc_u, tail_u))):
            at = slice(k * npad, (k + 1) * npad)
            merged = tn((tail.astype(F32) * inverse).astype(BF16), wg_ref[:, at])
            lc_ref[(1 + k) * RANK : (2 + k) * RANK, :] = (
                SCALE * (acc[off : off + RANK, :] + merged[off : off + RANK, :] * ratio[:, at])
            ).astype(BF16)
            lc_ref[3 * RANK + k : 3 * RANK + k + 1, :] = (gm_ref[0:1, at] / m_ref[0:1, at]).astype(BF16)
        lc_ref[3 * RANK + 2 :, :] = jnp.zeros((RANK - 2, npad), BF16)

        for o, m in cm.st_peers():
            ratio_copy(o, m).wait_recv()
        ratio_down = qs_ref[1:2, :]
        lc_ref[:RANK, :] = (
            SCALE
            * (acc_d[:RANK, :] + nt((bd_ref[...].astype(F32) * ratio_down).astype(BF16), wd_ref[:, :d])[:RANK, :])
        ).astype(BF16)
        sh_ref[2 * RANK :, :] = (
            SCALE * (acc_p[:RANK, :] + tn(wd_ref[:, d:], wd_ref[:, :d])[:RANK, :] * ratio_down)
        ).astype(BF16)

        def drain(i, carry_on):
            cm.ag_drain(i)
            stored(i).wait()
            return carry_on

        lax.fori_loop(0, nc, drain, 0)
        for o, m in cm.st_peers():
            ratio_copy(o, m).wait_send()

    dma = pltpu.SemaphoreType.DMA
    return call(
        kernel,
        "out_backward",
        (
            shape((t, fw), BF16),
            shape((t, LANES), BF16),
            shape((8, d), F32),
            shape((3 * RANK, d), BF16),
            shape((4 * RANK, npad), BF16),
            shape((t, d), BF16),
        ),
        [VM] * 11 + [ANY] * 8,
        (VM,) * 5 + (ANY,),
        ag_scratch(nl, nc, t, d)
        + [dma((nc,)), dma((2 * nl,)), dma((2 * nl,))]
        + [pltpu.VMEM((LANES, n), F32) for n in (d, npad, npad, npad, d)]
        + stream_scratch(tc, widths),
        5,
        60,
        (
            go, weights, b_out, ratios, w_gu, w_down, up_gu, b_down, gm_gu, square_gu, m_gu,
            u_full, lg_gu, gu, dp_gu, hidden, lg_down, lora_down, gp_full,
        ),
        late=(1, 2, 4, 5, 6, 7),
    )


def attention_backward(
    cfg, qkv, attended, grad, lse, seg_column, seg_row, first_block, block, cosine, sine, scale, rate, b_qkv
):
    t, fw = cfg[0], cfg[1]
    heads = fw // HD
    width = 3 * fw

    def kernel(
        io, qkv_ref, att_ref, grad_ref, lse_ref, sc_ref, sr_ref, first_ref, cos_ref, sin_ref, scale_ref, rate_ref, b_ref,
        dp_ref, st_ref, gm_ref, lg_ref, dq, dk, dv,
    ):
        def at(i):
            return pl.ds(pl.multiple_of(i * block, block), block)

        def columns(k, hd):
            return slice(k * fw + hd * HD, k * fw + (hd + 1) * HD)

        gm_ref[...] = jnp.zeros_like(gm_ref)
        dk[...] = jnp.zeros_like(dk)
        dv[...] = jnp.zeros_like(dv)

        def one_query(i, carry_on):
            queries = [qkv_ref[at(i), columns(0, hd)] for hd in range(heads)]
            grads = [grad_ref[at(i), columns(0, hd)] for hd in range(heads)]
            deltas = [
                ones_rows(grads[hd].astype(F32) * att_ref[at(i), columns(0, hd)].astype(F32))[0:1, :]
                for hd in range(heads)
            ]
            query_segment = sr_ref[0:1, at(i)]

            def one_key(j, accs):
                allowed = allowed_of(sc_ref[at(j), 0:1], query_segment, j, i, block)
                out = []
                for hd in range(heads):
                    keys = qkv_ref[at(j), columns(1, hd)]
                    s = nt(keys, queries[hd]) * (HD**-0.5)
                    p = jnp.where(allowed, jnp.exp(s - lse_ref[hd * 8 : hd * 8 + 1, at(i)]), 0.0)
                    ds = (p * (nt(qkv_ref[at(j), columns(2, hd)], grads[hd]) - deltas[hd])).astype(BF16)
                    dv[hd, at(j), :] += nn(p.astype(BF16), grads[hd])
                    dk[hd, at(j), :] += nn(ds, queries[hd])
                    out.append(accs[hd] + tn(ds, keys))
                return tuple(out)

            accs = lax.fori_loop(first_ref[i], i + 1, one_key, (jnp.zeros((block, HD), F32),) * heads)
            for hd in range(heads):
                dq[hd, at(i), :] = accs[hd]
            return carry_on

        lax.fori_loop(0, t // block, one_query, 0)

        def finish(i, carry_on):
            rows = at(i)
            cosine_here, sine_here = cos_ref[rows, :], sin_ref[rows, :]
            inner = jnp.zeros((block, HD), F32)
            for hd in range(heads):
                for n, source in enumerate((dq, dk, dv)):
                    where = columns(n, hd)
                    dout = source[hd, rows, :]
                    value = qkv_ref[rows, where].astype(F32)
                    if n < 2:
                        dout = dout * (HD**-0.5)
                        dout = dout * cosine_here - pltpu.roll(dout, HD // 2, 1) * sine_here
                        value = value * cosine_here - pltpu.roll(value, HD // 2, 1) * sine_here
                    product = dout * value
                    inner = inner + product
                    gm_ref[0:1, where] += row_sum(product)
                    dp_ref[rows, where] = (dout * scale_ref[0:1, where]).astype(BF16)
            st_ref[:, rows] = ones_rows(inner)
            lg_ref[rows, :] = (nt(dp_ref[rows, :], b_ref[...].astype(BF16)) * rate_ref[rows, :]).astype(BF16)
            return carry_on

        lax.fori_loop(0, t // block, finish, 0)

    return call(
        kernel,
        "attention_backward",
        (
            shape((t, width), BF16),
            shape((8, t), F32),
            shape((8, width), F32),
            shape((t, LANES), BF16),
        ),
        [VM] * 6 + [SM] + [VM] * 5,
        (VM,) * 4,
        [pltpu.VMEM((heads, t, HD), F32)] * 3,
        None,
        35,
        (qkv, attended, grad, lse, seg_column, seg_row, first_block, cosine, sine, scale, rate, b_qkv),
    )


def qkv_backward(
    cfg, ny, dp, stats, weights, rate, dm, x, shared, local_gu, w_out, up_qkv, b_out, ratios, gm_qkv, square_qkv,
    gm_out, gm_down, small, x_full, lg_qkv, lora_qkv, attended, lg_out, lora_out, go_full,
):
    t, fw, d, nl, nc, tc = cfg
    width = 3 * fw
    peers = 2 * nl
    step = 2 * tc if nc % 2 == 0 else tc
    parts = t // step
    widths = (d, LANES, LANES, fw, LANES, LANES, d)

    def kernel(
        io, dp_ref, st_ref, w_ref, rate_ref, dm_ref, x_ref, sh_ref, l_ref, wo_ref, up_ref, bo_ref, q_ref,
        gm_ref, sq_ref, gmo_ref, gmd_ref, m_ref, xf_hbm, lg_hbm, lq_hbm, at_hbm, lgo_hbm, lo_hbm, gf_hbm,
        out_ref, as_ref, bs_ref, ls_ref,
        sb, cb, gb, s1, r1, s2, r2, sa, ss, sr,
        stage, gs_s, gs_r, gs_l, group, gsum, gss, gsr, final_a, final_b, final_l, fs, fr, fl,
        a_ref, b_ref, acc_a, acc_b, acc_o, acc_p, *streams,
    ):
        cm = Comm(nl, nc, tc, fw, back_by_two=0.375)
        c, g = cm.c, cm.g
        y, h = lax.axis_index("y"), lax.axis_index("h")
        cm.rs_refs(sb, cb, gb, s1, r1, s2, r2)
        cm.st_refs(st_ref, sa, ss, sr)
        swap = Swap(cm)
        every = lambda n: pl.ds(0, n)
        stream = Stream(
            [
                (xf_hbm, every(d)),
                (lg_hbm, every(LANES)),
                (lq_hbm, every(LANES)),
                (at_hbm, every(fw)),
                (lgo_hbm, every(LANES)),
                (lo_hbm, every(LANES)),
                (gf_hbm, every(d)),
            ],
            streams[:-1],
            streams[-1],
            step,
        )
        stream.start(jnp.int32(0))
        senders = [
            {"y": lax.rem(y + ny - k, ny), "c": h, "h": hh} for k in range(1, ny) for hh in (0, 1)
        ]
        cm.barrier(senders + [{"c": h, "h": 1 - h}], [swap.partner, {"c": h, "h": h}])

        def gather_part(o, m):
            to_c, to_g = 1 - c if o else c, cm.after(m)
            k = o * nl + m
            return cm.copy(
                a_ref.at[:, cm.columns(to_c, to_g)], group.at[k], gss.at[k], gsr.at[k], to_c, to_g
            )

        def sums(k, e):
            device = {"y": lax.rem(y + k, ny), "c": lax.rem(c + e, 2), "h": c}
            slot = k * 2 + h
            return [
                pltpu.make_async_remote_copy(
                    src_ref=src, dst_ref=dst.at[slot], send_sem=fs.at[n, k * 2 + e], recv_sem=fr.at[n, slot],
                    device_id=device, device_id_type=MESH,
                )
                for n, (src, dst) in enumerate(((gsum, final_a), (b_ref, final_b), (l_ref, final_l)))
            ]

        def sums_here():
            return [
                pltpu.make_async_copy(src, dst.at[h], fl.at[n])
                for n, (src, dst) in enumerate(((gsum, final_a), (b_ref, final_b), (l_ref, final_l)))
            ]

        def stats_out(i, carry_on):
            cm.st_send(i)
            return carry_on

        lax.fori_loop(0, nc, stats_out, 0)
        for acc in (acc_a, acc_b, acc_o, acc_p):
            acc[...] = jnp.zeros_like(acc)

        def adapters(k):
            @pl.when(k + 1 < parts)
            def _():
                stream.start(k + 1)

            xf, lg, low_q, att, lg_o, low_o, gf = stream.wait(k)
            rows = pl.ds(pl.multiple_of(k * step, step), step)
            acc_a[...] += tn(lg, xf)
            acc_b[...] += tn(low_q, dp_ref[rows, :])
            acc_o[...] += tn(lg_o, att)
            acc_p[...] += tn(low_o, gf)

        def adapters_end():
            ratio = -gm_ref[0:1, :] / sq_ref[0:1, :]
            ratio_out = q_ref[0:1, :]
            tail = w_ref[:, width:]
            gain_row, gain_column = gain_rows(tail, 3 * RANK)
            term = nt((up_ref[...] * ratio).astype(BF16), w_ref[:, :width])
            a_ref[: 3 * RANK, :] = (
                SCALE * (acc_a[: 3 * RANK, :] * gain_row + term[: 3 * RANK, :] / gain_row)
            ).astype(BF16)
            merged = tn(
                (tail.astype(F32) / (gain_column * gain_column)).astype(BF16), w_ref[:, :width]
            )
            for k in range(3):
                at, low = slice(k * fw, (k + 1) * fw), slice(k * RANK, (k + 1) * RANK)
                b_ref[(1 + k) * RANK : (2 + k) * RANK, :] = (
                    SCALE * (acc_b[low, at] + merged[low, at] * ratio[:, at])
                ).astype(BF16)
                b_ref[4 * RANK + k : 4 * RANK + k + 1, :] = (gm_ref[0:1, at] / m_ref[k : k + 1, :]).astype(BF16)
            b_ref[4 * RANK + 3 : 4 * RANK + 4, :] = (gmo_ref[0:1, :] / m_ref[3:4, :]).astype(BF16)
            b_ref[4 * RANK + 4 : 4 * RANK + 5, :] = (gmd_ref[0:1, :] / m_ref[4:5, :]).astype(BF16)
            b_ref[4 * RANK + 5 :, :] = jnp.zeros((RANK - 5, fw), BF16)
            b_ref[:RANK, :] = (
                SCALE
                * (acc_o[:RANK, :] + nt((bo_ref[...].astype(F32) * ratio_out).astype(BF16), wo_ref[:, :d])[:RANK, :])
            ).astype(BF16)
            a_ref[3 * RANK : 4 * RANK, :] = (
                SCALE * (acc_p[:RANK, :] + tn(wo_ref[:, d:], wo_ref[:, :d])[:RANK, :] * ratio_out)
            ).astype(BF16)
            a_ref[4 * RANK :, :] = sh_ref[...]
            for o, m in cm.st_peers():
                gather_part(o, m).start()

        io.ready()

        def grad_swap(i):
            rows = cm.rows(i)
            return stage.at[rows], out_ref.at[rows], (gs_s.at[i], gs_r.at[i], gs_l.at[i])

        def body(i, carry_on):
            @pl.when(i < nc)
            def _():
                block = dp_ref[cm.rows(i), :]
                for role in range(2 * nl):
                    sb[i, role // nl, role % nl] = nt(
                        block, w_ref[role * fw : (role + 1) * fw, :width]
                    ).astype(BF16)
                cm.rs_across(i).start()

            cm.rs_steps(i)

            @pl.when(i < parts)
            def _():
                adapters(i)

            @pl.when(i == parts)
            def _():
                adapters_end()

            @pl.when(i == min(parts + 3, nc + 2))
            def _():
                total = a_ref[:, cm.columns(c, g)].astype(F32)
                for o, m in cm.st_peers():
                    gather_part(o, m).wait_recv()
                    total = total + group[o * nl + m].astype(F32)
                gsum[...] = total.astype(BF16)
                for k in range(ny):
                    for e in (0, 1):
                        if (k, e) == (0, 0):

                            @pl.when(swap.moves)
                            def _():
                                for copy in sums(0, 0):
                                    copy.start()

                            @pl.when(jnp.logical_not(swap.moves))
                            def _():
                                for copy in sums_here():
                                    copy.start()
                        else:
                            for copy in sums(k, e):
                                copy.start()

            @pl.when(i >= 3)
            def _():
                k = i - 3
                rows = cm.rows(k)
                cm.st_wait(k)
                r = rate_ref[rows, 0:1]
                inner = cm.st_sum(k)[:, 0:1]
                stage[rows, :] = (
                    dm_ref[rows, :]
                    + r * cm.rs_total(k)
                    - x_ref[rows, :].astype(F32) * (r * r * inner / d)
                ).astype(BF16)
                swap.start(*grad_swap(k))

            return carry_on

        lax.fori_loop(0, nc + 3, body, 0)

        for k in range(ny):
            for hh in (0, 1):
                slot = k * 2 + hh

                def arrived():
                    for n, dst in enumerate((final_a, final_b, final_l)):
                        src = (gsum, b_ref, l_ref)[n]
                        pltpu.make_async_remote_copy(
                            src_ref=src, dst_ref=dst.at[slot], send_sem=fs.at[n, 0], recv_sem=fr.at[n, slot],
                            device_id=swap.partner, device_id_type=MESH,
                        ).wait_recv()

                if k == 0:
                    here = jnp.logical_and(c == h, h == hh)

                    @pl.when(here)
                    def _():
                        for copy in sums_here():
                            copy.wait()

                    @pl.when(jnp.logical_not(here))
                    def _():
                        arrived()
                else:
                    arrived()
        for out, held in ((as_ref, final_a), (bs_ref, final_b), (ls_ref, final_l)):
            total = held[0].astype(F32)
            for slot in range(1, 2 * ny):
                total = total + held[slot].astype(F32)
            out[...] = total

        def drain(i, carry_on):
            swap.wait(*grad_swap(i))
            cm.rs_drain(i)
            cm.st_drain(i)
            swap.drain(*grad_swap(i))
            return carry_on

        lax.fori_loop(0, nc, drain, 0)
        for o, m in cm.st_peers():
            gather_part(o, m).wait_send()
        for k in range(ny):
            for e in (0, 1):
                if (k, e) == (0, 0):

                    @pl.when(swap.moves)
                    def _():
                        for copy in sums(0, 0):
                            copy.wait_send()
                else:
                    for copy in sums(k, e):
                        copy.wait_send()

    dma = pltpu.SemaphoreType.DMA
    na, nb, ng = 7 * RANK, (5 * RANK, fw), local_gu.shape
    return call(
        kernel,
        "qkv_backward",
        (shape((t, fw), BF16), shape((na, fw), F32), shape(nb, F32), shape(ng, F32)),
        [VM] * 17 + [ANY] * 7,
        (VM,) * 4,
        rs_scratch(nl, nc, tc, fw)
        + st_scratch(nl, nc, t)
        + [pltpu.VMEM((t, fw), BF16)]
        + [dma((nc,))] * 3
        + [pltpu.VMEM((peers, na, fw), BF16), pltpu.VMEM((na, fw), BF16), dma((peers,)), dma((peers,))]
        + [
            pltpu.VMEM((2 * ny, na, fw), BF16),
            pltpu.VMEM((2 * ny, *nb), BF16),
            pltpu.VMEM((2 * ny, *ng), BF16),
            dma((3, 2 * ny)),
            dma((3, 2 * ny)),
            dma((3,)),
            pltpu.VMEM((na, d), BF16),
            pltpu.VMEM(nb, BF16),
        ]
        + [pltpu.VMEM((LANES, n), F32) for n in (d, width, fw, d)]
        + stream_scratch(step, widths),
        6,
        70,
        (
            dp, stats, weights, rate, dm, x, shared, local_gu, w_out, up_qkv, b_out, ratios, gm_qkv, square_qkv,
            gm_out, gm_down, small, x_full, lg_qkv, lora_qkv, attended, lg_out, lora_out, go_full,
        ),
        late=(2, 3, 4, 5, 6, 7, 8, 9, 10, 11),
    )


def last_step(fw, nf, grad, result, shared, local, local_gu):
    def kernel(
        io, g_ref, r_ref, s_ref, l_ref, u_ref,
        result_ref, grad_ref, aq_ref, bq_ref, mq_ref, ao_ref, bo_ref, mo_ref,
        ag_ref, bg_ref, mg_ref, ad_ref, bd_ref, md_ref,
    ):
        result_ref[...] = r_ref[...]
        grad_ref[...] = g_ref[...].astype(F32)
        for k in range(3):
            aq_ref[k] = s_ref[k * RANK : (k + 1) * RANK, :]
            bq_ref[k] = l_ref[(1 + k) * RANK : (2 + k) * RANK, :]
        for k in range(2):
            ag_ref[k] = s_ref[(4 + k) * RANK : (5 + k) * RANK, :]
            bg_ref[k] = u_ref[(1 + k) * RANK : (2 + k) * RANK, :nf]
        mq_ref[...] = l_ref[4 * RANK : 4 * RANK + 3, :]
        mg_ref[...] = u_ref[3 * RANK : 3 * RANK + 2, :nf]
        ao_ref[...] = l_ref[:RANK, :]
        bo_ref[...] = s_ref[3 * RANK : 4 * RANK, :]
        mo_ref[...] = l_ref[4 * RANK + 3 : 4 * RANK + 4, :]
        ad_ref[...] = u_ref[:RANK, :nf]
        bd_ref[...] = s_ref[6 * RANK :, :]
        md_ref[...] = l_ref[4 * RANK + 4 : 4 * RANK + 5, :]

    f = [
        (3, RANK, fw), (3, RANK, fw), (3, fw), (RANK, fw), (RANK, fw), (1, fw),
        (2, RANK, fw), (2, RANK, nf), (2, nf), (RANK, nf), (RANK, fw), (1, fw),
    ]
    return call(
        kernel,
        "last_step",
        (shape(result.shape, BF16), shape(grad.shape, F32), *[shape(v, F32) for v in f]),
        [VM] * 5,
        (VM,) * 14,
        [],
        None,
        4,
        (grad, result, shared, local, local_gu),
    )


def positions_of(segment_row):
    index = jnp.arange(segment_row.shape[0], dtype=jnp.int32)
    starts = jnp.concatenate([jnp.ones((1,), jnp.bool_), segment_row[1:] != segment_row[:-1]])
    begin = lax.cummax(jnp.where(starts, index, 0), axis=0)
    return index - begin, begin


def padded(rows, total):
    return jnp.pad(rows, ((0, 0), (0, total - rows.shape[1])))


def on_device(ny, nl, *operands):
    (
        inputs, segments, gain_attn, gain_ffn, w_qkv, a_qkv, b_qkv, m_qkv, w_out, a_out, b_out, m_out,
        w_gu, a_gu, b_gu, m_gu, w_down, a_down, b_down, m_down, cotangent,
    ) = operands
    t, fw = inputs.shape
    mp = 2 * nl
    d = mp * fw
    nf = m_gu.shape[1]
    npad = -(-(nf + RANK) // LANES) * LANES
    width = 3 * fw
    nc = 8 if t % 1024 == 0 else 1
    cfg = (t, fw, d, nl, nc, t // nc)
    block = min(256, t)
    y, c, h, g = (lax.axis_index(name) for name in ("y", "c", "h", "g"))
    role = c * nl + g

    def merged_of(frozen, down, up):
        return frozen.astype(F32) + SCALE * jnp.einsum(
            "kdr,krn->kdn", down, up, precision=HIGHEST
        )

    def two_parts(gain):
        high = gain.astype(BF16)
        return [high[:, None], (gain - high.astype(F32)).astype(BF16)[:, None]]

    tail_qkv = padded(
        jnp.concatenate(
            [(a_qkv[k] * gain_attn[:, None]).astype(BF16) for k in range(3)] + two_parts(gain_attn), axis=1
        ),
        LANES,
    )
    tail_gu = jnp.stack(
        [
            jnp.pad(
                jnp.concatenate(
                    [(a_gu[k] * gain_ffn[:, None]).astype(BF16)] + two_parts(gain_ffn), axis=1
                ),
                ((0, 0), (nf, npad - nf - RANK - 2)),
            )
            for k in range(2)
        ]
    )
    gains = padded(jnp.stack([gain_attn, gain_ffn], axis=1), LANES)
    b_gu_padded = jnp.pad(
        b_gu.reshape(2, RANK, mp, nf), ((0, 0), (0, 0), (0, 0), (0, npad - nf))
    ).transpose(0, 2, 1, 3)
    rows_out = jnp.concatenate(
        [
            merged_of(w_out[None], a_out[None], b_out[None])[0].astype(BF16),
            padded(a_out, LANES).astype(BF16),
        ],
        axis=1,
    )
    small = jnp.concatenate([m_qkv, m_out[None], m_down[None], jnp.zeros((3, fw), F32)], axis=0)
    small_gu = jnp.broadcast_to(
        jnp.pad(m_gu, ((0, 0), (0, npad - nf)), constant_values=1.0).reshape(1, 2 * npad), (8, 2 * npad)
    )

    def take(whole, n, axis):
        return lax.dynamic_slice_in_dim(whole, role * n, n, axis)

    b_qkv_here = take(b_qkv, fw, 2)
    b_gu_here = take(b_gu, nf, 2)

    def block_up(up, pad):
        k, _, n = up.shape
        wide = jnp.pad(up, ((0, 0), (0, 0), (0, pad - n)))[:, :, None, :]
        same = (jnp.arange(k)[:, None] == jnp.arange(k)[None, :])[:, None, :, None]
        rows = jnp.where(same, wide, 0.0).reshape(k * RANK, k * pad)
        return jnp.pad(rows, ((0, LANES - k * RANK), (0, 0)))

    up_qkv = block_up(b_qkv_here, fw)
    up_gu = block_up(b_gu_here, npad)
    up_out = jnp.pad(b_out, ((0, LANES - RANK), (0, 0))).astype(BF16)
    up_down = jnp.pad(b_down, ((0, LANES - RANK), (0, 0))).astype(BF16)

    segment = lax.dynamic_index_in_dim(
        lax.all_gather(segments, "c", axis=0, tiled=True), h, 0, keepdims=False
    )
    positions, begin = positions_of(segment)
    first_block = begin[::block] // block
    seg_row = jnp.broadcast_to(segment[None, :], (8, t))
    seg_column = jnp.broadcast_to(segment[:, None], (t, LANES))
    frequencies = jnp.exp(jnp.arange(HD // 2, dtype=F32) * (-2.0 * math.log(10000.0) / HD))
    angles = positions.astype(F32)[:, None] * frequencies[None, :]
    cosine = jnp.cos(angles)
    sine = jnp.sin(angles)
    cosine = jnp.concatenate([cosine, cosine], axis=1)
    sine = jnp.concatenate([-sine, sine], axis=1)

    (
        x, weights_qkv, weights_out, small, small_gu, scale_qkv, square_qkv, qkv, lora_qkv_in, rate_attn,
        blocks_gu, x_full,
    ) = qkv_forward(
        cfg, ny, npad, nf, inputs, w_qkv, a_qkv, b_qkv, tail_qkv, gains, rows_out, small, small_gu, cosine, sine,
        w_gu, a_gu, b_gu_padded, tail_gu,
    )
    attended, lse = attention_forward(cfg, qkv, seg_column, seg_row, first_block, block)
    middle, u, stats, sc_out, square_out, lora_out, weights_gu, weights_down = out_forward(
        cfg, ny, npad, attended, weights_out, x, small, blocks_gu, w_down, a_down, b_down
    )
    (
        gu, hidden, block_out, gm_down, rate_ffn, gp, scale_gu, square_gu, sc_down, square_down,
        lora_down, grad_seed, u_full,
    ) = ffn_forward(
        cfg, npad, nf, u, stats, weights_gu, small_gu[0:1], weights_down, small, middle, cotangent
    )

    dm, go, gm_out, gm_gu, lg_gu, lg_down, dp_gu, gp_full = ffn_backward(
        cfg, npad, gp, gu, weights_gu, scale_gu, up_gu, weights_down, up_down, rate_ffn,
        grad_seed, middle, x, sc_out,
    )
    ratios = jnp.concatenate(
        [-gm_out[0:1] / square_out[0:1], -gm_down[0:1] / square_down[0:1], jnp.zeros((6, fw), F32)], axis=0
    )
    grad_attended, lg_out, ratios, shared, local_gu, go_full = out_backward(
        cfg, npad, nf, go, weights_out, up_out, ratios, weights_gu, weights_down, up_gu, up_down, gm_gu, square_gu,
        small_gu, u_full, lg_gu, gu, dp_gu, hidden, lg_down, lora_down, gp_full,
    )
    dp_qkv, inner, gm_qkv, lg_qkv = attention_backward(
        cfg, qkv, attended, grad_attended, lse, seg_column, seg_row, first_block, block, cosine, sine,
        scale_qkv, rate_attn, up_qkv,
    )

    grad_input, shared, local, local_gu = qkv_backward(
        cfg, ny, dp_qkv, inner, weights_qkv, rate_attn, dm, x, shared, local_gu, weights_out, up_qkv, up_out, ratios,
        gm_qkv, square_qkv, gm_out, gm_down, small, x_full, lg_qkv, lora_qkv_in, attended, lg_out, lora_out, go_full,
    )
    out = list(last_step(fw, nf, grad_input, block_out, shared, local, local_gu))
    out[2], out[8] = out[2].transpose(0, 2, 1), out[8].transpose(0, 2, 1)
    out[5], out[11] = out[5].T, out[11].T
    out[7], out[13] = out[7][0], out[13][0]
    return tuple(out)


def solution(mesh):
    dp, mp = mesh.shape["dp"], mesh.shape["mp"]
    ny, nl = dp // 2, mp // 2
    fine = Mesh(mesh.devices.reshape(ny, 2, 2, nl), ("y", "c", "h", "g"))
    rows, cols = ("y", "c"), ("h", "g")
    in_specs = (
        P(rows, cols),
        P(rows, None),
        P(cols),
        P(cols),
        P(None, cols, None),
        P(None, cols, None),
        P(),
        P(None, cols),
        P(cols, None),
        P(cols, None),
        P(),
        P(cols),
        P(None, cols, None),
        P(None, cols, None),
        P(),
        P(None, cols),
        P(cols, None),
        P(cols, None),
        P(),
        P(cols),
        P(rows, cols),
    )
    out_specs = (
        P(rows, cols),
        P(rows, cols),
        P(None, cols, None),
        P(None, None, cols),
        P(None, cols),
        P(cols, None),
        P(None, cols),
        P(cols),
        P(None, cols, None),
        P(None, None, cols),
        P(None, cols),
        P(cols, None),
        P(None, cols),
        P(cols),
    )
    return jax.shard_map(
        lambda *operands: on_device(ny, nl, *operands),
        mesh=fine,
        in_specs=in_specs,
        out_specs=out_specs,
        check_vma=False,
    )
```

```python
import math

import jax
import jax.numpy as jnp
from jax import lax
from jax.experimental import pallas as pl
from jax.experimental.pallas import tpu as pltpu
from jax.sharding import Mesh
from jax.sharding import PartitionSpec as P

HD = 128
RANK = 16
SCALE = 2.0
EPS = 1e-05
MASKED = -1e30
HIGHEST = lax.Precision.HIGHEST
MESH = pl.DeviceIdType.MESH
F32 = jnp.float32
BF16 = jnp.bfloat16
LANES = 128
VMEM_LIMIT = 60 * 1024 * 1024


def nt(a, b, precision=None):
    return lax.dot_general(
        a, b, (((1,), (1,)), ((), ())), precision=precision, preferred_element_type=F32
    )


def tn(a, b, precision=None):
    return lax.dot_general(
        a, b, (((0,), (0,)), ((), ())), precision=precision, preferred_element_type=F32
    )


def nn(a, b, precision=None):
    return lax.dot_general(
        a, b, (((1,), (0,)), ((), ())), precision=precision, preferred_element_type=F32
    )


WINDOW = 3
EARLY = 1


class Comm:
    def __init__(self, nl, nc, tc, fw, out_by_one=0.5, back_by_two=0.5):
        self.nl, self.nc, self.tc, self.fw = nl, nc, tc, fw
        self.square = nl == 4
        self.cut = int(tc * out_by_one) // 16 * 16
        self.back = int(tc * back_by_two) // 16 * 16
        self.c = lax.axis_index("c")
        self.g = lax.axis_index("g")

    def rows(self, i):
        return pl.ds(pl.multiple_of(i * self.tc, self.tc), self.tc)

    def after(self, m):
        return lax.rem(self.g + m, self.nl)

    def before(self, m):
        return lax.rem(self.g + self.nl - m, self.nl)

    def columns(self, c, g):
        return pl.ds(pl.multiple_of((c * self.nl + g) * self.fw, self.fw), self.fw)

    def copy(self, src, dst, send, recv, c, g):
        return pltpu.make_async_remote_copy(
            src_ref=src,
            dst_ref=dst,
            send_sem=send,
            recv_sem=recv,
            device_id={"c": c, "g": g},
            device_id_type=MESH,
        )

    def barrier(self, others=(), one_more=None):
        sem = pltpu.get_barrier_semaphore()
        everyone = [
            {"c": 1 - self.c if other else self.c, "g": self.after(m)}
            for other in (0, 1)
            for m in range(self.nl)
            if (other, m) != (0, 0)
        ] + list(others)
        for device in everyone:
            pl.semaphore_signal(sem, inc=1, device_id=device, device_id_type=MESH)
        if one_more is None:
            pl.semaphore_wait(sem, len(everyone))
        else:
            apart = self.c - lax.axis_index("h")

            @pl.when(apart != 0)
            def _():
                for device in one_more:
                    pl.semaphore_signal(sem, inc=1, device_id=device, device_id_type=MESH)

            pl.semaphore_wait(sem, len(everyone) + len(one_more) * apart * apart)

    def other(self, m):
        if m == 1:
            return self.g + 1 - 2 * lax.rem(self.g, 2)
        return lax.rem(self.g + 2, 4) if m == 2 else 3 - self.g

    def comes_from(self, m):
        if m == 0:
            return self.g
        return self.other(m) if self.square else self.before(m)

    def goes_to(self, m):
        return self.other(m) if self.square else self.after(m)

    def some(self, i, way):
        cut = self.cut
        start, size = (0, cut) if way == 0 else (cut, self.tc - cut)
        return pl.ds(pl.multiple_of(i * self.tc + start, 16), size)

    def ag_refs(self, x, full, own, sd, rd, sc, rc):
        self.x, self.full, self.own = x, full, own
        self.sd, self.rd, self.sc, self.rc = sd, rd, sc, rc

    def ag_steps(self):
        return (1, 2) if self.square else range(1, self.nl)

    def ag_direct(self, i, m):
        rows = self.rows(i)
        return self.copy(
            self.x.at[rows],
            self.full.at[rows, self.columns(self.c, self.g)],
            self.sd.at[i, m],
            self.rd.at[i, m],
            self.c,
            self.goes_to(m),
        )

    def ag_relay(self, i, way):
        rows = self.some(i, way)
        columns = self.columns(self.c, self.other(2 - way))
        return self.copy(
            self.full.at[rows, columns],
            self.full.at[rows, columns],
            self.sd.at[i, 3 * way],
            self.rd.at[i, 3 * way],
            self.c,
            self.other(1 + way),
        )

    def ag_across(self, i, m):
        rows = self.rows(i)
        columns = self.columns(self.c, self.comes_from(m))
        src = self.x.at[rows] if m == 0 else self.full.at[rows, columns]
        return self.copy(
            src,
            self.full.at[rows, columns],
            self.sc.at[i, m],
            self.rc.at[i, m],
            1 - self.c,
            self.g,
        )

    def ag_own(self, i):
        rows = self.rows(i)
        return pltpu.make_async_copy(
            self.x.at[rows],
            self.full.at[rows, self.columns(self.c, self.g)],
            self.own.at[i],
        )

    def ag_send(self, i):
        for m in self.ag_steps():
            self.ag_direct(i, m).start()
        self.ag_across(i, 0).start()
        self.ag_own(i).start()

    def ag_start(self):
        for i in range(min(WINDOW, self.nc)):
            self.ag_send(jnp.int32(i))

    def ag_forward(self, i):
        for m in self.ag_steps():
            self.ag_direct(i, m).wait_recv()
        if self.square:
            for way in (0, 1):
                self.ag_relay(i, way).start()
        for m in self.ag_steps():
            self.ag_across(i, m).start()

    def ag_corner(self, i):
        if self.square:
            for way in (0, 1):
                self.ag_relay(i, way).wait_recv()
            self.ag_across(i, 3).start()

    def ag_step(self, i, more=True):
        @pl.when(i < self.nc)
        def _():
            self.ag_forward(i)

        if more:

            @pl.when(i + WINDOW < self.nc)
            def _():
                self.ag_send(i + WINDOW)

        @pl.when((i >= 1) & (i <= self.nc))
        def _():
            self.ag_corner(i - 1)

    def ag_ahead(self):
        self.ag_step(jnp.int32(0))
        self.ag_step(jnp.int32(1))

    def ag_wait(self, i):
        self.ag_own(i).wait()
        for m in range(self.nl):
            self.ag_across(i, m).wait_recv()

    def ag_drain(self, i):
        for m in self.ag_steps():
            self.ag_direct(i, m).wait_send()
        if self.square:
            for way in (0, 1):
                self.ag_relay(i, way).wait_send()
        for m in range(self.nl):
            self.ag_across(i, m).wait_send()

    def rs_refs(self, sb, cb, gb, s1, r1, s2, r2):
        self.sb, self.cb, self.gb = sb, cb, gb
        self.s1, self.r1, self.s2, self.r2 = s1, r1, s2, r2

    def rs_across(self, i):
        return self.copy(
            self.sb.at[i, 1 - self.c],
            self.cb.at[i],
            self.s1.at[i],
            self.r1.at[i],
            1 - self.c,
            self.g,
        )

    def rs_direct(self, i, m):
        to = self.goes_to(m)
        return self.copy(
            self.sb.at[i, self.c, to],
            self.gb.at[i, m - 1],
            self.s2.at[i, m],
            self.r2.at[i, m],
            self.c,
            to,
        )

    def rs_corner(self, i, way):
        rows = pl.ds(0, self.back) if way == 0 else pl.ds(self.back, self.tc - self.back)
        return self.copy(
            self.sb.at[i, self.c, self.other(3), rows],
            self.gb.at[i, 2, rows],
            self.s2.at[i, 3 * way],
            self.r2.at[i, 3 * way],
            self.c,
            self.other(2 - way),
        )

    def rs_middle(self, i):
        self.rs_across(i).wait_recv()
        for gp in range(self.nl):
            mine = self.sb[i, self.c, gp].astype(F32) + self.cb[i, gp].astype(F32)
            self.sb[i, self.c, gp] = mine.astype(BF16)
        if self.square:
            for way in (0, 1):
                self.rs_corner(i, way).start()
        else:
            for m in range(1, self.nl):
                self.rs_direct(i, m).start()

    def rs_second(self, i):
        if not self.square:
            return
        for way in (0, 1):
            self.rs_corner(i, way).wait_recv()
            rows = pl.ds(0, self.back) if way == 0 else pl.ds(self.back, self.tc - self.back)
            to = self.other(1 + way)
            both = self.sb[i, self.c, to, rows].astype(F32) + self.gb[i, 2, rows].astype(F32)
            self.sb[i, self.c, to, rows] = both.astype(BF16)
        for m in (1, 2):
            self.rs_direct(i, m).start()

    def rs_total(self, i):
        steps = (1, 2) if self.square else range(1, self.nl)
        for m in steps:
            self.rs_direct(i, m).wait_recv()
        total = self.sb[i, self.c, self.g].astype(F32)
        for m in steps:
            total = total + self.gb[i, m - 1].astype(F32)
        return total

    def rs_drain(self, i):
        self.rs_across(i).wait_send()
        if self.square:
            for way in (0, 1):
                self.rs_corner(i, way).wait_send()
        for m in (1, 2) if self.square else range(1, self.nl):
            self.rs_direct(i, m).wait_send()

    def rs_steps(self, i):
        @pl.when((i >= 1) & (i <= self.nc))
        def _():
            self.rs_middle(i - 1)

        @pl.when((i >= 2) & (i <= self.nc + 1))
        def _():
            self.rs_second(i - 2)

    def st_refs(self, st, sa, ss, sr):
        self.st, self.sa, self.ss, self.sr = st, sa, ss, sr

    def st_copy(self, i, other, m):
        mine = self.c * self.nl + self.g
        src, dst = (self.st, self.sa.at[mine]) if i is None else (self.st.at[i], self.sa.at[mine, i])
        i = 0 if i is None else i
        return self.copy(
            src,
            dst,
            self.ss.at[i, other * self.nl + m],
            self.sr.at[i, other * self.nl + m],
            1 - self.c if other else self.c,
            self.after(m),
        )

    def st_peers(self):
        return [(o, m) for o in (0, 1) for m in range(self.nl) if (o, m) != (0, 0)]

    def st_send(self, i):
        for o, m in self.st_peers():
            self.st_copy(i, o, m).start()
        mine = self.c * self.nl + self.g
        if i is None:
            self.sa[mine] = self.st[...]
        else:
            self.sa[mine, i] = self.st[i]

    def st_wait(self, i):
        for o, m in self.st_peers():
            self.st_copy(i, o, m).wait_recv()

    def st_sum(self, i):
        total = self.sa[0, i]
        for role in range(1, 2 * self.nl):
            total = total + self.sa[role, i]
        return jnp.broadcast_to(total, (8, self.tc)).T[:, 0:1]

    def st_drain(self, i):
        for o, m in self.st_peers():
            self.st_copy(i, o, m).wait_send()

    def cs_refs(self, part, held, ss, sr):
        self.part, self.held, self.cs, self.cr = part, held, ss, sr

    def cs_copy(self, other, m):
        c, g = 1 - self.c if other else self.c, self.after(m)
        place = pl.ds(pl.multiple_of((self.c * self.nl + self.g) * 8, 8), 8)
        k = other * self.nl + m
        return self.copy(
            self.part.at[:, self.columns(c, g)], self.held.at[place], self.cs.at[k], self.cr.at[k], c, g
        )

    def cs_start(self, w_ref):
        for role in range(2 * self.nl):
            at = slice(role * self.fw, (role + 1) * self.fw)
            value = w_ref[:, at].astype(F32)
            self.part[:, at] = jnp.broadcast_to(row_sum(value * value), (8, self.fw))
        for o, m in self.st_peers():
            self.cs_copy(o, m).start()
        place = pl.ds(pl.multiple_of((self.c * self.nl + self.g) * 8, 8), 8)
        self.held[place, :] = self.part[:, self.columns(self.c, self.g)]

    def cs_total(self):
        for o, m in self.st_peers():
            self.cs_copy(o, m).wait_recv()
        return row_sum(self.held[...]) * 0.125

    def cs_drain(self):
        for o, m in self.st_peers():
            self.cs_copy(o, m).wait_send()


class Swap:
    def __init__(self, cm):
        self.cm = cm
        self.h = lax.axis_index("h")
        self.moves = cm.c != self.h
        self.partner = {"c": self.h, "h": cm.c}

    def far(self, src, dst, send, recv):
        return pltpu.make_async_remote_copy(
            src_ref=src, dst_ref=dst, send_sem=send, recv_sem=recv, device_id=self.partner, device_id_type=MESH
        )

    def start(self, src, dst, sems):
        @pl.when(self.moves)
        def _():
            self.far(src, dst, sems[0], sems[1]).start()

        @pl.when(jnp.logical_not(self.moves))
        def _():
            pltpu.make_async_copy(src, dst, sems[2]).start()

    def wait(self, src, dst, sems):
        @pl.when(self.moves)
        def _():
            self.far(src, dst, sems[0], sems[1]).wait_recv()

        @pl.when(jnp.logical_not(self.moves))
        def _():
            pltpu.make_async_copy(src, dst, sems[2]).wait()

    def drain(self, src, dst, sems):
        @pl.when(self.moves)
        def _():
            self.far(src, dst, sems[0], sems[1]).wait_send()


PIECES = 2


class RowMove:
    def __init__(self, swap, ny, part, e_ref, w_ref, ws, wr, wl, ys, yr):
        self.swap, self.ny, self.part, self.size = swap, ny, part, part // PIECES
        self.e, self.w = e_ref, w_ref
        self.ws, self.wr, self.wl, self.ys, self.yr = ws, wr, wl, ys, yr
        self.y = lax.axis_index("y")

    def rows(self, y, p):
        return pl.ds(pl.multiple_of(y * self.part + p * self.size, 16), self.size)

    def far(self, p):
        mine = self.rows(self.y, p)
        return self.swap.far(self.e.at[mine], self.w.at[mine], self.ws.at[p], self.wr.at[p])

    def near(self):
        every = pl.ds(0, self.part * self.ny)
        return pltpu.make_async_copy(self.e.at[every], self.w.at[every], self.wl)

    def shared(self, k, p, y):
        where = self.rows(y, p)
        return pltpu.make_async_remote_copy(
            src_ref=self.w.at[where], dst_ref=self.w.at[where],
            send_sem=self.ys.at[k - 1, p], recv_sem=self.yr.at[k - 1, p],
            device_id={"y": lax.rem(self.y + k, self.ny)}, device_id_type=MESH,
        )

    def start(self):
        @pl.when(self.swap.moves)
        def _():
            for p in range(PIECES):
                self.far(p).start()

        @pl.when(jnp.logical_not(self.swap.moves))
        def _():
            self.near().start()

    def pass_on(self):
        @pl.when(self.swap.moves)
        def _():
            for p in range(PIECES):
                self.far(p).wait_recv()
                for k in range(1, self.ny):
                    self.shared(k, p, self.y).start()

    def wait(self):
        @pl.when(self.swap.moves)
        def _():
            for k in range(1, self.ny):
                for p in range(PIECES):
                    self.shared(k, p, lax.rem(self.y + self.ny - k, self.ny)).wait_recv()

        @pl.when(jnp.logical_not(self.swap.moves))
        def _():
            self.near().wait()

    def drain(self):
        @pl.when(self.swap.moves)
        def _():
            for p in range(PIECES):
                self.far(p).wait_send()
                for k in range(1, self.ny):
                    self.shared(k, p, self.y).wait_send()


def row_move_scratch(ny):
    dma = pltpu.SemaphoreType.DMA
    between = dma((max(ny - 1, 1), PIECES))
    return [dma((PIECES,)), dma((PIECES,)), dma, between, between]


class Spread:
    def __init__(self, cm, ny, e_ref, w_ref, hs, hr, ps, pr, pn, ys, yr):
        self.cm, self.ny, self.e, self.w = cm, ny, e_ref, w_ref
        self.hs, self.hr, self.ps, self.pr, self.pn, self.ys, self.yr = hs, hr, ps, pr, pn, ys, yr
        self.y, self.h = lax.axis_index("y"), lax.axis_index("h")
        self.part = cm.fw // ny

    def place(self, hh, gg, yy):
        return self.w.at[
            pl.ds(pl.multiple_of((hh * self.cm.nl + gg) * self.cm.fw + yy * self.part, self.part), self.part)
        ]

    def piece(self, m):
        cm, to = self.cm, self.cm.after(m)
        return cm.copy(
            self.e.at[to], self.place(self.h, cm.g, self.y), self.ps.at[m], self.pr.at[m], cm.c, to
        )

    def here(self):
        return pltpu.make_async_copy(
            self.e.at[self.cm.g], self.place(self.h, self.cm.g, self.y), self.pn
        )

    def crossed(self, m, hh):
        where = self.place(hh, self.cm.before(m), self.y)
        return pltpu.make_async_remote_copy(
            src_ref=where, dst_ref=where, send_sem=self.hs.at[m], recv_sem=self.hr.at[m],
            device_id={"h": 1 - self.h}, device_id_type=MESH,
        )

    def shared(self, side, m, k, yy):
        where = self.place(self.h if side == 0 else 1 - self.h, self.cm.before(m), yy)
        return pltpu.make_async_remote_copy(
            src_ref=where, dst_ref=where,
            send_sem=self.ys.at[side, m, k - 1], recv_sem=self.yr.at[side, m, k - 1],
            device_id={"y": lax.rem(self.y + k, self.ny)}, device_id_type=MESH,
        )

    def start(self, steps):
        for m in steps:
            if m == 0:
                self.here().start()
            else:
                self.piece(m).start()

    def own(self, m):
        if m == 0:
            self.here().wait()
        else:
            self.piece(m).wait_recv()

    def start_crossing(self, m):
        self.crossed(m, self.h).start()

    def wait_crossing(self, m):
        self.crossed(m, 1 - self.h).wait_recv()

    def share(self, side, m):
        for k in range(1, self.ny):
            self.shared(side, m, k, self.y).start()

    def pass_own(self, m, cross=True):
        self.own(m)
        if cross:
            self.start_crossing(m)
        self.share(0, m)

    def pass_crossed(self, m, following=None):
        self.wait_crossing(m)
        if following is not None and following < self.cm.nl:
            self.start_crossing(following)
        self.share(1, m)

    def wait(self, side, steps):
        for m in steps:
            for k in range(1, self.ny):
                self.shared(side, m, k, lax.rem(self.y + self.ny - k, self.ny)).wait_recv()

    def drain_own(self, steps):
        for m in steps:
            if m > 0:
                self.piece(m).wait_send()

    def drain_crossing(self, steps):
        for m in steps:
            self.crossed(m, self.h).wait_send()

    def drain_shared(self, side, steps):
        for m in steps:
            for k in range(1, self.ny):
                self.shared(side, m, k, self.y).wait_send()


def spread_scratch(ny, nl):
    dma = pltpu.SemaphoreType.DMA
    return [
        dma((nl,)),
        dma((nl,)),
        dma((nl,)),
        dma((nl,)),
        dma,
        dma((2, nl, max(ny - 1, 1))),
        dma((2, nl, max(ny - 1, 1))),
    ]


def movers(ny):
    y, h = lax.axis_index("y"), lax.axis_index("h")
    return [{"y": lax.rem(y + k, ny)} for k in range(1, ny)] + [{"h": 1 - h}]


def ag_scratch(nl, nc, t, d):
    return [
        pltpu.VMEM((t, d), BF16),
        pltpu.SemaphoreType.DMA((nc,)),
        pltpu.SemaphoreType.DMA((nc, nl)),
        pltpu.SemaphoreType.DMA((nc, nl)),
        pltpu.SemaphoreType.DMA((nc, nl)),
        pltpu.SemaphoreType.DMA((nc, nl)),
    ]


def rs_scratch(nl, nc, tc, fw):
    return [
        pltpu.VMEM((nc, 2, nl, tc, fw), BF16),
        pltpu.VMEM((nc, nl, tc, fw), BF16),
        pltpu.VMEM((nc, nl - 1, tc, fw), BF16),
        pltpu.SemaphoreType.DMA((nc,)),
        pltpu.SemaphoreType.DMA((nc,)),
        pltpu.SemaphoreType.DMA((nc, nl)),
        pltpu.SemaphoreType.DMA((nc, nl)),
    ]


def st_scratch(nl, nc, t):
    return [
        pltpu.VMEM((2 * nl, nc, 1, t // nc), F32),
        pltpu.SemaphoreType.DMA((nc, 2 * nl)),
        pltpu.SemaphoreType.DMA((nc, 2 * nl)),
    ]


def cs_scratch(nl, d, fw):
    return [
        pltpu.VMEM((8, d), F32),
        pltpu.VMEM((2 * nl * 8, fw), F32),
        pltpu.SemaphoreType.DMA((2 * nl,)),
        pltpu.SemaphoreType.DMA((2 * nl,)),
    ]


VM = pl.BlockSpec(memory_space=pltpu.VMEM)
SM = pl.BlockSpec(memory_space=pltpu.SMEM)
ANY = pl.BlockSpec(memory_space=pl.ANY)


class Background:
    def __init__(self, loads, stores, step):
        self.loads, self.stores, self.step = loads, stores, step
        for copy in loads:
            copy.start()

    def ready(self):
        for copy in self.loads:
            copy.wait()

    def copy(self, k, i):
        held, out, sems = self.stores[k]
        rows = pl.ds(pl.multiple_of(i * self.step, self.step), self.step)
        return pltpu.make_async_copy(held.at[rows], out.at[rows], sems.at[i])

    def store(self, i, *which):
        for k in which:
            self.copy(k, i).start()

    def stored(self, i):
        for k in self.stores:
            self.copy(k, i).wait()


def call(kernel, name, outs, in_specs, out_specs, scratch, collective, us, args, late=(), flow=(), step=1, aliases=None):
    extra = {}
    if collective is not None:
        extra = {"collective_id": collective, "has_side_effects": True}
    single = not isinstance(outs, tuple)
    results = (outs,) if single else outs
    in_specs, out_specs = list(in_specs), [out_specs] if single else list(out_specs)
    n_in, n_out, n_scratch = len(args), len(results), len(scratch)
    dma = pltpu.SemaphoreType.DMA
    more = []
    for k in late:
        in_specs[k] = ANY
        more += [pltpu.VMEM(args[k].shape, args[k].dtype), dma]
    for k in flow:
        out_specs[k] = ANY
        more += [pltpu.VMEM(results[k].shape, results[k].dtype), dma((results[k].shape[0] // step,))]

    def whole(*refs):
        ins, results_here = list(refs[:n_in]), list(refs[n_in : n_in + n_out])
        own = refs[n_in + n_out : n_in + n_out + n_scratch]
        extras = list(refs[n_in + n_out + n_scratch :])
        loads, stores = [], {}
        for k in late:
            held, sem = extras.pop(0), extras.pop(0)
            loads.append(pltpu.make_async_copy(ins[k], held, sem))
            ins[k] = held
        for k in flow:
            held, sems = extras.pop(0), extras.pop(0)
            stores[k] = (held, results_here[k], sems)
            results_here[k] = held
        kernel(Background(loads, stores, step), *ins, *results_here, *own)

    return pl.pallas_call(
        whole,
        name=name,
        out_shape=outs,
        in_specs=in_specs,
        out_specs=out_specs[0] if single else tuple(out_specs),
        scratch_shapes=scratch + more,
        input_output_aliases=aliases or {},
        compiler_params=pltpu.CompilerParams(vmem_limit_bytes=VMEM_LIMIT, **extra),
        cost_estimate=pl.CostEstimate(
            flops=int(us * 5e8), bytes_accessed=int(us * 3e6), transcendentals=0
        ),
    )(*args)


def shape(s, dtype):
    return jax.ShapeDtypeStruct(s, dtype)


def ones_rows(values):
    folded = values[:, :LANES]
    for k in range(1, values.shape[1] // LANES):
        folded = folded + values[:, k * LANES : (k + 1) * LANES]
    return nt(jnp.ones((8, LANES), F32), folded, HIGHEST)


def row_sum(values):
    return jnp.sum(values, axis=0, keepdims=True)


def down_part(nf, ny):
    return -(-(-(-nf // ny)) // (16 * PIECES)) * 16 * PIECES


def merged_tile(frozen, down, up):
    return frozen.astype(F32) + SCALE * nn(down, up, HIGHEST)


def qkv_forward(
    cfg, ny, npad, nf, x_in, w_qkv, a_qkv, b_qkv, tail_qkv, gains, rows_out, small, small_gu, cosine, sine,
    w_gu, a_gu, b_gu, tail_gu, w_down, a_down, b_down,
):
    t, fw, d, nl, nc, tc = cfg
    width = 3 * fw
    wide = width + LANES
    part = fw // ny
    down_rows = down_part(nf, ny) * ny
    ff_half = w_gu.shape[2] // 2

    def kernel(
        io, x_ref, wq_hbm, aq_ref, bq_ref, tq_ref, gain_ref, eo_ref, m_ref, mg_ref, cos_ref, sin_ref,
        wg_hbm, ag_ref, bg_ref, tg_ref, wdown_ref, ad_ref, bd_ref,
        xs_ref, w_ref, wo_ref, ms_ref, mgs_ref, sc_ref, sq_ref, qkv_ref, lora_ref, rate_ref, eg_ref, ed_ref, wgs_ref, out_ref,
        full, own, sd, rd, sc, rc, keep, xs_s, xs_r, xs_l, small_sems,
        hs, hr, ps, pr, pn, ys, yr, os, orr, ol, oys, oyr,
        e_ref, wq, wg, wload, ghs, ghr, gps, gpr, gpn, gys, gyr,
    ):
        cm = Comm(nl, nc, tc, fw, out_by_one=0.9375)
        cm.ag_refs(xs_ref, full, own, sd, rd, sc, rc)
        swap = Swap(cm)
        weights = Spread(cm, ny, e_ref, w_ref, hs, hr, ps, pr, pn, ys, yr)
        mine = pl.ds(pl.multiple_of(weights.y * part, part), part)
        load_q = pltpu.make_async_copy(
            wq_hbm.at[:, mine, pl.ds(pl.multiple_of(cm.c * (d // 2), LANES), d // 2)], wq, wload.at[0]
        )
        load_g = pltpu.make_async_copy(
            wg_hbm.at[:, mine, pl.ds(pl.multiple_of(cm.c * ff_half, LANES), ff_half)], wg, wload.at[1]
        )
        load_q.start()
        load_g.start()
        later = Spread(cm, ny, eg_ref, wgs_ref, ghs, ghr, gps, gpr, gpn, gys, gyr)
        output = RowMove(swap, ny, fw // ny, eo_ref, wo_ref, os, orr, ol, oys, oyr)
        cm.barrier(movers(ny), [swap.partner])

        def token_swap(i):
            rows = cm.rows(i)
            return x_ref.at[rows], xs_ref.at[rows], (xs_s.at[i], xs_r.at[i], xs_l.at[i])

        m_swap = (m_ref, ms_ref, tuple(small_sems.at[k] for k in range(3)))
        mg_swap = (mg_ref, mgs_ref, tuple(small_sems.at[k] for k in range(3, 6)))

        def start_swap(i, carry_on):
            swap.start(*token_swap(i))
            return carry_on

        lax.fori_loop(0, min(WINDOW, nc), start_swap, 0)
        swap.start(*m_swap)
        swap.start(*mg_swap)
        load_q.wait()
        gain_attn, gain_ffn = gain_ref[mine, 0:1], gain_ref[mine, 1:2]
        for gg in range(nl):
            columns = pl.ds(pl.multiple_of((cm.c * nl + gg) * fw, fw), fw)
            for k in range(3):
                tile = merged_tile(wq[k, :, gg * fw : (gg + 1) * fw], aq_ref[k, mine, :], bq_ref[k, :, columns])
                e_ref[gg, :, k * fw : (k + 1) * fw] = (tile * gain_attn).astype(BF16)
            e_ref[gg, :, width:] = tq_ref[mine, :]
        weights.start(range(nl))

        def gate_up(gg):
            off = gg * nf % LANES
            window = -(-(off + nf) // LANES) * LANES
            for k in range(2):
                raw = wg[k, :, gg * nf - off : gg * nf - off + window].astype(F32)
                if off:
                    raw = pltpu.roll(raw, window - off, 1)
                tile = merged_tile(raw[:, :npad], ag_ref[k, mine, :], bg_ref[k, cm.c * nl + gg]) * gain_ffn
                lane = lax.broadcasted_iota(jnp.int32, tile.shape, 1)
                eg_ref[gg, :, k * npad : (k + 1) * npad] = jnp.where(
                    lane < nf, tile, tg_ref[k, mine, :].astype(F32)
                ).astype(BF16)

        def down_tiles(k):
            if k == 0:
                if down_rows > nf:
                    ed_ref[nf:, :] = jnp.zeros((down_rows - nf, ed_ref.shape[1]), BF16)
                ed_ref[:nf, d:] = jnp.zeros((nf, LANES), BF16)
                ed_ref[:nf, d : d + RANK] = ad_ref[...].astype(BF16)
            for n in (2 * k, 2 * k + 1):
                at = slice(n * fw, (n + 1) * fw)
                ed_ref[:nf, at] = merged_tile(wdown_ref[:, at], ad_ref[...], bd_ref[:, at]).astype(BF16)

        def gather(i, carry_on):
            swap.wait(*token_swap(i))

            @pl.when(i + WINDOW < nc)
            def _():
                swap.start(*token_swap(i + WINDOW))

            cm.ag_send(i)
            return carry_on

        def forward(i, carry_on):
            cm.ag_step(i, more=False)
            return carry_on

        weights.pass_own(0)
        half = nc // 2
        lax.fori_loop(0, half, gather, 0)
        weights.pass_own(1)
        lax.fori_loop(half, nc, gather, 0)
        for m in range(2, nl):
            weights.pass_own(m, cross=False)
        load_g.wait()
        io.ready()
        for m in range(nl):
            lax.fori_loop(nc * m // nl, nc * (m + 1) // nl, forward, 0)
            gate_up(m)
            weights.pass_crossed(m, m + 2)
            down_tiles(m)
        output.start()
        later.start(range(EARLY + 1))
        for m in range(EARLY):
            later.own(m)
            later.start_crossing(m)
        cm.ag_step(jnp.int32(nc), more=False)

        def stored(i):
            rows = cm.rows(i)
            return pltpu.make_async_copy(full.at[rows], out_ref.at[rows], keep.at[i])

        def rates(i, carry_on):
            cm.ag_wait(i)
            stored(i).start()
            wide_block = full[cm.rows(i), :].astype(F32)
            rate = lax.rsqrt(jnp.sum(wide_block * wide_block, axis=1, keepdims=True) / d + EPS)
            rate_ref[cm.rows(i), :] = jnp.broadcast_to(rate, (tc, LANES))
            return carry_on

        lax.fori_loop(0, nc, rates, 0)
        for side in (0, 1):
            weights.wait(side, range(nl))
        output.pass_on()

        def squares(i, total):
            rows = pl.ds(pl.multiple_of(i * fw, fw), fw)
            tail = w_ref[rows, width:].astype(F32)
            gain = tail[:, 3 * RANK : 3 * RANK + 1] + tail[:, 3 * RANK + 1 : 3 * RANK + 2]
            value = w_ref[rows, :width].astype(F32) * (1.0 / gain)
            return total + row_sum(value * value)

        square = lax.fori_loop(0, 2 * nl, squares, jnp.zeros((1, width), F32))
        swap.wait(*m_swap)
        sq_ref[...] = jnp.broadcast_to(square, (8, width))
        for k in range(3):
            at = slice(k * fw, (k + 1) * fw)
            sc_ref[:, at] = jnp.broadcast_to(ms_ref[k : k + 1, :] * lax.rsqrt(square[:, at]), (8, fw))
        sc_ref[:, width:] = jnp.ones((8, LANES), F32)

        big = 2 * tc if nc % 2 == 0 else tc

        def body(i, carry_on):
            rows = pl.ds(pl.multiple_of(i * big, big), big)
            out = nn(full[rows, :], w_ref[...]) * rate_ref[rows, 0:1] * sc_ref[0:1, :]
            cosine_here, sine_here = cos_ref[rows, :], sin_ref[rows, :]
            for k in range(3):
                for hd in range(fw // HD):
                    at = k * fw + hd * HD
                    value = out[:, at : at + HD]
                    if k < 2:
                        value = value * cosine_here + pltpu.roll(value, HD // 2, 1) * sine_here
                    qkv_ref[rows, at : at + HD] = value.astype(BF16)
            lora_ref[rows, :] = out[:, width:].astype(BF16)
            for k in range(big // tc):
                io.store(i * (big // tc) + k, 7, 8, 9)
            return carry_on

        lax.fori_loop(0, t // big, body, 0)
        for m in range(EARLY):
            later.wait_crossing(m)
        later.own(EARLY)
        output.wait()
        swap.wait(*mg_swap)

        def drain(i, carry_on):
            cm.ag_drain(i)
            stored(i).wait()
            io.stored(i)
            swap.drain(*token_swap(i))
            return carry_on

        lax.fori_loop(0, nc, drain, 0)
        swap.drain(*m_swap)
        swap.drain(*mg_swap)
        weights.drain_own(range(nl))
        weights.drain_crossing(range(nl))
        for side in (0, 1):
            weights.drain_shared(side, range(nl))
        later.drain_own(range(EARLY + 1))
        later.drain_crossing(range(EARLY))
        output.drain()

    dma = pltpu.SemaphoreType.DMA
    return call(
        kernel,
        "qkv_forward",
        (
            shape((t, fw), BF16),
            shape((d, wide), BF16),
            shape(rows_out.shape, BF16),
            shape(small.shape, F32),
            shape(small_gu.shape, F32),
            shape((8, wide), F32),
            shape((8, width), F32),
            shape((t, width), BF16),
            shape((t, LANES), BF16),
            shape((t, LANES), F32),
            shape((nl, part, 2 * npad), BF16),
            shape((down_rows, d + LANES), BF16),
            shape((d, 2 * npad), BF16),
            shape((t, d), BF16),
        ),
        [VM, ANY, VM, VM, VM, VM, ANY, VM, VM, VM, VM, ANY, VM, VM, VM, VM, VM, VM],
        (VM,) * 12 + (ANY, ANY),
        ag_scratch(nl, nc, t, d)
        + [dma((nc,))] * 4
        + [dma((6,))]
        + spread_scratch(ny, nl)
        + row_move_scratch(ny)
        + [
            pltpu.VMEM((nl, part, wide), BF16),
            pltpu.VMEM((3, part, d // 2), BF16),
            pltpu.VMEM((2, part, ff_half), BF16),
            dma((2,)),
        ]
        + spread_scratch(ny, nl),
        1,
        90,
        (
            x_in, w_qkv, a_qkv, b_qkv, tail_qkv, gains, rows_out, small, small_gu, cosine, sine,
            w_gu, a_gu, b_gu, tail_gu, w_down, a_down, b_down,
        ),
        late=(9, 10, 12, 13, 14, 15, 16, 17),
        flow=(7, 8, 9),
        step=tc,
    )


def allowed_of(key_segment, query_segment, j, i, block):
    key_at = j * block + lax.broadcasted_iota(jnp.int32, (block, block), 0)
    query_at = i * block + lax.broadcasted_iota(jnp.int32, (block, block), 1)
    return (key_segment == query_segment) & (key_at <= query_at)


def attention_forward(cfg, qkv, seg_column, seg_row, first_block, block):
    t, fw = cfg[0], cfg[1]
    heads = fw // HD

    def kernel(io, qkv_ref, sc_ref, sr_ref, first_ref, out_ref, lse_ref):
        def at(i):
            return pl.ds(pl.multiple_of(i * block, block), block)

        def columns(k, hd):
            return slice(k * fw + hd * HD, k * fw + (hd + 1) * HD)

        def one_query(i, carry_on):
            queries = [qkv_ref[at(i), columns(0, hd)] for hd in range(heads)]
            query_segment = sr_ref[0:1, at(i)]

            def one_key(j, carry):
                allowed = allowed_of(sc_ref[at(j), 0:1], query_segment, j, i, block)
                out = []
                for hd in range(heads):
                    top, total, acc = carry[hd]
                    s = nt(qkv_ref[at(j), columns(1, hd)], queries[hd]) * (HD**-0.5)
                    s = jnp.where(allowed, s, MASKED)
                    new = jnp.maximum(top, jnp.max(s, axis=0, keepdims=True))
                    p = jnp.exp(s - new)
                    shrink = jnp.exp(top - new)
                    total = total * shrink + jnp.sum(p, axis=0, keepdims=True)
                    acc = acc * shrink + tn(qkv_ref[at(j), columns(2, hd)], p.astype(BF16))
                    out.append((new, total, acc))
                return tuple(out)

            first = (
                jnp.full((1, block), MASKED, F32),
                jnp.zeros((1, block), F32),
                jnp.zeros((HD, block), F32),
            )
            out = lax.fori_loop(first_ref[i], i + 1, one_key, (first,) * heads)
            for hd in range(heads):
                top, total, acc = out[hd]
                out_ref[at(i), hd * HD : (hd + 1) * HD] = (acc / total).T.astype(BF16)
                lse_ref[hd * 8 : hd * 8 + 8, at(i)] = jnp.broadcast_to(
                    top + jnp.log(total), (8, block)
                )
            return carry_on

        lax.fori_loop(0, t // block, one_query, 0)

    return call(
        kernel,
        "attention_forward",
        (shape((t, fw), BF16), shape((heads * 8, t), F32)),
        [VM, VM, VM, SM],
        (VM, VM),
        [],
        None,
        15,
        (qkv, seg_column, seg_row, first_block),
    )


def out_forward(cfg, ny, npad, attended, weights, x, magnitude, w_gu, blocks, rows_down):
    t, fw, d, nl, nc, tc = cfg
    part = rows_down.shape[0] // ny

    def kernel(
        io, a_ref, w_ref, x_ref, m_ref, w_in, e_ref, ed_ref,
        mid_ref, u_ref, st_ref, sc_ref, sq_ref, lora_ref, wg_ref, wd_ref,
        sb, cb, gb, s1, r1, s2, r2, cpart, cheld, css, csr,
        hs, hr, ps, pr, pn, ys, yr, dws, dwr, dwl, dys, dyr,
    ):
        cm = Comm(nl, nc, tc, fw, back_by_two=0.0625)
        cm.rs_refs(sb, cb, gb, s1, r1, s2, r2)
        cm.cs_refs(cpart, cheld, css, csr)
        columns = Spread(cm, ny, e_ref, wg_ref, hs, hr, ps, pr, pn, ys, yr)
        swap = Swap(cm)
        down_rows = RowMove(swap, ny, part, ed_ref, wd_ref, dws, dwr, dwl, dys, dyr)
        cm.barrier(movers(ny), [swap.partner])
        down_rows.start()
        columns.start_crossing(EARLY)
        columns.start(range(EARLY + 1, nl))
        for m in range(EARLY):
            columns.share(0, m)
            columns.share(1, m)
        columns.share(0, EARLY)
        cm.cs_start(w_ref)
        if part * ny < npad:
            wd_ref[part * ny :, :] = jnp.zeros((npad - part * ny, wd_ref.shape[1]), BF16)
        def body(i, carry_on):
            @pl.when(i < nc)
            def _():
                block = a_ref[cm.rows(i), :]
                for role in range(2 * nl):
                    sb[i, role // nl, role % nl] = nn(
                        block, w_ref[:, role * fw : (role + 1) * fw]
                    ).astype(BF16)
                cm.rs_across(i).start()
                lora_ref[cm.rows(i), :] = nn(block, w_ref[:, d:]).astype(BF16)
                io.store(i, 5)

            cm.rs_steps(i)

            @pl.when(i == 3)
            def _():
                total = cm.cs_total()
                sq_ref[...] = jnp.broadcast_to(total, (8, fw))
                sc_ref[...] = jnp.broadcast_to(m_ref[3:4, :] * lax.rsqrt(total), (8, fw))

            @pl.when(i == 5)
            def _():
                down_rows.pass_on()

            @pl.when(i == 1)
            def _():
                columns.pass_own(EARLY + 1)

            @pl.when(i == 3)
            def _():
                for m in range(EARLY + 2, nl):
                    columns.pass_own(m, cross=False)

            @pl.when(i == min(6, nc + 2))
            def _():
                columns.pass_crossed(EARLY, EARLY + 2)

            @pl.when((i >= 3) & (i <= nc + 2))
            def _():
                rows = cm.rows(i - 3)
                middle = x_ref[rows, :].astype(F32) + cm.rs_total(i - 3) * sc_ref[0:1, :]
                mid_ref[rows, :] = middle
                u_ref[rows, :] = middle.astype(BF16)
                st_ref[i - 3] = ones_rows(middle * middle)[0:1, :]
                io.store(i - 3, 0, 1)

            return carry_on

        lax.fori_loop(0, nc + 3, body, 0)

        def drain(i, carry_on):
            cm.rs_drain(i)
            io.stored(i)
            return carry_on

        for m in range(EARLY + 1, nl):
            columns.pass_crossed(m, m + 2)
        for side in (0, 1):
            columns.wait(side, range(nl))
        down_rows.wait()
        lax.fori_loop(0, nc, drain, 0)
        cm.cs_drain()
        columns.drain_own(range(EARLY + 1, nl))
        columns.drain_crossing(range(EARLY, nl))
        for side in (0, 1):
            columns.drain_shared(side, range(nl))
        down_rows.drain()

    return call(
        kernel,
        "out_forward",
        (
            shape((t, fw), F32),
            shape((t, fw), BF16),
            shape((nc, 1, tc), F32),
            shape((8, fw), F32),
            shape((8, fw), F32),
            shape((t, LANES), BF16),
            shape(w_gu.shape, BF16),
            shape((npad, d + LANES), BF16),
        ),
        [VM] * 4 + [ANY, ANY, ANY],
        (VM,) * 6 + (ANY, VM),
        rs_scratch(nl, nc, tc, fw)
        + cs_scratch(nl, d, fw)
        + spread_scratch(ny, nl)
        + row_move_scratch(ny),
        2,
        90,
        (attended, weights, x, magnitude, w_gu, blocks, rows_down),
        flow=(0, 1, 5),
        step=tc,
        aliases={4: 6},
    )


def ffn_forward(cfg, npad, nf, u, stats, w_gu, m_gu, w_down, small, middle, cotangent):
    t, fw, d, nl, nc, tc = cfg

    def kernel(
        io, u_ref, st_ref, wg_ref, mg_ref, wd_ref, m_ref, mid_ref, cin_ref,
        gu_ref, hid_ref, out_ref, gm_ref, rate_ref, gp_ref, sg_ref, qg_ref, sd_ref, qd_ref, lora_ref, cot_ref, uf_ref,
        full, own, sd, rd, sc, rc, sb, cb, gb, s1, r1, s2, r2, sa, ss, sr, cpart, cheld, css, csr, keep,
        cs_s, cs_r, cs_l,
    ):
        cm = Comm(nl, nc, tc, fw, out_by_one=0.625, back_by_two=0.375)
        cm.ag_refs(u_ref, full, own, sd, rd, sc, rc)
        cm.rs_refs(sb, cb, gb, s1, r1, s2, r2)
        cm.st_refs(st_ref, sa, ss, sr)
        cm.cs_refs(cpart, cheld, css, csr)
        swap = Swap(cm)
        cm.barrier((), [swap.partner])

        def cot_swap(i):
            rows = cm.rows(i)
            return cin_ref.at[rows], cot_ref.at[rows], (cs_s.at[i], cs_r.at[i], cs_l.at[i])

        cm.st_send(None)
        cm.ag_start()
        io.ready()

        def cot_out(i, carry_on):
            swap.start(*cot_swap(i))
            return carry_on


        def squares(i, total):
            rows = pl.ds(pl.multiple_of(i * fw, fw), fw)
            gain = (
                wg_ref[rows, nf + RANK : nf + RANK + 1].astype(F32)
                + wg_ref[rows, nf + RANK + 1 : nf + RANK + 2].astype(F32)
            )
            value = wg_ref[rows, :].astype(F32) * (1.0 / gain)
            return total + row_sum(value * value)

        square = lax.fori_loop(0, 2 * nl, squares, jnp.zeros((1, 2 * npad), F32))
        column = lax.rem(lax.broadcasted_iota(jnp.int32, (1, 2 * npad), 1), npad)
        square = jnp.where(column < nf, square, 1.0)
        qg_ref[...] = jnp.broadcast_to(square, (8, 2 * npad))
        sg_ref[...] = jnp.broadcast_to(mg_ref[...] * lax.rsqrt(square), (8, 2 * npad))
        cm.ag_ahead()
        gm_ref[...] = jnp.zeros_like(gm_ref)

        def stored(i):
            rows = cm.rows(i)
            return pltpu.make_async_copy(full.at[rows], uf_ref.at[rows], keep.at[i])

        cm.cs_start(wd_ref)
        lax.fori_loop(0, nc, cot_out, 0)

        def body(i, carry_on):
            @pl.when(i < nc)
            def _():
                cm.ag_step(i + 2)
                cm.ag_wait(i)

                @pl.when(i == 0)
                def _():
                    cm.st_wait(None)

                stored(i).start()
                rows = cm.rows(i)
                rate = lax.rsqrt(cm.st_sum(i) / d + EPS)
                rate_ref[rows, :] = jnp.broadcast_to(rate, (tc, LANES))
                out = nn(full[rows, :], wg_ref[...]) * rate * sg_ref[0:1, :]
                gu_ref[rows, :] = out.astype(BF16)
                gate, up = out[:, :npad], out[:, npad:]
                hidden = (gate / (1.0 + jnp.exp(-gate)) * up).astype(BF16)
                hid_ref[rows, :] = hidden
                for role in range(2 * nl):
                    sb[i, role // nl, role % nl] = nn(
                        hidden, wd_ref[:, role * fw : (role + 1) * fw]
                    ).astype(BF16)
                cm.rs_across(i).start()
                lora_ref[rows, :] = nn(hidden, wd_ref[:, d:]).astype(BF16)
                io.store(i, 0, 1, 4, 10)

            cm.rs_steps(i)

            @pl.when(i == 3)
            def _():
                total = cm.cs_total()
                qd_ref[...] = jnp.broadcast_to(total, (8, fw))
                sd_ref[...] = jnp.broadcast_to(m_ref[4:5, :] * lax.rsqrt(total), (8, fw))

            @pl.when(i >= 3)
            def _():
                rows = cm.rows(i - 3)
                down = cm.rs_total(i - 3) * sd_ref[0:1, :]
                out_ref[rows, :] = (mid_ref[rows, :] + down).astype(BF16)
                swap.wait(*cot_swap(i - 3))
                seed = cot_ref[rows, :].astype(F32)
                gm_ref[0:1, :] += row_sum(seed * down)
                gp_ref[rows, :] = (seed * sd_ref[0:1, :]).astype(BF16)
                io.store(i - 3, 2, 5)

            return carry_on

        lax.fori_loop(0, nc + 3, body, 0)

        def drain(i, carry_on):
            cm.ag_drain(i)
            cm.rs_drain(i)
            stored(i).wait()
            io.stored(i)
            swap.drain(*cot_swap(i))
            return carry_on

        lax.fori_loop(0, nc, drain, 0)
        cm.st_drain(None)
        cm.cs_drain()

    dma = pltpu.SemaphoreType.DMA
    return call(
        kernel,
        "ffn_forward",
        (
            shape((t, 2 * npad), BF16),
            shape((t, npad), BF16),
            shape((t, fw), BF16),
            shape((8, fw), F32),
            shape((t, LANES), F32),
            shape((t, fw), BF16),
            shape((8, 2 * npad), F32),
            shape((8, 2 * npad), F32),
            shape((8, fw), F32),
            shape((8, fw), F32),
            shape((t, LANES), BF16),
            shape((t, fw), BF16),
            shape((t, d), BF16),
        ),
        [VM] * 8,
        (VM,) * 12 + (ANY,),
        ag_scratch(nl, nc, t, d)
        + rs_scratch(nl, nc, tc, fw)
        + st_scratch(nl, nc, t)
        + cs_scratch(nl, d, fw)
        + [dma((nc,))] * 4,
        3,
        110,
        (u, stats, w_gu, m_gu, w_down, small, middle, cotangent),
        late=(2, 4, 6),
        flow=(0, 1, 2, 4, 5, 10),
        step=tc,
    )


def ffn_backward(cfg, npad, gp, gu, w_gu, sc_gu, b_gu, w_down, b_down, rate, cotangent, middle, x, sc_out):
    t, fw, d, nl, nc, tc = cfg

    def kernel(
        io, gp_ref, gu_hbm, wg_ref, sg_ref, bg_ref, wd_ref, bd_ref, rate_ref, cot_ref, mid_ref, x_ref, so_ref,
        dm_ref, go_ref, gmo_ref, gm_ref, lg_ref, ld_ref, dp_hbm, gf_ref,
        full, own, sd, rd, sc, rc, sb, cb, gb, s1, r1, s2, r2, sa, ss, sr, st, gu_s, keep, load, save,
    ):
        cm = Comm(nl, nc, tc, fw)
        cm.ag_refs(gp_ref, full, own, sd, rd, sc, rc)
        cm.rs_refs(sb, cb, gb, s1, r1, s2, r2)
        cm.st_refs(st, sa, ss, sr)

        def loaded(i):
            rows = cm.rows(i)
            return pltpu.make_async_copy(gu_hbm.at[rows], gu_s.at[rows], load.at[i])

        def saved(i):
            rows = cm.rows(i)
            return pltpu.make_async_copy(gu_s.at[rows], dp_hbm.at[rows], save.at[i])

        def stored(i):
            rows = cm.rows(i)
            return pltpu.make_async_copy(full.at[rows], gf_ref.at[rows], keep.at[i])

        cm.barrier()
        cm.ag_start()

        def start_loads(i, carry_on):
            loaded(i).start()
            return carry_on

        lax.fori_loop(0, nc, start_loads, 0)
        cm.ag_ahead()
        io.ready()
        gm_ref[...] = jnp.zeros_like(gm_ref)
        gmo_ref[...] = jnp.zeros_like(gmo_ref)

        def body(i, carry_on):
            @pl.when(i < nc)
            def _():
                cm.ag_step(i + 2)
                cm.ag_wait(i)
                stored(i).start()
                loaded(i).wait()
                rows = cm.rows(i)
                block = full[rows, :]
                dh = nt(block, wd_ref[:, :d])
                ld_ref[rows, :] = nt(block, bd_ref[...]).astype(BF16)
                gate = gu_s[rows, :npad].astype(F32)
                up = gu_s[rows, npad:].astype(F32)
                sig = 1.0 / (1.0 + jnp.exp(-gate))
                dgate = dh * up * (sig * (1.0 + gate * (1.0 - sig)))
                dup = dh * (gate * sig)
                pg, pu = dgate * gate, dup * up
                gm_ref[0:1, :npad] += jnp.sum(pg, axis=0, keepdims=True)
                gm_ref[0:1, npad:] += jnp.sum(pu, axis=0, keepdims=True)
                st[i] = ones_rows(pg + pu)[0:1, :]
                cm.st_send(i)
                gu_s[rows, :npad] = (dgate * sg_ref[0:1, :npad]).astype(BF16)
                gu_s[rows, npad:] = (dup * sg_ref[0:1, npad:]).astype(BF16)
                saved(i).start()
                dp = gu_s[rows, :]
                lg_ref[rows, :] = (nt(dp, bg_ref[...].astype(BF16)) * rate_ref[rows, :]).astype(BF16)
                io.store(i, 4, 5)
                for role in range(2 * nl):
                    sb[i, role // nl, role % nl] = nt(
                        dp, wg_ref[role * fw : (role + 1) * fw, :]
                    ).astype(BF16)
                cm.rs_across(i).start()

            cm.rs_steps(i)

            @pl.when(i >= 3)
            def _():
                k = i - 3
                rows = cm.rows(k)
                cm.st_wait(k)
                r = rate_ref[rows, 0:1]
                inner = cm.st_sum(k)
                mid = mid_ref[rows, :]
                dm = (
                    cot_ref[rows, :].astype(F32)
                    + r * cm.rs_total(k)
                    - mid * (r * r * inner / d)
                )
                dm_ref[rows, :] = dm
                go_ref[rows, :] = (dm * so_ref[0:1, :]).astype(BF16)
                io.store(k, 0, 1)
                gmo_ref[0:1, :] += jnp.sum(
                    dm * (mid - x_ref[rows, :].astype(F32)), axis=0, keepdims=True
                )

            return carry_on

        lax.fori_loop(0, nc + 3, body, 0)

        def drain(i, carry_on):
            cm.ag_drain(i)
            cm.rs_drain(i)
            cm.st_drain(i)
            stored(i).wait()
            saved(i).wait()
            io.stored(i)
            return carry_on

        lax.fori_loop(0, nc, drain, 0)

    return call(
        kernel,
        "ffn_backward",
        (
            shape((t, fw), F32),
            shape((t, fw), BF16),
            shape((8, fw), F32),
            shape((8, 2 * npad), F32),
            shape((t, LANES), BF16),
            shape((t, LANES), BF16),
            shape((t, 2 * npad), BF16),
            shape((t, d), BF16),
        ),
        [VM, ANY] + [VM] * 10,
        (VM,) * 6 + (ANY, ANY),
        ag_scratch(nl, nc, t, d)
        + rs_scratch(nl, nc, tc, fw)
        + st_scratch(nl, nc, t)
        + [
            pltpu.VMEM((nc, 1, tc), F32),
            pltpu.VMEM((t, 2 * npad), BF16),
            pltpu.SemaphoreType.DMA((nc,)),
            pltpu.SemaphoreType.DMA((nc,)),
            pltpu.SemaphoreType.DMA((nc,)),
        ],
        4,
        120,
        (gp, gu, w_gu, sc_gu, b_gu, w_down, b_down, rate, cotangent, middle, x, sc_out),
        late=(2, 4, 5, 6, 7, 8, 9, 10),
        flow=(0, 1, 4, 5),
        step=tc,
    )


def gain_rows(tail, at):
    lane = lax.broadcasted_iota(jnp.int32, (8, LANES), 1)
    pick = jnp.where((lane == at) | (lane == at + 1), 1.0, 0.0).astype(BF16)
    column = tail[:, at : at + 1].astype(F32) + tail[:, at + 1 : at + 2].astype(F32)
    return nt(pick, tail)[0:1, :], column


class Stream:
    def __init__(self, sources, slots, sems, step):
        self.sources, self.slots, self.sems, self.step = sources, slots, sems, step

    def copies(self, i):
        rows = pl.ds(pl.multiple_of(i * self.step, self.step), self.step)
        slot = lax.rem(i, 2)
        return [
            pltpu.make_async_copy(src.at[rows, columns], held.at[slot], self.sems.at[k, slot])
            for k, ((src, columns), held) in enumerate(zip(self.sources, self.slots))
        ]

    def start(self, i):
        for copy in self.copies(i):
            copy.start()

    def wait(self, i):
        for copy in self.copies(i):
            copy.wait()
        return [held[lax.rem(i, 2)] for held in self.slots]


def stream_scratch(step, widths):
    return [pltpu.VMEM((2, step, n), BF16) for n in widths] + [pltpu.SemaphoreType.DMA((len(widths), 2))]


def out_backward(
    cfg, npad, nf, go, weights, b_out, ratios, w_gu, w_down, up_gu, b_down, gm_gu, square_gu, m_gu,
    u_full, lg_gu, gu, dp_gu, hidden, lg_down, lora_down, gp_full, result,
):
    t, fw, d, nl, nc, tc = cfg
    off = nf - (npad - LANES)
    widths = (d, LANES, LANES, LANES, 2 * npad, npad, LANES, LANES, d)

    def kernel(
        io, go_ref, w_ref, b_ref, q_ref, wg_ref, wd_ref, up_ref, bd_ref, gm_ref, sq_ref, m_ref,
        uf_hbm, lg_hbm, gu_hbm, dp_hbm, hid_hbm, ld_hbm, lo2_hbm, gp_hbm, res_hbm,
        da_ref, lo_ref, qs_ref, sh_ref, lc_ref, gf_ref, moved_ref,
        full, own, sd, rd, sc, rc, keep, qss, qsr, res_sems, acc_a, acc_g, acc_u, acc_d, acc_p, *streams,
    ):
        cm = Comm(nl, nc, tc, fw, out_by_one=0.75)
        swap = Swap(cm)
        result_swap = (res_hbm, moved_ref, tuple(res_sems.at[k] for k in range(3)))
        cm.ag_refs(go_ref, full, own, sd, rd, sc, rc)
        every = lambda n: pl.ds(0, n)
        stream = Stream(
            [
                (uf_hbm, every(d)),
                (lg_hbm, every(LANES)),
                (gu_hbm, pl.ds(npad - LANES, LANES)),
                (gu_hbm, pl.ds(2 * npad - LANES, LANES)),
                (dp_hbm, every(2 * npad)),
                (hid_hbm, every(npad)),
                (ld_hbm, every(LANES)),
                (lo2_hbm, every(LANES)),
                (gp_hbm, every(d)),
            ],
            streams[:-1],
            streams[-1],
            tc,
        )
        stream.start(jnp.int32(0))
        cm.barrier((), [swap.partner])

        def ratio_copy(o, m):
            k = o * nl + m
            return cm.copy(
                q_ref, qs_ref.at[:, cm.columns(cm.c, cm.g)], qss.at[k], qsr.at[k], 1 - cm.c if o else cm.c, cm.after(m)
            )

        cm.ag_start()
        for o, m in cm.st_peers():
            ratio_copy(o, m).start()
        qs_ref[:, cm.columns(cm.c, cm.g)] = q_ref[...]
        swap.start(*result_swap)
        for acc in (acc_a, acc_g, acc_u, acc_d, acc_p):
            acc[...] = jnp.zeros_like(acc)
        cm.ag_ahead()
        io.ready()

        def stored(i):
            rows = cm.rows(i)
            return pltpu.make_async_copy(full.at[rows], gf_ref.at[rows], keep.at[i])

        def body(i, carry_on):
            cm.ag_step(i + 2)

            @pl.when(i + 1 < nc)
            def _():
                stream.start(i + 1)

            u, lg, low_g, low_u, dp, hid, ld, low_d, gp = stream.wait(i)
            acc_a[...] += tn(lg, u)
            acc_g[...] += tn(low_g, dp[:, :npad])
            acc_u[...] += tn(low_u, dp[:, npad:])
            acc_d[...] += tn(ld, hid)
            acc_p[...] += tn(low_d, gp)
            cm.ag_wait(i)
            stored(i).start()
            rows = cm.rows(i)
            block = full[rows, :]
            da_ref[rows, :] = nt(block, w_ref[:, :d]).astype(BF16)
            lo_ref[rows, :] = nt(block, b_ref[...]).astype(BF16)
            return carry_on

        lax.fori_loop(0, nc, body, 0)

        ratio = -gm_ref[0:1, :] / sq_ref[0:1, :]
        term = nt((up_ref[...] * ratio).astype(BF16), wg_ref[...])
        tail_g, tail_u = wg_ref[:, npad - LANES : npad], wg_ref[:, 2 * npad - LANES :]
        gain_row, gain_column = gain_rows(tail_g, off + RANK)
        inverse = 1.0 / (gain_column * gain_column)
        sh_ref[: 2 * RANK, :] = (
            SCALE * (acc_a[: 2 * RANK, :] * gain_row + term[: 2 * RANK, :] / gain_row)
        ).astype(BF16)
        for k, (acc, tail) in enumerate(((acc_g, tail_g), (acc_u, tail_u))):
            at = slice(k * npad, (k + 1) * npad)
            merged = tn((tail.astype(F32) * inverse).astype(BF16), wg_ref[:, at])
            lc_ref[(1 + k) * RANK : (2 + k) * RANK, :] = (
                SCALE * (acc[off : off + RANK, :] + merged[off : off + RANK, :] * ratio[:, at])
            ).astype(BF16)
            lc_ref[3 * RANK + k : 3 * RANK + k + 1, :] = (gm_ref[0:1, at] / m_ref[0:1, at]).astype(BF16)
        lc_ref[3 * RANK + 2 :, :] = jnp.zeros((RANK - 2, npad), BF16)

        for o, m in cm.st_peers():
            ratio_copy(o, m).wait_recv()
        ratio_down = qs_ref[1:2, :]
        lc_ref[:RANK, :] = (
            SCALE
            * (acc_d[:RANK, :] + nt((bd_ref[...].astype(F32) * ratio_down).astype(BF16), wd_ref[:, :d])[:RANK, :])
        ).astype(BF16)
        sh_ref[2 * RANK :, :] = (
            SCALE * (acc_p[:RANK, :] + tn(wd_ref[:, d:], wd_ref[:, :d])[:RANK, :] * ratio_down)
        ).astype(BF16)

        def drain(i, carry_on):
            cm.ag_drain(i)
            stored(i).wait()
            return carry_on

        lax.fori_loop(0, nc, drain, 0)
        swap.wait(*result_swap)
        swap.drain(*result_swap)
        for o, m in cm.st_peers():
            ratio_copy(o, m).wait_send()

    dma = pltpu.SemaphoreType.DMA
    return call(
        kernel,
        "out_backward",
        (
            shape((t, fw), BF16),
            shape((t, LANES), BF16),
            shape((8, d), F32),
            shape((3 * RANK, d), BF16),
            shape((4 * RANK, npad), BF16),
            shape((t, d), BF16),
            shape((t, fw), BF16),
        ),
        [VM] * 11 + [ANY] * 9,
        (VM,) * 5 + (ANY, ANY),
        ag_scratch(nl, nc, t, d)
        + [dma((nc,)), dma((2 * nl,)), dma((2 * nl,)), dma((3,))]
        + [pltpu.VMEM((LANES, n), F32) for n in (d, npad, npad, npad, d)]
        + stream_scratch(tc, widths),
        5,
        60,
        (
            go, weights, b_out, ratios, w_gu, w_down, up_gu, b_down, gm_gu, square_gu, m_gu,
            u_full, lg_gu, gu, dp_gu, hidden, lg_down, lora_down, gp_full, result,
        ),
        late=(1, 2, 4, 5, 6, 7),
    )


def attention_backward(
    cfg, qkv, attended, grad, lse, seg_column, seg_row, first_block, block, cosine, sine, scale, rate, b_qkv
):
    t, fw = cfg[0], cfg[1]
    heads = fw // HD
    width = 3 * fw

    def kernel(
        io, qkv_ref, att_ref, grad_ref, lse_ref, sc_ref, sr_ref, first_ref, cos_ref, sin_ref, scale_ref, rate_ref, b_ref,
        dp_ref, st_ref, gm_ref, lg_ref, dq, dk, dv,
    ):
        def at(i):
            return pl.ds(pl.multiple_of(i * block, block), block)

        def columns(k, hd):
            return slice(k * fw + hd * HD, k * fw + (hd + 1) * HD)

        gm_ref[...] = jnp.zeros_like(gm_ref)
        dk[...] = jnp.zeros_like(dk)
        dv[...] = jnp.zeros_like(dv)

        def one_query(i, carry_on):
            queries = [qkv_ref[at(i), columns(0, hd)] for hd in range(heads)]
            grads = [grad_ref[at(i), columns(0, hd)] for hd in range(heads)]
            deltas = [
                ones_rows(grads[hd].astype(F32) * att_ref[at(i), columns(0, hd)].astype(F32))[0:1, :]
                for hd in range(heads)
            ]
            query_segment = sr_ref[0:1, at(i)]

            def one_key(j, accs):
                allowed = allowed_of(sc_ref[at(j), 0:1], query_segment, j, i, block)
                out = []
                for hd in range(heads):
                    keys = qkv_ref[at(j), columns(1, hd)]
                    s = nt(keys, queries[hd]) * (HD**-0.5)
                    p = jnp.where(allowed, jnp.exp(s - lse_ref[hd * 8 : hd * 8 + 1, at(i)]), 0.0)
                    ds = (p * (nt(qkv_ref[at(j), columns(2, hd)], grads[hd]) - deltas[hd])).astype(BF16)
                    dv[hd, at(j), :] += nn(p.astype(BF16), grads[hd])
                    dk[hd, at(j), :] += nn(ds, queries[hd])
                    out.append(accs[hd] + tn(ds, keys))
                return tuple(out)

            accs = lax.fori_loop(first_ref[i], i + 1, one_key, (jnp.zeros((block, HD), F32),) * heads)
            for hd in range(heads):
                dq[hd, at(i), :] = accs[hd]
            return carry_on

        lax.fori_loop(0, t // block, one_query, 0)

        def finish(i, carry_on):
            rows = at(i)
            cosine_here, sine_here = cos_ref[rows, :], sin_ref[rows, :]
            inner = jnp.zeros((block, HD), F32)
            for hd in range(heads):
                for n, source in enumerate((dq, dk, dv)):
                    where = columns(n, hd)
                    dout = source[hd, rows, :]
                    value = qkv_ref[rows, where].astype(F32)
                    if n < 2:
                        dout = dout * (HD**-0.5)
                        dout = dout * cosine_here - pltpu.roll(dout, HD // 2, 1) * sine_here
                        value = value * cosine_here - pltpu.roll(value, HD // 2, 1) * sine_here
                    product = dout * value
                    inner = inner + product
                    gm_ref[0:1, where] += row_sum(product)
                    dp_ref[rows, where] = (dout * scale_ref[0:1, where]).astype(BF16)
            st_ref[i] = ones_rows(inner)[0:1, :]
            lg_ref[rows, :] = (nt(dp_ref[rows, :], b_ref[...].astype(BF16)) * rate_ref[rows, :]).astype(BF16)
            return carry_on

        lax.fori_loop(0, t // block, finish, 0)

    return call(
        kernel,
        "attention_backward",
        (
            shape((t, width), BF16),
            shape((t // block, 1, block), F32),
            shape((8, width), F32),
            shape((t, LANES), BF16),
        ),
        [VM] * 6 + [SM] + [VM] * 5,
        (VM,) * 4,
        [pltpu.VMEM((heads, t, HD), F32)] * 3,
        None,
        35,
        (qkv, attended, grad, lse, seg_column, seg_row, first_block, cosine, sine, scale, rate, b_qkv),
    )


def qkv_backward(
    cfg, ny, dp, stats, weights, rate, dm, x, shared, local_gu, w_out, up_qkv, b_out, ratios, gm_qkv, square_qkv,
    gm_out, gm_down, small, x_full, lg_qkv, lora_qkv, attended, lg_out, lora_out, go_full,
):
    t, fw, d, nl, nc, tc = cfg
    width = 3 * fw
    peers = 2 * nl
    step = 2 * tc if nc % 2 == 0 else tc
    parts = t // step
    widths = (d, LANES, LANES, fw, LANES, LANES, d)

    def kernel(
        io, dp_ref, st_ref, w_ref, rate_ref, dm_ref, x_ref, sh_ref, l_ref, wo_ref, up_ref, bo_ref, q_ref,
        gm_ref, sq_ref, gmo_ref, gmd_ref, m_ref, xf_hbm, lg_hbm, lq_hbm, at_hbm, lgo_hbm, lo_hbm, gf_hbm,
        out_ref, as_ref, bs_ref, ls_ref,
        sb, cb, gb, s1, r1, s2, r2, sa, ss, sr,
        stage, gs_s, gs_r, gs_l, group, gsum, gss, gsr, final_a, final_b, final_l, fs, fr, fl,
        a_ref, b_ref, acc_a, acc_b, acc_o, acc_p, *streams,
    ):
        cm = Comm(nl, nc, tc, fw, back_by_two=0.25)
        c, g = cm.c, cm.g
        y, h = lax.axis_index("y"), lax.axis_index("h")
        cm.rs_refs(sb, cb, gb, s1, r1, s2, r2)
        cm.st_refs(st_ref, sa, ss, sr)
        swap = Swap(cm)
        every = lambda n: pl.ds(0, n)
        stream = Stream(
            [
                (xf_hbm, every(d)),
                (lg_hbm, every(LANES)),
                (lq_hbm, every(LANES)),
                (at_hbm, every(fw)),
                (lgo_hbm, every(LANES)),
                (lo_hbm, every(LANES)),
                (gf_hbm, every(d)),
            ],
            streams[:-1],
            streams[-1],
            step,
        )
        stream.start(jnp.int32(0))
        senders = [
            {"y": lax.rem(y + ny - k, ny), "c": h, "h": hh} for k in range(1, ny) for hh in (0, 1)
        ]
        cm.barrier(senders + [{"c": h, "h": 1 - h}], [swap.partner, {"c": h, "h": h}])

        def gather_part(o, m):
            to_c, to_g = 1 - c if o else c, cm.after(m)
            k = o * nl + m
            return cm.copy(
                a_ref.at[:, cm.columns(to_c, to_g)], group.at[k], gss.at[k], gsr.at[k], to_c, to_g
            )

        def sums(k, e):
            device = {"y": lax.rem(y + k, ny), "c": lax.rem(c + e, 2), "h": c}
            slot = k * 2 + h
            return [
                pltpu.make_async_remote_copy(
                    src_ref=src, dst_ref=dst.at[slot], send_sem=fs.at[n, k * 2 + e], recv_sem=fr.at[n, slot],
                    device_id=device, device_id_type=MESH,
                )
                for n, (src, dst) in enumerate(((gsum, final_a), (b_ref, final_b), (l_ref, final_l)))
            ]

        def sums_here():
            return [
                pltpu.make_async_copy(src, dst.at[h], fl.at[n])
                for n, (src, dst) in enumerate(((gsum, final_a), (b_ref, final_b), (l_ref, final_l)))
            ]

        cm.st_send(None)
        for acc in (acc_a, acc_b, acc_o, acc_p):
            acc[...] = jnp.zeros_like(acc)

        def adapters(k):
            @pl.when(k + 1 < parts)
            def _():
                stream.start(k + 1)

            xf, lg, low_q, att, lg_o, low_o, gf = stream.wait(k)
            rows = pl.ds(pl.multiple_of(k * step, step), step)
            acc_a[...] += tn(lg, xf)
            acc_b[...] += tn(low_q, dp_ref[rows, :])
            acc_o[...] += tn(lg_o, att)
            acc_p[...] += tn(low_o, gf)

        def adapters_end():
            ratio = -gm_ref[0:1, :] / sq_ref[0:1, :]
            ratio_out = q_ref[0:1, :]
            tail = w_ref[:, width:]
            gain_row, gain_column = gain_rows(tail, 3 * RANK)
            term = nt((up_ref[...] * ratio).astype(BF16), w_ref[:, :width])
            a_ref[: 3 * RANK, :] = (
                SCALE * (acc_a[: 3 * RANK, :] * gain_row + term[: 3 * RANK, :] / gain_row)
            ).astype(BF16)
            merged = tn(
                (tail.astype(F32) / (gain_column * gain_column)).astype(BF16), w_ref[:, :width]
            )
            for k in range(3):
                at, low = slice(k * fw, (k + 1) * fw), slice(k * RANK, (k + 1) * RANK)
                b_ref[(1 + k) * RANK : (2 + k) * RANK, :] = (
                    SCALE * (acc_b[low, at] + merged[low, at] * ratio[:, at])
                ).astype(BF16)
                b_ref[4 * RANK + k : 4 * RANK + k + 1, :] = (gm_ref[0:1, at] / m_ref[k : k + 1, :]).astype(BF16)
            b_ref[4 * RANK + 3 : 4 * RANK + 4, :] = (gmo_ref[0:1, :] / m_ref[3:4, :]).astype(BF16)
            b_ref[4 * RANK + 4 : 4 * RANK + 5, :] = (gmd_ref[0:1, :] / m_ref[4:5, :]).astype(BF16)
            b_ref[4 * RANK + 5 :, :] = jnp.zeros((RANK - 5, fw), BF16)
            b_ref[:RANK, :] = (
                SCALE
                * (acc_o[:RANK, :] + nt((bo_ref[...].astype(F32) * ratio_out).astype(BF16), wo_ref[:, :d])[:RANK, :])
            ).astype(BF16)
            a_ref[3 * RANK : 4 * RANK, :] = (
                SCALE * (acc_p[:RANK, :] + tn(wo_ref[:, d:], wo_ref[:, :d])[:RANK, :] * ratio_out)
            ).astype(BF16)
            a_ref[4 * RANK :, :] = sh_ref[...]
            for o, m in cm.st_peers():
                gather_part(o, m).start()

        io.ready()

        def grad_swap(i):
            rows = cm.rows(i)
            return stage.at[rows], out_ref.at[rows], (gs_s.at[i], gs_r.at[i], gs_l.at[i])

        def body(i, carry_on):
            @pl.when(i < nc)
            def _():
                block = dp_ref[cm.rows(i), :]
                for role in range(2 * nl):
                    sb[i, role // nl, role % nl] = nt(
                        block, w_ref[role * fw : (role + 1) * fw, :width]
                    ).astype(BF16)
                cm.rs_across(i).start()

            cm.rs_steps(i)

            @pl.when(i < parts)
            def _():
                adapters(i)

            @pl.when(i == parts)
            def _():
                adapters_end()

            @pl.when(i == min(parts + 3, nc + 2))
            def _():
                total = a_ref[:, cm.columns(c, g)].astype(F32)
                for o, m in cm.st_peers():
                    gather_part(o, m).wait_recv()
                    total = total + group[o * nl + m].astype(F32)
                gsum[...] = total.astype(BF16)
                for k in range(ny):
                    for e in (0, 1):
                        if (k, e) == (0, 0):

                            @pl.when(swap.moves)
                            def _():
                                for copy in sums(0, 0):
                                    copy.start()

                            @pl.when(jnp.logical_not(swap.moves))
                            def _():
                                for copy in sums_here():
                                    copy.start()
                        else:
                            for copy in sums(k, e):
                                copy.start()

            @pl.when(i >= 3)
            def _():
                k = i - 3
                rows = cm.rows(k)

                @pl.when(k == 0)
                def _():
                    cm.st_wait(None)

                r = rate_ref[rows, 0:1]
                inner = cm.st_sum(k)
                stage[rows, :] = (
                    dm_ref[rows, :]
                    + r * cm.rs_total(k)
                    - x_ref[rows, :].astype(F32) * (r * r * inner / d)
                ).astype(BF16)
                swap.start(*grad_swap(k))

            return carry_on

        lax.fori_loop(0, nc + 3, body, 0)

        for k in range(ny):
            for hh in (0, 1):
                slot = k * 2 + hh

                def arrived():
                    for n, dst in enumerate((final_a, final_b, final_l)):
                        src = (gsum, b_ref, l_ref)[n]
                        pltpu.make_async_remote_copy(
                            src_ref=src, dst_ref=dst.at[slot], send_sem=fs.at[n, 0], recv_sem=fr.at[n, slot],
                            device_id=swap.partner, device_id_type=MESH,
                        ).wait_recv()

                if k == 0:
                    here = jnp.logical_and(c == h, h == hh)

                    @pl.when(here)
                    def _():
                        for copy in sums_here():
                            copy.wait()

                    @pl.when(jnp.logical_not(here))
                    def _():
                        arrived()
                else:
                    arrived()
        for out, held in ((as_ref, final_a), (bs_ref, final_b), (ls_ref, final_l)):
            total = held[0].astype(F32)
            for slot in range(1, 2 * ny):
                total = total + held[slot].astype(F32)
            out[...] = total

        def drain(i, carry_on):
            swap.wait(*grad_swap(i))
            cm.rs_drain(i)
            swap.drain(*grad_swap(i))
            return carry_on

        lax.fori_loop(0, nc, drain, 0)
        cm.st_drain(None)
        for o, m in cm.st_peers():
            gather_part(o, m).wait_send()
        for k in range(ny):
            for e in (0, 1):
                if (k, e) == (0, 0):

                    @pl.when(swap.moves)
                    def _():
                        for copy in sums(0, 0):
                            copy.wait_send()
                else:
                    for copy in sums(k, e):
                        copy.wait_send()

    dma = pltpu.SemaphoreType.DMA
    na, nb, ng = 7 * RANK, (5 * RANK, fw), local_gu.shape
    return call(
        kernel,
        "qkv_backward",
        (shape((t, fw), BF16), shape((na, fw), F32), shape(nb, F32), shape(ng, F32)),
        [VM] * 17 + [ANY] * 7,
        (VM,) * 4,
        rs_scratch(nl, nc, tc, fw)
        + st_scratch(nl, nc, t)
        + [pltpu.VMEM((t, fw), BF16)]
        + [dma((nc,))] * 3
        + [pltpu.VMEM((peers, na, fw), BF16), pltpu.VMEM((na, fw), BF16), dma((peers,)), dma((peers,))]
        + [
            pltpu.VMEM((2 * ny, na, fw), BF16),
            pltpu.VMEM((2 * ny, *nb), BF16),
            pltpu.VMEM((2 * ny, *ng), BF16),
            dma((3, 2 * ny)),
            dma((3, 2 * ny)),
            dma((3,)),
            pltpu.VMEM((na, d), BF16),
            pltpu.VMEM(nb, BF16),
        ]
        + [pltpu.VMEM((LANES, n), F32) for n in (d, width, fw, d)]
        + stream_scratch(step, widths),
        6,
        70,
        (
            dp, stats, weights, rate, dm, x, shared, local_gu, w_out, up_qkv, b_out, ratios, gm_qkv, square_qkv,
            gm_out, gm_down, small, x_full, lg_qkv, lora_qkv, attended, lg_out, lora_out, go_full,
        ),
        late=(2, 3, 4, 5, 6, 7, 8, 9, 10, 11),
    )


def last_step(fw, nf, grad, result, shared, local, local_gu):
    def kernel(
        io, g_ref, r_ref, s_ref, l_ref, u_ref,
        result_ref, grad_ref, aq_ref, bq_ref, mq_ref, ao_ref, bo_ref, mo_ref,
        ag_ref, bg_ref, mg_ref, ad_ref, bd_ref, md_ref,
    ):
        result_ref[...] = r_ref[...]
        grad_ref[...] = g_ref[...].astype(F32)
        for k in range(3):
            aq_ref[k] = s_ref[k * RANK : (k + 1) * RANK, :]
            bq_ref[k] = l_ref[(1 + k) * RANK : (2 + k) * RANK, :]
        for k in range(2):
            ag_ref[k] = s_ref[(4 + k) * RANK : (5 + k) * RANK, :]
            bg_ref[k] = u_ref[(1 + k) * RANK : (2 + k) * RANK, :nf]
        mq_ref[...] = l_ref[4 * RANK : 4 * RANK + 3, :]
        mg_ref[...] = u_ref[3 * RANK : 3 * RANK + 2, :nf]
        ao_ref[...] = l_ref[:RANK, :]
        bo_ref[...] = s_ref[3 * RANK : 4 * RANK, :]
        mo_ref[...] = l_ref[4 * RANK + 3 : 4 * RANK + 4, :]
        ad_ref[...] = u_ref[:RANK, :nf]
        bd_ref[...] = s_ref[6 * RANK :, :]
        md_ref[...] = l_ref[4 * RANK + 4 : 4 * RANK + 5, :]

    f = [
        (3, RANK, fw), (3, RANK, fw), (3, fw), (RANK, fw), (RANK, fw), (1, fw),
        (2, RANK, fw), (2, RANK, nf), (2, nf), (RANK, nf), (RANK, fw), (1, fw),
    ]
    return call(
        kernel,
        "last_step",
        (shape(result.shape, BF16), shape(grad.shape, F32), *[shape(v, F32) for v in f]),
        [VM] * 5,
        (VM,) * 14,
        [],
        None,
        4,
        (grad, result, shared, local, local_gu),
    )


def positions_of(segment_row):
    index = jnp.arange(segment_row.shape[0], dtype=jnp.int32)
    starts = jnp.concatenate([jnp.ones((1,), jnp.bool_), segment_row[1:] != segment_row[:-1]])
    begin = lax.cummax(jnp.where(starts, index, 0), axis=0)
    return index - begin, begin


def padded(rows, total):
    return jnp.pad(rows, ((0, 0), (0, total - rows.shape[1])))


def on_device(ny, nl, *operands):
    (
        inputs, segments, gain_attn, gain_ffn, w_qkv, a_qkv, b_qkv, m_qkv, w_out, a_out, b_out, m_out,
        w_gu, a_gu, b_gu, m_gu, w_down, a_down, b_down, m_down, cotangent,
    ) = operands
    t, fw = inputs.shape
    mp = 2 * nl
    d = mp * fw
    nf = m_gu.shape[1]
    npad = -(-(nf + RANK) // LANES) * LANES
    width = 3 * fw
    nc = t // 256 if t % 256 == 0 else 1
    block = t // nc
    cfg = (t, fw, d, nl, nc, block)
    y, c, h, g = (lax.axis_index(name) for name in ("y", "c", "h", "g"))
    role = c * nl + g

    def merged_of(frozen, down, up):
        return frozen.astype(F32) + SCALE * jnp.einsum(
            "kdr,krn->kdn", down, up, precision=HIGHEST
        )

    def two_parts(gain):
        high = gain.astype(BF16)
        return [high[:, None], (gain - high.astype(F32)).astype(BF16)[:, None]]

    tail_qkv = padded(
        jnp.concatenate(
            [(a_qkv[k] * gain_attn[:, None]).astype(BF16) for k in range(3)] + two_parts(gain_attn), axis=1
        ),
        LANES,
    )
    tail_gu = jnp.stack(
        [
            jnp.pad(
                jnp.concatenate(
                    [(a_gu[k] * gain_ffn[:, None]).astype(BF16)] + two_parts(gain_ffn), axis=1
                ),
                ((0, 0), (nf, npad - nf - RANK - 2)),
            )
            for k in range(2)
        ]
    )
    gains = padded(jnp.stack([gain_attn, gain_ffn], axis=1), LANES)
    b_gu_padded = jnp.pad(
        b_gu.reshape(2, RANK, mp, nf), ((0, 0), (0, 0), (0, 0), (0, npad - nf))
    ).transpose(0, 2, 1, 3)
    rows_out = jnp.concatenate(
        [
            merged_of(w_out[None], a_out[None], b_out[None])[0].astype(BF16),
            padded(a_out, LANES).astype(BF16),
        ],
        axis=1,
    )
    small = jnp.concatenate([m_qkv, m_out[None], m_down[None], jnp.zeros((3, fw), F32)], axis=0)
    small_gu = jnp.broadcast_to(
        jnp.pad(m_gu, ((0, 0), (0, npad - nf)), constant_values=1.0).reshape(1, 2 * npad), (8, 2 * npad)
    )

    def take(whole, n, axis):
        return lax.dynamic_slice_in_dim(whole, role * n, n, axis)

    b_qkv_here = take(b_qkv, fw, 2)
    b_gu_here = take(b_gu, nf, 2)

    def block_up(up, pad):
        k, _, n = up.shape
        wide = jnp.pad(up, ((0, 0), (0, 0), (0, pad - n)))[:, :, None, :]
        same = (jnp.arange(k)[:, None] == jnp.arange(k)[None, :])[:, None, :, None]
        rows = jnp.where(same, wide, 0.0).reshape(k * RANK, k * pad)
        return jnp.pad(rows, ((0, LANES - k * RANK), (0, 0)))

    up_qkv = block_up(b_qkv_here, fw)
    up_gu = block_up(b_gu_here, npad)
    up_out = jnp.pad(b_out, ((0, LANES - RANK), (0, 0))).astype(BF16)
    up_down = jnp.pad(b_down, ((0, LANES - RANK), (0, 0))).astype(BF16)

    segment = lax.dynamic_index_in_dim(
        lax.all_gather(segments, "c", axis=0, tiled=True), h, 0, keepdims=False
    )
    positions, begin = positions_of(segment)
    first_block = begin[::block] // block
    seg_row = jnp.broadcast_to(segment[None, :], (8, t))
    seg_column = jnp.broadcast_to(segment[:, None], (t, LANES))
    frequencies = jnp.exp(jnp.arange(HD // 2, dtype=F32) * (-2.0 * math.log(10000.0) / HD))
    angles = positions.astype(F32)[:, None] * frequencies[None, :]
    cosine = jnp.cos(angles)
    sine = jnp.sin(angles)
    cosine = jnp.concatenate([cosine, cosine], axis=1)
    sine = jnp.concatenate([-sine, sine], axis=1)

    (
        x, weights_qkv, weights_out, small, small_gu, scale_qkv, square_qkv, qkv, lora_qkv_in, rate_attn,
        blocks_gu, rows_down, weights_gu, x_full,
    ) = qkv_forward(
        cfg, ny, npad, nf, inputs, w_qkv, a_qkv, b_qkv, tail_qkv, gains, rows_out, small, small_gu, cosine, sine,
        w_gu, a_gu, b_gu_padded, tail_gu, w_down, a_down, b_down,
    )
    attended, lse = attention_forward(cfg, qkv, seg_column, seg_row, first_block, block)
    middle, u, stats, sc_out, square_out, lora_out, weights_gu, weights_down = out_forward(
        cfg, ny, npad, attended, weights_out, x, small, weights_gu, blocks_gu, rows_down
    )
    (
        gu, hidden, block_out, gm_down, rate_ffn, gp, scale_gu, square_gu, sc_down, square_down,
        lora_down, grad_seed, u_full,
    ) = ffn_forward(
        cfg, npad, nf, u, stats, weights_gu, small_gu[0:1], weights_down, small, middle, cotangent
    )

    dm, go, gm_out, gm_gu, lg_gu, lg_down, dp_gu, gp_full = ffn_backward(
        cfg, npad, gp, gu, weights_gu, scale_gu, up_gu, weights_down, up_down, rate_ffn,
        grad_seed, middle, x, sc_out,
    )
    ratios = jnp.concatenate(
        [-gm_out[0:1] / square_out[0:1], -gm_down[0:1] / square_down[0:1], jnp.zeros((6, fw), F32)], axis=0
    )
    grad_attended, lg_out, ratios, shared, local_gu, go_full, block_out = out_backward(
        cfg, npad, nf, go, weights_out, up_out, ratios, weights_gu, weights_down, up_gu, up_down, gm_gu, square_gu,
        small_gu, u_full, lg_gu, gu, dp_gu, hidden, lg_down, lora_down, gp_full, block_out,
    )
    dp_qkv, inner, gm_qkv, lg_qkv = attention_backward(
        cfg, qkv, attended, grad_attended, lse, seg_column, seg_row, first_block, block, cosine, sine,
        scale_qkv, rate_attn, up_qkv,
    )

    grad_input, shared, local, local_gu = qkv_backward(
        cfg, ny, dp_qkv, inner, weights_qkv, rate_attn, dm, x, shared, local_gu, weights_out, up_qkv, up_out, ratios,
        gm_qkv, square_qkv, gm_out, gm_down, small, x_full, lg_qkv, lora_qkv_in, attended, lg_out, lora_out, go_full,
    )
    out = list(last_step(fw, nf, grad_input, block_out, shared, local, local_gu))
    out[2], out[8] = out[2].transpose(0, 2, 1), out[8].transpose(0, 2, 1)
    out[5], out[11] = out[5].T, out[11].T
    out[7], out[13] = out[7][0], out[13][0]
    return tuple(out)


def solution(mesh):
    dp, mp = mesh.shape["dp"], mesh.shape["mp"]
    ny, nl = dp // 2, mp // 2
    fine = Mesh(mesh.devices.reshape(ny, 2, 2, nl), ("y", "c", "h", "g"))
    rows, cols = ("y", "c"), ("h", "g")
    in_specs = (
        P(rows, cols),
        P(rows, None),
        P(cols),
        P(cols),
        P(None, cols, None),
        P(None, cols, None),
        P(),
        P(None, cols),
        P(cols, None),
        P(cols, None),
        P(),
        P(cols),
        P(None, cols, None),
        P(None, cols, None),
        P(),
        P(None, cols),
        P(cols, None),
        P(cols, None),
        P(),
        P(cols),
        P(rows, cols),
    )
    out_specs = (
        P(rows, cols),
        P(rows, cols),
        P(None, cols, None),
        P(None, None, cols),
        P(None, cols),
        P(cols, None),
        P(None, cols),
        P(cols),
        P(None, cols, None),
        P(None, None, cols),
        P(None, cols),
        P(cols, None),
        P(None, cols),
        P(cols),
    )
    return jax.shard_map(
        lambda *operands: on_device(ny, nl, *operands),
        mesh=fine,
        in_specs=in_specs,
        out_specs=out_specs,
        check_vma=False,
    )
```

```python
import jax
import jax.numpy as jnp
import numpy as np
from jax import lax
from jax.experimental import pallas as pl
from jax.experimental.pallas import tpu as pltpu
from jax.sharding import Mesh
from jax.sharding import PartitionSpec as P

HD = 128
RANK = 16
SCALE = 2.0
EPS = 1e-05
MASKED = -1e30
HIGHEST = lax.Precision.HIGHEST
MESH = pl.DeviceIdType.MESH
F32 = jnp.float32
BF16 = jnp.bfloat16
LANES = 128
SEGMENTS = 8
VMEM_LIMIT = 60 * 1024 * 1024


def nt(a, b, precision=None):
    return lax.dot_general(
        a, b, (((1,), (1,)), ((), ())), precision=precision, preferred_element_type=F32
    )


def tn(a, b, precision=None):
    return lax.dot_general(
        a, b, (((0,), (0,)), ((), ())), precision=precision, preferred_element_type=F32
    )


def nn(a, b, precision=None):
    return lax.dot_general(
        a, b, (((1,), (0,)), ((), ())), precision=precision, preferred_element_type=F32
    )


WINDOW = 3
EARLY = 1


class Comm:
    def __init__(self, nl, nc, tc, fw, out_by_one=0.5, back_by_two=0.5):
        self.nl, self.nc, self.tc, self.fw = nl, nc, tc, fw
        self.square = nl == 4
        self.cut = int(tc * out_by_one) // 16 * 16
        self.back = int(tc * back_by_two) // 16 * 16
        self.c = lax.axis_index("c")
        self.g = lax.axis_index("g")

    def rows(self, i):
        return pl.ds(pl.multiple_of(i * self.tc, self.tc), self.tc)

    def after(self, m):
        return lax.rem(self.g + m, self.nl)

    def before(self, m):
        return lax.rem(self.g + self.nl - m, self.nl)

    def columns(self, c, g):
        return pl.ds(pl.multiple_of((c * self.nl + g) * self.fw, self.fw), self.fw)

    def copy(self, src, dst, send, recv, c, g):
        return pltpu.make_async_remote_copy(
            src_ref=src,
            dst_ref=dst,
            send_sem=send,
            recv_sem=recv,
            device_id={"c": c, "g": g},
            device_id_type=MESH,
        )

    def barrier(self, others=(), one_more=None):
        sem = pltpu.get_barrier_semaphore()
        everyone = [
            {"c": 1 - self.c if other else self.c, "g": self.after(m)}
            for other in (0, 1)
            for m in range(self.nl)
            if (other, m) != (0, 0)
        ] + list(others)
        for device in everyone:
            pl.semaphore_signal(sem, inc=1, device_id=device, device_id_type=MESH)
        if one_more is None:
            pl.semaphore_wait(sem, len(everyone))
        else:
            apart = self.c - lax.axis_index("h")

            @pl.when(apart != 0)
            def _():
                for device in one_more:
                    pl.semaphore_signal(sem, inc=1, device_id=device, device_id_type=MESH)

            pl.semaphore_wait(sem, len(everyone) + len(one_more) * apart * apart)

    def other(self, m):
        if m == 1:
            return self.g + 1 - 2 * lax.rem(self.g, 2)
        return lax.rem(self.g + 2, 4) if m == 2 else 3 - self.g

    def comes_from(self, m):
        if m == 0:
            return self.g
        return self.other(m) if self.square else self.before(m)

    def goes_to(self, m):
        return self.other(m) if self.square else self.after(m)

    def some(self, i, way):
        cut = self.cut
        start, size = (0, cut) if way == 0 else (cut, self.tc - cut)
        return pl.ds(pl.multiple_of(i * self.tc + start, 16), size)

    def ag_refs(self, x, full, own, sd, rd, sc, rc):
        self.x, self.full, self.own = x, full, own
        self.sd, self.rd, self.sc, self.rc = sd, rd, sc, rc

    def ag_steps(self):
        return (1, 2) if self.square else range(1, self.nl)

    def ag_direct(self, i, m):
        rows = self.rows(i)
        return self.copy(
            self.x.at[rows],
            self.full.at[rows, self.columns(self.c, self.g)],
            self.sd.at[i, m],
            self.rd.at[i, m],
            self.c,
            self.goes_to(m),
        )

    def ag_relay(self, i, way):
        rows = self.some(i, way)
        columns = self.columns(self.c, self.other(2 - way))
        return self.copy(
            self.full.at[rows, columns],
            self.full.at[rows, columns],
            self.sd.at[i, 3 * way],
            self.rd.at[i, 3 * way],
            self.c,
            self.other(1 + way),
        )

    def ag_across(self, i, m):
        rows = self.rows(i)
        columns = self.columns(self.c, self.comes_from(m))
        src = self.x.at[rows] if m == 0 else self.full.at[rows, columns]
        return self.copy(
            src,
            self.full.at[rows, columns],
            self.sc.at[i, m],
            self.rc.at[i, m],
            1 - self.c,
            self.g,
        )

    def ag_own(self, i):
        rows = self.rows(i)
        return pltpu.make_async_copy(
            self.x.at[rows],
            self.full.at[rows, self.columns(self.c, self.g)],
            self.own.at[i],
        )

    def ag_send(self, i):
        for m in self.ag_steps():
            self.ag_direct(i, m).start()
        self.ag_across(i, 0).start()
        self.ag_own(i).start()

    def ag_start(self):
        for i in range(min(WINDOW, self.nc)):
            self.ag_send(jnp.int32(i))

    def ag_forward(self, i):
        for m in self.ag_steps():
            self.ag_direct(i, m).wait_recv()
        if self.square:
            for way in (0, 1):
                self.ag_relay(i, way).start()
        for m in self.ag_steps():
            self.ag_across(i, m).start()

    def ag_corner(self, i):
        if self.square:
            for way in (0, 1):
                self.ag_relay(i, way).wait_recv()
            self.ag_across(i, 3).start()

    def ag_step(self, i, more=True):
        @pl.when(i < self.nc)
        def _():
            self.ag_forward(i)

        if more:

            @pl.when(i + WINDOW < self.nc)
            def _():
                self.ag_send(i + WINDOW)

        @pl.when((i >= 1) & (i <= self.nc))
        def _():
            self.ag_corner(i - 1)

    def ag_ahead(self):
        self.ag_step(jnp.int32(0))
        self.ag_step(jnp.int32(1))

    def ag_wait(self, i):
        self.ag_own(i).wait()
        for m in range(self.nl):
            self.ag_across(i, m).wait_recv()

    def ag_drain(self, i):
        for m in self.ag_steps():
            self.ag_direct(i, m).wait_send()
        if self.square:
            for way in (0, 1):
                self.ag_relay(i, way).wait_send()
        for m in range(self.nl):
            self.ag_across(i, m).wait_send()

    def rs_refs(self, sb, cb, gb, s1, r1, s2, r2):
        self.sb, self.cb, self.gb = sb, cb, gb
        self.s1, self.r1, self.s2, self.r2 = s1, r1, s2, r2

    def rs_across(self, i):
        return self.copy(
            self.sb.at[i, 1 - self.c],
            self.cb.at[i],
            self.s1.at[i],
            self.r1.at[i],
            1 - self.c,
            self.g,
        )

    def rs_direct(self, i, m):
        to = self.goes_to(m)
        return self.copy(
            self.sb.at[i, self.c, to],
            self.gb.at[i, m - 1],
            self.s2.at[i, m],
            self.r2.at[i, m],
            self.c,
            to,
        )

    def rs_corner(self, i, way):
        rows = pl.ds(0, self.back) if way == 0 else pl.ds(self.back, self.tc - self.back)
        return self.copy(
            self.sb.at[i, self.c, self.other(3), rows],
            self.gb.at[i, 2, rows],
            self.s2.at[i, 3 * way],
            self.r2.at[i, 3 * way],
            self.c,
            self.other(2 - way),
        )

    def rs_middle(self, i):
        self.rs_across(i).wait_recv()
        for gp in range(self.nl):
            mine = self.sb[i, self.c, gp].astype(F32) + self.cb[i, gp].astype(F32)
            self.sb[i, self.c, gp] = mine.astype(BF16)
        if self.square:
            for way in (0, 1):
                self.rs_corner(i, way).start()
        else:
            for m in range(1, self.nl):
                self.rs_direct(i, m).start()

    def rs_second(self, i):
        if not self.square:
            return
        for way in (0, 1):
            self.rs_corner(i, way).wait_recv()
            rows = pl.ds(0, self.back) if way == 0 else pl.ds(self.back, self.tc - self.back)
            to = self.other(1 + way)
            both = self.sb[i, self.c, to, rows].astype(F32) + self.gb[i, 2, rows].astype(F32)
            self.sb[i, self.c, to, rows] = both.astype(BF16)
        for m in (1, 2):
            self.rs_direct(i, m).start()

    def rs_total(self, i):
        steps = (1, 2) if self.square else range(1, self.nl)
        for m in steps:
            self.rs_direct(i, m).wait_recv()
        total = self.sb[i, self.c, self.g].astype(F32)
        for m in steps:
            total = total + self.gb[i, m - 1].astype(F32)
        return total

    def rs_drain(self, i):
        self.rs_across(i).wait_send()
        if self.square:
            for way in (0, 1):
                self.rs_corner(i, way).wait_send()
        for m in (1, 2) if self.square else range(1, self.nl):
            self.rs_direct(i, m).wait_send()

    def rs_steps(self, i):
        @pl.when((i >= 1) & (i <= self.nc))
        def _():
            self.rs_middle(i - 1)

        @pl.when((i >= 2) & (i <= self.nc + 1))
        def _():
            self.rs_second(i - 2)

    def st_refs(self, st, sa, ss, sr):
        self.st, self.sa, self.ss, self.sr = st, sa, ss, sr

    def st_copy(self, i, other, m):
        mine = self.c * self.nl + self.g
        src, dst = (self.st, self.sa.at[mine]) if i is None else (self.st.at[i], self.sa.at[mine, i])
        i = 0 if i is None else i
        return self.copy(
            src,
            dst,
            self.ss.at[i, other * self.nl + m],
            self.sr.at[i, other * self.nl + m],
            1 - self.c if other else self.c,
            self.after(m),
        )

    def st_peers(self):
        return [(o, m) for o in (0, 1) for m in range(self.nl) if (o, m) != (0, 0)]

    def st_send(self, i):
        for o, m in self.st_peers():
            self.st_copy(i, o, m).start()
        mine = self.c * self.nl + self.g
        if i is None:
            self.sa[mine] = self.st[...]
        else:
            self.sa[mine, i] = self.st[i]

    def st_wait(self, i):
        for o, m in self.st_peers():
            self.st_copy(i, o, m).wait_recv()

    def st_sum(self, i):
        total = self.sa[0, i]
        for role in range(1, 2 * self.nl):
            total = total + self.sa[role, i]
        return jnp.broadcast_to(total, (8, self.tc)).T[:, 0:1]

    def st_drain(self, i):
        for o, m in self.st_peers():
            self.st_copy(i, o, m).wait_send()

    def cs_refs(self, part, held, ss, sr):
        self.part, self.held, self.cs, self.cr = part, held, ss, sr

    def cs_copy(self, other, m):
        c, g = 1 - self.c if other else self.c, self.after(m)
        place = pl.ds(pl.multiple_of((self.c * self.nl + self.g) * 8, 8), 8)
        k = other * self.nl + m
        return self.copy(
            self.part.at[:, self.columns(c, g)], self.held.at[place], self.cs.at[k], self.cr.at[k], c, g
        )

    def cs_start(self, w_ref):
        for role in range(2 * self.nl):
            at = slice(role * self.fw, (role + 1) * self.fw)
            value = w_ref[:, at].astype(F32)
            self.part[:, at] = jnp.broadcast_to(row_sum(value * value), (8, self.fw))
        for o, m in self.st_peers():
            self.cs_copy(o, m).start()
        place = pl.ds(pl.multiple_of((self.c * self.nl + self.g) * 8, 8), 8)
        self.held[place, :] = self.part[:, self.columns(self.c, self.g)]

    def cs_total(self):
        for o, m in self.st_peers():
            self.cs_copy(o, m).wait_recv()
        return row_sum(self.held[...]) * 0.125

    def cs_drain(self):
        for o, m in self.st_peers():
            self.cs_copy(o, m).wait_send()


class Swap:
    def __init__(self, cm):
        self.cm = cm
        self.h = lax.axis_index("h")
        self.moves = cm.c != self.h
        self.partner = {"c": self.h, "h": cm.c}

    def far(self, src, dst, send, recv):
        return pltpu.make_async_remote_copy(
            src_ref=src, dst_ref=dst, send_sem=send, recv_sem=recv, device_id=self.partner, device_id_type=MESH
        )

    def start(self, src, dst, sems):
        @pl.when(self.moves)
        def _():
            self.far(src, dst, sems[0], sems[1]).start()

        @pl.when(jnp.logical_not(self.moves))
        def _():
            pltpu.make_async_copy(src, dst, sems[2]).start()

    def wait(self, src, dst, sems):
        @pl.when(self.moves)
        def _():
            self.far(src, dst, sems[0], sems[1]).wait_recv()

        @pl.when(jnp.logical_not(self.moves))
        def _():
            pltpu.make_async_copy(src, dst, sems[2]).wait()

    def drain(self, src, dst, sems):
        @pl.when(self.moves)
        def _():
            self.far(src, dst, sems[0], sems[1]).wait_send()


PIECES = 2


class RowMove:
    def __init__(self, swap, ny, part, e_ref, w_ref, ws, wr, wl, ys, yr):
        self.swap, self.ny, self.part, self.size = swap, ny, part, part // PIECES
        self.e, self.w = e_ref, w_ref
        self.ws, self.wr, self.wl, self.ys, self.yr = ws, wr, wl, ys, yr
        self.y = lax.axis_index("y")

    def rows(self, y, p):
        return pl.ds(pl.multiple_of(y * self.part + p * self.size, 16), self.size)

    def far(self, p):
        mine = self.rows(self.y, p)
        return self.swap.far(self.e.at[mine], self.w.at[mine], self.ws.at[p], self.wr.at[p])

    def near(self):
        every = pl.ds(0, self.part * self.ny)
        return pltpu.make_async_copy(self.e.at[every], self.w.at[every], self.wl)

    def shared(self, k, p, y):
        where = self.rows(y, p)
        return pltpu.make_async_remote_copy(
            src_ref=self.w.at[where], dst_ref=self.w.at[where],
            send_sem=self.ys.at[k - 1, p], recv_sem=self.yr.at[k - 1, p],
            device_id={"y": lax.rem(self.y + k, self.ny)}, device_id_type=MESH,
        )

    def start(self):
        @pl.when(self.swap.moves)
        def _():
            for p in range(PIECES):
                self.far(p).start()

        @pl.when(jnp.logical_not(self.swap.moves))
        def _():
            self.near().start()

    def pass_on(self):
        @pl.when(self.swap.moves)
        def _():
            for p in range(PIECES):
                self.far(p).wait_recv()
                for k in range(1, self.ny):
                    self.shared(k, p, self.y).start()

    def wait(self):
        @pl.when(self.swap.moves)
        def _():
            for k in range(1, self.ny):
                for p in range(PIECES):
                    self.shared(k, p, lax.rem(self.y + self.ny - k, self.ny)).wait_recv()

        @pl.when(jnp.logical_not(self.swap.moves))
        def _():
            self.near().wait()

    def drain(self):
        @pl.when(self.swap.moves)
        def _():
            for p in range(PIECES):
                self.far(p).wait_send()
                for k in range(1, self.ny):
                    self.shared(k, p, self.y).wait_send()


def row_move_scratch(ny):
    dma = pltpu.SemaphoreType.DMA
    between = dma((max(ny - 1, 1), PIECES))
    return [dma((PIECES,)), dma((PIECES,)), dma, between, between]


class Spread:
    def __init__(self, cm, ny, e_ref, w_ref, hs, hr, ps, pr, pn, ys, yr):
        self.cm, self.ny, self.e, self.w = cm, ny, e_ref, w_ref
        self.hs, self.hr, self.ps, self.pr, self.pn, self.ys, self.yr = hs, hr, ps, pr, pn, ys, yr
        self.y, self.h = lax.axis_index("y"), lax.axis_index("h")
        self.part = cm.fw // ny

    def place(self, hh, gg, yy):
        return self.w.at[
            pl.ds(pl.multiple_of((hh * self.cm.nl + gg) * self.cm.fw + yy * self.part, self.part), self.part)
        ]

    def piece(self, m):
        cm, to = self.cm, self.cm.after(m)
        return cm.copy(
            self.e.at[to], self.place(self.h, cm.g, self.y), self.ps.at[m], self.pr.at[m], cm.c, to
        )

    def here(self):
        return pltpu.make_async_copy(
            self.e.at[self.cm.g], self.place(self.h, self.cm.g, self.y), self.pn
        )

    def crossed(self, m, hh):
        where = self.place(hh, self.cm.before(m), self.y)
        return pltpu.make_async_remote_copy(
            src_ref=where, dst_ref=where, send_sem=self.hs.at[m], recv_sem=self.hr.at[m],
            device_id={"h": 1 - self.h}, device_id_type=MESH,
        )

    def shared(self, side, m, k, yy):
        where = self.place(self.h if side == 0 else 1 - self.h, self.cm.before(m), yy)
        return pltpu.make_async_remote_copy(
            src_ref=where, dst_ref=where,
            send_sem=self.ys.at[side, m, k - 1], recv_sem=self.yr.at[side, m, k - 1],
            device_id={"y": lax.rem(self.y + k, self.ny)}, device_id_type=MESH,
        )

    def start(self, steps):
        for m in steps:
            if m == 0:
                self.here().start()
            else:
                self.piece(m).start()

    def own(self, m):
        if m == 0:
            self.here().wait()
        else:
            self.piece(m).wait_recv()

    def start_crossing(self, m):
        self.crossed(m, self.h).start()

    def wait_crossing(self, m):
        self.crossed(m, 1 - self.h).wait_recv()

    def share(self, side, m):
        for k in range(1, self.ny):
            self.shared(side, m, k, self.y).start()

    def pass_own(self, m, cross=True):
        self.own(m)
        if cross:
            self.start_crossing(m)
        self.share(0, m)

    def pass_crossed(self, m, following=None):
        self.wait_crossing(m)
        if following is not None and following < self.cm.nl:
            self.start_crossing(following)
        self.share(1, m)

    def wait(self, side, steps):
        for m in steps:
            for k in range(1, self.ny):
                self.shared(side, m, k, lax.rem(self.y + self.ny - k, self.ny)).wait_recv()

    def drain_own(self, steps):
        for m in steps:
            if m > 0:
                self.piece(m).wait_send()

    def drain_crossing(self, steps):
        for m in steps:
            self.crossed(m, self.h).wait_send()

    def drain_shared(self, side, steps):
        for m in steps:
            for k in range(1, self.ny):
                self.shared(side, m, k, self.y).wait_send()


def spread_scratch(ny, nl):
    dma = pltpu.SemaphoreType.DMA
    return [
        dma((nl,)),
        dma((nl,)),
        dma((nl,)),
        dma((nl,)),
        dma,
        dma((2, nl, max(ny - 1, 1))),
        dma((2, nl, max(ny - 1, 1))),
    ]


def movers(ny):
    y, h = lax.axis_index("y"), lax.axis_index("h")
    return [{"y": lax.rem(y + k, ny)} for k in range(1, ny)] + [{"h": 1 - h}]


def ag_scratch(nl, nc, t, d):
    return [
        pltpu.VMEM((t, d), BF16),
        pltpu.SemaphoreType.DMA((nc,)),
        pltpu.SemaphoreType.DMA((nc, nl)),
        pltpu.SemaphoreType.DMA((nc, nl)),
        pltpu.SemaphoreType.DMA((nc, nl)),
        pltpu.SemaphoreType.DMA((nc, nl)),
    ]


def rs_scratch(nl, nc, tc, fw):
    return [
        pltpu.VMEM((nc, 2, nl, tc, fw), BF16),
        pltpu.VMEM((nc, nl, tc, fw), BF16),
        pltpu.VMEM((nc, nl - 1, tc, fw), BF16),
        pltpu.SemaphoreType.DMA((nc,)),
        pltpu.SemaphoreType.DMA((nc,)),
        pltpu.SemaphoreType.DMA((nc, nl)),
        pltpu.SemaphoreType.DMA((nc, nl)),
    ]


def st_scratch(nl, nc, t):
    return [
        pltpu.VMEM((2 * nl, nc, 1, t // nc), F32),
        pltpu.SemaphoreType.DMA((nc, 2 * nl)),
        pltpu.SemaphoreType.DMA((nc, 2 * nl)),
    ]


def cs_scratch(nl, d, fw):
    return [
        pltpu.VMEM((8, d), F32),
        pltpu.VMEM((2 * nl * 8, fw), F32),
        pltpu.SemaphoreType.DMA((2 * nl,)),
        pltpu.SemaphoreType.DMA((2 * nl,)),
    ]


VM = pl.BlockSpec(memory_space=pltpu.VMEM)
SM = pl.BlockSpec(memory_space=pltpu.SMEM)
ANY = pl.BlockSpec(memory_space=pl.ANY)


class Background:
    def __init__(self, loads, stores, step):
        self.loads, self.stores, self.step = loads, stores, step
        for copy in loads:
            copy.start()

    def ready(self):
        for copy in self.loads:
            copy.wait()

    def copy(self, k, i):
        held, out, sems = self.stores[k]
        rows = pl.ds(pl.multiple_of(i * self.step, self.step), self.step)
        return pltpu.make_async_copy(held.at[rows], out.at[rows], sems.at[i])

    def store(self, i, *which):
        for k in which:
            self.copy(k, i).start()

    def stored(self, i):
        for k in self.stores:
            self.copy(k, i).wait()


def call(kernel, name, outs, in_specs, out_specs, scratch, collective, us, args, late=(), flow=(), step=1, aliases=None):
    extra = {}
    if collective is not None:
        extra = {"collective_id": collective, "has_side_effects": True}
    single = not isinstance(outs, tuple)
    results = (outs,) if single else outs
    in_specs, out_specs = list(in_specs), [out_specs] if single else list(out_specs)
    n_in, n_out, n_scratch = len(args), len(results), len(scratch)
    dma = pltpu.SemaphoreType.DMA
    more = []
    for k in late:
        in_specs[k] = ANY
        more += [pltpu.VMEM(args[k].shape, args[k].dtype), dma]
    for k in flow:
        out_specs[k] = ANY
        more += [pltpu.VMEM(results[k].shape, results[k].dtype), dma((results[k].shape[0] // step,))]

    def whole(*refs):
        ins, results_here = list(refs[:n_in]), list(refs[n_in : n_in + n_out])
        own = refs[n_in + n_out : n_in + n_out + n_scratch]
        extras = list(refs[n_in + n_out + n_scratch :])
        loads, stores = [], {}
        for k in late:
            held, sem = extras.pop(0), extras.pop(0)
            loads.append(pltpu.make_async_copy(ins[k], held, sem))
            ins[k] = held
        for k in flow:
            held, sems = extras.pop(0), extras.pop(0)
            stores[k] = (held, results_here[k], sems)
            results_here[k] = held
        kernel(Background(loads, stores, step), *ins, *results_here, *own)

    return pl.pallas_call(
        whole,
        name=name,
        out_shape=outs,
        in_specs=in_specs,
        out_specs=out_specs[0] if single else tuple(out_specs),
        scratch_shapes=scratch + more,
        input_output_aliases=aliases or {},
        compiler_params=pltpu.CompilerParams(vmem_limit_bytes=VMEM_LIMIT, **extra),
        cost_estimate=pl.CostEstimate(
            flops=int(us * 5e8), bytes_accessed=int(us * 3e6), transcendentals=0
        ),
    )(*args)


def shape(s, dtype):
    return jax.ShapeDtypeStruct(s, dtype)


def ones_rows(values):
    folded = values[:, :LANES]
    for k in range(1, values.shape[1] // LANES):
        folded = folded + values[:, k * LANES : (k + 1) * LANES]
    return nt(jnp.ones((8, LANES), F32), folded, HIGHEST)


def row_sum(values):
    return jnp.sum(values, axis=0, keepdims=True)


def down_part(nf, ny):
    return -(-(-(-nf // ny)) // (16 * PIECES)) * 16 * PIECES


def merged_tile(frozen, down, up):
    down_high, up_high = down.astype(BF16), up.astype(BF16)
    down_low = (down - down_high.astype(F32)).astype(BF16)
    up_low = (up - up_high.astype(F32)).astype(BF16)
    low = nn(down_high, up_high) + (nn(down_high, up_low) + nn(down_low, up_high))
    return frozen.astype(F32) + SCALE * low


def qkv_forward(
    cfg, ny, npad, nf, x_in, w_qkv, a_qkv, b_qkv, tail_qkv, gains, w_out, small, small_gu, segments, turns,
    w_gu, a_gu, b_gu, tail_gu, w_down, a_down, b_down, a_out, b_out,
):
    t, fw, d, nl, nc, tc = cfg
    width = 3 * fw
    wide = width + LANES
    part = fw // ny
    down_rows = down_part(nf, ny) * ny
    ff_half = w_gu.shape[2] // 2

    def kernel(
        io, x_ref, wq_hbm, aq_ref, bq_ref, tq_ref, gain_ref, wout_ref, m_ref, mg_ref, seg_ref, ta_ref, tb_ref,
        wg_hbm, ag_ref, bg_ref, tg_ref, wdown_ref, ad_ref, bd_ref, ao_ref, bo_ref,
        xs_ref, w_ref, wo_ref, ms_ref, mgs_ref, sc_ref, sq_ref, qkv_ref, lora_ref, rate_ref, eg_ref, ed_ref, wgs_ref, out_ref, cos_ref, sin_ref, sgc_ref, sgr_ref,
        full, own, sd, rd, sc, rc, keep, xs_s, xs_r, xs_l, small_sems,
        hs, hr, ps, pr, pn, ys, yr, os, orr, ol, oys, oyr,
        e_ref, wq, wg, wload, eo_ref, sg, place, ghs, ghr, gps, gpr, gpn, gys, gyr,
    ):
        cm = Comm(nl, nc, tc, fw, out_by_one=0.9375)
        cm.ag_refs(xs_ref, full, own, sd, rd, sc, rc)
        swap = Swap(cm)
        weights = Spread(cm, ny, e_ref, w_ref, hs, hr, ps, pr, pn, ys, yr)
        mine = pl.ds(pl.multiple_of(weights.y * part, part), part)
        load_q = pltpu.make_async_copy(
            wq_hbm.at[:, mine, pl.ds(pl.multiple_of(cm.c * (d // 2), LANES), d // 2)], wq, wload.at[0]
        )
        load_g = pltpu.make_async_copy(
            wg_hbm.at[:, mine, pl.ds(pl.multiple_of(cm.c * ff_half, LANES), ff_half)], wg, wload.at[1]
        )
        load_q.start()
        load_g.start()
        later = Spread(cm, ny, eg_ref, wgs_ref, ghs, ghr, gps, gpr, gpn, gys, gyr)
        output = RowMove(swap, ny, fw // ny, eo_ref, wo_ref, os, orr, ol, oys, oyr)
        cm.barrier(movers(ny), [swap.partner])

        def token_swap(i):
            rows = cm.rows(i)
            return x_ref.at[rows], xs_ref.at[rows], (xs_s.at[i], xs_r.at[i], xs_l.at[i])

        m_swap = (m_ref, ms_ref, tuple(small_sems.at[k] for k in range(3)))
        mg_swap = (mg_ref, mgs_ref, tuple(small_sems.at[k] for k in range(3, 6)))

        seg_swap = (seg_ref, sg, tuple(small_sems.at[k] for k in range(6, 9)))

        def start_swap(i, carry_on):
            swap.start(*token_swap(i))
            return carry_on

        lax.fori_loop(0, min(WINDOW, nc), start_swap, 0)
        swap.start(*m_swap)
        swap.start(*mg_swap)
        swap.start(*seg_swap)
        load_q.wait()
        gain_attn, gain_ffn = gain_ref[mine, 0:1], gain_ref[mine, 1:2]
        for gg in range(nl):
            columns = pl.ds(pl.multiple_of((cm.c * nl + gg) * fw, fw), fw)
            for k in range(3):
                tile = merged_tile(wq[k, :, gg * fw : (gg + 1) * fw], aq_ref[k, mine, :], bq_ref[k, :, columns])
                e_ref[gg, :, k * fw : (k + 1) * fw] = (tile * gain_attn).astype(BF16)
            e_ref[gg, :, width:] = tq_ref[mine, :]
        weights.start(range(nl))

        def gate_up(gg):
            off = gg * nf % LANES
            window = -(-(off + nf) // LANES) * LANES
            for k in range(2):
                raw = wg[k, :, gg * nf - off : gg * nf - off + window].astype(F32)
                if off:
                    raw = pltpu.roll(raw, window - off, 1)
                tile = merged_tile(raw[:, :npad], ag_ref[k, mine, :], bg_ref[k, cm.c * nl + gg]) * gain_ffn
                lane = lax.broadcasted_iota(jnp.int32, tile.shape, 1)
                eg_ref[gg, :, k * npad : (k + 1) * npad] = jnp.where(
                    lane < nf, tile, tg_ref[k, mine, :].astype(F32)
                ).astype(BF16)

        def merged_rows(k):
            if k == 0:
                if down_rows > nf:
                    ed_ref[nf:, :] = jnp.zeros((down_rows - nf, ed_ref.shape[1]), BF16)
                ed_ref[:nf, d:] = jnp.zeros((nf, LANES), BF16)
                ed_ref[:nf, d : d + RANK] = ad_ref[...].astype(BF16)
                eo_ref[:, d:] = jnp.zeros((fw, LANES), BF16)
                eo_ref[:, d : d + RANK] = ao_ref[...].astype(BF16)
            for n in (2 * k, 2 * k + 1):
                at = slice(n * fw, (n + 1) * fw)
                eo_ref[:, at] = merged_tile(wout_ref[:, at], ao_ref[...], bo_ref[:, at]).astype(BF16)
                ed_ref[:nf, at] = merged_tile(wdown_ref[:, at], ad_ref[...], bd_ref[:, at]).astype(BF16)

        def gather(i, carry_on):
            swap.wait(*token_swap(i))

            @pl.when(i + WINDOW < nc)
            def _():
                swap.start(*token_swap(i + WINDOW))

            cm.ag_send(i)
            return carry_on

        def forward(i, carry_on):
            cm.ag_step(i, more=False)
            return carry_on

        weights.pass_own(0)
        half = nc // 2
        lax.fori_loop(0, half, gather, 0)
        weights.pass_own(1)
        lax.fori_loop(half, nc, gather, 0)
        for m in range(2, nl):
            weights.pass_own(m, cross=False)
        load_g.wait()
        io.ready()
        for m in range(nl):
            lax.fori_loop(nc * m // nl, nc * (m + 1) // nl, forward, 0)
            gate_up(m)
            weights.pass_crossed(m, m + 2)
            merged_rows(m)
        output.start()
        later.start(range(EARLY + 1))
        for m in range(EARLY):
            later.own(m)
            later.start_crossing(m)
        cm.ag_step(jnp.int32(nc), more=False)

        def stored(i):
            rows = cm.rows(i)
            return pltpu.make_async_copy(full.at[rows], out_ref.at[rows], keep.at[i])

        swap.wait(*seg_swap)
        number = sg[...]
        begin = jnp.zeros((1, t), F32)
        for n in range(1, SEGMENTS):
            before = jnp.sum(jnp.where(number < n, 1.0, 0.0), axis=1, keepdims=True)
            begin = jnp.where(number == n, before, begin)
        standing = lax.broadcasted_iota(jnp.int32, (1, t), 1).astype(F32) - begin
        high = jnp.floor(standing * (1.0 / 32.0))
        place[0:1, :] = high.astype(jnp.int32)
        place[1:2, :] = (standing - 32.0 * high).astype(jnp.int32)
        sgr_ref[...] = jnp.broadcast_to(number, (8, t))

        def turn_tables(rows):
            def chosen(row, count):
                return jnp.where(lax.broadcasted_iota(jnp.int32, (count, tc), 0) == row, 1.0, 0.0)

            def looked_up(row, table):
                parts = tn(chosen(row, 32).astype(BF16), table)
                both = parts[:, : 2 * HD] + parts[:, 2 * HD :]
                return both[:, :HD], both[:, HD:]

            ca, sa = looked_up(place[0:1, rows], ta_ref[...])
            cb, sb = looked_up(place[1:2, rows], tb_ref[...])
            sign = jnp.where(lax.broadcasted_iota(jnp.int32, (tc, HD), 1) < HD // 2, -1.0, 1.0)
            cos_ref[rows, :] = ca * cb - sa * sb
            sin_ref[rows, :] = (sa * cb + ca * sb) * sign
            numbers = lax.broadcasted_iota(jnp.int32, (SEGMENTS, LANES), 0).astype(F32)
            sgc_ref[rows, :] = tn(chosen(sgr_ref[0:1, rows], SEGMENTS), numbers).astype(jnp.int32)

        def rates(i, carry_on):
            turn_tables(cm.rows(i))
            cm.ag_wait(i)
            stored(i).start()
            wide_block = full[cm.rows(i), :].astype(F32)
            rate = lax.rsqrt(jnp.sum(wide_block * wide_block, axis=1, keepdims=True) / d + EPS)
            rate_ref[cm.rows(i), :] = jnp.broadcast_to(rate, (tc, LANES))
            return carry_on

        lax.fori_loop(0, nc, rates, 0)
        for side in (0, 1):
            weights.wait(side, range(nl))

        def squares(i, total):
            rows = pl.ds(pl.multiple_of(i * fw, fw), fw)
            tail = w_ref[rows, width:].astype(F32)
            gain = tail[:, 3 * RANK : 3 * RANK + 1] + tail[:, 3 * RANK + 1 : 3 * RANK + 2]
            value = w_ref[rows, :width].astype(F32) * (1.0 / gain)
            return total + row_sum(value * value)

        square = lax.fori_loop(0, 2 * nl, squares, jnp.zeros((1, width), F32))
        swap.wait(*m_swap)
        sq_ref[...] = jnp.broadcast_to(square, (8, width))
        for k in range(3):
            at = slice(k * fw, (k + 1) * fw)
            sc_ref[:, at] = jnp.broadcast_to(ms_ref[k : k + 1, :] * lax.rsqrt(square[:, at]), (8, fw))
        sc_ref[:, width:] = jnp.ones((8, LANES), F32)

        big = 2 * tc if nc % 2 == 0 else tc

        def body(i, carry_on):
            rows = pl.ds(pl.multiple_of(i * big, big), big)
            out = nn(full[rows, :], w_ref[...]) * rate_ref[rows, 0:1] * sc_ref[0:1, :]
            cosine_here, sine_here = cos_ref[rows, :], sin_ref[rows, :]
            for k in range(3):
                for hd in range(fw // HD):
                    at = k * fw + hd * HD
                    value = out[:, at : at + HD]
                    if k < 2:
                        value = value * cosine_here + pltpu.roll(value, HD // 2, 1) * sine_here
                    qkv_ref[rows, at : at + HD] = value.astype(BF16)
            lora_ref[rows, :] = out[:, width:].astype(BF16)
            for k in range(big // tc):
                io.store(i * (big // tc) + k, 7, 8, 9, 14, 15, 16)
            return carry_on

        lax.fori_loop(0, t // big, body, 0)
        output.pass_on()
        for m in range(EARLY):
            later.wait_crossing(m)
        later.own(EARLY)
        output.wait()
        swap.wait(*mg_swap)

        def drain(i, carry_on):
            cm.ag_drain(i)
            stored(i).wait()
            io.stored(i)
            swap.drain(*token_swap(i))
            return carry_on

        lax.fori_loop(0, nc, drain, 0)
        swap.drain(*m_swap)
        swap.drain(*mg_swap)
        swap.drain(*seg_swap)
        weights.drain_own(range(nl))
        weights.drain_crossing(range(nl))
        for side in (0, 1):
            weights.drain_shared(side, range(nl))
        later.drain_own(range(EARLY + 1))
        later.drain_crossing(range(EARLY))
        output.drain()

    dma = pltpu.SemaphoreType.DMA
    return call(
        kernel,
        "qkv_forward",
        (
            shape((t, fw), BF16),
            shape((d, wide), BF16),
            shape((fw, d + LANES), BF16),
            shape(small.shape, F32),
            shape(small_gu.shape, F32),
            shape((8, wide), F32),
            shape((8, width), F32),
            shape((t, width), BF16),
            shape((t, LANES), BF16),
            shape((t, LANES), F32),
            shape((nl, part, 2 * npad), BF16),
            shape((down_rows, d + LANES), BF16),
            shape((d, 2 * npad), BF16),
            shape((t, d), BF16),
            shape((t, HD), F32),
            shape((t, HD), F32),
            shape((t, LANES), jnp.int32),
            shape((8, t), jnp.int32),
        ),
        [VM, ANY] + [VM] * 10 + [ANY] + [VM] * 8,
        (VM,) * 12 + (ANY, ANY) + (VM,) * 4,
        ag_scratch(nl, nc, t, d)
        + [dma((nc,))] * 4
        + [dma((9,))]
        + spread_scratch(ny, nl)
        + row_move_scratch(ny)
        + [
            pltpu.VMEM((nl, part, wide), BF16),
            pltpu.VMEM((3, part, d // 2), BF16),
            pltpu.VMEM((2, part, ff_half), BF16),
            dma((2,)),
            pltpu.VMEM((fw, d + LANES), BF16),
            pltpu.VMEM((1, t), jnp.int32),
            pltpu.VMEM((8, t), jnp.int32),
        ]
        + spread_scratch(ny, nl),
        1,
        90,
        (
            x_in, w_qkv, a_qkv, b_qkv, tail_qkv, gains, w_out, small, small_gu, segments, *turns,
            w_gu, a_gu, b_gu, tail_gu, w_down, a_down, b_down, a_out, b_out,
        ),
        late=(6, 10, 11, *range(13, 21)),
        flow=(7, 8, 9, 14, 15, 16),
        step=tc,
    )


def allowed_of(key_segment, query_segment, j, i, block):
    key_at = j * block + lax.broadcasted_iota(jnp.int32, (block, block), 0)
    query_at = i * block + lax.broadcasted_iota(jnp.int32, (block, block), 1)
    return (key_segment == query_segment) & (key_at <= query_at)


def attention_forward(cfg, qkv, seg_column, seg_row, first_block, block):
    t, fw = cfg[0], cfg[1]
    heads = fw // HD

    def kernel(io, qkv_ref, sc_ref, sr_ref, first_ref, out_ref, lse_ref):
        def at(i):
            return pl.ds(pl.multiple_of(i * block, block), block)

        def columns(k, hd):
            return slice(k * fw + hd * HD, k * fw + (hd + 1) * HD)

        def one_query(i, carry_on):
            queries = [qkv_ref[at(i), columns(0, hd)] for hd in range(heads)]
            query_segment = sr_ref[0:1, at(i)]

            def one_key(j, carry):
                allowed = allowed_of(sc_ref[at(j), 0:1], query_segment, j, i, block)
                out = []
                for hd in range(heads):
                    top, total, acc = carry[hd]
                    s = nt(qkv_ref[at(j), columns(1, hd)], queries[hd]) * (HD**-0.5)
                    s = jnp.where(allowed, s, MASKED)
                    new = jnp.maximum(top, jnp.max(s, axis=0, keepdims=True))
                    p = jnp.exp(s - new)
                    shrink = jnp.exp(top - new)
                    total = total * shrink + jnp.sum(p, axis=0, keepdims=True)
                    acc = acc * shrink + tn(qkv_ref[at(j), columns(2, hd)], p.astype(BF16))
                    out.append((new, total, acc))
                return tuple(out)

            first = (
                jnp.full((1, block), MASKED, F32),
                jnp.zeros((1, block), F32),
                jnp.zeros((HD, block), F32),
            )
            out = lax.fori_loop(first_ref[i], i + 1, one_key, (first,) * heads)
            for hd in range(heads):
                top, total, acc = out[hd]
                out_ref[at(i), hd * HD : (hd + 1) * HD] = (acc / total).T.astype(BF16)
                lse_ref[hd * 8 : hd * 8 + 8, at(i)] = jnp.broadcast_to(
                    top + jnp.log(total), (8, block)
                )
            return carry_on

        lax.fori_loop(0, t // block, one_query, 0)

    return call(
        kernel,
        "attention_forward",
        (shape((t, fw), BF16), shape((heads * 8, t), F32)),
        [VM, VM, VM, SM],
        (VM, VM),
        [],
        None,
        15,
        (qkv, seg_column, seg_row, first_block),
    )


def out_forward(cfg, ny, npad, attended, weights, x, magnitude, w_gu, blocks, rows_down):
    t, fw, d, nl, nc, tc = cfg
    part = rows_down.shape[0] // ny

    def kernel(
        io, a_ref, w_ref, x_ref, m_ref, w_in, e_ref, ed_ref,
        mid_ref, u_ref, st_ref, sc_ref, sq_ref, lora_ref, wg_ref, wd_ref,
        sb, cb, gb, s1, r1, s2, r2, cpart, cheld, css, csr,
        hs, hr, ps, pr, pn, ys, yr, dws, dwr, dwl, dys, dyr,
    ):
        cm = Comm(nl, nc, tc, fw, back_by_two=0.0625)
        cm.rs_refs(sb, cb, gb, s1, r1, s2, r2)
        cm.cs_refs(cpart, cheld, css, csr)
        columns = Spread(cm, ny, e_ref, wg_ref, hs, hr, ps, pr, pn, ys, yr)
        swap = Swap(cm)
        down_rows = RowMove(swap, ny, part, ed_ref, wd_ref, dws, dwr, dwl, dys, dyr)
        cm.barrier(movers(ny), [swap.partner])
        down_rows.start()
        columns.start_crossing(EARLY)
        columns.start(range(EARLY + 1, nl))
        for m in range(EARLY):
            columns.share(0, m)
            columns.share(1, m)
        columns.share(0, EARLY)
        cm.cs_start(w_ref)
        if part * ny < npad:
            wd_ref[part * ny :, :] = jnp.zeros((npad - part * ny, wd_ref.shape[1]), BF16)
        def body(i, carry_on):
            @pl.when(i < nc)
            def _():
                block = a_ref[cm.rows(i), :]
                for role in range(2 * nl):
                    sb[i, role // nl, role % nl] = nn(
                        block, w_ref[:, role * fw : (role + 1) * fw]
                    ).astype(BF16)
                cm.rs_across(i).start()
                lora_ref[cm.rows(i), :] = nn(block, w_ref[:, d:]).astype(BF16)
                io.store(i, 5)

            cm.rs_steps(i)

            @pl.when(i == 3)
            def _():
                total = cm.cs_total()
                sq_ref[...] = jnp.broadcast_to(total, (8, fw))
                sc_ref[...] = jnp.broadcast_to(m_ref[3:4, :] * lax.rsqrt(total), (8, fw))

            @pl.when(i == 5)
            def _():
                down_rows.pass_on()

            @pl.when(i == 1)
            def _():
                columns.pass_own(EARLY + 1)

            @pl.when(i == 3)
            def _():
                for m in range(EARLY + 2, nl):
                    columns.pass_own(m, cross=False)

            @pl.when(i == min(6, nc + 2))
            def _():
                columns.pass_crossed(EARLY, EARLY + 2)

            @pl.when((i >= 3) & (i <= nc + 2))
            def _():
                rows = cm.rows(i - 3)
                middle = x_ref[rows, :].astype(F32) + cm.rs_total(i - 3) * sc_ref[0:1, :]
                mid_ref[rows, :] = middle
                u_ref[rows, :] = middle.astype(BF16)
                st_ref[i - 3] = ones_rows(middle * middle)[0:1, :]
                io.store(i - 3, 0, 1)

            return carry_on

        lax.fori_loop(0, nc + 3, body, 0)

        def drain(i, carry_on):
            cm.rs_drain(i)
            io.stored(i)
            return carry_on

        for m in range(EARLY + 1, nl):
            columns.pass_crossed(m, m + 2)
        for side in (0, 1):
            columns.wait(side, range(nl))
        down_rows.wait()
        lax.fori_loop(0, nc, drain, 0)
        cm.cs_drain()
        columns.drain_own(range(EARLY + 1, nl))
        columns.drain_crossing(range(EARLY, nl))
        for side in (0, 1):
            columns.drain_shared(side, range(nl))
        down_rows.drain()

    return call(
        kernel,
        "out_forward",
        (
            shape((t, fw), F32),
            shape((t, fw), BF16),
            shape((nc, 1, tc), F32),
            shape((8, fw), F32),
            shape((8, fw), F32),
            shape((t, LANES), BF16),
            shape(w_gu.shape, BF16),
            shape((npad, d + LANES), BF16),
        ),
        [VM] * 4 + [ANY, ANY, ANY],
        (VM,) * 6 + (ANY, VM),
        rs_scratch(nl, nc, tc, fw)
        + cs_scratch(nl, d, fw)
        + spread_scratch(ny, nl)
        + row_move_scratch(ny),
        2,
        90,
        (attended, weights, x, magnitude, w_gu, blocks, rows_down),
        flow=(0, 1, 5),
        step=tc,
        aliases={4: 6},
    )


def ffn_forward(cfg, npad, nf, u, stats, w_gu, m_gu, w_down, small, middle, cotangent):
    t, fw, d, nl, nc, tc = cfg

    def kernel(
        io, u_ref, st_ref, wg_ref, mg_ref, wd_ref, m_ref, mid_ref, cin_ref,
        gu_ref, hid_ref, out_ref, gm_ref, rate_ref, gp_ref, sg_ref, qg_ref, sd_ref, qd_ref, lora_ref, cot_ref, uf_ref,
        full, own, sd, rd, sc, rc, sb, cb, gb, s1, r1, s2, r2, sa, ss, sr, cpart, cheld, css, csr, keep,
        cs_s, cs_r, cs_l,
    ):
        cm = Comm(nl, nc, tc, fw, out_by_one=0.5, back_by_two=0.5)
        cm.ag_refs(u_ref, full, own, sd, rd, sc, rc)
        cm.rs_refs(sb, cb, gb, s1, r1, s2, r2)
        cm.st_refs(st_ref, sa, ss, sr)
        cm.cs_refs(cpart, cheld, css, csr)
        swap = Swap(cm)
        cm.barrier((), [swap.partner])

        def cot_swap(i):
            rows = cm.rows(i)
            return cin_ref.at[rows], cot_ref.at[rows], (cs_s.at[i], cs_r.at[i], cs_l.at[i])

        cm.st_send(None)
        cm.ag_start()
        io.ready()

        def cot_out(i, carry_on):
            swap.start(*cot_swap(i))
            return carry_on


        def squares(i, total):
            rows = pl.ds(pl.multiple_of(i * fw, fw), fw)
            gain = (
                wg_ref[rows, nf + RANK : nf + RANK + 1].astype(F32)
                + wg_ref[rows, nf + RANK + 1 : nf + RANK + 2].astype(F32)
            )
            value = wg_ref[rows, :].astype(F32) * (1.0 / gain)
            return total + row_sum(value * value)

        square = lax.fori_loop(0, 2 * nl, squares, jnp.zeros((1, 2 * npad), F32))
        column = lax.rem(lax.broadcasted_iota(jnp.int32, (1, 2 * npad), 1), npad)
        square = jnp.where(column < nf, square, 1.0)
        qg_ref[...] = jnp.broadcast_to(square, (8, 2 * npad))
        sg_ref[...] = jnp.broadcast_to(mg_ref[...] * lax.rsqrt(square), (8, 2 * npad))
        cm.ag_ahead()
        gm_ref[...] = jnp.zeros_like(gm_ref)

        def stored(i):
            rows = cm.rows(i)
            return pltpu.make_async_copy(full.at[rows], uf_ref.at[rows], keep.at[i])

        cm.cs_start(wd_ref)
        lax.fori_loop(0, nc, cot_out, 0)

        def body(i, carry_on):
            @pl.when(i < nc)
            def _():
                cm.ag_step(i + 2)
                cm.ag_wait(i)

                @pl.when(i == 0)
                def _():
                    cm.st_wait(None)

                stored(i).start()
                rows = cm.rows(i)
                rate = lax.rsqrt(cm.st_sum(i) / d + EPS)
                rate_ref[rows, :] = jnp.broadcast_to(rate, (tc, LANES))
                out = nn(full[rows, :], wg_ref[...]) * rate * sg_ref[0:1, :]
                gu_ref[rows, :] = out.astype(BF16)
                gate, up = out[:, :npad], out[:, npad:]
                hidden = (gate / (1.0 + jnp.exp(-gate)) * up).astype(BF16)
                hid_ref[rows, :] = hidden
                for role in range(2 * nl):
                    sb[i, role // nl, role % nl] = nn(
                        hidden, wd_ref[:, role * fw : (role + 1) * fw]
                    ).astype(BF16)
                cm.rs_across(i).start()
                lora_ref[rows, :] = nn(hidden, wd_ref[:, d:]).astype(BF16)
                io.store(i, 0, 1, 4, 10)

            cm.rs_steps(i)

            @pl.when(i == 3)
            def _():
                total = cm.cs_total()
                qd_ref[...] = jnp.broadcast_to(total, (8, fw))
                sd_ref[...] = jnp.broadcast_to(m_ref[4:5, :] * lax.rsqrt(total), (8, fw))

            @pl.when(i >= 3)
            def _():
                rows = cm.rows(i - 3)
                down = cm.rs_total(i - 3) * sd_ref[0:1, :]
                out_ref[rows, :] = (mid_ref[rows, :] + down).astype(BF16)
                swap.wait(*cot_swap(i - 3))
                seed = cot_ref[rows, :].astype(F32)
                gm_ref[0:1, :] += row_sum(seed * down)
                gp_ref[rows, :] = (seed * sd_ref[0:1, :]).astype(BF16)
                io.store(i - 3, 2, 5)

            return carry_on

        lax.fori_loop(0, nc + 3, body, 0)

        def drain(i, carry_on):
            cm.ag_drain(i)
            cm.rs_drain(i)
            stored(i).wait()
            io.stored(i)
            swap.drain(*cot_swap(i))
            return carry_on

        lax.fori_loop(0, nc, drain, 0)
        cm.st_drain(None)
        cm.cs_drain()

    dma = pltpu.SemaphoreType.DMA
    return call(
        kernel,
        "ffn_forward",
        (
            shape((t, 2 * npad), BF16),
            shape((t, npad), BF16),
            shape((t, fw), BF16),
            shape((8, fw), F32),
            shape((t, LANES), F32),
            shape((t, fw), BF16),
            shape((8, 2 * npad), F32),
            shape((8, 2 * npad), F32),
            shape((8, fw), F32),
            shape((8, fw), F32),
            shape((t, LANES), BF16),
            shape((t, fw), BF16),
            shape((t, d), BF16),
        ),
        [VM] * 8,
        (VM,) * 12 + (ANY,),
        ag_scratch(nl, nc, t, d)
        + rs_scratch(nl, nc, tc, fw)
        + st_scratch(nl, nc, t)
        + cs_scratch(nl, d, fw)
        + [dma((nc,))] * 4,
        3,
        110,
        (u, stats, w_gu, m_gu, w_down, small, middle, cotangent),
        late=(2, 4, 6),
        flow=(0, 1, 2, 4, 5, 10),
        step=tc,
    )


def ffn_backward(cfg, npad, gp, gu, w_gu, sc_gu, b_gu, w_down, b_down, rate, cotangent, middle, x, sc_out):
    t, fw, d, nl, nc, tc = cfg

    def kernel(
        io, gp_ref, gu_hbm, wg_ref, sg_ref, bg_ref, wd_ref, bd_ref, rate_ref, cot_ref, mid_ref, x_ref, so_ref,
        dm_ref, go_ref, gmo_ref, gm_ref, lg_ref, ld_ref, dp_hbm, gf_ref,
        full, own, sd, rd, sc, rc, sb, cb, gb, s1, r1, s2, r2, sa, ss, sr, st, gu_s, keep, load, save,
    ):
        cm = Comm(nl, nc, tc, fw)
        cm.ag_refs(gp_ref, full, own, sd, rd, sc, rc)
        cm.rs_refs(sb, cb, gb, s1, r1, s2, r2)
        cm.st_refs(st, sa, ss, sr)

        def loaded(i):
            rows = cm.rows(i)
            return pltpu.make_async_copy(gu_hbm.at[rows], gu_s.at[rows], load.at[i])

        def saved(i):
            rows = cm.rows(i)
            return pltpu.make_async_copy(gu_s.at[rows], dp_hbm.at[rows], save.at[i])

        def stored(i):
            rows = cm.rows(i)
            return pltpu.make_async_copy(full.at[rows], gf_ref.at[rows], keep.at[i])

        cm.barrier()
        cm.ag_start()

        def start_loads(i, carry_on):
            loaded(i).start()
            return carry_on

        lax.fori_loop(0, nc, start_loads, 0)
        cm.ag_ahead()
        io.ready()
        gm_ref[...] = jnp.zeros_like(gm_ref)
        gmo_ref[...] = jnp.zeros_like(gmo_ref)

        def body(i, carry_on):
            @pl.when(i < nc)
            def _():
                cm.ag_step(i + 2)
                cm.ag_wait(i)
                stored(i).start()
                loaded(i).wait()
                rows = cm.rows(i)
                block = full[rows, :]
                dh = nt(block, wd_ref[:, :d])
                ld_ref[rows, :] = nt(block, bd_ref[...]).astype(BF16)
                gate = gu_s[rows, :npad].astype(F32)
                up = gu_s[rows, npad:].astype(F32)
                sig = 1.0 / (1.0 + jnp.exp(-gate))
                dgate = dh * up * (sig * (1.0 + gate * (1.0 - sig)))
                dup = dh * (gate * sig)
                pg, pu = dgate * gate, dup * up
                gm_ref[0:1, :npad] += jnp.sum(pg, axis=0, keepdims=True)
                gm_ref[0:1, npad:] += jnp.sum(pu, axis=0, keepdims=True)
                st[i] = ones_rows(pg + pu)[0:1, :]
                cm.st_send(i)
                gu_s[rows, :npad] = (dgate * sg_ref[0:1, :npad]).astype(BF16)
                gu_s[rows, npad:] = (dup * sg_ref[0:1, npad:]).astype(BF16)
                saved(i).start()
                dp = gu_s[rows, :]
                lg_ref[rows, :] = (nt(dp, bg_ref[...].astype(BF16)) * rate_ref[rows, :]).astype(BF16)
                io.store(i, 4, 5)
                for role in range(2 * nl):
                    sb[i, role // nl, role % nl] = nt(
                        dp, wg_ref[role * fw : (role + 1) * fw, :]
                    ).astype(BF16)
                cm.rs_across(i).start()

            cm.rs_steps(i)

            @pl.when(i >= 3)
            def _():
                k = i - 3
                rows = cm.rows(k)
                cm.st_wait(k)
                r = rate_ref[rows, 0:1]
                inner = cm.st_sum(k)
                mid = mid_ref[rows, :]
                dm = (
                    cot_ref[rows, :].astype(F32)
                    + r * cm.rs_total(k)
                    - mid * (r * r * inner / d)
                )
                dm_ref[rows, :] = dm
                go_ref[rows, :] = (dm * so_ref[0:1, :]).astype(BF16)
                io.store(k, 0, 1)
                gmo_ref[0:1, :] += jnp.sum(
                    dm * (mid - x_ref[rows, :].astype(F32)), axis=0, keepdims=True
                )

            return carry_on

        lax.fori_loop(0, nc + 3, body, 0)

        def drain(i, carry_on):
            cm.ag_drain(i)
            cm.rs_drain(i)
            cm.st_drain(i)
            stored(i).wait()
            saved(i).wait()
            io.stored(i)
            return carry_on

        lax.fori_loop(0, nc, drain, 0)

    return call(
        kernel,
        "ffn_backward",
        (
            shape((t, fw), F32),
            shape((t, fw), BF16),
            shape((8, fw), F32),
            shape((8, 2 * npad), F32),
            shape((t, LANES), BF16),
            shape((t, LANES), BF16),
            shape((t, 2 * npad), BF16),
            shape((t, d), BF16),
        ),
        [VM, ANY] + [VM] * 10,
        (VM,) * 6 + (ANY, ANY),
        ag_scratch(nl, nc, t, d)
        + rs_scratch(nl, nc, tc, fw)
        + st_scratch(nl, nc, t)
        + [
            pltpu.VMEM((nc, 1, tc), F32),
            pltpu.VMEM((t, 2 * npad), BF16),
            pltpu.SemaphoreType.DMA((nc,)),
            pltpu.SemaphoreType.DMA((nc,)),
            pltpu.SemaphoreType.DMA((nc,)),
        ],
        4,
        120,
        (gp, gu, w_gu, sc_gu, b_gu, w_down, b_down, rate, cotangent, middle, x, sc_out),
        late=(2, 4, 5, 6, 7, 8, 9, 10),
        flow=(0, 1, 4, 5),
        step=tc,
    )


def gain_rows(tail, at):
    lane = lax.broadcasted_iota(jnp.int32, (8, LANES), 1)
    pick = jnp.where((lane == at) | (lane == at + 1), 1.0, 0.0).astype(BF16)
    column = tail[:, at : at + 1].astype(F32) + tail[:, at + 1 : at + 2].astype(F32)
    return nt(pick, tail)[0:1, :], column


class Stream:
    def __init__(self, sources, slots, sems, step):
        self.sources, self.slots, self.sems, self.step = sources, slots, sems, step

    def copies(self, i):
        rows = pl.ds(pl.multiple_of(i * self.step, self.step), self.step)
        slot = lax.rem(i, 2)
        return [
            pltpu.make_async_copy(src.at[rows, columns], held.at[slot], self.sems.at[k, slot])
            for k, ((src, columns), held) in enumerate(zip(self.sources, self.slots))
        ]

    def start(self, i):
        for copy in self.copies(i):
            copy.start()

    def wait(self, i):
        for copy in self.copies(i):
            copy.wait()
        return [held[lax.rem(i, 2)] for held in self.slots]


def stream_scratch(step, widths):
    return [pltpu.VMEM((2, step, n), BF16) for n in widths] + [pltpu.SemaphoreType.DMA((len(widths), 2))]


def out_backward(
    cfg, npad, nf, go, weights, b_out, ratios, w_gu, w_down, up_gu, b_down, gm_gu, square_gu, m_gu,
    u_full, lg_gu, gu, dp_gu, hidden, lg_down, lora_down, gp_full, result,
):
    t, fw, d, nl, nc, tc = cfg
    off = nf - (npad - LANES)
    widths = (d, LANES, LANES, LANES, 2 * npad, npad, LANES, LANES, d)

    def kernel(
        io, go_ref, w_ref, b_ref, q_ref, wg_ref, wd_ref, up_ref, bd_ref, gm_ref, sq_ref, m_ref,
        uf_hbm, lg_hbm, gu_hbm, dp_hbm, hid_hbm, ld_hbm, lo2_hbm, gp_hbm, res_hbm,
        da_ref, lo_ref, qs_ref, sh_ref, lc_ref, gf_ref, moved_ref,
        full, own, sd, rd, sc, rc, keep, qss, qsr, res_sems, acc_a, acc_g, acc_u, acc_d, acc_p, *streams,
    ):
        cm = Comm(nl, nc, tc, fw, out_by_one=0.75)
        swap = Swap(cm)
        result_swap = (res_hbm, moved_ref, tuple(res_sems.at[k] for k in range(3)))
        cm.ag_refs(go_ref, full, own, sd, rd, sc, rc)
        every = lambda n: pl.ds(0, n)
        stream = Stream(
            [
                (uf_hbm, every(d)),
                (lg_hbm, every(LANES)),
                (gu_hbm, pl.ds(npad - LANES, LANES)),
                (gu_hbm, pl.ds(2 * npad - LANES, LANES)),
                (dp_hbm, every(2 * npad)),
                (hid_hbm, every(npad)),
                (ld_hbm, every(LANES)),
                (lo2_hbm, every(LANES)),
                (gp_hbm, every(d)),
            ],
            streams[:-1],
            streams[-1],
            tc,
        )
        stream.start(jnp.int32(0))
        cm.barrier((), [swap.partner])

        def ratio_copy(o, m):
            k = o * nl + m
            return cm.copy(
                q_ref, qs_ref.at[:, cm.columns(cm.c, cm.g)], qss.at[k], qsr.at[k], 1 - cm.c if o else cm.c, cm.after(m)
            )

        cm.ag_start()
        for o, m in cm.st_peers():
            ratio_copy(o, m).start()
        qs_ref[:, cm.columns(cm.c, cm.g)] = q_ref[...]
        swap.start(*result_swap)
        for acc in (acc_a, acc_g, acc_u, acc_d, acc_p):
            acc[...] = jnp.zeros_like(acc)
        cm.ag_ahead()
        io.ready()

        def stored(i):
            rows = cm.rows(i)
            return pltpu.make_async_copy(full.at[rows], gf_ref.at[rows], keep.at[i])

        def body(i, carry_on):
            cm.ag_step(i + 2)

            @pl.when(i + 1 < nc)
            def _():
                stream.start(i + 1)

            u, lg, low_g, low_u, dp, hid, ld, low_d, gp = stream.wait(i)
            acc_a[...] += tn(lg, u)
            acc_g[...] += tn(low_g, dp[:, :npad])
            acc_u[...] += tn(low_u, dp[:, npad:])
            acc_d[...] += tn(ld, hid)
            acc_p[...] += tn(low_d, gp)
            cm.ag_wait(i)
            stored(i).start()
            rows = cm.rows(i)
            block = full[rows, :]
            da_ref[rows, :] = nt(block, w_ref[:, :d]).astype(BF16)
            lo_ref[rows, :] = nt(block, b_ref[...]).astype(BF16)
            return carry_on

        lax.fori_loop(0, nc, body, 0)

        ratio = -gm_ref[0:1, :] / sq_ref[0:1, :]
        term = nt((up_ref[...] * ratio).astype(BF16), wg_ref[...])
        tail_g, tail_u = wg_ref[:, npad - LANES : npad], wg_ref[:, 2 * npad - LANES :]
        gain_row, gain_column = gain_rows(tail_g, off + RANK)
        inverse = 1.0 / (gain_column * gain_column)
        sh_ref[: 2 * RANK, :] = (
            SCALE * (acc_a[: 2 * RANK, :] * gain_row + term[: 2 * RANK, :] / gain_row)
        ).astype(BF16)
        for k, (acc, tail) in enumerate(((acc_g, tail_g), (acc_u, tail_u))):
            at = slice(k * npad, (k + 1) * npad)
            merged = tn((tail.astype(F32) * inverse).astype(BF16), wg_ref[:, at])
            lc_ref[(1 + k) * RANK : (2 + k) * RANK, :] = (
                SCALE * (acc[off : off + RANK, :] + merged[off : off + RANK, :] * ratio[:, at])
            ).astype(BF16)
            lc_ref[3 * RANK + k : 3 * RANK + k + 1, :] = (gm_ref[0:1, at] / m_ref[0:1, at]).astype(BF16)
        lc_ref[3 * RANK + 2 :, :] = jnp.zeros((RANK - 2, npad), BF16)

        for o, m in cm.st_peers():
            ratio_copy(o, m).wait_recv()
        ratio_down = qs_ref[1:2, :]
        lc_ref[:RANK, :] = (
            SCALE
            * (acc_d[:RANK, :] + nt((bd_ref[...].astype(F32) * ratio_down).astype(BF16), wd_ref[:, :d])[:RANK, :])
        ).astype(BF16)
        sh_ref[2 * RANK :, :] = (
            SCALE * (acc_p[:RANK, :] + tn(wd_ref[:, d:], wd_ref[:, :d])[:RANK, :] * ratio_down)
        ).astype(BF16)

        def drain(i, carry_on):
            cm.ag_drain(i)
            stored(i).wait()
            return carry_on

        lax.fori_loop(0, nc, drain, 0)
        swap.wait(*result_swap)
        swap.drain(*result_swap)
        for o, m in cm.st_peers():
            ratio_copy(o, m).wait_send()

    dma = pltpu.SemaphoreType.DMA
    return call(
        kernel,
        "out_backward",
        (
            shape((t, fw), BF16),
            shape((t, LANES), BF16),
            shape((8, d), F32),
            shape((3 * RANK, d), BF16),
            shape((4 * RANK, npad), BF16),
            shape((t, d), BF16),
            shape((t, fw), BF16),
        ),
        [VM] * 11 + [ANY] * 9,
        (VM,) * 5 + (ANY, ANY),
        ag_scratch(nl, nc, t, d)
        + [dma((nc,)), dma((2 * nl,)), dma((2 * nl,)), dma((3,))]
        + [pltpu.VMEM((LANES, n), F32) for n in (d, npad, npad, npad, d)]
        + stream_scratch(tc, widths),
        5,
        60,
        (
            go, weights, b_out, ratios, w_gu, w_down, up_gu, b_down, gm_gu, square_gu, m_gu,
            u_full, lg_gu, gu, dp_gu, hidden, lg_down, lora_down, gp_full, result,
        ),
        late=(1, 2, 4, 5, 6, 7),
    )


def attention_backward(
    cfg, qkv, attended, grad, lse, seg_column, seg_row, first_block, block, cosine, sine, scale, rate, b_qkv
):
    t, fw = cfg[0], cfg[1]
    heads = fw // HD
    width = 3 * fw

    def kernel(
        io, qkv_ref, att_ref, grad_ref, lse_ref, sc_ref, sr_ref, first_ref, cos_ref, sin_ref, scale_ref, rate_ref, b_ref,
        dp_ref, st_ref, gm_ref, lg_ref, dq, dk, dv,
    ):
        def at(i):
            return pl.ds(pl.multiple_of(i * block, block), block)

        def columns(k, hd):
            return slice(k * fw + hd * HD, k * fw + (hd + 1) * HD)

        gm_ref[...] = jnp.zeros_like(gm_ref)
        dk[...] = jnp.zeros_like(dk)
        dv[...] = jnp.zeros_like(dv)

        def one_query(i, carry_on):
            queries = [qkv_ref[at(i), columns(0, hd)] for hd in range(heads)]
            grads = [grad_ref[at(i), columns(0, hd)] for hd in range(heads)]
            deltas = [
                ones_rows(grads[hd].astype(F32) * att_ref[at(i), columns(0, hd)].astype(F32))[0:1, :]
                for hd in range(heads)
            ]
            query_segment = sr_ref[0:1, at(i)]

            def one_key(j, accs):
                allowed = allowed_of(sc_ref[at(j), 0:1], query_segment, j, i, block)
                out = []
                for hd in range(heads):
                    keys = qkv_ref[at(j), columns(1, hd)]
                    s = nt(keys, queries[hd]) * (HD**-0.5)
                    p = jnp.where(allowed, jnp.exp(s - lse_ref[hd * 8 : hd * 8 + 1, at(i)]), 0.0)
                    ds = (p * (nt(qkv_ref[at(j), columns(2, hd)], grads[hd]) - deltas[hd])).astype(BF16)
                    dv[hd, at(j), :] += nn(p.astype(BF16), grads[hd])
                    dk[hd, at(j), :] += nn(ds, queries[hd])
                    out.append(accs[hd] + tn(ds, keys))
                return tuple(out)

            accs = lax.fori_loop(first_ref[i], i + 1, one_key, (jnp.zeros((block, HD), F32),) * heads)
            for hd in range(heads):
                dq[hd, at(i), :] = accs[hd]
            return carry_on

        lax.fori_loop(0, t // block, one_query, 0)

        def finish(i, carry_on):
            rows = at(i)
            cosine_here, sine_here = cos_ref[rows, :], sin_ref[rows, :]
            inner = jnp.zeros((block, HD), F32)
            for hd in range(heads):
                for n, source in enumerate((dq, dk, dv)):
                    where = columns(n, hd)
                    dout = source[hd, rows, :]
                    value = qkv_ref[rows, where].astype(F32)
                    if n < 2:
                        dout = dout * (HD**-0.5)
                        dout = dout * cosine_here - pltpu.roll(dout, HD // 2, 1) * sine_here
                        value = value * cosine_here - pltpu.roll(value, HD // 2, 1) * sine_here
                    product = dout * value
                    inner = inner + product
                    gm_ref[0:1, where] += row_sum(product)
                    dp_ref[rows, where] = (dout * scale_ref[0:1, where]).astype(BF16)
            st_ref[i] = ones_rows(inner)[0:1, :]
            lg_ref[rows, :] = (nt(dp_ref[rows, :], b_ref[...].astype(BF16)) * rate_ref[rows, :]).astype(BF16)
            return carry_on

        lax.fori_loop(0, t // block, finish, 0)

    return call(
        kernel,
        "attention_backward",
        (
            shape((t, width), BF16),
            shape((t // block, 1, block), F32),
            shape((8, width), F32),
            shape((t, LANES), BF16),
        ),
        [VM] * 6 + [SM] + [VM] * 5,
        (VM,) * 4,
        [pltpu.VMEM((heads, t, HD), F32)] * 3,
        None,
        35,
        (qkv, attended, grad, lse, seg_column, seg_row, first_block, cosine, sine, scale, rate, b_qkv),
    )


def qkv_backward(
    cfg, ny, dp, stats, weights, rate, dm, x, shared, local_gu, w_out, up_qkv, b_out, ratios, gm_qkv, square_qkv,
    gm_out, gm_down, small, x_full, lg_qkv, lora_qkv, attended, lg_out, lora_out, go_full,
):
    t, fw, d, nl, nc, tc = cfg
    width = 3 * fw
    peers = 2 * nl
    step = 2 * tc if nc % 2 == 0 else tc
    parts = t // step
    widths = (d, LANES, LANES, fw, LANES, LANES, d)

    def kernel(
        io, dp_ref, st_ref, w_ref, rate_ref, dm_ref, x_ref, sh_ref, l_ref, wo_ref, up_ref, bo_ref, q_ref,
        gm_ref, sq_ref, gmo_ref, gmd_ref, m_ref, xf_hbm, lg_hbm, lq_hbm, at_hbm, lgo_hbm, lo_hbm, gf_hbm,
        out_ref, as_ref, bs_ref, ls_ref,
        sb, cb, gb, s1, r1, s2, r2, sa, ss, sr,
        stage, gs_s, gs_r, gs_l, group, gsum, gss, gsr, final_a, final_b, final_l, fs, fr, fl,
        a_ref, b_ref, acc_a, acc_b, acc_o, acc_p, *streams,
    ):
        cm = Comm(nl, nc, tc, fw, back_by_two=0.25)
        c, g = cm.c, cm.g
        y, h = lax.axis_index("y"), lax.axis_index("h")
        cm.rs_refs(sb, cb, gb, s1, r1, s2, r2)
        cm.st_refs(st_ref, sa, ss, sr)
        swap = Swap(cm)
        every = lambda n: pl.ds(0, n)
        stream = Stream(
            [
                (xf_hbm, every(d)),
                (lg_hbm, every(LANES)),
                (lq_hbm, every(LANES)),
                (at_hbm, every(fw)),
                (lgo_hbm, every(LANES)),
                (lo_hbm, every(LANES)),
                (gf_hbm, every(d)),
            ],
            streams[:-1],
            streams[-1],
            step,
        )
        stream.start(jnp.int32(0))
        senders = [
            {"y": lax.rem(y + ny - k, ny), "c": h, "h": hh} for k in range(1, ny) for hh in (0, 1)
        ]
        cm.barrier(senders + [{"c": h, "h": 1 - h}], [swap.partner, {"c": h, "h": h}])

        def gather_part(o, m):
            to_c, to_g = 1 - c if o else c, cm.after(m)
            k = o * nl + m
            return cm.copy(
                a_ref.at[:, cm.columns(to_c, to_g)], group.at[k], gss.at[k], gsr.at[k], to_c, to_g
            )

        def sums(k, e):
            device = {"y": lax.rem(y + k, ny), "c": lax.rem(c + e, 2), "h": c}
            slot = k * 2 + h
            return [
                pltpu.make_async_remote_copy(
                    src_ref=src, dst_ref=dst.at[slot], send_sem=fs.at[n, k * 2 + e], recv_sem=fr.at[n, slot],
                    device_id=device, device_id_type=MESH,
                )
                for n, (src, dst) in enumerate(((gsum, final_a), (b_ref, final_b), (l_ref, final_l)))
            ]

        def sums_here():
            return [
                pltpu.make_async_copy(src, dst.at[h], fl.at[n])
                for n, (src, dst) in enumerate(((gsum, final_a), (b_ref, final_b), (l_ref, final_l)))
            ]

        cm.st_send(None)
        for acc in (acc_a, acc_b, acc_o, acc_p):
            acc[...] = jnp.zeros_like(acc)

        def adapters(k):
            @pl.when(k + 1 < parts)
            def _():
                stream.start(k + 1)

            xf, lg, low_q, att, lg_o, low_o, gf = stream.wait(k)
            rows = pl.ds(pl.multiple_of(k * step, step), step)
            acc_a[...] += tn(lg, xf)
            acc_b[...] += tn(low_q, dp_ref[rows, :])
            acc_o[...] += tn(lg_o, att)
            acc_p[...] += tn(low_o, gf)

        def adapters_end():
            ratio = -gm_ref[0:1, :] / sq_ref[0:1, :]
            ratio_out = q_ref[0:1, :]
            tail = w_ref[:, width:]
            gain_row, gain_column = gain_rows(tail, 3 * RANK)
            term = nt((up_ref[...] * ratio).astype(BF16), w_ref[:, :width])
            a_ref[: 3 * RANK, :] = (
                SCALE * (acc_a[: 3 * RANK, :] * gain_row + term[: 3 * RANK, :] / gain_row)
            ).astype(BF16)
            merged = tn(
                (tail.astype(F32) / (gain_column * gain_column)).astype(BF16), w_ref[:, :width]
            )
            for k in range(3):
                at, low = slice(k * fw, (k + 1) * fw), slice(k * RANK, (k + 1) * RANK)
                b_ref[(1 + k) * RANK : (2 + k) * RANK, :] = (
                    SCALE * (acc_b[low, at] + merged[low, at] * ratio[:, at])
                ).astype(BF16)
                b_ref[4 * RANK + k : 4 * RANK + k + 1, :] = (gm_ref[0:1, at] / m_ref[k : k + 1, :]).astype(BF16)
            b_ref[4 * RANK + 3 : 4 * RANK + 4, :] = (gmo_ref[0:1, :] / m_ref[3:4, :]).astype(BF16)
            b_ref[4 * RANK + 4 : 4 * RANK + 5, :] = (gmd_ref[0:1, :] / m_ref[4:5, :]).astype(BF16)
            b_ref[4 * RANK + 5 :, :] = jnp.zeros((RANK - 5, fw), BF16)
            b_ref[:RANK, :] = (
                SCALE
                * (acc_o[:RANK, :] + nt((bo_ref[...].astype(F32) * ratio_out).astype(BF16), wo_ref[:, :d])[:RANK, :])
            ).astype(BF16)
            a_ref[3 * RANK : 4 * RANK, :] = (
                SCALE * (acc_p[:RANK, :] + tn(wo_ref[:, d:], wo_ref[:, :d])[:RANK, :] * ratio_out)
            ).astype(BF16)
            a_ref[4 * RANK :, :] = sh_ref[...]
            for o, m in cm.st_peers():
                gather_part(o, m).start()

        io.ready()

        def grad_swap(i):
            rows = cm.rows(i)
            return stage.at[rows], out_ref.at[rows], (gs_s.at[i], gs_r.at[i], gs_l.at[i])

        def body(i, carry_on):
            @pl.when(i < nc)
            def _():
                block = dp_ref[cm.rows(i), :]
                for role in range(2 * nl):
                    sb[i, role // nl, role % nl] = nt(
                        block, w_ref[role * fw : (role + 1) * fw, :width]
                    ).astype(BF16)
                cm.rs_across(i).start()

            cm.rs_steps(i)

            @pl.when(i < parts)
            def _():
                adapters(i)

            @pl.when(i == parts)
            def _():
                adapters_end()

            @pl.when(i == min(parts + 3, nc + 2))
            def _():
                total = a_ref[:, cm.columns(c, g)].astype(F32)
                for o, m in cm.st_peers():
                    gather_part(o, m).wait_recv()
                    total = total + group[o * nl + m].astype(F32)
                gsum[...] = total.astype(BF16)
                for k in range(ny):
                    for e in (0, 1):
                        if (k, e) == (0, 0):

                            @pl.when(swap.moves)
                            def _():
                                for copy in sums(0, 0):
                                    copy.start()

                            @pl.when(jnp.logical_not(swap.moves))
                            def _():
                                for copy in sums_here():
                                    copy.start()
                        else:
                            for copy in sums(k, e):
                                copy.start()

            @pl.when(i >= 3)
            def _():
                k = i - 3
                rows = cm.rows(k)

                @pl.when(k == 0)
                def _():
                    cm.st_wait(None)

                r = rate_ref[rows, 0:1]
                inner = cm.st_sum(k)
                stage[rows, :] = (
                    dm_ref[rows, :]
                    + r * cm.rs_total(k)
                    - x_ref[rows, :].astype(F32) * (r * r * inner / d)
                ).astype(BF16)
                swap.start(*grad_swap(k))

            return carry_on

        lax.fori_loop(0, nc + 3, body, 0)

        for k in range(ny):
            for hh in (0, 1):
                slot = k * 2 + hh

                def arrived():
                    for n, dst in enumerate((final_a, final_b, final_l)):
                        src = (gsum, b_ref, l_ref)[n]
                        pltpu.make_async_remote_copy(
                            src_ref=src, dst_ref=dst.at[slot], send_sem=fs.at[n, 0], recv_sem=fr.at[n, slot],
                            device_id=swap.partner, device_id_type=MESH,
                        ).wait_recv()

                if k == 0:
                    here = jnp.logical_and(c == h, h == hh)

                    @pl.when(here)
                    def _():
                        for copy in sums_here():
                            copy.wait()

                    @pl.when(jnp.logical_not(here))
                    def _():
                        arrived()
                else:
                    arrived()
        for out, held in ((as_ref, final_a), (bs_ref, final_b), (ls_ref, final_l)):
            total = held[0].astype(F32)
            for slot in range(1, 2 * ny):
                total = total + held[slot].astype(F32)
            out[...] = total

        def drain(i, carry_on):
            swap.wait(*grad_swap(i))
            cm.rs_drain(i)
            swap.drain(*grad_swap(i))
            return carry_on

        lax.fori_loop(0, nc, drain, 0)
        cm.st_drain(None)
        for o, m in cm.st_peers():
            gather_part(o, m).wait_send()
        for k in range(ny):
            for e in (0, 1):
                if (k, e) == (0, 0):

                    @pl.when(swap.moves)
                    def _():
                        for copy in sums(0, 0):
                            copy.wait_send()
                else:
                    for copy in sums(k, e):
                        copy.wait_send()

    dma = pltpu.SemaphoreType.DMA
    na, nb, ng = 7 * RANK, (5 * RANK, fw), local_gu.shape
    return call(
        kernel,
        "qkv_backward",
        (shape((t, fw), BF16), shape((na, fw), F32), shape(nb, F32), shape(ng, F32)),
        [VM] * 17 + [ANY] * 7,
        (VM,) * 4,
        rs_scratch(nl, nc, tc, fw)
        + st_scratch(nl, nc, t)
        + [pltpu.VMEM((t, fw), BF16)]
        + [dma((nc,))] * 3
        + [pltpu.VMEM((peers, na, fw), BF16), pltpu.VMEM((na, fw), BF16), dma((peers,)), dma((peers,))]
        + [
            pltpu.VMEM((2 * ny, na, fw), BF16),
            pltpu.VMEM((2 * ny, *nb), BF16),
            pltpu.VMEM((2 * ny, *ng), BF16),
            dma((3, 2 * ny)),
            dma((3, 2 * ny)),
            dma((3,)),
            pltpu.VMEM((na, d), BF16),
            pltpu.VMEM(nb, BF16),
        ]
        + [pltpu.VMEM((LANES, n), F32) for n in (d, width, fw, d)]
        + stream_scratch(step, widths),
        6,
        70,
        (
            dp, stats, weights, rate, dm, x, shared, local_gu, w_out, up_qkv, b_out, ratios, gm_qkv, square_qkv,
            gm_out, gm_down, small, x_full, lg_qkv, lora_qkv, attended, lg_out, lora_out, go_full,
        ),
        late=(2, 3, 4, 5, 6, 7, 8, 9, 10, 11),
    )


def last_step(fw, nf, grad, result, shared, local, local_gu):
    def kernel(
        io, g_ref, r_ref, s_ref, l_ref, u_ref,
        result_ref, grad_ref, aq_ref, bq_ref, mq_ref, ao_ref, bo_ref, mo_ref,
        ag_ref, bg_ref, mg_ref, ad_ref, bd_ref, md_ref,
    ):
        result_ref[...] = r_ref[...]
        grad_ref[...] = g_ref[...].astype(F32)
        for k in range(3):
            aq_ref[k] = s_ref[k * RANK : (k + 1) * RANK, :]
            bq_ref[k] = l_ref[(1 + k) * RANK : (2 + k) * RANK, :]
        for k in range(2):
            ag_ref[k] = s_ref[(4 + k) * RANK : (5 + k) * RANK, :]
            bg_ref[k] = u_ref[(1 + k) * RANK : (2 + k) * RANK, :nf]
        mq_ref[...] = l_ref[4 * RANK : 4 * RANK + 3, :]
        mg_ref[...] = u_ref[3 * RANK : 3 * RANK + 2, :nf]
        ao_ref[...] = l_ref[:RANK, :]
        bo_ref[...] = s_ref[3 * RANK : 4 * RANK, :]
        mo_ref[...] = l_ref[4 * RANK + 3 : 4 * RANK + 4, :]
        ad_ref[...] = u_ref[:RANK, :nf]
        bd_ref[...] = s_ref[6 * RANK :, :]
        md_ref[...] = l_ref[4 * RANK + 4 : 4 * RANK + 5, :]

    f = [
        (3, RANK, fw), (3, RANK, fw), (3, fw), (RANK, fw), (RANK, fw), (1, fw),
        (2, RANK, fw), (2, RANK, nf), (2, nf), (RANK, nf), (RANK, fw), (1, fw),
    ]
    return call(
        kernel,
        "last_step",
        (shape(result.shape, BF16), shape(grad.shape, F32), *[shape(v, F32) for v in f]),
        [VM] * 5,
        (VM,) * 14,
        [],
        None,
        4,
        (grad, result, shared, local, local_gu),
    )


def turn_constants():
    f = 10000.0 ** (-2.0 * np.arange(HD // 2) / HD)
    out = []
    for scale in (32.0, 1.0):
        angle = scale * np.arange(32)[:, None] * f[None, :]
        table = np.concatenate([np.cos(angle), np.cos(angle), np.sin(angle), np.sin(angle)], axis=1)
        high = table.astype(BF16)
        low = (table - high.astype(np.float64)).astype(BF16)
        out.append(jnp.asarray(np.concatenate([high, low], axis=1)))
    return out


def padded(rows, total):
    return jnp.pad(rows, ((0, 0), (0, total - rows.shape[1])))


def on_device(ny, nl, *operands):
    (
        inputs, segments, gain_attn, gain_ffn, w_qkv, a_qkv, b_qkv, m_qkv, w_out, a_out, b_out, m_out,
        w_gu, a_gu, b_gu, m_gu, w_down, a_down, b_down, m_down, cotangent,
    ) = operands
    t, fw = inputs.shape
    mp = 2 * nl
    d = mp * fw
    nf = m_gu.shape[1]
    npad = -(-(nf + RANK) // LANES) * LANES
    width = 3 * fw
    nc = t // 256 if t % 256 == 0 else 1
    block = t // nc
    cfg = (t, fw, d, nl, nc, block)
    y, c, h, g = (lax.axis_index(name) for name in ("y", "c", "h", "g"))
    role = c * nl + g

    def two_parts(gain):
        high = gain.astype(BF16)
        return [high[:, None], (gain - high.astype(F32)).astype(BF16)[:, None]]

    tail_qkv = padded(
        jnp.concatenate(
            [(a_qkv[k] * gain_attn[:, None]).astype(BF16) for k in range(3)] + two_parts(gain_attn), axis=1
        ),
        LANES,
    )
    tail_gu = jnp.stack(
        [
            jnp.pad(
                jnp.concatenate(
                    [(a_gu[k] * gain_ffn[:, None]).astype(BF16)] + two_parts(gain_ffn), axis=1
                ),
                ((0, 0), (nf, npad - nf - RANK - 2)),
            )
            for k in range(2)
        ]
    )
    gains = padded(jnp.stack([gain_attn, gain_ffn], axis=1), LANES)
    b_gu_padded = jnp.pad(
        b_gu.reshape(2, RANK, mp, nf), ((0, 0), (0, 0), (0, 0), (0, npad - nf))
    ).transpose(0, 2, 1, 3)
    small = jnp.concatenate([m_qkv, m_out[None], m_down[None], jnp.zeros((3, fw), F32)], axis=0)
    small_gu = jnp.broadcast_to(
        jnp.pad(m_gu, ((0, 0), (0, npad - nf)), constant_values=1.0).reshape(1, 2 * npad), (8, 2 * npad)
    )

    def take(whole, n, axis):
        return lax.dynamic_slice_in_dim(whole, role * n, n, axis)

    b_qkv_here = take(b_qkv, fw, 2)
    b_gu_here = take(b_gu, nf, 2)

    def block_up(up, pad):
        k, _, n = up.shape
        wide = jnp.pad(up, ((0, 0), (0, 0), (0, pad - n)))[:, :, None, :]
        same = (jnp.arange(k)[:, None] == jnp.arange(k)[None, :])[:, None, :, None]
        rows = jnp.where(same, wide, 0.0).reshape(k * RANK, k * pad)
        return jnp.pad(rows, ((0, LANES - k * RANK), (0, 0)))

    up_qkv = block_up(b_qkv_here, fw)
    up_gu = block_up(b_gu_here, npad)
    up_out = jnp.pad(b_out, ((0, LANES - RANK), (0, 0))).astype(BF16)
    up_down = jnp.pad(b_down, ((0, LANES - RANK), (0, 0))).astype(BF16)

    (
        x, weights_qkv, weights_out, small, small_gu, scale_qkv, square_qkv, qkv, lora_qkv_in, rate_attn,
        blocks_gu, rows_down, weights_gu, x_full, cosine, sine, seg_column, seg_row,
    ) = qkv_forward(
        cfg, ny, npad, nf, inputs, w_qkv, a_qkv, b_qkv, tail_qkv, gains, w_out, small, small_gu, segments,
        turn_constants(), w_gu, a_gu, b_gu_padded, tail_gu, w_down, a_down, b_down, a_out, b_out,
    )
    first_number = seg_row[0, ::block]
    first_block = jnp.sum((seg_row[0][None, :] < first_number[:, None]).astype(jnp.int32), axis=1) // block
    attended, lse = attention_forward(cfg, qkv, seg_column, seg_row, first_block, block)
    middle, u, stats, sc_out, square_out, lora_out, weights_gu, weights_down = out_forward(
        cfg, ny, npad, attended, weights_out, x, small, weights_gu, blocks_gu, rows_down
    )
    (
        gu, hidden, block_out, gm_down, rate_ffn, gp, scale_gu, square_gu, sc_down, square_down,
        lora_down, grad_seed, u_full,
    ) = ffn_forward(
        cfg, npad, nf, u, stats, weights_gu, small_gu[0:1], weights_down, small, middle, cotangent
    )

    dm, go, gm_out, gm_gu, lg_gu, lg_down, dp_gu, gp_full = ffn_backward(
        cfg, npad, gp, gu, weights_gu, scale_gu, up_gu, weights_down, up_down, rate_ffn,
        grad_seed, middle, x, sc_out,
    )
    ratios = jnp.concatenate(
        [-gm_out[0:1] / square_out[0:1], -gm_down[0:1] / square_down[0:1], jnp.zeros((6, fw), F32)], axis=0
    )
    grad_attended, lg_out, ratios, shared, local_gu, go_full, block_out = out_backward(
        cfg, npad, nf, go, weights_out, up_out, ratios, weights_gu, weights_down, up_gu, up_down, gm_gu, square_gu,
        small_gu, u_full, lg_gu, gu, dp_gu, hidden, lg_down, lora_down, gp_full, block_out,
    )
    dp_qkv, inner, gm_qkv, lg_qkv = attention_backward(
        cfg, qkv, attended, grad_attended, lse, seg_column, seg_row, first_block, block, cosine, sine,
        scale_qkv, rate_attn, up_qkv,
    )

    grad_input, shared, local, local_gu = qkv_backward(
        cfg, ny, dp_qkv, inner, weights_qkv, rate_attn, dm, x, shared, local_gu, weights_out, up_qkv, up_out, ratios,
        gm_qkv, square_qkv, gm_out, gm_down, small, x_full, lg_qkv, lora_qkv_in, attended, lg_out, lora_out, go_full,
    )
    out = list(last_step(fw, nf, grad_input, block_out, shared, local, local_gu))
    out[2], out[8] = out[2].transpose(0, 2, 1), out[8].transpose(0, 2, 1)
    out[5], out[11] = out[5].T, out[11].T
    out[7], out[13] = out[7][0], out[13][0]
    return tuple(out)


def solution(mesh):
    dp, mp = mesh.shape["dp"], mesh.shape["mp"]
    ny, nl = dp // 2, mp // 2
    fine = Mesh(mesh.devices.reshape(ny, 2, 2, nl), ("y", "c", "h", "g"))
    rows, cols = ("y", "c"), ("h", "g")
    in_specs = (
        P(rows, cols),
        P(rows, None),
        P(cols),
        P(cols),
        P(None, cols, None),
        P(None, cols, None),
        P(),
        P(None, cols),
        P(cols, None),
        P(cols, None),
        P(),
        P(cols),
        P(None, cols, None),
        P(None, cols, None),
        P(),
        P(None, cols),
        P(cols, None),
        P(cols, None),
        P(),
        P(cols),
        P(rows, cols),
    )
    out_specs = (
        P(rows, cols),
        P(rows, cols),
        P(None, cols, None),
        P(None, None, cols),
        P(None, cols),
        P(cols, None),
        P(None, cols),
        P(cols),
        P(None, cols, None),
        P(None, None, cols),
        P(None, cols),
        P(cols, None),
        P(None, cols),
        P(cols),
    )
    return jax.shard_map(
        lambda *operands: on_device(ny, nl, *operands),
        mesh=fine,
        in_specs=in_specs,
        out_specs=out_specs,
        check_vma=False,
    )
```

```python
import jax
import jax.numpy as jnp
import numpy as np
from jax import lax
from jax.experimental import pallas as pl
from jax.experimental.pallas import tpu as pltpu
from jax.sharding import Mesh
from jax.sharding import PartitionSpec as P

HD = 128
RANK = 16
SCALE = 2.0
EPS = 1e-05
MASKED = -1e30
HIGHEST = lax.Precision.HIGHEST
MESH = pl.DeviceIdType.MESH
F32 = jnp.float32
BF16 = jnp.bfloat16
LANES = 128
SEGMENTS = 8
VMEM_LIMIT = 60 * 1024 * 1024


def nt(a, b, precision=None):
    return lax.dot_general(
        a, b, (((1,), (1,)), ((), ())), precision=precision, preferred_element_type=F32
    )


def tn(a, b, precision=None):
    return lax.dot_general(
        a, b, (((0,), (0,)), ((), ())), precision=precision, preferred_element_type=F32
    )


def nn(a, b, precision=None):
    return lax.dot_general(
        a, b, (((1,), (0,)), ((), ())), precision=precision, preferred_element_type=F32
    )


WINDOW = 3
EARLY = 1


class Comm:
    def __init__(self, nl, nc, tc, fw, out_by_one=0.5, back_by_two=0.5):
        self.nl, self.nc, self.tc, self.fw = nl, nc, tc, fw
        self.square = nl == 4
        self.cut = int(tc * out_by_one) // 16 * 16
        self.back = int(tc * back_by_two) // 16 * 16
        self.c = lax.axis_index("c")
        self.g = lax.axis_index("g")

    def rows(self, i):
        return pl.ds(pl.multiple_of(i * self.tc, self.tc), self.tc)

    def after(self, m):
        return lax.rem(self.g + m, self.nl)

    def before(self, m):
        return lax.rem(self.g + self.nl - m, self.nl)

    def columns(self, c, g):
        return pl.ds(pl.multiple_of((c * self.nl + g) * self.fw, self.fw), self.fw)

    def copy(self, src, dst, send, recv, c, g):
        return pltpu.make_async_remote_copy(
            src_ref=src,
            dst_ref=dst,
            send_sem=send,
            recv_sem=recv,
            device_id={"c": c, "g": g},
            device_id_type=MESH,
        )

    def barrier(self, others=(), one_more=None):
        sem = pltpu.get_barrier_semaphore()
        everyone = [
            {"c": 1 - self.c if other else self.c, "g": self.after(m)}
            for other in (0, 1)
            for m in range(self.nl)
            if (other, m) != (0, 0)
        ] + list(others)
        for device in everyone:
            pl.semaphore_signal(sem, inc=1, device_id=device, device_id_type=MESH)
        if one_more is None:
            pl.semaphore_wait(sem, len(everyone))
        else:
            apart = self.c - lax.axis_index("h")

            @pl.when(apart != 0)
            def _():
                for device in one_more:
                    pl.semaphore_signal(sem, inc=1, device_id=device, device_id_type=MESH)

            pl.semaphore_wait(sem, len(everyone) + len(one_more) * apart * apart)

    def other(self, m):
        if m == 1:
            return self.g + 1 - 2 * lax.rem(self.g, 2)
        return lax.rem(self.g + 2, 4) if m == 2 else 3 - self.g

    def comes_from(self, m):
        if m == 0:
            return self.g
        return self.other(m) if self.square else self.before(m)

    def goes_to(self, m):
        return self.other(m) if self.square else self.after(m)

    def some(self, i, way):
        cut = self.cut
        start, size = (0, cut) if way == 0 else (cut, self.tc - cut)
        return pl.ds(pl.multiple_of(i * self.tc + start, 16), size)

    def ag_refs(self, x, full, own, sd, rd, sc, rc):
        self.x, self.full, self.own = x, full, own
        self.sd, self.rd, self.sc, self.rc = sd, rd, sc, rc

    def ag_steps(self):
        return (1, 2) if self.square else range(1, self.nl)

    def ag_direct(self, i, m):
        rows = self.rows(i)
        return self.copy(
            self.x.at[rows],
            self.full.at[rows, self.columns(self.c, self.g)],
            self.sd.at[i, m],
            self.rd.at[i, m],
            self.c,
            self.goes_to(m),
        )

    def ag_relay(self, i, way):
        rows = self.some(i, way)
        columns = self.columns(self.c, self.other(2 - way))
        return self.copy(
            self.full.at[rows, columns],
            self.full.at[rows, columns],
            self.sd.at[i, 3 * way],
            self.rd.at[i, 3 * way],
            self.c,
            self.other(1 + way),
        )

    def ag_across(self, i, m):
        rows = self.rows(i)
        columns = self.columns(self.c, self.comes_from(m))
        src = self.x.at[rows] if m == 0 else self.full.at[rows, columns]
        return self.copy(
            src,
            self.full.at[rows, columns],
            self.sc.at[i, m],
            self.rc.at[i, m],
            1 - self.c,
            self.g,
        )

    def ag_own(self, i):
        rows = self.rows(i)
        return pltpu.make_async_copy(
            self.x.at[rows],
            self.full.at[rows, self.columns(self.c, self.g)],
            self.own.at[i],
        )

    def ag_send(self, i):
        for m in self.ag_steps():
            self.ag_direct(i, m).start()
        self.ag_across(i, 0).start()
        self.ag_own(i).start()

    def ag_start(self):
        for i in range(min(WINDOW, self.nc)):
            self.ag_send(jnp.int32(i))

    def ag_forward(self, i):
        for m in self.ag_steps():
            self.ag_direct(i, m).wait_recv()
        if self.square:
            for way in (0, 1):
                self.ag_relay(i, way).start()
        for m in self.ag_steps():
            self.ag_across(i, m).start()

    def ag_corner(self, i):
        if self.square:
            for way in (0, 1):
                self.ag_relay(i, way).wait_recv()
            self.ag_across(i, 3).start()

    def ag_step(self, i, more=True):
        @pl.when(i < self.nc)
        def _():
            self.ag_forward(i)

        if more:

            @pl.when(i + WINDOW < self.nc)
            def _():
                self.ag_send(i + WINDOW)

        @pl.when((i >= 1) & (i <= self.nc))
        def _():
            self.ag_corner(i - 1)

    def ag_ahead(self):
        self.ag_step(jnp.int32(0))
        self.ag_step(jnp.int32(1))

    def ag_wait(self, i):
        self.ag_own(i).wait()
        for m in range(self.nl):
            self.ag_across(i, m).wait_recv()

    def ag_drain(self, i):
        for m in self.ag_steps():
            self.ag_direct(i, m).wait_send()
        if self.square:
            for way in (0, 1):
                self.ag_relay(i, way).wait_send()
        for m in range(self.nl):
            self.ag_across(i, m).wait_send()

    def rs_refs(self, sb, cb, gb, s1, r1, s2, r2):
        self.sb, self.cb, self.gb = sb, cb, gb
        self.s1, self.r1, self.s2, self.r2 = s1, r1, s2, r2

    def rs_across(self, i):
        return self.copy(
            self.sb.at[i, 1 - self.c],
            self.cb.at[i],
            self.s1.at[i],
            self.r1.at[i],
            1 - self.c,
            self.g,
        )

    def rs_direct(self, i, m):
        to = self.goes_to(m)
        return self.copy(
            self.sb.at[i, self.c, to],
            self.gb.at[i, m - 1],
            self.s2.at[i, m],
            self.r2.at[i, m],
            self.c,
            to,
        )

    def rs_corner(self, i, way):
        rows = pl.ds(0, self.back) if way == 0 else pl.ds(self.back, self.tc - self.back)
        return self.copy(
            self.sb.at[i, self.c, self.other(3), rows],
            self.gb.at[i, 2, rows],
            self.s2.at[i, 3 * way],
            self.r2.at[i, 3 * way],
            self.c,
            self.other(2 - way),
        )

    def rs_middle(self, i):
        self.rs_across(i).wait_recv()
        for gp in range(self.nl):
            mine = self.sb[i, self.c, gp].astype(F32) + self.cb[i, gp].astype(F32)
            self.sb[i, self.c, gp] = mine.astype(BF16)
        if self.square:
            for way in (0, 1):
                self.rs_corner(i, way).start()
        else:
            for m in range(1, self.nl):
                self.rs_direct(i, m).start()

    def rs_second(self, i):
        if not self.square:
            return
        for way in (0, 1):
            self.rs_corner(i, way).wait_recv()
            rows = pl.ds(0, self.back) if way == 0 else pl.ds(self.back, self.tc - self.back)
            to = self.other(1 + way)
            both = self.sb[i, self.c, to, rows].astype(F32) + self.gb[i, 2, rows].astype(F32)
            self.sb[i, self.c, to, rows] = both.astype(BF16)
        for m in (1, 2):
            self.rs_direct(i, m).start()

    def rs_total(self, i):
        steps = (1, 2) if self.square else range(1, self.nl)
        for m in steps:
            self.rs_direct(i, m).wait_recv()
        total = self.sb[i, self.c, self.g].astype(F32)
        for m in steps:
            total = total + self.gb[i, m - 1].astype(F32)
        return total

    def rs_drain(self, i):
        self.rs_across(i).wait_send()
        if self.square:
            for way in (0, 1):
                self.rs_corner(i, way).wait_send()
        for m in (1, 2) if self.square else range(1, self.nl):
            self.rs_direct(i, m).wait_send()

    def rs_steps(self, i):
        @pl.when((i >= 1) & (i <= self.nc))
        def _():
            self.rs_middle(i - 1)

        @pl.when((i >= 2) & (i <= self.nc + 1))
        def _():
            self.rs_second(i - 2)

    def st_refs(self, st, sa, ss, sr):
        self.st, self.sa, self.ss, self.sr = st, sa, ss, sr

    def st_copy(self, i, other, m):
        mine = self.c * self.nl + self.g
        src, dst = (self.st, self.sa.at[mine]) if i is None else (self.st.at[i], self.sa.at[mine, i])
        i = 0 if i is None else i
        return self.copy(
            src,
            dst,
            self.ss.at[i, other * self.nl + m],
            self.sr.at[i, other * self.nl + m],
            1 - self.c if other else self.c,
            self.after(m),
        )

    def st_peers(self):
        return [(o, m) for o in (0, 1) for m in range(self.nl) if (o, m) != (0, 0)]

    def st_send(self, i):
        for o, m in self.st_peers():
            self.st_copy(i, o, m).start()
        mine = self.c * self.nl + self.g
        if i is None:
            self.sa[mine] = self.st[...]
        else:
            self.sa[mine, i] = self.st[i]

    def st_wait(self, i):
        for o, m in self.st_peers():
            self.st_copy(i, o, m).wait_recv()

    def st_sum(self, i):
        total = self.sa[0, i]
        for role in range(1, 2 * self.nl):
            total = total + self.sa[role, i]
        return jnp.broadcast_to(total, (8, self.tc)).T[:, 0:1]

    def st_drain(self, i):
        for o, m in self.st_peers():
            self.st_copy(i, o, m).wait_send()

    def cs_refs(self, part, held, ss, sr):
        self.part, self.held, self.cs, self.cr = part, held, ss, sr

    def cs_copy(self, other, m):
        c, g = 1 - self.c if other else self.c, self.after(m)
        place = pl.ds(pl.multiple_of((self.c * self.nl + self.g) * 8, 8), 8)
        k = other * self.nl + m
        return self.copy(
            self.part.at[:, self.columns(c, g)], self.held.at[place], self.cs.at[k], self.cr.at[k], c, g
        )

    def cs_start(self, w_ref):
        for role in range(2 * self.nl):
            at = slice(role * self.fw, (role + 1) * self.fw)
            value = w_ref[:, at].astype(F32)
            self.part[:, at] = jnp.broadcast_to(row_sum(value * value), (8, self.fw))
        for o, m in self.st_peers():
            self.cs_copy(o, m).start()
        place = pl.ds(pl.multiple_of((self.c * self.nl + self.g) * 8, 8), 8)
        self.held[place, :] = self.part[:, self.columns(self.c, self.g)]

    def cs_total(self):
        for o, m in self.st_peers():
            self.cs_copy(o, m).wait_recv()
        return row_sum(self.held[...]) * 0.125

    def cs_drain(self):
        for o, m in self.st_peers():
            self.cs_copy(o, m).wait_send()


class Swap:
    def __init__(self, cm):
        self.cm = cm
        self.h = lax.axis_index("h")
        self.moves = cm.c != self.h
        self.partner = {"c": self.h, "h": cm.c}

    def far(self, src, dst, send, recv):
        return pltpu.make_async_remote_copy(
            src_ref=src, dst_ref=dst, send_sem=send, recv_sem=recv, device_id=self.partner, device_id_type=MESH
        )

    def start(self, src, dst, sems):
        @pl.when(self.moves)
        def _():
            self.far(src, dst, sems[0], sems[1]).start()

        @pl.when(jnp.logical_not(self.moves))
        def _():
            pltpu.make_async_copy(src, dst, sems[2]).start()

    def wait(self, src, dst, sems):
        @pl.when(self.moves)
        def _():
            self.far(src, dst, sems[0], sems[1]).wait_recv()

        @pl.when(jnp.logical_not(self.moves))
        def _():
            pltpu.make_async_copy(src, dst, sems[2]).wait()

    def drain(self, src, dst, sems):
        @pl.when(self.moves)
        def _():
            self.far(src, dst, sems[0], sems[1]).wait_send()


PIECES = 2


class RowMove:
    def __init__(self, swap, ny, part, e_ref, w_ref, ws, wr, wl, ys, yr):
        self.swap, self.ny, self.part, self.size = swap, ny, part, part // PIECES
        self.e, self.w = e_ref, w_ref
        self.ws, self.wr, self.wl, self.ys, self.yr = ws, wr, wl, ys, yr
        self.y = lax.axis_index("y")

    def rows(self, y, p):
        return pl.ds(pl.multiple_of(y * self.part + p * self.size, 16), self.size)

    def far(self, p):
        mine = self.rows(self.y, p)
        return self.swap.far(self.e.at[mine], self.w.at[mine], self.ws.at[p], self.wr.at[p])

    def near(self):
        every = pl.ds(0, self.part * self.ny)
        return pltpu.make_async_copy(self.e.at[every], self.w.at[every], self.wl)

    def shared(self, k, p, y):
        where = self.rows(y, p)
        return pltpu.make_async_remote_copy(
            src_ref=self.w.at[where], dst_ref=self.w.at[where],
            send_sem=self.ys.at[k - 1, p], recv_sem=self.yr.at[k - 1, p],
            device_id={"y": lax.rem(self.y + k, self.ny)}, device_id_type=MESH,
        )

    def start(self):
        @pl.when(self.swap.moves)
        def _():
            for p in range(PIECES):
                self.far(p).start()

        @pl.when(jnp.logical_not(self.swap.moves))
        def _():
            self.near().start()

    def pass_on(self):
        @pl.when(self.swap.moves)
        def _():
            for p in range(PIECES):
                self.far(p).wait_recv()
                for k in range(1, self.ny):
                    self.shared(k, p, self.y).start()

    def wait(self):
        @pl.when(self.swap.moves)
        def _():
            for k in range(1, self.ny):
                for p in range(PIECES):
                    self.shared(k, p, lax.rem(self.y + self.ny - k, self.ny)).wait_recv()

        @pl.when(jnp.logical_not(self.swap.moves))
        def _():
            self.near().wait()

    def drain(self):
        @pl.when(self.swap.moves)
        def _():
            for p in range(PIECES):
                self.far(p).wait_send()
                for k in range(1, self.ny):
                    self.shared(k, p, self.y).wait_send()


def row_move_scratch(ny):
    dma = pltpu.SemaphoreType.DMA
    between = dma((max(ny - 1, 1), PIECES))
    return [dma((PIECES,)), dma((PIECES,)), dma, between, between]


class Spread:
    def __init__(self, cm, ny, e_ref, w_ref, hs, hr, ps, pr, pn, ys, yr):
        self.cm, self.ny, self.e, self.w = cm, ny, e_ref, w_ref
        self.hs, self.hr, self.ps, self.pr, self.pn, self.ys, self.yr = hs, hr, ps, pr, pn, ys, yr
        self.y, self.h = lax.axis_index("y"), lax.axis_index("h")
        self.part = cm.fw // ny

    def place(self, hh, gg, yy):
        return self.w.at[
            pl.ds(pl.multiple_of((hh * self.cm.nl + gg) * self.cm.fw + yy * self.part, self.part), self.part)
        ]

    def piece(self, m):
        cm, to = self.cm, self.cm.after(m)
        return cm.copy(
            self.e.at[to], self.place(self.h, cm.g, self.y), self.ps.at[m], self.pr.at[m], cm.c, to
        )

    def here(self):
        return pltpu.make_async_copy(
            self.e.at[self.cm.g], self.place(self.h, self.cm.g, self.y), self.pn
        )

    def crossed(self, m, hh):
        where = self.place(hh, self.cm.before(m), self.y)
        return pltpu.make_async_remote_copy(
            src_ref=where, dst_ref=where, send_sem=self.hs.at[m], recv_sem=self.hr.at[m],
            device_id={"h": 1 - self.h}, device_id_type=MESH,
        )

    def shared(self, side, m, k, yy):
        where = self.place(self.h if side == 0 else 1 - self.h, self.cm.before(m), yy)
        return pltpu.make_async_remote_copy(
            src_ref=where, dst_ref=where,
            send_sem=self.ys.at[side, m, k - 1], recv_sem=self.yr.at[side, m, k - 1],
            device_id={"y": lax.rem(self.y + k, self.ny)}, device_id_type=MESH,
        )

    def start(self, steps):
        for m in steps:
            if m == 0:
                self.here().start()
            else:
                self.piece(m).start()

    def own(self, m):
        if m == 0:
            self.here().wait()
        else:
            self.piece(m).wait_recv()

    def start_crossing(self, m):
        self.crossed(m, self.h).start()

    def wait_crossing(self, m):
        self.crossed(m, 1 - self.h).wait_recv()

    def share(self, side, m):
        for k in range(1, self.ny):
            self.shared(side, m, k, self.y).start()

    def pass_own(self, m, cross=True):
        self.own(m)
        if cross:
            self.start_crossing(m)
        self.share(0, m)

    def pass_crossed(self, m, following=None):
        self.wait_crossing(m)
        if following is not None and following < self.cm.nl:
            self.start_crossing(following)
        self.share(1, m)

    def wait(self, side, steps):
        for m in steps:
            for k in range(1, self.ny):
                self.shared(side, m, k, lax.rem(self.y + self.ny - k, self.ny)).wait_recv()

    def drain_own(self, steps):
        for m in steps:
            if m > 0:
                self.piece(m).wait_send()

    def drain_crossing(self, steps):
        for m in steps:
            self.crossed(m, self.h).wait_send()

    def drain_shared(self, side, steps):
        for m in steps:
            for k in range(1, self.ny):
                self.shared(side, m, k, self.y).wait_send()


def spread_scratch(ny, nl):
    dma = pltpu.SemaphoreType.DMA
    return [
        dma((nl,)),
        dma((nl,)),
        dma((nl,)),
        dma((nl,)),
        dma,
        dma((2, nl, max(ny - 1, 1))),
        dma((2, nl, max(ny - 1, 1))),
    ]


def movers(ny):
    y, h = lax.axis_index("y"), lax.axis_index("h")
    return [{"y": lax.rem(y + k, ny)} for k in range(1, ny)] + [{"h": 1 - h}]


def ag_scratch(nl, nc, t, d):
    return [
        pltpu.VMEM((t, d), BF16),
        pltpu.SemaphoreType.DMA((nc,)),
        pltpu.SemaphoreType.DMA((nc, nl)),
        pltpu.SemaphoreType.DMA((nc, nl)),
        pltpu.SemaphoreType.DMA((nc, nl)),
        pltpu.SemaphoreType.DMA((nc, nl)),
    ]


def rs_scratch(nl, nc, tc, fw):
    return [
        pltpu.VMEM((nc, 2, nl, tc, fw), BF16),
        pltpu.VMEM((nc, nl, tc, fw), BF16),
        pltpu.VMEM((nc, nl - 1, tc, fw), BF16),
        pltpu.SemaphoreType.DMA((nc,)),
        pltpu.SemaphoreType.DMA((nc,)),
        pltpu.SemaphoreType.DMA((nc, nl)),
        pltpu.SemaphoreType.DMA((nc, nl)),
    ]


def st_scratch(nl, nc, t):
    return [
        pltpu.VMEM((2 * nl, nc, 1, t // nc), F32),
        pltpu.SemaphoreType.DMA((nc, 2 * nl)),
        pltpu.SemaphoreType.DMA((nc, 2 * nl)),
    ]


def cs_scratch(nl, d, fw):
    return [
        pltpu.VMEM((8, d), F32),
        pltpu.VMEM((2 * nl * 8, fw), F32),
        pltpu.SemaphoreType.DMA((2 * nl,)),
        pltpu.SemaphoreType.DMA((2 * nl,)),
    ]


VM = pl.BlockSpec(memory_space=pltpu.VMEM)
SM = pl.BlockSpec(memory_space=pltpu.SMEM)
ANY = pl.BlockSpec(memory_space=pl.ANY)


class Background:
    def __init__(self, loads, stores, step):
        self.loads, self.stores, self.step = loads, stores, step
        for copy in loads:
            copy.start()

    def ready(self):
        for copy in self.loads:
            copy.wait()

    def copy(self, k, i):
        held, out, sems = self.stores[k]
        rows = pl.ds(pl.multiple_of(i * self.step, self.step), self.step)
        return pltpu.make_async_copy(held.at[rows], out.at[rows], sems.at[i])

    def store(self, i, *which):
        for k in which:
            self.copy(k, i).start()

    def stored(self, i):
        for k in self.stores:
            self.copy(k, i).wait()


def call(kernel, name, outs, in_specs, out_specs, scratch, collective, us, args, late=(), flow=(), step=1, aliases=None):
    extra = {}
    if collective is not None:
        extra = {"collective_id": collective, "has_side_effects": True}
    single = not isinstance(outs, tuple)
    results = (outs,) if single else outs
    in_specs, out_specs = list(in_specs), [out_specs] if single else list(out_specs)
    n_in, n_out, n_scratch = len(args), len(results), len(scratch)
    dma = pltpu.SemaphoreType.DMA
    more = []
    for k in late:
        in_specs[k] = ANY
        more += [pltpu.VMEM(args[k].shape, args[k].dtype), dma]
    for k in flow:
        out_specs[k] = ANY
        more += [pltpu.VMEM(results[k].shape, results[k].dtype), dma((results[k].shape[0] // step,))]

    def whole(*refs):
        ins, results_here = list(refs[:n_in]), list(refs[n_in : n_in + n_out])
        own = refs[n_in + n_out : n_in + n_out + n_scratch]
        extras = list(refs[n_in + n_out + n_scratch :])
        loads, stores = [], {}
        for k in late:
            held, sem = extras.pop(0), extras.pop(0)
            loads.append(pltpu.make_async_copy(ins[k], held, sem))
            ins[k] = held
        for k in flow:
            held, sems = extras.pop(0), extras.pop(0)
            stores[k] = (held, results_here[k], sems)
            results_here[k] = held
        kernel(Background(loads, stores, step), *ins, *results_here, *own)

    return pl.pallas_call(
        whole,
        name=name,
        out_shape=outs,
        in_specs=in_specs,
        out_specs=out_specs[0] if single else tuple(out_specs),
        scratch_shapes=scratch + more,
        input_output_aliases=aliases or {},
        compiler_params=pltpu.CompilerParams(vmem_limit_bytes=VMEM_LIMIT, **extra),
        cost_estimate=pl.CostEstimate(
            flops=int(us * 5e8), bytes_accessed=int(us * 3e6), transcendentals=0
        ),
    )(*args)


def shape(s, dtype):
    return jax.ShapeDtypeStruct(s, dtype)


def ones_rows(values):
    folded = values[:, :LANES]
    for k in range(1, values.shape[1] // LANES):
        folded = folded + values[:, k * LANES : (k + 1) * LANES]
    return nt(jnp.ones((8, LANES), F32), folded, HIGHEST)


def row_sum(values):
    return jnp.sum(values, axis=0, keepdims=True)


def down_part(nf, ny):
    return -(-(-(-nf // ny)) // (16 * PIECES)) * 16 * PIECES


def merged_tile(frozen, down, up):
    down_high, up_high = down.astype(BF16), up.astype(BF16)
    down_low = (down - down_high.astype(F32)).astype(BF16)
    up_low = (up - up_high.astype(F32)).astype(BF16)
    low = nn(down_high, up_high) + (nn(down_high, up_low) + nn(down_low, up_high))
    return frozen.astype(F32) + SCALE * low


def qkv_forward(
    cfg, ny, npad, nf, x_in, w_qkv, a_qkv, b_qkv, tail_qkv, gains, w_out, small, small_gu, segments, turns,
    w_gu, a_gu, b_gu, tail_gu, w_down, a_down, b_down, a_out, b_out,
):
    t, fw, d, nl, nc, tc = cfg
    width = 3 * fw
    wide = width + LANES
    part = fw // ny
    down_rows = down_part(nf, ny) * ny
    ff_half = w_gu.shape[2] // 2

    def kernel(
        io, x_ref, wq_hbm, aq_ref, bq_ref, tq_ref, gain_ref, wout_ref, m_ref, mg_ref, seg_ref, ta_ref, tb_ref,
        wg_hbm, ag_ref, bg_ref, tg_ref, wdown_ref, ad_ref, bd_ref, ao_ref, bo_ref,
        xs_ref, w_ref, wo_ref, ms_ref, mgs_ref, sc_ref, sq_ref, qkv_ref, lora_ref, rate_ref, eg_ref, ed_ref, wgs_ref, out_ref, cos_ref, sin_ref, sgc_ref, sgr_ref,
        full, own, sd, rd, sc, rc, keep, xs_s, xs_r, xs_l, small_sems,
        hs, hr, ps, pr, pn, ys, yr, os, orr, ol, oys, oyr,
        e_ref, wq, wg, wload, eo_ref, sg, place, aq_t, ag_t, ao_t, ghs, ghr, gps, gpr, gpn, gys, gyr,
    ):
        cm = Comm(nl, nc, tc, fw, out_by_one=0.9375)
        cm.ag_refs(xs_ref, full, own, sd, rd, sc, rc)
        swap = Swap(cm)
        weights = Spread(cm, ny, e_ref, w_ref, hs, hr, ps, pr, pn, ys, yr)
        mine = pl.ds(pl.multiple_of(weights.y * part, part), part)
        load_q = pltpu.make_async_copy(
            wq_hbm.at[:, mine, pl.ds(pl.multiple_of(cm.c * (d // 2), LANES), d // 2)], wq, wload.at[0]
        )
        load_g = pltpu.make_async_copy(
            wg_hbm.at[:, mine, pl.ds(pl.multiple_of(cm.c * ff_half, LANES), ff_half)], wg, wload.at[1]
        )
        load_q.start()
        load_g.start()
        later = Spread(cm, ny, eg_ref, wgs_ref, ghs, ghr, gps, gpr, gpn, gys, gyr)
        output = RowMove(swap, ny, fw // ny, eo_ref, wo_ref, os, orr, ol, oys, oyr)
        cm.barrier(movers(ny), [swap.partner])

        def token_swap(i):
            rows = cm.rows(i)
            return x_ref.at[rows], xs_ref.at[rows], (xs_s.at[i], xs_r.at[i], xs_l.at[i])

        m_swap = (m_ref, ms_ref, tuple(small_sems.at[k] for k in range(3)))
        mg_swap = (mg_ref, mgs_ref, tuple(small_sems.at[k] for k in range(3, 6)))

        seg_swap = (seg_ref, sg, tuple(small_sems.at[k] for k in range(6, 9)))

        def start_swap(i, carry_on):
            swap.start(*token_swap(i))
            return carry_on

        lax.fori_loop(0, min(WINDOW, nc), start_swap, 0)
        swap.start(*m_swap)
        swap.start(*mg_swap)
        swap.start(*seg_swap)
        for k in range(3):
            aq_t[k] = aq_ref[k].T
        load_q.wait()
        gain_attn, gain_ffn = gain_ref[mine, 0:1], gain_ref[mine, 1:2]
        for gg in range(nl):
            columns = pl.ds(pl.multiple_of((cm.c * nl + gg) * fw, fw), fw)
            for k in range(3):
                tile = merged_tile(wq[k, :, gg * fw : (gg + 1) * fw], aq_t[k, mine, :], bq_ref[k, :, columns])
                e_ref[gg, :, k * fw : (k + 1) * fw] = (tile * gain_attn).astype(BF16)
            e_ref[gg, :, width:] = tq_ref[mine, :]
        weights.start(range(nl))

        def gate_up(gg):
            off = gg * nf % LANES
            window = -(-(off + nf) // LANES) * LANES
            for k in range(2):
                raw = wg[k, :, gg * nf - off : gg * nf - off + window].astype(F32)
                if off:
                    raw = pltpu.roll(raw, window - off, 1)
                tile = merged_tile(raw[:, :npad], ag_t[k, mine, :], bg_ref[k, cm.c * nl + gg]) * gain_ffn
                lane = lax.broadcasted_iota(jnp.int32, tile.shape, 1)
                eg_ref[gg, :, k * npad : (k + 1) * npad] = jnp.where(
                    lane < nf, tile, tg_ref[k, mine, :].astype(F32)
                ).astype(BF16)

        def merged_rows(k):
            if k == 0:
                if down_rows > nf:
                    ed_ref[nf:, :] = jnp.zeros((down_rows - nf, ed_ref.shape[1]), BF16)
                ed_ref[:nf, d:] = jnp.zeros((nf, LANES), BF16)
                ed_ref[:nf, d : d + RANK] = ad_ref[...].astype(BF16)
                eo_ref[:, d:] = jnp.zeros((fw, LANES), BF16)
                eo_ref[:, d : d + RANK] = ao_t[...].astype(BF16)
            for n in (2 * k, 2 * k + 1):
                at = slice(n * fw, (n + 1) * fw)
                eo_ref[:, at] = merged_tile(wout_ref[:, at], ao_t[...], bo_ref[:, at]).astype(BF16)
                ed_ref[:nf, at] = merged_tile(wdown_ref[:, at], ad_ref[...], bd_ref[:, at]).astype(BF16)

        def gather(i, carry_on):
            swap.wait(*token_swap(i))

            @pl.when(i + WINDOW < nc)
            def _():
                swap.start(*token_swap(i + WINDOW))

            cm.ag_send(i)
            return carry_on

        def forward(i, carry_on):
            cm.ag_step(i, more=False)
            return carry_on

        weights.pass_own(0)
        half = nc // 2
        lax.fori_loop(0, half, gather, 0)
        weights.pass_own(1)
        lax.fori_loop(half, nc, gather, 0)
        for m in range(2, nl):
            weights.pass_own(m, cross=False)
        load_g.wait()
        io.ready()
        for k in range(2):
            ag_t[k] = ag_ref[k].T
        ao_t[...] = ao_ref[...].T
        for m in range(nl):
            lax.fori_loop(nc * m // nl, nc * (m + 1) // nl, forward, 0)
            gate_up(m)
            weights.pass_crossed(m, m + 2)
            merged_rows(m)
        output.start()
        later.start(range(EARLY + 1))
        for m in range(EARLY):
            later.own(m)
            later.start_crossing(m)
        cm.ag_step(jnp.int32(nc), more=False)

        def stored(i):
            rows = cm.rows(i)
            return pltpu.make_async_copy(full.at[rows], out_ref.at[rows], keep.at[i])

        swap.wait(*seg_swap)
        number = sg[...]
        begin = jnp.zeros((1, t), F32)
        for n in range(1, SEGMENTS):
            before = jnp.sum(jnp.where(number < n, 1.0, 0.0), axis=1, keepdims=True)
            begin = jnp.where(number == n, before, begin)
        standing = lax.broadcasted_iota(jnp.int32, (1, t), 1).astype(F32) - begin
        high = jnp.floor(standing * (1.0 / 32.0))
        place[0:1, :] = high.astype(jnp.int32)
        place[1:2, :] = (standing - 32.0 * high).astype(jnp.int32)
        sgr_ref[...] = jnp.broadcast_to(number, (8, t))

        def turn_tables(rows):
            def chosen(row, count):
                return jnp.where(lax.broadcasted_iota(jnp.int32, (count, tc), 0) == row, 1.0, 0.0)

            def looked_up(row, table):
                parts = tn(chosen(row, 32).astype(BF16), table)
                both = parts[:, : 2 * HD] + parts[:, 2 * HD :]
                return both[:, :HD], both[:, HD:]

            ca, sa = looked_up(place[0:1, rows], ta_ref[...])
            cb, sb = looked_up(place[1:2, rows], tb_ref[...])
            sign = jnp.where(lax.broadcasted_iota(jnp.int32, (tc, HD), 1) < HD // 2, -1.0, 1.0)
            cos_ref[rows, :] = ca * cb - sa * sb
            sin_ref[rows, :] = (sa * cb + ca * sb) * sign
            numbers = lax.broadcasted_iota(jnp.int32, (SEGMENTS, LANES), 0).astype(F32)
            sgc_ref[rows, :] = tn(chosen(sgr_ref[0:1, rows], SEGMENTS), numbers).astype(jnp.int32)

        def rates(i, carry_on):
            turn_tables(cm.rows(i))
            cm.ag_wait(i)
            stored(i).start()
            wide_block = full[cm.rows(i), :].astype(F32)
            rate = lax.rsqrt(jnp.sum(wide_block * wide_block, axis=1, keepdims=True) / d + EPS)
            rate_ref[cm.rows(i), :] = jnp.broadcast_to(rate, (tc, LANES))
            return carry_on

        lax.fori_loop(0, nc, rates, 0)
        for side in (0, 1):
            weights.wait(side, range(nl))

        def squares(i, total):
            rows = pl.ds(pl.multiple_of(i * fw, fw), fw)
            tail = w_ref[rows, width:].astype(F32)
            gain = tail[:, 3 * RANK : 3 * RANK + 1] + tail[:, 3 * RANK + 1 : 3 * RANK + 2]
            value = w_ref[rows, :width].astype(F32) * (1.0 / gain)
            return total + row_sum(value * value)

        square = lax.fori_loop(0, 2 * nl, squares, jnp.zeros((1, width), F32))
        swap.wait(*m_swap)
        sq_ref[...] = jnp.broadcast_to(square, (8, width))
        for k in range(3):
            at = slice(k * fw, (k + 1) * fw)
            sc_ref[:, at] = jnp.broadcast_to(ms_ref[k : k + 1, :] * lax.rsqrt(square[:, at]), (8, fw))
        sc_ref[:, width:] = jnp.ones((8, LANES), F32)

        big = 2 * tc if nc % 2 == 0 else tc

        def body(i, carry_on):
            rows = pl.ds(pl.multiple_of(i * big, big), big)
            out = nn(full[rows, :], w_ref[...]) * rate_ref[rows, 0:1] * sc_ref[0:1, :]
            cosine_here, sine_here = cos_ref[rows, :], sin_ref[rows, :]
            for k in range(3):
                for hd in range(fw // HD):
                    at = k * fw + hd * HD
                    value = out[:, at : at + HD]
                    if k < 2:
                        value = value * cosine_here + pltpu.roll(value, HD // 2, 1) * sine_here
                    qkv_ref[rows, at : at + HD] = value.astype(BF16)
            lora_ref[rows, :] = out[:, width:].astype(BF16)
            for k in range(big // tc):
                io.store(i * (big // tc) + k, 7, 8, 9, 14, 15, 16)
            return carry_on

        lax.fori_loop(0, t // big, body, 0)
        output.pass_on()
        for m in range(EARLY):
            later.wait_crossing(m)
        later.own(EARLY)
        output.wait()
        swap.wait(*mg_swap)

        def drain(i, carry_on):
            cm.ag_drain(i)
            stored(i).wait()
            io.stored(i)
            swap.drain(*token_swap(i))
            return carry_on

        lax.fori_loop(0, nc, drain, 0)
        swap.drain(*m_swap)
        swap.drain(*mg_swap)
        swap.drain(*seg_swap)
        weights.drain_own(range(nl))
        weights.drain_crossing(range(nl))
        for side in (0, 1):
            weights.drain_shared(side, range(nl))
        later.drain_own(range(EARLY + 1))
        later.drain_crossing(range(EARLY))
        output.drain()

    dma = pltpu.SemaphoreType.DMA
    return call(
        kernel,
        "qkv_forward",
        (
            shape((t, fw), BF16),
            shape((d, wide), BF16),
            shape((fw, d + LANES), BF16),
            shape(small.shape, F32),
            shape(small_gu.shape, F32),
            shape((8, wide), F32),
            shape((8, width), F32),
            shape((t, width), BF16),
            shape((t, LANES), BF16),
            shape((t, LANES), F32),
            shape((nl, part, 2 * npad), BF16),
            shape((down_rows, d + LANES), BF16),
            shape((d, 2 * npad), BF16),
            shape((t, d), BF16),
            shape((t, HD), F32),
            shape((t, HD), F32),
            shape((t, LANES), jnp.int32),
            shape((8, t), jnp.int32),
        ),
        [VM, ANY] + [VM] * 10 + [ANY] + [VM] * 8,
        (VM,) * 12 + (ANY, ANY) + (VM,) * 4,
        ag_scratch(nl, nc, t, d)
        + [dma((nc,))] * 4
        + [dma((9,))]
        + spread_scratch(ny, nl)
        + row_move_scratch(ny)
        + [
            pltpu.VMEM((nl, part, wide), BF16),
            pltpu.VMEM((3, part, d // 2), BF16),
            pltpu.VMEM((2, part, ff_half), BF16),
            dma((2,)),
            pltpu.VMEM((fw, d + LANES), BF16),
            pltpu.VMEM((1, t), jnp.int32),
            pltpu.VMEM((8, t), jnp.int32),
            pltpu.VMEM((3, fw, RANK), F32),
            pltpu.VMEM((2, fw, RANK), F32),
            pltpu.VMEM((fw, RANK), F32),
        ]
        + spread_scratch(ny, nl),
        1,
        90,
        (
            x_in, w_qkv, a_qkv, b_qkv, tail_qkv, gains, w_out, small, small_gu, segments, *turns,
            w_gu, a_gu, b_gu, tail_gu, w_down, a_down, b_down, a_out, b_out,
        ),
        late=(6, 10, 11, *range(13, 21)),
        flow=(7, 8, 9, 14, 15, 16),
        step=tc,
    )


def allowed_of(key_segment, query_segment, j, i, block):
    key_at = j * block + lax.broadcasted_iota(jnp.int32, (block, block), 0)
    query_at = i * block + lax.broadcasted_iota(jnp.int32, (block, block), 1)
    return (key_segment == query_segment) & (key_at <= query_at)


def attention_forward(cfg, qkv, seg_column, seg_row, first_block, block):
    t, fw = cfg[0], cfg[1]
    heads = fw // HD

    def kernel(io, qkv_ref, sc_ref, sr_ref, first_ref, out_ref, lse_ref):
        def at(i):
            return pl.ds(pl.multiple_of(i * block, block), block)

        def columns(k, hd):
            return slice(k * fw + hd * HD, k * fw + (hd + 1) * HD)

        def one_query(i, carry_on):
            queries = [qkv_ref[at(i), columns(0, hd)] for hd in range(heads)]
            query_segment = sr_ref[0:1, at(i)]

            def one_key(j, carry):
                allowed = allowed_of(sc_ref[at(j), 0:1], query_segment, j, i, block)
                out = []
                for hd in range(heads):
                    top, total, acc = carry[hd]
                    s = nt(qkv_ref[at(j), columns(1, hd)], queries[hd]) * (HD**-0.5)
                    s = jnp.where(allowed, s, MASKED)
                    new = jnp.maximum(top, jnp.max(s, axis=0, keepdims=True))
                    p = jnp.exp(s - new)
                    shrink = jnp.exp(top - new)
                    total = total * shrink + jnp.sum(p, axis=0, keepdims=True)
                    acc = acc * shrink + tn(qkv_ref[at(j), columns(2, hd)], p.astype(BF16))
                    out.append((new, total, acc))
                return tuple(out)

            first = (
                jnp.full((1, block), MASKED, F32),
                jnp.zeros((1, block), F32),
                jnp.zeros((HD, block), F32),
            )
            out = lax.fori_loop(first_ref[i], i + 1, one_key, (first,) * heads)
            for hd in range(heads):
                top, total, acc = out[hd]
                out_ref[at(i), hd * HD : (hd + 1) * HD] = (acc / total).T.astype(BF16)
                lse_ref[hd * 8 : hd * 8 + 8, at(i)] = jnp.broadcast_to(
                    top + jnp.log(total), (8, block)
                )
            return carry_on

        lax.fori_loop(0, t // block, one_query, 0)

    return call(
        kernel,
        "attention_forward",
        (shape((t, fw), BF16), shape((heads * 8, t), F32)),
        [VM, VM, VM, SM],
        (VM, VM),
        [],
        None,
        15,
        (qkv, seg_column, seg_row, first_block),
    )


def out_forward(cfg, ny, npad, attended, weights, x, magnitude, w_gu, blocks, rows_down):
    t, fw, d, nl, nc, tc = cfg
    part = rows_down.shape[0] // ny

    def kernel(
        io, a_ref, w_ref, x_ref, m_ref, w_in, e_ref, ed_ref,
        mid_ref, u_ref, st_ref, sc_ref, sq_ref, lora_ref, wg_ref, wd_ref,
        sb, cb, gb, s1, r1, s2, r2, cpart, cheld, css, csr,
        hs, hr, ps, pr, pn, ys, yr, dws, dwr, dwl, dys, dyr,
    ):
        cm = Comm(nl, nc, tc, fw, back_by_two=0.0625)
        cm.rs_refs(sb, cb, gb, s1, r1, s2, r2)
        cm.cs_refs(cpart, cheld, css, csr)
        columns = Spread(cm, ny, e_ref, wg_ref, hs, hr, ps, pr, pn, ys, yr)
        swap = Swap(cm)
        down_rows = RowMove(swap, ny, part, ed_ref, wd_ref, dws, dwr, dwl, dys, dyr)
        cm.barrier(movers(ny), [swap.partner])
        down_rows.start()
        columns.start_crossing(EARLY)
        columns.start(range(EARLY + 1, nl))
        for m in range(EARLY):
            columns.share(0, m)
            columns.share(1, m)
        columns.share(0, EARLY)
        cm.cs_start(w_ref)
        if part * ny < npad:
            wd_ref[part * ny :, :] = jnp.zeros((npad - part * ny, wd_ref.shape[1]), BF16)
        def body(i, carry_on):
            @pl.when(i < nc)
            def _():
                block = a_ref[cm.rows(i), :]
                for role in range(2 * nl):
                    sb[i, role // nl, role % nl] = nn(
                        block, w_ref[:, role * fw : (role + 1) * fw]
                    ).astype(BF16)
                cm.rs_across(i).start()
                lora_ref[cm.rows(i), :] = nn(block, w_ref[:, d:]).astype(BF16)
                io.store(i, 5)

            cm.rs_steps(i)

            @pl.when(i == 3)
            def _():
                total = cm.cs_total()
                sq_ref[...] = jnp.broadcast_to(total, (8, fw))
                sc_ref[...] = jnp.broadcast_to(m_ref[3:4, :] * lax.rsqrt(total), (8, fw))

            @pl.when(i == 5)
            def _():
                down_rows.pass_on()

            @pl.when(i == 1)
            def _():
                columns.pass_own(EARLY + 1)

            @pl.when(i == 3)
            def _():
                for m in range(EARLY + 2, nl):
                    columns.pass_own(m, cross=False)

            @pl.when(i == min(6, nc + 2))
            def _():
                columns.pass_crossed(EARLY, EARLY + 2)

            @pl.when((i >= 3) & (i <= nc + 2))
            def _():
                rows = cm.rows(i - 3)
                middle = x_ref[rows, :].astype(F32) + cm.rs_total(i - 3) * sc_ref[0:1, :]
                mid_ref[rows, :] = middle
                u_ref[rows, :] = middle.astype(BF16)
                st_ref[i - 3] = ones_rows(middle * middle)[0:1, :]
                io.store(i - 3, 0, 1)

            return carry_on

        lax.fori_loop(0, nc + 3, body, 0)

        def drain(i, carry_on):
            cm.rs_drain(i)
            io.stored(i)
            return carry_on

        for m in range(EARLY + 1, nl):
            columns.pass_crossed(m, m + 2)
        for side in (0, 1):
            columns.wait(side, range(nl))
        down_rows.wait()
        lax.fori_loop(0, nc, drain, 0)
        cm.cs_drain()
        columns.drain_own(range(EARLY + 1, nl))
        columns.drain_crossing(range(EARLY, nl))
        for side in (0, 1):
            columns.drain_shared(side, range(nl))
        down_rows.drain()

    return call(
        kernel,
        "out_forward",
        (
            shape((t, fw), F32),
            shape((t, fw), BF16),
            shape((nc, 1, tc), F32),
            shape((8, fw), F32),
            shape((8, fw), F32),
            shape((t, LANES), BF16),
            shape(w_gu.shape, BF16),
            shape((npad, d + LANES), BF16),
        ),
        [VM] * 4 + [ANY, ANY, ANY],
        (VM,) * 6 + (ANY, VM),
        rs_scratch(nl, nc, tc, fw)
        + cs_scratch(nl, d, fw)
        + spread_scratch(ny, nl)
        + row_move_scratch(ny),
        2,
        90,
        (attended, weights, x, magnitude, w_gu, blocks, rows_down),
        flow=(0, 1, 5),
        step=tc,
        aliases={4: 6},
    )


def ffn_forward(cfg, npad, nf, u, stats, w_gu, m_gu, w_down, small, middle, cotangent):
    t, fw, d, nl, nc, tc = cfg

    def kernel(
        io, u_ref, st_ref, wg_ref, mg_ref, wd_ref, m_ref, mid_ref, cin_ref,
        gu_ref, hid_ref, out_ref, gm_ref, rate_ref, gp_ref, sg_ref, qg_ref, sd_ref, qd_ref, lora_ref, cot_ref, am_ref, ad_ref, uf_ref,
        full, own, sd, rd, sc, rc, sb, cb, gb, s1, r1, s2, r2, sa, ss, sr, cpart, cheld, css, csr, keep,
        cs_s, cs_r, cs_l,
    ):
        cm = Comm(nl, nc, tc, fw, out_by_one=0.5, back_by_two=0.5)
        cm.ag_refs(u_ref, full, own, sd, rd, sc, rc)
        cm.rs_refs(sb, cb, gb, s1, r1, s2, r2)
        cm.st_refs(st_ref, sa, ss, sr)
        cm.cs_refs(cpart, cheld, css, csr)
        swap = Swap(cm)
        cm.barrier((), [swap.partner])

        def cot_swap(i):
            rows = cm.rows(i)
            return cin_ref.at[rows], cot_ref.at[rows], (cs_s.at[i], cs_r.at[i], cs_l.at[i])

        cm.st_send(None)
        cm.ag_start()
        io.ready()

        def cot_out(i, carry_on):
            swap.start(*cot_swap(i))
            return carry_on


        def squares(i, total):
            rows = pl.ds(pl.multiple_of(i * fw, fw), fw)
            gain = (
                wg_ref[rows, nf + RANK : nf + RANK + 1].astype(F32)
                + wg_ref[rows, nf + RANK + 1 : nf + RANK + 2].astype(F32)
            )
            value = wg_ref[rows, :].astype(F32) * (1.0 / gain)
            return total + row_sum(value * value)

        square = lax.fori_loop(0, 2 * nl, squares, jnp.zeros((1, 2 * npad), F32))
        column = lax.rem(lax.broadcasted_iota(jnp.int32, (1, 2 * npad), 1), npad)
        square = jnp.where(column < nf, square, 1.0)
        qg_ref[...] = jnp.broadcast_to(square, (8, 2 * npad))
        sg_ref[...] = jnp.broadcast_to(mg_ref[...] * lax.rsqrt(square), (8, 2 * npad))
        cm.ag_ahead()
        gm_ref[...] = jnp.zeros_like(gm_ref)

        def stored(i):
            rows = cm.rows(i)
            return pltpu.make_async_copy(full.at[rows], uf_ref.at[rows], keep.at[i])

        cm.cs_start(wd_ref)
        lax.fori_loop(0, nc, cot_out, 0)

        def body(i, carry_on):
            @pl.when(i < nc)
            def _():
                cm.ag_step(i + 2)
                cm.ag_wait(i)

                @pl.when(i == 0)
                def _():
                    cm.st_wait(None)

                stored(i).start()
                rows = cm.rows(i)
                rate = lax.rsqrt(cm.st_sum(i) / d + EPS)
                rate_ref[rows, :] = jnp.broadcast_to(rate, (tc, LANES))
                out = nn(full[rows, :], wg_ref[...]) * rate * sg_ref[0:1, :]
                gu_ref[rows, :] = out.astype(BF16)
                gate, up = out[:, :npad], out[:, npad:]
                hidden = (gate / (1.0 + jnp.exp(-gate)) * up).astype(BF16)
                hid_ref[rows, :] = hidden
                for role in range(2 * nl):
                    sb[i, role // nl, role % nl] = nn(
                        hidden, wd_ref[:, role * fw : (role + 1) * fw]
                    ).astype(BF16)
                cm.rs_across(i).start()
                lora_ref[rows, :] = nn(hidden, wd_ref[:, d:]).astype(BF16)
                io.store(i, 0, 1, 4, 10)

            @pl.when(i == nc)
            def _():
                off = nf - (npad - LANES)
                for k in range(2):
                    tail = wg_ref[:, (k + 1) * npad - LANES : (k + 1) * npad]
                    _, gain = gain_rows(tail, off + RANK)
                    factor = (tail.astype(F32) / (gain * gain)).astype(BF16)
                    product = tn(factor, wg_ref[:, k * npad : (k + 1) * npad])
                    am_ref[k * RANK : (k + 1) * RANK, :] = product[off : off + RANK, :]
                ad_ref[...] = tn(wd_ref[:, d:], wd_ref[:, :d])[:RANK, :]

            cm.rs_steps(i)

            @pl.when(i == 3)
            def _():
                total = cm.cs_total()
                qd_ref[...] = jnp.broadcast_to(total, (8, fw))
                sd_ref[...] = jnp.broadcast_to(m_ref[4:5, :] * lax.rsqrt(total), (8, fw))

            @pl.when(i >= 3)
            def _():
                rows = cm.rows(i - 3)
                down = cm.rs_total(i - 3) * sd_ref[0:1, :]
                out_ref[rows, :] = (mid_ref[rows, :] + down).astype(BF16)
                swap.wait(*cot_swap(i - 3))
                seed = cot_ref[rows, :].astype(F32)
                gm_ref[0:1, :] += row_sum(seed * down)
                gp_ref[rows, :] = (seed * sd_ref[0:1, :]).astype(BF16)
                io.store(i - 3, 2, 5)

            return carry_on

        lax.fori_loop(0, nc + 3, body, 0)

        def drain(i, carry_on):
            cm.ag_drain(i)
            cm.rs_drain(i)
            stored(i).wait()
            io.stored(i)
            swap.drain(*cot_swap(i))
            return carry_on

        lax.fori_loop(0, nc, drain, 0)
        cm.st_drain(None)
        cm.cs_drain()

    dma = pltpu.SemaphoreType.DMA
    return call(
        kernel,
        "ffn_forward",
        (
            shape((t, 2 * npad), BF16),
            shape((t, npad), BF16),
            shape((t, fw), BF16),
            shape((8, fw), F32),
            shape((t, LANES), F32),
            shape((t, fw), BF16),
            shape((8, 2 * npad), F32),
            shape((8, 2 * npad), F32),
            shape((8, fw), F32),
            shape((8, fw), F32),
            shape((t, LANES), BF16),
            shape((t, fw), BF16),
            shape((2 * RANK, npad), F32),
            shape((RANK, d), F32),
            shape((t, d), BF16),
        ),
        [VM] * 8,
        (VM,) * 14 + (ANY,),
        ag_scratch(nl, nc, t, d)
        + rs_scratch(nl, nc, tc, fw)
        + st_scratch(nl, nc, t)
        + cs_scratch(nl, d, fw)
        + [dma((nc,))] * 4,
        3,
        110,
        (u, stats, w_gu, m_gu, w_down, small, middle, cotangent),
        late=(2, 4, 6),
        flow=(0, 1, 2, 4, 5, 10),
        step=tc,
    )


def ffn_backward(cfg, npad, gp, gu, w_gu, sc_gu, b_gu, w_down, b_down, rate, cotangent, middle, x, sc_out):
    t, fw, d, nl, nc, tc = cfg

    def kernel(
        io, gp_ref, gu_hbm, wg_ref, sg_ref, bg_ref, wd_ref, bd_ref, rate_ref, cot_ref, mid_ref, x_ref, so_ref,
        dm_ref, go_ref, gmo_ref, gm_ref, lg_ref, ld_ref, dp_hbm, gf_ref,
        full, own, sd, rd, sc, rc, sb, cb, gb, s1, r1, s2, r2, sa, ss, sr, st, gu_s, keep, load, save,
    ):
        cm = Comm(nl, nc, tc, fw)
        cm.ag_refs(gp_ref, full, own, sd, rd, sc, rc)
        cm.rs_refs(sb, cb, gb, s1, r1, s2, r2)
        cm.st_refs(st, sa, ss, sr)

        def loaded(i):
            rows = cm.rows(i)
            return pltpu.make_async_copy(gu_hbm.at[rows], gu_s.at[rows], load.at[i])

        def saved(i):
            rows = cm.rows(i)
            return pltpu.make_async_copy(gu_s.at[rows], dp_hbm.at[rows], save.at[i])

        def stored(i):
            rows = cm.rows(i)
            return pltpu.make_async_copy(full.at[rows], gf_ref.at[rows], keep.at[i])

        cm.barrier()
        cm.ag_start()

        def start_loads(i, carry_on):
            loaded(i).start()
            return carry_on

        lax.fori_loop(0, nc, start_loads, 0)
        cm.ag_ahead()
        io.ready()
        gm_ref[...] = jnp.zeros_like(gm_ref)
        gmo_ref[...] = jnp.zeros_like(gmo_ref)

        def body(i, carry_on):
            @pl.when(i < nc)
            def _():
                cm.ag_step(i + 2)
                cm.ag_wait(i)
                stored(i).start()
                loaded(i).wait()
                rows = cm.rows(i)
                block = full[rows, :]
                dh = nt(block, wd_ref[:, :d])
                ld_ref[rows, :] = nt(block, bd_ref[...]).astype(BF16)
                gate = gu_s[rows, :npad].astype(F32)
                up = gu_s[rows, npad:].astype(F32)
                sig = 1.0 / (1.0 + jnp.exp(-gate))
                dgate = dh * up * (sig * (1.0 + gate * (1.0 - sig)))
                dup = dh * (gate * sig)
                pg, pu = dgate * gate, dup * up
                gm_ref[0:1, :npad] += jnp.sum(pg, axis=0, keepdims=True)
                gm_ref[0:1, npad:] += jnp.sum(pu, axis=0, keepdims=True)
                st[i] = ones_rows(pg + pu)[0:1, :]
                cm.st_send(i)
                gu_s[rows, :npad] = (dgate * sg_ref[0:1, :npad]).astype(BF16)
                gu_s[rows, npad:] = (dup * sg_ref[0:1, npad:]).astype(BF16)
                saved(i).start()
                dp = gu_s[rows, :]
                lg_ref[rows, :] = (nt(dp, bg_ref[...].astype(BF16)) * rate_ref[rows, :]).astype(BF16)
                io.store(i, 4, 5)
                for role in range(2 * nl):
                    sb[i, role // nl, role % nl] = nt(
                        dp, wg_ref[role * fw : (role + 1) * fw, :]
                    ).astype(BF16)
                cm.rs_across(i).start()

            cm.rs_steps(i)

            @pl.when(i >= 3)
            def _():
                k = i - 3
                rows = cm.rows(k)
                cm.st_wait(k)
                r = rate_ref[rows, 0:1]
                inner = cm.st_sum(k)
                mid = mid_ref[rows, :]
                dm = (
                    cot_ref[rows, :].astype(F32)
                    + r * cm.rs_total(k)
                    - mid * (r * r * inner / d)
                )
                dm_ref[rows, :] = dm
                go_ref[rows, :] = (dm * so_ref[0:1, :]).astype(BF16)
                io.store(k, 0, 1)
                gmo_ref[0:1, :] += jnp.sum(
                    dm * (mid - x_ref[rows, :].astype(F32)), axis=0, keepdims=True
                )

            return carry_on

        lax.fori_loop(0, nc + 3, body, 0)

        def drain(i, carry_on):
            cm.ag_drain(i)
            cm.rs_drain(i)
            cm.st_drain(i)
            stored(i).wait()
            saved(i).wait()
            io.stored(i)
            return carry_on

        lax.fori_loop(0, nc, drain, 0)

    return call(
        kernel,
        "ffn_backward",
        (
            shape((t, fw), F32),
            shape((t, fw), BF16),
            shape((8, fw), F32),
            shape((8, 2 * npad), F32),
            shape((t, LANES), BF16),
            shape((t, LANES), BF16),
            shape((t, 2 * npad), BF16),
            shape((t, d), BF16),
        ),
        [VM, ANY] + [VM] * 10,
        (VM,) * 6 + (ANY, ANY),
        ag_scratch(nl, nc, t, d)
        + rs_scratch(nl, nc, tc, fw)
        + st_scratch(nl, nc, t)
        + [
            pltpu.VMEM((nc, 1, tc), F32),
            pltpu.VMEM((t, 2 * npad), BF16),
            pltpu.SemaphoreType.DMA((nc,)),
            pltpu.SemaphoreType.DMA((nc,)),
            pltpu.SemaphoreType.DMA((nc,)),
        ],
        4,
        120,
        (gp, gu, w_gu, sc_gu, b_gu, w_down, b_down, rate, cotangent, middle, x, sc_out),
        late=(2, 4, 5, 6, 7, 8, 9, 10),
        flow=(0, 1, 4, 5),
        step=tc,
    )


def gain_rows(tail, at):
    lane = lax.broadcasted_iota(jnp.int32, (8, LANES), 1)
    pick = jnp.where((lane == at) | (lane == at + 1), 1.0, 0.0).astype(BF16)
    column = tail[:, at : at + 1].astype(F32) + tail[:, at + 1 : at + 2].astype(F32)
    return nt(pick, tail)[0:1, :], column


class Stream:
    def __init__(self, sources, slots, sems, step):
        self.sources, self.slots, self.sems, self.step = sources, slots, sems, step

    def copies(self, i):
        rows = pl.ds(pl.multiple_of(i * self.step, self.step), self.step)
        slot = lax.rem(i, 2)
        return [
            pltpu.make_async_copy(src.at[rows, columns], held.at[slot], self.sems.at[k, slot])
            for k, ((src, columns), held) in enumerate(zip(self.sources, self.slots))
        ]

    def start(self, i):
        for copy in self.copies(i):
            copy.start()

    def wait(self, i):
        for copy in self.copies(i):
            copy.wait()
        return [held[lax.rem(i, 2)] for held in self.slots]


def stream_scratch(step, widths):
    return [pltpu.VMEM((2, step, n), BF16) for n in widths] + [pltpu.SemaphoreType.DMA((len(widths), 2))]


def out_backward(
    cfg, npad, nf, go, weights, b_out, sums, w_gu, w_down, up_gu, b_down, gm_gu, square_gu, m_gu,
    u_full, lg_gu, gu, dp_gu, hidden, lg_down, lora_down, gp_full, result, merged_low_gu, merged_low_down,
):
    t, fw, d, nl, nc, tc = cfg
    off = nf - (npad - LANES)
    widths = (d, LANES, LANES, LANES, 2 * npad, npad, LANES, LANES, d)

    def kernel(
        io, go_ref, w_ref, b_ref, s1_ref, s2_ref, s3_ref, s4_ref, wg_ref, wd_ref, up_ref, bd_ref, gm_ref, sq_ref, m_ref,
        uf_hbm, lg_hbm, gu_hbm, dp_hbm, hid_hbm, ld_hbm, lo2_hbm, gp_hbm, res_hbm, am_ref, amd_ref,
        da_ref, lo_ref, qs_ref, sh_ref, lc_ref, gf_ref, moved_ref,
        full, own, sd, rd, sc, rc, keep, qss, qsr, res_sems, acc_a, acc_g, acc_u, acc_d, acc_p, term, term_d, q_ref, *streams,
    ):
        cm = Comm(nl, nc, tc, fw, out_by_one=0.75)
        swap = Swap(cm)
        result_swap = (res_hbm, moved_ref, tuple(res_sems.at[k] for k in range(3)))
        cm.ag_refs(go_ref, full, own, sd, rd, sc, rc)
        every = lambda n: pl.ds(0, n)
        stream = Stream(
            [
                (uf_hbm, every(d)),
                (lg_hbm, every(LANES)),
                (gu_hbm, pl.ds(npad - LANES, LANES)),
                (gu_hbm, pl.ds(2 * npad - LANES, LANES)),
                (dp_hbm, every(2 * npad)),
                (hid_hbm, every(npad)),
                (ld_hbm, every(LANES)),
                (lo2_hbm, every(LANES)),
                (gp_hbm, every(d)),
            ],
            streams[:-1],
            streams[-1],
            tc,
        )
        stream.start(jnp.int32(0))
        cm.barrier((), [swap.partner])

        def ratio_copy(o, m):
            k = o * nl + m
            return cm.copy(
                q_ref, qs_ref.at[:, cm.columns(cm.c, cm.g)], qss.at[k], qsr.at[k], 1 - cm.c if o else cm.c, cm.after(m)
            )

        cm.ag_start()
        q_ref[...] = jnp.zeros_like(q_ref)
        q_ref[0:1, :] = -s1_ref[0:1, :] / s2_ref[0:1, :]
        q_ref[1:2, :] = -s3_ref[0:1, :] / s4_ref[0:1, :]
        for o, m in cm.st_peers():
            ratio_copy(o, m).start()
        qs_ref[:, cm.columns(cm.c, cm.g)] = q_ref[...]
        swap.start(*result_swap)
        for acc in (acc_a, acc_g, acc_u, acc_d, acc_p):
            acc[...] = jnp.zeros_like(acc)
        io.ready()
        ratio = -gm_ref[0:1, :] / sq_ref[0:1, :]
        term[...] = nt((up_ref[...] * ratio).astype(BF16), wg_ref[...])[: 2 * RANK, :]
        cm.ag_ahead()

        def stored(i):
            rows = cm.rows(i)
            return pltpu.make_async_copy(full.at[rows], gf_ref.at[rows], keep.at[i])

        def body(i, carry_on):
            cm.ag_step(i + 2)

            @pl.when(i == min(2, nc - 1))
            def _():
                for o, m in cm.st_peers():
                    ratio_copy(o, m).wait_recv()
                term_d[...] = nt((bd_ref[...].astype(F32) * qs_ref[1:2, :]).astype(BF16), wd_ref[:, :d])[:RANK, :]

            @pl.when(i + 1 < nc)
            def _():
                stream.start(i + 1)

            u, lg, low_g, low_u, dp, hid, ld, low_d, gp = stream.wait(i)
            acc_a[...] += tn(lg, u)
            acc_g[...] += tn(low_g, dp[:, :npad])
            acc_u[...] += tn(low_u, dp[:, npad:])
            acc_d[...] += tn(ld, hid)
            acc_p[...] += tn(low_d, gp)
            cm.ag_wait(i)
            stored(i).start()
            rows = cm.rows(i)
            block = full[rows, :]
            da_ref[rows, :] = nt(block, w_ref[:, :d]).astype(BF16)
            lo_ref[rows, :] = nt(block, b_ref[...]).astype(BF16)
            return carry_on

        lax.fori_loop(0, nc, body, 0)

        gain_row, _ = gain_rows(wg_ref[:, npad - LANES : npad], off + RANK)
        sh_ref[: 2 * RANK, :] = (SCALE * (acc_a[: 2 * RANK, :] * gain_row + term[...] / gain_row)).astype(BF16)
        for k, acc in enumerate((acc_g, acc_u)):
            at, low = slice(k * npad, (k + 1) * npad), slice(k * RANK, (k + 1) * RANK)
            lc_ref[(1 + k) * RANK : (2 + k) * RANK, :] = (
                SCALE * (acc[off : off + RANK, :] + am_ref[low, :] * ratio[:, at])
            ).astype(BF16)
            lc_ref[3 * RANK + k : 3 * RANK + k + 1, :] = (gm_ref[0:1, at] / m_ref[0:1, at]).astype(BF16)
        lc_ref[3 * RANK + 2 :, :] = jnp.zeros((RANK - 2, npad), BF16)
        lc_ref[:RANK, :] = (SCALE * (acc_d[:RANK, :] + term_d[...])).astype(BF16)
        sh_ref[2 * RANK :, :] = (SCALE * (acc_p[:RANK, :] + amd_ref[...] * qs_ref[1:2, :])).astype(BF16)

        def drain(i, carry_on):
            cm.ag_drain(i)
            stored(i).wait()
            return carry_on

        lax.fori_loop(0, nc, drain, 0)
        swap.wait(*result_swap)
        swap.drain(*result_swap)
        for o, m in cm.st_peers():
            ratio_copy(o, m).wait_send()

    dma = pltpu.SemaphoreType.DMA
    return call(
        kernel,
        "out_backward",
        (
            shape((t, fw), BF16),
            shape((t, LANES), BF16),
            shape((8, d), F32),
            shape((3 * RANK, d), BF16),
            shape((4 * RANK, npad), BF16),
            shape((t, d), BF16),
            shape((t, fw), BF16),
        ),
        [VM] * 14 + [ANY] * 9 + [VM] * 2,
        (VM,) * 5 + (ANY, ANY),
        ag_scratch(nl, nc, t, d)
        + [dma((nc,)), dma((2 * nl,)), dma((2 * nl,)), dma((3,))]
        + [pltpu.VMEM((LANES, n), F32) for n in (d, npad, npad, npad, d)]
        + [pltpu.VMEM((2 * RANK, d), F32), pltpu.VMEM((RANK, npad), F32), pltpu.VMEM((8, fw), F32)]
        + stream_scratch(tc, widths),
        5,
        60,
        (
            go, weights, b_out, *sums, w_gu, w_down, up_gu, b_down, gm_gu, square_gu, m_gu,
            u_full, lg_gu, gu, dp_gu, hidden, lg_down, lora_down, gp_full, result, merged_low_gu, merged_low_down,
        ),
        late=(1, 2, 7, 8, 9, 10),
    )


def attention_backward(
    cfg, qkv, attended, grad, lse, seg_column, seg_row, first_block, block, cosine, sine, scale, rate, b_qkv
):
    t, fw = cfg[0], cfg[1]
    heads = fw // HD
    width = 3 * fw

    def kernel(
        io, qkv_ref, att_ref, grad_ref, lse_ref, sc_ref, sr_ref, first_ref, cos_ref, sin_ref, scale_ref, rate_ref, b_ref,
        dp_ref, st_ref, gm_ref, lg_ref, dq, dk, dv,
    ):
        def at(i):
            return pl.ds(pl.multiple_of(i * block, block), block)

        def columns(k, hd):
            return slice(k * fw + hd * HD, k * fw + (hd + 1) * HD)

        gm_ref[...] = jnp.zeros_like(gm_ref)
        dk[...] = jnp.zeros_like(dk)
        dv[...] = jnp.zeros_like(dv)

        def one_query(i, carry_on):
            queries = [qkv_ref[at(i), columns(0, hd)] for hd in range(heads)]
            grads = [grad_ref[at(i), columns(0, hd)] for hd in range(heads)]
            deltas = [
                ones_rows(grads[hd].astype(F32) * att_ref[at(i), columns(0, hd)].astype(F32))[0:1, :]
                for hd in range(heads)
            ]
            query_segment = sr_ref[0:1, at(i)]

            def one_key(j, accs):
                allowed = allowed_of(sc_ref[at(j), 0:1], query_segment, j, i, block)
                out = []
                for hd in range(heads):
                    keys = qkv_ref[at(j), columns(1, hd)]
                    s = nt(keys, queries[hd]) * (HD**-0.5)
                    p = jnp.where(allowed, jnp.exp(s - lse_ref[hd * 8 : hd * 8 + 1, at(i)]), 0.0)
                    ds = (p * (nt(qkv_ref[at(j), columns(2, hd)], grads[hd]) - deltas[hd])).astype(BF16)
                    dv[hd, at(j), :] += nn(p.astype(BF16), grads[hd])
                    dk[hd, at(j), :] += nn(ds, queries[hd])
                    out.append(accs[hd] + tn(ds, keys))
                return tuple(out)

            accs = lax.fori_loop(first_ref[i], i + 1, one_key, (jnp.zeros((block, HD), F32),) * heads)
            for hd in range(heads):
                dq[hd, at(i), :] = accs[hd]
            return carry_on

        lax.fori_loop(0, t // block, one_query, 0)

        def finish(i, carry_on):
            rows = at(i)
            cosine_here, sine_here = cos_ref[rows, :], sin_ref[rows, :]
            inner = jnp.zeros((block, HD), F32)
            for hd in range(heads):
                for n, source in enumerate((dq, dk, dv)):
                    where = columns(n, hd)
                    dout = source[hd, rows, :]
                    value = qkv_ref[rows, where].astype(F32)
                    if n < 2:
                        dout = dout * (HD**-0.5)
                        dout = dout * cosine_here - pltpu.roll(dout, HD // 2, 1) * sine_here
                        value = value * cosine_here - pltpu.roll(value, HD // 2, 1) * sine_here
                    product = dout * value
                    inner = inner + product
                    gm_ref[0:1, where] += row_sum(product)
                    dp_ref[rows, where] = (dout * scale_ref[0:1, where]).astype(BF16)
            st_ref[i] = ones_rows(inner)[0:1, :]
            lg_ref[rows, :] = (nt(dp_ref[rows, :], b_ref[...].astype(BF16)) * rate_ref[rows, :]).astype(BF16)
            return carry_on

        lax.fori_loop(0, t // block, finish, 0)

    return call(
        kernel,
        "attention_backward",
        (
            shape((t, width), BF16),
            shape((t // block, 1, block), F32),
            shape((8, width), F32),
            shape((t, LANES), BF16),
        ),
        [VM] * 6 + [SM] + [VM] * 5,
        (VM,) * 4,
        [pltpu.VMEM((heads, t, HD), F32)] * 3,
        None,
        35,
        (qkv, attended, grad, lse, seg_column, seg_row, first_block, cosine, sine, scale, rate, b_qkv),
    )


def qkv_backward(
    cfg, ny, dp, stats, weights, rate, dm, x, shared, local_gu, w_out, up_qkv, b_out, ratios, gm_qkv, square_qkv,
    gm_out, gm_down, small, x_full, lg_qkv, lora_qkv, attended, lg_out, lora_out, go_full,
):
    t, fw, d, nl, nc, tc = cfg
    width = 3 * fw
    peers = 2 * nl
    step = 2 * tc if nc % 2 == 0 else tc
    parts = t // step
    widths = (d, LANES, LANES, fw, LANES, LANES, d)

    def kernel(
        io, dp_ref, st_ref, w_ref, rate_ref, dm_ref, x_ref, sh_ref, l_ref, wo_ref, up_ref, bo_ref, q_ref,
        gm_ref, sq_ref, gmo_ref, gmd_ref, m_ref, xf_hbm, lg_hbm, lq_hbm, at_hbm, lgo_hbm, lo_hbm, gf_hbm,
        out_ref, as_ref, bs_ref, ls_ref,
        sb, cb, gb, s1, r1, s2, r2, sa, ss, sr,
        stage, gs_s, gs_r, gs_l, group, gsum, gss, gsr, final_a, final_b, final_l, fs, fr, fl,
        a_ref, b_ref, acc_a, acc_b, acc_o, acc_p, *streams,
    ):
        cm = Comm(nl, nc, tc, fw, back_by_two=0.25)
        c, g = cm.c, cm.g
        y, h = lax.axis_index("y"), lax.axis_index("h")
        cm.rs_refs(sb, cb, gb, s1, r1, s2, r2)
        cm.st_refs(st_ref, sa, ss, sr)
        swap = Swap(cm)
        every = lambda n: pl.ds(0, n)
        stream = Stream(
            [
                (xf_hbm, every(d)),
                (lg_hbm, every(LANES)),
                (lq_hbm, every(LANES)),
                (at_hbm, every(fw)),
                (lgo_hbm, every(LANES)),
                (lo_hbm, every(LANES)),
                (gf_hbm, every(d)),
            ],
            streams[:-1],
            streams[-1],
            step,
        )
        stream.start(jnp.int32(0))
        senders = [
            {"y": lax.rem(y + ny - k, ny), "c": h, "h": hh} for k in range(1, ny) for hh in (0, 1)
        ]
        cm.barrier(senders + [{"c": h, "h": 1 - h}], [swap.partner, {"c": h, "h": h}])

        def gather_part(o, m):
            to_c, to_g = 1 - c if o else c, cm.after(m)
            k = o * nl + m
            return cm.copy(
                a_ref.at[:, cm.columns(to_c, to_g)], group.at[k], gss.at[k], gsr.at[k], to_c, to_g
            )

        def sums(k, e):
            device = {"y": lax.rem(y + k, ny), "c": lax.rem(c + e, 2), "h": c}
            slot = k * 2 + h
            return [
                pltpu.make_async_remote_copy(
                    src_ref=src, dst_ref=dst.at[slot], send_sem=fs.at[n, k * 2 + e], recv_sem=fr.at[n, slot],
                    device_id=device, device_id_type=MESH,
                )
                for n, (src, dst) in enumerate(((gsum, final_a), (b_ref, final_b), (l_ref, final_l)))
            ]

        def sums_here():
            return [
                pltpu.make_async_copy(src, dst.at[h], fl.at[n])
                for n, (src, dst) in enumerate(((gsum, final_a), (b_ref, final_b), (l_ref, final_l)))
            ]

        cm.st_send(None)
        for acc in (acc_a, acc_b, acc_o, acc_p):
            acc[...] = jnp.zeros_like(acc)

        def adapters(k):
            @pl.when(k + 1 < parts)
            def _():
                stream.start(k + 1)

            xf, lg, low_q, att, lg_o, low_o, gf = stream.wait(k)
            rows = pl.ds(pl.multiple_of(k * step, step), step)
            acc_a[...] += tn(lg, xf)
            acc_b[...] += tn(low_q, dp_ref[rows, :])
            acc_o[...] += tn(lg_o, att)
            acc_p[...] += tn(low_o, gf)

        def adapters_end():
            ratio = -gm_ref[0:1, :] / sq_ref[0:1, :]
            ratio_out = q_ref[0:1, :]
            tail = w_ref[:, width:]
            gain_row, gain_column = gain_rows(tail, 3 * RANK)
            term = nt((up_ref[...] * ratio).astype(BF16), w_ref[:, :width])
            a_ref[: 3 * RANK, :] = (
                SCALE * (acc_a[: 3 * RANK, :] * gain_row + term[: 3 * RANK, :] / gain_row)
            ).astype(BF16)
            merged = tn(
                (tail.astype(F32) / (gain_column * gain_column)).astype(BF16), w_ref[:, :width]
            )
            for k in range(3):
                at, low = slice(k * fw, (k + 1) * fw), slice(k * RANK, (k + 1) * RANK)
                b_ref[(1 + k) * RANK : (2 + k) * RANK, :] = (
                    SCALE * (acc_b[low, at] + merged[low, at] * ratio[:, at])
                ).astype(BF16)
                b_ref[4 * RANK + k : 4 * RANK + k + 1, :] = (gm_ref[0:1, at] / m_ref[k : k + 1, :]).astype(BF16)
            b_ref[4 * RANK + 3 : 4 * RANK + 4, :] = (gmo_ref[0:1, :] / m_ref[3:4, :]).astype(BF16)
            b_ref[4 * RANK + 4 : 4 * RANK + 5, :] = (gmd_ref[0:1, :] / m_ref[4:5, :]).astype(BF16)
            b_ref[4 * RANK + 5 :, :] = jnp.zeros((RANK - 5, fw), BF16)
            b_ref[:RANK, :] = (
                SCALE
                * (acc_o[:RANK, :] + nt((bo_ref[...].astype(F32) * ratio_out).astype(BF16), wo_ref[:, :d])[:RANK, :])
            ).astype(BF16)
            a_ref[3 * RANK : 4 * RANK, :] = (
                SCALE * (acc_p[:RANK, :] + tn(wo_ref[:, d:], wo_ref[:, :d])[:RANK, :] * ratio_out)
            ).astype(BF16)
            a_ref[4 * RANK :, :] = sh_ref[...]
            for o, m in cm.st_peers():
                gather_part(o, m).start()

        io.ready()

        def grad_swap(i):
            rows = cm.rows(i)
            return stage.at[rows], out_ref.at[rows], (gs_s.at[i], gs_r.at[i], gs_l.at[i])

        def body(i, carry_on):
            @pl.when(i < nc)
            def _():
                block = dp_ref[cm.rows(i), :]
                for role in range(2 * nl):
                    sb[i, role // nl, role % nl] = nt(
                        block, w_ref[role * fw : (role + 1) * fw, :width]
                    ).astype(BF16)
                cm.rs_across(i).start()

            cm.rs_steps(i)

            @pl.when(i < parts)
            def _():
                adapters(i)

            @pl.when(i == parts)
            def _():
                adapters_end()

            @pl.when(i == min(parts + 3, nc + 2))
            def _():
                total = a_ref[:, cm.columns(c, g)].astype(F32)
                for o, m in cm.st_peers():
                    gather_part(o, m).wait_recv()
                    total = total + group[o * nl + m].astype(F32)
                gsum[...] = total.astype(BF16)
                for k in range(ny):
                    for e in (0, 1):
                        if (k, e) == (0, 0):

                            @pl.when(swap.moves)
                            def _():
                                for copy in sums(0, 0):
                                    copy.start()

                            @pl.when(jnp.logical_not(swap.moves))
                            def _():
                                for copy in sums_here():
                                    copy.start()
                        else:
                            for copy in sums(k, e):
                                copy.start()

            @pl.when(i >= 3)
            def _():
                k = i - 3
                rows = cm.rows(k)

                @pl.when(k == 0)
                def _():
                    cm.st_wait(None)

                r = rate_ref[rows, 0:1]
                inner = cm.st_sum(k)
                stage[rows, :] = (
                    dm_ref[rows, :]
                    + r * cm.rs_total(k)
                    - x_ref[rows, :].astype(F32) * (r * r * inner / d)
                ).astype(BF16)
                swap.start(*grad_swap(k))

            return carry_on

        lax.fori_loop(0, nc + 3, body, 0)

        for k in range(ny):
            for hh in (0, 1):
                slot = k * 2 + hh

                def arrived():
                    for n, dst in enumerate((final_a, final_b, final_l)):
                        src = (gsum, b_ref, l_ref)[n]
                        pltpu.make_async_remote_copy(
                            src_ref=src, dst_ref=dst.at[slot], send_sem=fs.at[n, 0], recv_sem=fr.at[n, slot],
                            device_id=swap.partner, device_id_type=MESH,
                        ).wait_recv()

                if k == 0:
                    here = jnp.logical_and(c == h, h == hh)

                    @pl.when(here)
                    def _():
                        for copy in sums_here():
                            copy.wait()

                    @pl.when(jnp.logical_not(here))
                    def _():
                        arrived()
                else:
                    arrived()
        for out, held in ((as_ref, final_a), (bs_ref, final_b), (ls_ref, final_l)):
            total = held[0].astype(F32)
            for slot in range(1, 2 * ny):
                total = total + held[slot].astype(F32)
            out[...] = total

        def drain(i, carry_on):
            swap.wait(*grad_swap(i))
            cm.rs_drain(i)
            swap.drain(*grad_swap(i))
            return carry_on

        lax.fori_loop(0, nc, drain, 0)
        cm.st_drain(None)
        for o, m in cm.st_peers():
            gather_part(o, m).wait_send()
        for k in range(ny):
            for e in (0, 1):
                if (k, e) == (0, 0):

                    @pl.when(swap.moves)
                    def _():
                        for copy in sums(0, 0):
                            copy.wait_send()
                else:
                    for copy in sums(k, e):
                        copy.wait_send()

    dma = pltpu.SemaphoreType.DMA
    na, nb, ng = 7 * RANK, (5 * RANK, fw), local_gu.shape
    return call(
        kernel,
        "qkv_backward",
        (shape((t, fw), BF16), shape((na, fw), F32), shape(nb, F32), shape(ng, F32)),
        [VM] * 17 + [ANY] * 7,
        (VM,) * 4,
        rs_scratch(nl, nc, tc, fw)
        + st_scratch(nl, nc, t)
        + [pltpu.VMEM((t, fw), BF16)]
        + [dma((nc,))] * 3
        + [pltpu.VMEM((peers, na, fw), BF16), pltpu.VMEM((na, fw), BF16), dma((peers,)), dma((peers,))]
        + [
            pltpu.VMEM((2 * ny, na, fw), BF16),
            pltpu.VMEM((2 * ny, *nb), BF16),
            pltpu.VMEM((2 * ny, *ng), BF16),
            dma((3, 2 * ny)),
            dma((3, 2 * ny)),
            dma((3,)),
            pltpu.VMEM((na, d), BF16),
            pltpu.VMEM(nb, BF16),
        ]
        + [pltpu.VMEM((LANES, n), F32) for n in (d, width, fw, d)]
        + stream_scratch(step, widths),
        6,
        70,
        (
            dp, stats, weights, rate, dm, x, shared, local_gu, w_out, up_qkv, b_out, ratios, gm_qkv, square_qkv,
            gm_out, gm_down, small, x_full, lg_qkv, lora_qkv, attended, lg_out, lora_out, go_full,
        ),
        late=(2, 3, 4, 5, 6, 7, 8, 9, 10, 11),
    )


def last_step(fw, nf, grad, result, shared, local, local_gu):
    def kernel(
        io, g_ref, r_ref, s_ref, l_ref, u_ref,
        result_ref, grad_ref, aq_ref, bq_ref, mq_ref, ao_ref, bo_ref, mo_ref,
        ag_ref, bg_ref, mg_ref, ad_ref, bd_ref, md_ref,
    ):
        result_ref[...] = r_ref[...]
        grad_ref[...] = g_ref[...].astype(F32)
        for k in range(3):
            aq_ref[k] = s_ref[k * RANK : (k + 1) * RANK, :]
            bq_ref[k] = l_ref[(1 + k) * RANK : (2 + k) * RANK, :]
        for k in range(2):
            ag_ref[k] = s_ref[(4 + k) * RANK : (5 + k) * RANK, :]
            bg_ref[k] = u_ref[(1 + k) * RANK : (2 + k) * RANK, :nf]
        mq_ref[...] = l_ref[4 * RANK : 4 * RANK + 3, :]
        mg_ref[...] = u_ref[3 * RANK : 3 * RANK + 2, :nf]
        ao_ref[...] = l_ref[:RANK, :]
        bo_ref[...] = s_ref[3 * RANK : 4 * RANK, :]
        mo_ref[...] = l_ref[4 * RANK + 3 : 4 * RANK + 4, :]
        ad_ref[...] = u_ref[:RANK, :nf]
        bd_ref[...] = s_ref[6 * RANK :, :]
        md_ref[...] = l_ref[4 * RANK + 4 : 4 * RANK + 5, :]

    f = [
        (3, RANK, fw), (3, RANK, fw), (3, fw), (RANK, fw), (RANK, fw), (1, fw),
        (2, RANK, fw), (2, RANK, nf), (2, nf), (RANK, nf), (RANK, fw), (1, fw),
    ]
    return call(
        kernel,
        "last_step",
        (shape(result.shape, BF16), shape(grad.shape, F32), *[shape(v, F32) for v in f]),
        [VM] * 5,
        (VM,) * 14,
        [],
        None,
        4,
        (grad, result, shared, local, local_gu),
    )


def turn_constants():
    f = 10000.0 ** (-2.0 * np.arange(HD // 2) / HD)
    out = []
    for scale in (32.0, 1.0):
        angle = scale * np.arange(32)[:, None] * f[None, :]
        table = np.concatenate([np.cos(angle), np.cos(angle), np.sin(angle), np.sin(angle)], axis=1)
        high = table.astype(BF16)
        low = (table - high.astype(np.float64)).astype(BF16)
        out.append(jnp.asarray(np.concatenate([high, low], axis=1)))
    return out


def padded(rows, total):
    return jnp.pad(rows, ((0, 0), (0, total - rows.shape[1])))


def on_device(ny, nl, *operands):
    (
        inputs, segments, gain_attn, gain_ffn, w_qkv, a_qkv, b_qkv, m_qkv, w_out, a_out, b_out, m_out,
        w_gu, a_gu, b_gu, m_gu, w_down, a_down, b_down, m_down, cotangent,
    ) = operands
    t, fw = inputs.shape
    mp = 2 * nl
    d = mp * fw
    nf = m_gu.shape[1]
    npad = -(-(nf + RANK) // LANES) * LANES
    width = 3 * fw
    nc = t // 256 if t % 256 == 0 else 1
    block = t // nc
    cfg = (t, fw, d, nl, nc, block)
    y, c, h, g = (lax.axis_index(name) for name in ("y", "c", "h", "g"))
    role = c * nl + g

    def two_parts(gain):
        high = gain.astype(BF16)
        return [high[:, None], (gain - high.astype(F32)).astype(BF16)[:, None]]

    tail_qkv = padded(
        jnp.concatenate(
            [(a_qkv[k] * gain_attn[:, None]).astype(BF16) for k in range(3)] + two_parts(gain_attn), axis=1
        ),
        LANES,
    )
    tail_gu = jnp.stack(
        [
            jnp.pad(
                jnp.concatenate(
                    [(a_gu[k] * gain_ffn[:, None]).astype(BF16)] + two_parts(gain_ffn), axis=1
                ),
                ((0, 0), (nf, npad - nf - RANK - 2)),
            )
            for k in range(2)
        ]
    )
    gains = padded(jnp.stack([gain_attn, gain_ffn], axis=1), LANES)
    b_gu_padded = jnp.pad(
        b_gu.reshape(2, RANK, mp, nf), ((0, 0), (0, 0), (0, 0), (0, npad - nf))
    ).transpose(0, 2, 1, 3)
    small = jnp.concatenate([m_qkv, m_out[None], m_down[None], jnp.zeros((3, fw), F32)], axis=0)
    small_gu = jnp.broadcast_to(
        jnp.pad(m_gu, ((0, 0), (0, npad - nf)), constant_values=1.0).reshape(1, 2 * npad), (8, 2 * npad)
    )

    def take(whole, n, axis):
        return lax.dynamic_slice_in_dim(whole, role * n, n, axis)

    b_qkv_here = take(b_qkv, fw, 2)
    b_gu_here = take(b_gu, nf, 2)

    def block_up(up, pad):
        k, _, n = up.shape
        wide = jnp.pad(up, ((0, 0), (0, 0), (0, pad - n)))[:, :, None, :]
        same = (jnp.arange(k)[:, None] == jnp.arange(k)[None, :])[:, None, :, None]
        rows = jnp.where(same, wide, 0.0).reshape(k * RANK, k * pad)
        return jnp.pad(rows, ((0, LANES - k * RANK), (0, 0)))

    up_qkv = block_up(b_qkv_here, fw)
    up_gu = block_up(b_gu_here, npad)
    up_out = jnp.pad(b_out, ((0, LANES - RANK), (0, 0))).astype(BF16)
    up_down = jnp.pad(b_down, ((0, LANES - RANK), (0, 0))).astype(BF16)

    (
        x, weights_qkv, weights_out, small, small_gu, scale_qkv, square_qkv, qkv, lora_qkv_in, rate_attn,
        blocks_gu, rows_down, weights_gu, x_full, cosine, sine, seg_column, seg_row,
    ) = qkv_forward(
        cfg, ny, npad, nf, inputs, w_qkv, a_qkv.transpose(0, 2, 1), b_qkv, tail_qkv, gains, w_out, small, small_gu, segments,
        turn_constants(), w_gu, a_gu.transpose(0, 2, 1), b_gu_padded, tail_gu, w_down, a_down, b_down, a_out.T, b_out,
    )
    first_number = seg_row[0, ::block]
    first_block = jnp.sum((seg_row[0][None, :] < first_number[:, None]).astype(jnp.int32), axis=1) // block
    attended, lse = attention_forward(cfg, qkv, seg_column, seg_row, first_block, block)
    middle, u, stats, sc_out, square_out, lora_out, weights_gu, weights_down = out_forward(
        cfg, ny, npad, attended, weights_out, x, small, weights_gu, blocks_gu, rows_down
    )
    (
        gu, hidden, block_out, gm_down, rate_ffn, gp, scale_gu, square_gu, sc_down, square_down,
        lora_down, grad_seed, merged_low_gu, merged_low_down, u_full,
    ) = ffn_forward(
        cfg, npad, nf, u, stats, weights_gu, small_gu[0:1], weights_down, small, middle, cotangent
    )

    dm, go, gm_out, gm_gu, lg_gu, lg_down, dp_gu, gp_full = ffn_backward(
        cfg, npad, gp, gu, weights_gu, scale_gu, up_gu, weights_down, up_down, rate_ffn,
        grad_seed, middle, x, sc_out,
    )
    grad_attended, lg_out, ratios, shared, local_gu, go_full, block_out = out_backward(
        cfg, npad, nf, go, weights_out, up_out, (gm_out, square_out, gm_down, square_down), weights_gu, weights_down, up_gu, up_down, gm_gu, square_gu,
        small_gu, u_full, lg_gu, gu, dp_gu, hidden, lg_down, lora_down, gp_full, block_out,
        merged_low_gu, merged_low_down,
    )
    dp_qkv, inner, gm_qkv, lg_qkv = attention_backward(
        cfg, qkv, attended, grad_attended, lse, seg_column, seg_row, first_block, block, cosine, sine,
        scale_qkv, rate_attn, up_qkv,
    )

    grad_input, shared, local, local_gu = qkv_backward(
        cfg, ny, dp_qkv, inner, weights_qkv, rate_attn, dm, x, shared, local_gu, weights_out, up_qkv, up_out, ratios,
        gm_qkv, square_qkv, gm_out, gm_down, small, x_full, lg_qkv, lora_qkv_in, attended, lg_out, lora_out, go_full,
    )
    out = list(last_step(fw, nf, grad_input, block_out, shared, local, local_gu))
    out[2], out[8] = out[2].transpose(0, 2, 1), out[8].transpose(0, 2, 1)
    out[5], out[11] = out[5].T, out[11].T
    out[7], out[13] = out[7][0], out[13][0]
    return tuple(out)


def solution(mesh):
    dp, mp = mesh.shape["dp"], mesh.shape["mp"]
    ny, nl = dp // 2, mp // 2
    fine = Mesh(mesh.devices.reshape(ny, 2, 2, nl), ("y", "c", "h", "g"))
    rows, cols = ("y", "c"), ("h", "g")
    in_specs = (
        P(rows, cols),
        P(rows, None),
        P(cols),
        P(cols),
        P(None, cols, None),
        P(None, cols, None),
        P(),
        P(None, cols),
        P(cols, None),
        P(cols, None),
        P(),
        P(cols),
        P(None, cols, None),
        P(None, cols, None),
        P(),
        P(None, cols),
        P(cols, None),
        P(cols, None),
        P(),
        P(cols),
        P(rows, cols),
    )
    out_specs = (
        P(rows, cols),
        P(rows, cols),
        P(None, cols, None),
        P(None, None, cols),
        P(None, cols),
        P(cols, None),
        P(None, cols),
        P(cols),
        P(None, cols, None),
        P(None, None, cols),
        P(None, cols),
        P(cols, None),
        P(None, cols),
        P(cols),
    )
    return jax.shard_map(
        lambda *operands: on_device(ny, nl, *operands),
        mesh=fine,
        in_specs=in_specs,
        out_specs=out_specs,
        check_vma=False,
    )
```

```python
import jax
import jax.numpy as jnp
import numpy as np
from jax import lax
from jax.experimental import pallas as pl
from jax.experimental.pallas import tpu as pltpu
from jax.sharding import Mesh
from jax.sharding import PartitionSpec as P

HD = 128
RANK = 16
SCALE = 2.0
EPS = 1e-05
MASKED = -1e30
HIGHEST = lax.Precision.HIGHEST
MESH = pl.DeviceIdType.MESH
F32 = jnp.float32
BF16 = jnp.bfloat16
LANES = 128
SEGMENTS = 8
VMEM_LIMIT = 60 * 1024 * 1024


def nt(a, b, precision=None):
    return lax.dot_general(
        a, b, (((1,), (1,)), ((), ())), precision=precision, preferred_element_type=F32
    )


def tn(a, b, precision=None):
    return lax.dot_general(
        a, b, (((0,), (0,)), ((), ())), precision=precision, preferred_element_type=F32
    )


def nn(a, b, precision=None):
    return lax.dot_general(
        a, b, (((1,), (0,)), ((), ())), precision=precision, preferred_element_type=F32
    )


WINDOW = 3
EARLY = 1


class Comm:
    def __init__(self, nl, nc, tc, fw, out_by_one=0.5, back_by_two=0.5):
        self.nl, self.nc, self.tc, self.fw = nl, nc, tc, fw
        self.square = nl == 4
        self.cut = int(tc * out_by_one) // 16 * 16
        self.back = int(tc * back_by_two) // 16 * 16
        self.c = lax.axis_index("c")
        self.g = lax.axis_index("g")

    def rows(self, i):
        return pl.ds(pl.multiple_of(i * self.tc, self.tc), self.tc)

    def after(self, m):
        return lax.rem(self.g + m, self.nl)

    def before(self, m):
        return lax.rem(self.g + self.nl - m, self.nl)

    def columns(self, c, g):
        return pl.ds(pl.multiple_of((c * self.nl + g) * self.fw, self.fw), self.fw)

    def copy(self, src, dst, send, recv, c, g):
        return pltpu.make_async_remote_copy(
            src_ref=src,
            dst_ref=dst,
            send_sem=send,
            recv_sem=recv,
            device_id={"c": c, "g": g},
            device_id_type=MESH,
        )

    def barrier(self, others=(), one_more=None):
        sem = pltpu.get_barrier_semaphore()
        everyone = [
            {"c": 1 - self.c if other else self.c, "g": self.after(m)}
            for other in (0, 1)
            for m in range(self.nl)
            if (other, m) != (0, 0)
        ] + list(others)
        for device in everyone:
            pl.semaphore_signal(sem, inc=1, device_id=device, device_id_type=MESH)
        if one_more is None:
            pl.semaphore_wait(sem, len(everyone))
        else:
            apart = self.c - lax.axis_index("h")

            @pl.when(apart != 0)
            def _():
                for device in one_more:
                    pl.semaphore_signal(sem, inc=1, device_id=device, device_id_type=MESH)

            pl.semaphore_wait(sem, len(everyone) + len(one_more) * apart * apart)

    def other(self, m):
        if m == 1:
            return self.g + 1 - 2 * lax.rem(self.g, 2)
        return lax.rem(self.g + 2, 4) if m == 2 else 3 - self.g

    def comes_from(self, m):
        if m == 0:
            return self.g
        return self.other(m) if self.square else self.before(m)

    def goes_to(self, m):
        return self.other(m) if self.square else self.after(m)

    def some(self, i, way):
        cut = self.cut
        start, size = (0, cut) if way == 0 else (cut, self.tc - cut)
        return pl.ds(pl.multiple_of(i * self.tc + start, 16), size)

    def ag_refs(self, x, full, own, sd, rd, sc, rc):
        self.x, self.full, self.own = x, full, own
        self.sd, self.rd, self.sc, self.rc = sd, rd, sc, rc

    def ag_steps(self):
        return (1, 2) if self.square else range(1, self.nl)

    def ag_direct(self, i, m):
        rows = self.rows(i)
        return self.copy(
            self.x.at[rows],
            self.full.at[rows, self.columns(self.c, self.g)],
            self.sd.at[i, m],
            self.rd.at[i, m],
            self.c,
            self.goes_to(m),
        )

    def ag_relay(self, i, way):
        rows = self.some(i, way)
        columns = self.columns(self.c, self.other(2 - way))
        return self.copy(
            self.full.at[rows, columns],
            self.full.at[rows, columns],
            self.sd.at[i, 3 * way],
            self.rd.at[i, 3 * way],
            self.c,
            self.other(1 + way),
        )

    def ag_across(self, i, m):
        rows = self.rows(i)
        columns = self.columns(self.c, self.comes_from(m))
        src = self.x.at[rows] if m == 0 else self.full.at[rows, columns]
        return self.copy(
            src,
            self.full.at[rows, columns],
            self.sc.at[i, m],
            self.rc.at[i, m],
            1 - self.c,
            self.g,
        )

    def ag_own(self, i):
        rows = self.rows(i)
        return pltpu.make_async_copy(
            self.x.at[rows],
            self.full.at[rows, self.columns(self.c, self.g)],
            self.own.at[i],
        )

    def ag_send(self, i):
        for m in self.ag_steps():
            self.ag_direct(i, m).start()
        self.ag_across(i, 0).start()
        self.ag_own(i).start()

    def ag_start(self):
        for i in range(min(WINDOW, self.nc)):
            self.ag_send(jnp.int32(i))

    def ag_forward(self, i):
        for m in self.ag_steps():
            self.ag_direct(i, m).wait_recv()
        if self.square:
            for way in (0, 1):
                self.ag_relay(i, way).start()
        for m in self.ag_steps():
            self.ag_across(i, m).start()

    def ag_corner(self, i):
        if self.square:
            for way in (0, 1):
                self.ag_relay(i, way).wait_recv()
            self.ag_across(i, 3).start()

    def ag_step(self, i, more=True):
        @pl.when(i < self.nc)
        def _():
            self.ag_forward(i)

        if more:

            @pl.when(i + WINDOW < self.nc)
            def _():
                self.ag_send(i + WINDOW)

        @pl.when((i >= 1) & (i <= self.nc))
        def _():
            self.ag_corner(i - 1)

    def ag_ahead(self):
        self.ag_step(jnp.int32(0))
        self.ag_step(jnp.int32(1))

    def ag_wait(self, i):
        self.ag_own(i).wait()
        for m in range(self.nl):
            self.ag_across(i, m).wait_recv()

    def ag_drain(self, i):
        for m in self.ag_steps():
            self.ag_direct(i, m).wait_send()
        if self.square:
            for way in (0, 1):
                self.ag_relay(i, way).wait_send()
        for m in range(self.nl):
            self.ag_across(i, m).wait_send()

    def rs_refs(self, sb, cb, gb, s1, r1, s2, r2):
        self.sb, self.cb, self.gb = sb, cb, gb
        self.s1, self.r1, self.s2, self.r2 = s1, r1, s2, r2

    def rs_across(self, i):
        return self.copy(
            self.sb.at[i, 1 - self.c],
            self.cb.at[i],
            self.s1.at[i],
            self.r1.at[i],
            1 - self.c,
            self.g,
        )

    def rs_direct(self, i, m):
        to = self.goes_to(m)
        return self.copy(
            self.sb.at[i, self.c, to],
            self.gb.at[i, m - 1],
            self.s2.at[i, m],
            self.r2.at[i, m],
            self.c,
            to,
        )

    def rs_corner(self, i, way):
        rows = pl.ds(0, self.back) if way == 0 else pl.ds(self.back, self.tc - self.back)
        return self.copy(
            self.sb.at[i, self.c, self.other(3), rows],
            self.gb.at[i, 2, rows],
            self.s2.at[i, 3 * way],
            self.r2.at[i, 3 * way],
            self.c,
            self.other(2 - way),
        )

    def rs_middle(self, i):
        self.rs_across(i).wait_recv()
        for gp in range(self.nl):
            mine = self.sb[i, self.c, gp].astype(F32) + self.cb[i, gp].astype(F32)
            self.sb[i, self.c, gp] = mine.astype(BF16)
        if self.square:
            for way in (0, 1):
                self.rs_corner(i, way).start()
        else:
            for m in range(1, self.nl):
                self.rs_direct(i, m).start()

    def rs_second(self, i):
        if not self.square:
            return
        for way in (0, 1):
            self.rs_corner(i, way).wait_recv()
            rows = pl.ds(0, self.back) if way == 0 else pl.ds(self.back, self.tc - self.back)
            to = self.other(1 + way)
            both = self.sb[i, self.c, to, rows].astype(F32) + self.gb[i, 2, rows].astype(F32)
            self.sb[i, self.c, to, rows] = both.astype(BF16)
        for m in (1, 2):
            self.rs_direct(i, m).start()

    def rs_total(self, i):
        steps = (1, 2) if self.square else range(1, self.nl)
        for m in steps:
            self.rs_direct(i, m).wait_recv()
        total = self.sb[i, self.c, self.g].astype(F32)
        for m in steps:
            total = total + self.gb[i, m - 1].astype(F32)
        return total

    def rs_drain(self, i):
        self.rs_across(i).wait_send()
        if self.square:
            for way in (0, 1):
                self.rs_corner(i, way).wait_send()
        for m in (1, 2) if self.square else range(1, self.nl):
            self.rs_direct(i, m).wait_send()

    def rs_steps(self, i):
        @pl.when((i >= 1) & (i <= self.nc))
        def _():
            self.rs_middle(i - 1)

        @pl.when((i >= 2) & (i <= self.nc + 1))
        def _():
            self.rs_second(i - 2)

    def st_refs(self, st, sa, ss, sr):
        self.st, self.sa, self.ss, self.sr = st, sa, ss, sr

    def st_copy(self, i, other, m):
        mine = self.c * self.nl + self.g
        src, dst = (self.st, self.sa.at[mine]) if i is None else (self.st.at[i], self.sa.at[mine, i])
        i = 0 if i is None else i
        return self.copy(
            src,
            dst,
            self.ss.at[i, other * self.nl + m],
            self.sr.at[i, other * self.nl + m],
            1 - self.c if other else self.c,
            self.after(m),
        )

    def st_peers(self):
        return [(o, m) for o in (0, 1) for m in range(self.nl) if (o, m) != (0, 0)]

    def st_send(self, i):
        for o, m in self.st_peers():
            self.st_copy(i, o, m).start()
        mine = self.c * self.nl + self.g
        if i is None:
            self.sa[mine] = self.st[...]
        else:
            self.sa[mine, i] = self.st[i]

    def st_wait(self, i):
        for o, m in self.st_peers():
            self.st_copy(i, o, m).wait_recv()

    def st_sum(self, i):
        total = self.sa[0, i]
        for role in range(1, 2 * self.nl):
            total = total + self.sa[role, i]
        return jnp.broadcast_to(total, (8, self.tc)).T[:, 0:1]

    def st_drain(self, i):
        for o, m in self.st_peers():
            self.st_copy(i, o, m).wait_send()

    def cs_refs(self, part, held, ss, sr):
        self.part, self.held, self.cs, self.cr = part, held, ss, sr

    def cs_copy(self, other, m):
        c, g = 1 - self.c if other else self.c, self.after(m)
        place = pl.ds(pl.multiple_of((self.c * self.nl + self.g) * 8, 8), 8)
        k = other * self.nl + m
        return self.copy(
            self.part.at[:, self.columns(c, g)], self.held.at[place], self.cs.at[k], self.cr.at[k], c, g
        )

    def cs_start(self, w_ref):
        for role in range(2 * self.nl):
            at = slice(role * self.fw, (role + 1) * self.fw)
            value = w_ref[:, at].astype(F32)
            self.part[:, at] = jnp.broadcast_to(row_sum(value * value), (8, self.fw))
        for o, m in self.st_peers():
            self.cs_copy(o, m).start()
        place = pl.ds(pl.multiple_of((self.c * self.nl + self.g) * 8, 8), 8)
        self.held[place, :] = self.part[:, self.columns(self.c, self.g)]

    def cs_total(self):
        for o, m in self.st_peers():
            self.cs_copy(o, m).wait_recv()
        return row_sum(self.held[...]) * 0.125

    def cs_drain(self):
        for o, m in self.st_peers():
            self.cs_copy(o, m).wait_send()


class Swap:
    def __init__(self, cm):
        self.cm = cm
        self.h = lax.axis_index("h")
        self.moves = cm.c != self.h
        self.partner = {"c": self.h, "h": cm.c}

    def far(self, src, dst, send, recv):
        return pltpu.make_async_remote_copy(
            src_ref=src, dst_ref=dst, send_sem=send, recv_sem=recv, device_id=self.partner, device_id_type=MESH
        )

    def start(self, src, dst, sems):
        @pl.when(self.moves)
        def _():
            self.far(src, dst, sems[0], sems[1]).start()

        @pl.when(jnp.logical_not(self.moves))
        def _():
            pltpu.make_async_copy(src, dst, sems[2]).start()

    def wait(self, src, dst, sems):
        @pl.when(self.moves)
        def _():
            self.far(src, dst, sems[0], sems[1]).wait_recv()

        @pl.when(jnp.logical_not(self.moves))
        def _():
            pltpu.make_async_copy(src, dst, sems[2]).wait()

    def drain(self, src, dst, sems):
        @pl.when(self.moves)
        def _():
            self.far(src, dst, sems[0], sems[1]).wait_send()


PIECES = 2


class RowMove:
    def __init__(self, swap, ny, part, e_ref, w_ref, ws, wr, wl, ys, yr):
        self.swap, self.ny, self.part, self.size = swap, ny, part, part // PIECES
        self.e, self.w = e_ref, w_ref
        self.ws, self.wr, self.wl, self.ys, self.yr = ws, wr, wl, ys, yr
        self.y = lax.axis_index("y")

    def rows(self, y, p):
        return pl.ds(pl.multiple_of(y * self.part + p * self.size, 16), self.size)

    def far(self, p):
        mine = self.rows(self.y, p)
        return self.swap.far(self.e.at[mine], self.w.at[mine], self.ws.at[p], self.wr.at[p])

    def near(self):
        every = pl.ds(0, self.part * self.ny)
        return pltpu.make_async_copy(self.e.at[every], self.w.at[every], self.wl)

    def shared(self, k, p, y):
        where = self.rows(y, p)
        return pltpu.make_async_remote_copy(
            src_ref=self.w.at[where], dst_ref=self.w.at[where],
            send_sem=self.ys.at[k - 1, p], recv_sem=self.yr.at[k - 1, p],
            device_id={"y": lax.rem(self.y + k, self.ny)}, device_id_type=MESH,
        )

    def start(self):
        @pl.when(self.swap.moves)
        def _():
            for p in range(PIECES):
                self.far(p).start()

        @pl.when(jnp.logical_not(self.swap.moves))
        def _():
            self.near().start()

    def pass_on(self):
        @pl.when(self.swap.moves)
        def _():
            for p in range(PIECES):
                self.far(p).wait_recv()
                for k in range(1, self.ny):
                    self.shared(k, p, self.y).start()

    def wait(self):
        @pl.when(self.swap.moves)
        def _():
            for k in range(1, self.ny):
                for p in range(PIECES):
                    self.shared(k, p, lax.rem(self.y + self.ny - k, self.ny)).wait_recv()

        @pl.when(jnp.logical_not(self.swap.moves))
        def _():
            self.near().wait()

    def drain(self):
        @pl.when(self.swap.moves)
        def _():
            for p in range(PIECES):
                self.far(p).wait_send()
                for k in range(1, self.ny):
                    self.shared(k, p, self.y).wait_send()


def row_move_scratch(ny):
    dma = pltpu.SemaphoreType.DMA
    between = dma((max(ny - 1, 1), PIECES))
    return [dma((PIECES,)), dma((PIECES,)), dma, between, between]


class Spread:
    def __init__(self, cm, ny, e_ref, w_ref, hs, hr, ps, pr, pn, ys, yr):
        self.cm, self.ny, self.e, self.w = cm, ny, e_ref, w_ref
        self.hs, self.hr, self.ps, self.pr, self.pn, self.ys, self.yr = hs, hr, ps, pr, pn, ys, yr
        self.y, self.h = lax.axis_index("y"), lax.axis_index("h")
        self.part = cm.fw // ny

    def place(self, hh, gg, yy):
        return self.w.at[
            pl.ds(pl.multiple_of((hh * self.cm.nl + gg) * self.cm.fw + yy * self.part, self.part), self.part)
        ]

    def piece(self, m):
        cm, to = self.cm, self.cm.after(m)
        return cm.copy(
            self.e.at[to], self.place(self.h, cm.g, self.y), self.ps.at[m], self.pr.at[m], cm.c, to
        )

    def here(self):
        return pltpu.make_async_copy(
            self.e.at[self.cm.g], self.place(self.h, self.cm.g, self.y), self.pn
        )

    def crossed(self, m, hh):
        where = self.place(hh, self.cm.before(m), self.y)
        return pltpu.make_async_remote_copy(
            src_ref=where, dst_ref=where, send_sem=self.hs.at[m], recv_sem=self.hr.at[m],
            device_id={"h": 1 - self.h}, device_id_type=MESH,
        )

    def shared(self, side, m, k, yy):
        where = self.place(self.h if side == 0 else 1 - self.h, self.cm.before(m), yy)
        return pltpu.make_async_remote_copy(
            src_ref=where, dst_ref=where,
            send_sem=self.ys.at[side, m, k - 1], recv_sem=self.yr.at[side, m, k - 1],
            device_id={"y": lax.rem(self.y + k, self.ny)}, device_id_type=MESH,
        )

    def start(self, steps):
        for m in steps:
            if m == 0:
                self.here().start()
            else:
                self.piece(m).start()

    def own(self, m):
        if m == 0:
            self.here().wait()
        else:
            self.piece(m).wait_recv()

    def start_crossing(self, m):
        self.crossed(m, self.h).start()

    def wait_crossing(self, m):
        self.crossed(m, 1 - self.h).wait_recv()

    def share(self, side, m):
        for k in range(1, self.ny):
            self.shared(side, m, k, self.y).start()

    def pass_own(self, m, cross=True):
        self.own(m)
        if cross:
            self.start_crossing(m)
        self.share(0, m)

    def pass_crossed(self, m, following=None):
        self.wait_crossing(m)
        if following is not None and following < self.cm.nl:
            self.start_crossing(following)
        self.share(1, m)

    def wait(self, side, steps):
        for m in steps:
            for k in range(1, self.ny):
                self.shared(side, m, k, lax.rem(self.y + self.ny - k, self.ny)).wait_recv()

    def drain_own(self, steps):
        for m in steps:
            if m > 0:
                self.piece(m).wait_send()

    def drain_crossing(self, steps):
        for m in steps:
            self.crossed(m, self.h).wait_send()

    def drain_shared(self, side, steps):
        for m in steps:
            for k in range(1, self.ny):
                self.shared(side, m, k, self.y).wait_send()


def spread_scratch(ny, nl):
    dma = pltpu.SemaphoreType.DMA
    return [
        dma((nl,)),
        dma((nl,)),
        dma((nl,)),
        dma((nl,)),
        dma,
        dma((2, nl, max(ny - 1, 1))),
        dma((2, nl, max(ny - 1, 1))),
    ]


def movers(ny):
    y, h = lax.axis_index("y"), lax.axis_index("h")
    return [{"y": lax.rem(y + k, ny)} for k in range(1, ny)] + [{"h": 1 - h}]


def ag_scratch(nl, nc, t, d):
    return [
        pltpu.VMEM((t, d), BF16),
        pltpu.SemaphoreType.DMA((nc,)),
        pltpu.SemaphoreType.DMA((nc, nl)),
        pltpu.SemaphoreType.DMA((nc, nl)),
        pltpu.SemaphoreType.DMA((nc, nl)),
        pltpu.SemaphoreType.DMA((nc, nl)),
    ]


def rs_scratch(nl, nc, tc, fw):
    return [
        pltpu.VMEM((nc, 2, nl, tc, fw), BF16),
        pltpu.VMEM((nc, nl, tc, fw), BF16),
        pltpu.VMEM((nc, nl - 1, tc, fw), BF16),
        pltpu.SemaphoreType.DMA((nc,)),
        pltpu.SemaphoreType.DMA((nc,)),
        pltpu.SemaphoreType.DMA((nc, nl)),
        pltpu.SemaphoreType.DMA((nc, nl)),
    ]


def st_scratch(nl, nc, t):
    return [
        pltpu.VMEM((2 * nl, nc, 1, t // nc), F32),
        pltpu.SemaphoreType.DMA((nc, 2 * nl)),
        pltpu.SemaphoreType.DMA((nc, 2 * nl)),
    ]


def cs_scratch(nl, d, fw):
    return [
        pltpu.VMEM((8, d), F32),
        pltpu.VMEM((2 * nl * 8, fw), F32),
        pltpu.SemaphoreType.DMA((2 * nl,)),
        pltpu.SemaphoreType.DMA((2 * nl,)),
    ]


VM = pl.BlockSpec(memory_space=pltpu.VMEM)
SM = pl.BlockSpec(memory_space=pltpu.SMEM)
ANY = pl.BlockSpec(memory_space=pl.ANY)


class Background:
    def __init__(self, loads, stores, step):
        self.loads, self.stores, self.step = loads, stores, step
        for copy in loads:
            copy.start()

    def ready(self):
        for copy in self.loads:
            copy.wait()

    def copy(self, k, i):
        held, out, sems = self.stores[k]
        rows = pl.ds(pl.multiple_of(i * self.step, self.step), self.step)
        return pltpu.make_async_copy(held.at[rows], out.at[rows], sems.at[i])

    def store(self, i, *which):
        for k in which:
            self.copy(k, i).start()

    def stored(self, i):
        for k in self.stores:
            self.copy(k, i).wait()


def call(kernel, name, outs, in_specs, out_specs, scratch, collective, us, args, late=(), flow=(), step=1, aliases=None):
    extra = {}
    if collective is not None:
        extra = {"collective_id": collective, "has_side_effects": True}
    single = not isinstance(outs, tuple)
    results = (outs,) if single else outs
    in_specs, out_specs = list(in_specs), [out_specs] if single else list(out_specs)
    n_in, n_out, n_scratch = len(args), len(results), len(scratch)
    dma = pltpu.SemaphoreType.DMA
    more = []
    for k in late:
        in_specs[k] = ANY
        more += [pltpu.VMEM(args[k].shape, args[k].dtype), dma]
    for k in flow:
        out_specs[k] = ANY
        more += [pltpu.VMEM(results[k].shape, results[k].dtype), dma((results[k].shape[0] // step,))]

    def whole(*refs):
        ins, results_here = list(refs[:n_in]), list(refs[n_in : n_in + n_out])
        own = refs[n_in + n_out : n_in + n_out + n_scratch]
        extras = list(refs[n_in + n_out + n_scratch :])
        loads, stores = [], {}
        for k in late:
            held, sem = extras.pop(0), extras.pop(0)
            loads.append(pltpu.make_async_copy(ins[k], held, sem))
            ins[k] = held
        for k in flow:
            held, sems = extras.pop(0), extras.pop(0)
            stores[k] = (held, results_here[k], sems)
            results_here[k] = held
        kernel(Background(loads, stores, step), *ins, *results_here, *own)

    return pl.pallas_call(
        whole,
        name=name,
        out_shape=outs,
        in_specs=in_specs,
        out_specs=out_specs[0] if single else tuple(out_specs),
        scratch_shapes=scratch + more,
        input_output_aliases=aliases or {},
        compiler_params=pltpu.CompilerParams(vmem_limit_bytes=VMEM_LIMIT, **extra),
        cost_estimate=pl.CostEstimate(
            flops=int(us * 5e8), bytes_accessed=int(us * 3e6), transcendentals=0
        ),
    )(*args)


def shape(s, dtype):
    return jax.ShapeDtypeStruct(s, dtype)


def ones_rows(values):
    folded = values[:, :LANES]
    for k in range(1, values.shape[1] // LANES):
        folded = folded + values[:, k * LANES : (k + 1) * LANES]
    return nt(jnp.ones((8, LANES), F32), folded, HIGHEST)


def row_sum(values):
    return jnp.sum(values, axis=0, keepdims=True)


def down_part(nf, ny):
    return -(-(-(-nf // ny)) // (16 * PIECES)) * 16 * PIECES


def merged_tile(frozen, down, up):
    down_high, up_high = down.astype(BF16), up.astype(BF16)
    down_low = (down - down_high.astype(F32)).astype(BF16)
    up_low = (up - up_high.astype(F32)).astype(BF16)
    low = nn(down_high, up_high) + (nn(down_high, up_low) + nn(down_low, up_high))
    return frozen.astype(F32) + SCALE * low


def qkv_forward(
    cfg, ny, npad, nf, x_in, w_qkv, a_qkv, b_qkv, tail_qkv, gains, w_out, small, small_gu, segments, turns,
    w_gu, a_gu, b_gu, tail_gu, w_down, a_down, b_down, a_out, b_out,
):
    t, fw, d, nl, nc, tc = cfg
    width = 3 * fw
    wide = width + LANES
    part = fw // ny
    down_rows = down_part(nf, ny) * ny
    ff_half = w_gu.shape[2] // 2

    def kernel(
        io, x_ref, wq_hbm, aq_ref, bq_ref, tq_ref, gain_ref, wout_ref, m_ref, mg_ref, seg_ref, ta_ref, tb_ref,
        wg_hbm, ag_ref, bg_ref, tg_ref, wdown_ref, ad_ref, bd_ref, ao_ref, bo_ref,
        xs_ref, w_ref, wo_ref, ms_ref, mgs_ref, sc_ref, sq_ref, qkv_ref, lora_ref, rate_ref, eg_ref, ed_ref, wgs_ref, out_ref, cos_ref, sin_ref, sgc_ref, sgr_ref,
        full, own, sd, rd, sc, rc, keep, xs_s, xs_r, xs_l, small_sems,
        hs, hr, ps, pr, pn, ys, yr, os, orr, ol, oys, oyr,
        e_ref, wq, wg, wload, eo_ref, sg, place, aq_t, ag_t, ao_t, ghs, ghr, gps, gpr, gpn, gys, gyr,
    ):
        cm = Comm(nl, nc, tc, fw, out_by_one=0.9375)
        cm.ag_refs(xs_ref, full, own, sd, rd, sc, rc)
        swap = Swap(cm)
        weights = Spread(cm, ny, e_ref, w_ref, hs, hr, ps, pr, pn, ys, yr)
        mine = pl.ds(pl.multiple_of(weights.y * part, part), part)
        load_q = pltpu.make_async_copy(
            wq_hbm.at[:, mine, pl.ds(pl.multiple_of(cm.c * (d // 2), LANES), d // 2)], wq, wload.at[0]
        )
        load_g = pltpu.make_async_copy(
            wg_hbm.at[:, mine, pl.ds(pl.multiple_of(cm.c * ff_half, LANES), ff_half)], wg, wload.at[1]
        )
        load_q.start()
        load_g.start()
        later = Spread(cm, ny, eg_ref, wgs_ref, ghs, ghr, gps, gpr, gpn, gys, gyr)
        output = RowMove(swap, ny, fw // ny, eo_ref, wo_ref, os, orr, ol, oys, oyr)
        cm.barrier(movers(ny), [swap.partner])

        def token_swap(i):
            rows = cm.rows(i)
            return x_ref.at[rows], xs_ref.at[rows], (xs_s.at[i], xs_r.at[i], xs_l.at[i])

        m_swap = (m_ref, ms_ref, tuple(small_sems.at[k] for k in range(3)))
        mg_swap = (mg_ref, mgs_ref, tuple(small_sems.at[k] for k in range(3, 6)))

        seg_swap = (seg_ref, sg, tuple(small_sems.at[k] for k in range(6, 9)))

        def start_swap(i, carry_on):
            swap.start(*token_swap(i))
            return carry_on

        lax.fori_loop(0, min(WINDOW, nc), start_swap, 0)
        swap.start(*m_swap)
        swap.start(*mg_swap)
        swap.start(*seg_swap)
        for k in range(3):
            aq_t[k] = aq_ref[k].T
        load_q.wait()
        gain_attn, gain_ffn = gain_ref[mine, 0:1], gain_ref[mine, 1:2]
        for gg in range(nl):
            columns = pl.ds(pl.multiple_of((cm.c * nl + gg) * fw, fw), fw)
            for k in range(3):
                tile = merged_tile(wq[k, :, gg * fw : (gg + 1) * fw], aq_t[k, mine, :], bq_ref[k, :, columns])
                e_ref[gg, :, k * fw : (k + 1) * fw] = (tile * gain_attn).astype(BF16)
            e_ref[gg, :, width:] = tq_ref[mine, :]
        weights.start(range(nl))

        def gate_up(gg):
            off = gg * nf % LANES
            window = -(-(off + nf) // LANES) * LANES
            for k in range(2):
                raw = wg[k, :, gg * nf - off : gg * nf - off + window].astype(F32)
                if off:
                    raw = pltpu.roll(raw, window - off, 1)
                tile = merged_tile(raw[:, :npad], ag_t[k, mine, :], bg_ref[k, cm.c * nl + gg]) * gain_ffn
                lane = lax.broadcasted_iota(jnp.int32, tile.shape, 1)
                eg_ref[gg, :, k * npad : (k + 1) * npad] = jnp.where(
                    lane < nf, tile, tg_ref[k, mine, :].astype(F32)
                ).astype(BF16)

        def merged_rows(k):
            if k == 0:
                if down_rows > nf:
                    ed_ref[nf:, :] = jnp.zeros((down_rows - nf, ed_ref.shape[1]), BF16)
                ed_ref[:nf, d:] = jnp.zeros((nf, LANES), BF16)
                ed_ref[:nf, d : d + RANK] = ad_ref[...].astype(BF16)
                eo_ref[:, d:] = jnp.zeros((fw, LANES), BF16)
                eo_ref[:, d : d + RANK] = ao_t[...].astype(BF16)
            for n in (2 * k, 2 * k + 1):
                at = slice(n * fw, (n + 1) * fw)
                eo_ref[:, at] = merged_tile(wout_ref[:, at], ao_t[...], bo_ref[:, at]).astype(BF16)
                ed_ref[:nf, at] = merged_tile(wdown_ref[:, at], ad_ref[...], bd_ref[:, at]).astype(BF16)

        def gather(i, carry_on):
            swap.wait(*token_swap(i))

            @pl.when(i + WINDOW < nc)
            def _():
                swap.start(*token_swap(i + WINDOW))

            cm.ag_send(i)
            return carry_on

        def forward(i, carry_on):
            cm.ag_step(i, more=False)
            return carry_on

        weights.pass_own(0)
        half = nc // 2
        lax.fori_loop(0, half, gather, 0)
        weights.pass_own(1)
        lax.fori_loop(half, nc, gather, 0)
        for m in range(2, nl):
            weights.pass_own(m, cross=False)
        load_g.wait()
        io.ready()
        for k in range(2):
            ag_t[k] = ag_ref[k].T
        ao_t[...] = ao_ref[...].T
        for m in range(nl):
            lax.fori_loop(nc * m // nl, nc * (m + 1) // nl, forward, 0)
            gate_up(m)
            weights.pass_crossed(m, m + 2)
            merged_rows(m)
        output.start()
        later.start(range(EARLY + 1))
        for m in range(EARLY):
            later.own(m)
            later.start_crossing(m)
        cm.ag_step(jnp.int32(nc), more=False)

        def stored(i):
            rows = cm.rows(i)
            return pltpu.make_async_copy(full.at[rows], out_ref.at[rows], keep.at[i])

        swap.wait(*seg_swap)
        number = sg[...]
        begin = jnp.zeros((1, t), F32)
        for n in range(1, SEGMENTS):
            before = jnp.sum(jnp.where(number < n, 1.0, 0.0), axis=1, keepdims=True)
            begin = jnp.where(number == n, before, begin)
        standing = lax.broadcasted_iota(jnp.int32, (1, t), 1).astype(F32) - begin
        high = jnp.floor(standing * (1.0 / 32.0))
        place[0:1, :] = high.astype(jnp.int32)
        place[1:2, :] = (standing - 32.0 * high).astype(jnp.int32)
        sgr_ref[...] = jnp.broadcast_to(number, (8, t))

        def turn_tables(rows):
            def chosen(row, count):
                return jnp.where(lax.broadcasted_iota(jnp.int32, (count, tc), 0) == row, 1.0, 0.0)

            def looked_up(row, table):
                parts = tn(chosen(row, 32).astype(BF16), table)
                both = parts[:, : 2 * HD] + parts[:, 2 * HD :]
                return both[:, :HD], both[:, HD:]

            ca, sa = looked_up(place[0:1, rows], ta_ref[...])
            cb, sb = looked_up(place[1:2, rows], tb_ref[...])
            sign = jnp.where(lax.broadcasted_iota(jnp.int32, (tc, HD), 1) < HD // 2, -1.0, 1.0)
            cos_ref[rows, :] = ca * cb - sa * sb
            sin_ref[rows, :] = (sa * cb + ca * sb) * sign
            numbers = lax.broadcasted_iota(jnp.int32, (SEGMENTS, LANES), 0).astype(F32)
            sgc_ref[rows, :] = tn(chosen(sgr_ref[0:1, rows], SEGMENTS), numbers).astype(jnp.int32)

        def rates(i, carry_on):
            turn_tables(cm.rows(i))
            cm.ag_wait(i)
            stored(i).start()
            wide_block = full[cm.rows(i), :].astype(F32)
            rate = lax.rsqrt(jnp.sum(wide_block * wide_block, axis=1, keepdims=True) / d + EPS)
            rate_ref[cm.rows(i), :] = jnp.broadcast_to(rate, (tc, LANES))
            return carry_on

        lax.fori_loop(0, nc, rates, 0)
        for side in (0, 1):
            weights.wait(side, range(nl))

        def squares(i, total):
            rows = pl.ds(pl.multiple_of(i * fw, fw), fw)
            tail = w_ref[rows, width:].astype(F32)
            gain = tail[:, 3 * RANK : 3 * RANK + 1] + tail[:, 3 * RANK + 1 : 3 * RANK + 2]
            value = w_ref[rows, :width].astype(F32) * (1.0 / gain)
            return total + row_sum(value * value)

        square = lax.fori_loop(0, 2 * nl, squares, jnp.zeros((1, width), F32))
        swap.wait(*m_swap)
        sq_ref[...] = jnp.broadcast_to(square, (8, width))
        for k in range(3):
            at = slice(k * fw, (k + 1) * fw)
            sc_ref[:, at] = jnp.broadcast_to(ms_ref[k : k + 1, :] * lax.rsqrt(square[:, at]), (8, fw))
        sc_ref[:, width:] = jnp.ones((8, LANES), F32)

        big = 2 * tc if nc % 2 == 0 else tc

        def body(i, carry_on):
            rows = pl.ds(pl.multiple_of(i * big, big), big)
            out = nn(full[rows, :], w_ref[...]) * rate_ref[rows, 0:1] * sc_ref[0:1, :]
            cosine_here, sine_here = cos_ref[rows, :], sin_ref[rows, :]
            for k in range(3):
                for hd in range(fw // HD):
                    at = k * fw + hd * HD
                    value = out[:, at : at + HD]
                    if k < 2:
                        value = value * cosine_here + pltpu.roll(value, HD // 2, 1) * sine_here
                    qkv_ref[rows, at : at + HD] = value.astype(BF16)
            lora_ref[rows, :] = out[:, width:].astype(BF16)
            for k in range(big // tc):
                io.store(i * (big // tc) + k, 7, 8, 9, 14, 15, 16)
            return carry_on

        lax.fori_loop(0, t // big, body, 0)
        output.pass_on()
        for m in range(EARLY):
            later.wait_crossing(m)
        later.own(EARLY)
        output.wait()
        swap.wait(*mg_swap)

        def drain(i, carry_on):
            cm.ag_drain(i)
            stored(i).wait()
            io.stored(i)
            swap.drain(*token_swap(i))
            return carry_on

        lax.fori_loop(0, nc, drain, 0)
        swap.drain(*m_swap)
        swap.drain(*mg_swap)
        swap.drain(*seg_swap)
        weights.drain_own(range(nl))
        weights.drain_crossing(range(nl))
        for side in (0, 1):
            weights.drain_shared(side, range(nl))
        later.drain_own(range(EARLY + 1))
        later.drain_crossing(range(EARLY))
        output.drain()

    dma = pltpu.SemaphoreType.DMA
    return call(
        kernel,
        "qkv_forward",
        (
            shape((t, fw), BF16),
            shape((d, wide), BF16),
            shape((fw, d + LANES), BF16),
            shape(small.shape, F32),
            shape(small_gu.shape, F32),
            shape((8, wide), F32),
            shape((8, width), F32),
            shape((t, width), BF16),
            shape((t, LANES), BF16),
            shape((t, LANES), F32),
            shape((nl, part, 2 * npad), BF16),
            shape((down_rows, d + LANES), BF16),
            shape((d, 2 * npad), BF16),
            shape((t, d), BF16),
            shape((t, HD), F32),
            shape((t, HD), F32),
            shape((t, LANES), jnp.int32),
            shape((8, t), jnp.int32),
        ),
        [VM, ANY] + [VM] * 10 + [ANY] + [VM] * 8,
        (VM,) * 12 + (ANY, ANY) + (VM,) * 4,
        ag_scratch(nl, nc, t, d)
        + [dma((nc,))] * 4
        + [dma((9,))]
        + spread_scratch(ny, nl)
        + row_move_scratch(ny)
        + [
            pltpu.VMEM((nl, part, wide), BF16),
            pltpu.VMEM((3, part, d // 2), BF16),
            pltpu.VMEM((2, part, ff_half), BF16),
            dma((2,)),
            pltpu.VMEM((fw, d + LANES), BF16),
            pltpu.VMEM((1, t), jnp.int32),
            pltpu.VMEM((8, t), jnp.int32),
            pltpu.VMEM((3, fw, RANK), F32),
            pltpu.VMEM((2, fw, RANK), F32),
            pltpu.VMEM((fw, RANK), F32),
        ]
        + spread_scratch(ny, nl),
        1,
        90,
        (
            x_in, w_qkv, a_qkv, b_qkv, tail_qkv, gains, w_out, small, small_gu, segments, *turns,
            w_gu, a_gu, b_gu, tail_gu, w_down, a_down, b_down, a_out, b_out,
        ),
        late=(6, 10, 11, *range(13, 21)),
        flow=(7, 8, 9, 14, 15, 16),
        step=tc,
    )


def allowed_of(key_segment, query_segment, j, i, block):
    key_at = j * block + lax.broadcasted_iota(jnp.int32, (block, block), 0)
    query_at = i * block + lax.broadcasted_iota(jnp.int32, (block, block), 1)
    return (key_segment == query_segment) & (key_at <= query_at)


def attention_forward(cfg, qkv, seg_column, seg_row, first_block, block):
    t, fw = cfg[0], cfg[1]
    heads = fw // HD

    def kernel(io, qkv_ref, sc_ref, sr_ref, first_ref, out_ref, lse_ref):
        def at(i):
            return pl.ds(pl.multiple_of(i * block, block), block)

        def columns(k, hd):
            return slice(k * fw + hd * HD, k * fw + (hd + 1) * HD)

        def one_query(i, carry_on):
            queries = [qkv_ref[at(i), columns(0, hd)] for hd in range(heads)]
            query_segment = sr_ref[0:1, at(i)]

            def one_key(j, carry):
                allowed = allowed_of(sc_ref[at(j), 0:1], query_segment, j, i, block)
                out = []
                for hd in range(heads):
                    top, total, acc = carry[hd]
                    s = nt(qkv_ref[at(j), columns(1, hd)], queries[hd]) * (HD**-0.5)
                    s = jnp.where(allowed, s, MASKED)
                    new = jnp.maximum(top, jnp.max(s, axis=0, keepdims=True))
                    p = jnp.exp(s - new)
                    shrink = jnp.exp(top - new)
                    total = total * shrink + jnp.sum(p, axis=0, keepdims=True)
                    acc = acc * shrink + tn(qkv_ref[at(j), columns(2, hd)], p.astype(BF16))
                    out.append((new, total, acc))
                return tuple(out)

            first = (
                jnp.full((1, block), MASKED, F32),
                jnp.zeros((1, block), F32),
                jnp.zeros((HD, block), F32),
            )
            out = lax.fori_loop(first_ref[i], i + 1, one_key, (first,) * heads)
            for hd in range(heads):
                top, total, acc = out[hd]
                out_ref[at(i), hd * HD : (hd + 1) * HD] = (acc / total).T.astype(BF16)
                lse_ref[hd * 8 : hd * 8 + 8, at(i)] = jnp.broadcast_to(
                    top + jnp.log(total), (8, block)
                )
            return carry_on

        lax.fori_loop(0, t // block, one_query, 0)

    return call(
        kernel,
        "attention_forward",
        (shape((t, fw), BF16), shape((heads * 8, t), F32)),
        [VM, VM, VM, SM],
        (VM, VM),
        [],
        None,
        15,
        (qkv, seg_column, seg_row, first_block),
    )


def out_forward(cfg, ny, npad, attended, weights, x, magnitude, w_gu, blocks, rows_down):
    t, fw, d, nl, nc, tc = cfg
    part = rows_down.shape[0] // ny

    def kernel(
        io, a_ref, w_ref, x_ref, m_ref, w_in, e_ref, ed_ref,
        mid_ref, u_ref, st_ref, sc_ref, sq_ref, lora_ref, wg_ref, wd_ref,
        sb, cb, gb, s1, r1, s2, r2, cpart, cheld, css, csr,
        hs, hr, ps, pr, pn, ys, yr, dws, dwr, dwl, dys, dyr,
    ):
        cm = Comm(nl, nc, tc, fw, back_by_two=0.0625)
        cm.rs_refs(sb, cb, gb, s1, r1, s2, r2)
        cm.cs_refs(cpart, cheld, css, csr)
        columns = Spread(cm, ny, e_ref, wg_ref, hs, hr, ps, pr, pn, ys, yr)
        swap = Swap(cm)
        down_rows = RowMove(swap, ny, part, ed_ref, wd_ref, dws, dwr, dwl, dys, dyr)
        cm.barrier(movers(ny), [swap.partner])
        down_rows.start()
        columns.start_crossing(EARLY)
        columns.start(range(EARLY + 1, nl))
        for m in range(EARLY):
            columns.share(0, m)
            columns.share(1, m)
        columns.share(0, EARLY)
        cm.cs_start(w_ref)
        if part * ny < npad:
            wd_ref[part * ny :, :] = jnp.zeros((npad - part * ny, wd_ref.shape[1]), BF16)
        def body(i, carry_on):
            @pl.when(i < nc)
            def _():
                block = a_ref[cm.rows(i), :]
                for role in range(2 * nl):
                    sb[i, role // nl, role % nl] = nn(
                        block, w_ref[:, role * fw : (role + 1) * fw]
                    ).astype(BF16)
                cm.rs_across(i).start()
                lora_ref[cm.rows(i), :] = nn(block, w_ref[:, d:]).astype(BF16)
                io.store(i, 5)

            cm.rs_steps(i)

            @pl.when(i == 3)
            def _():
                total = cm.cs_total()
                sq_ref[...] = jnp.broadcast_to(total, (8, fw))
                sc_ref[...] = jnp.broadcast_to(m_ref[3:4, :] * lax.rsqrt(total), (8, fw))

            @pl.when(i == 5)
            def _():
                down_rows.pass_on()

            @pl.when(i == 1)
            def _():
                columns.pass_own(EARLY + 1, cross=False)

            @pl.when(i == 3)
            def _():
                for m in range(EARLY + 2, nl):
                    columns.pass_own(m, cross=False)

            @pl.when(i == min(4, nc + 2))
            def _():
                columns.pass_crossed(EARLY, EARLY + 1)

            @pl.when(i == min(7, nc + 2))
            def _():
                columns.pass_crossed(EARLY + 1, EARLY + 2)

            @pl.when((i >= 3) & (i <= nc + 2))
            def _():
                rows = cm.rows(i - 3)
                middle = x_ref[rows, :].astype(F32) + cm.rs_total(i - 3) * sc_ref[0:1, :]
                mid_ref[rows, :] = middle
                u_ref[rows, :] = middle.astype(BF16)
                st_ref[i - 3] = ones_rows(middle * middle)[0:1, :]
                io.store(i - 3, 0, 1)

            return carry_on

        lax.fori_loop(0, nc + 3, body, 0)

        def drain(i, carry_on):
            cm.rs_drain(i)
            io.stored(i)
            return carry_on

        for m in range(EARLY + 2, nl):
            columns.pass_crossed(m, m + 1)
        for side in (0, 1):
            columns.wait(side, range(nl))
        down_rows.wait()
        lax.fori_loop(0, nc, drain, 0)
        cm.cs_drain()
        columns.drain_own(range(EARLY + 1, nl))
        columns.drain_crossing(range(EARLY, nl))
        for side in (0, 1):
            columns.drain_shared(side, range(nl))
        down_rows.drain()

    return call(
        kernel,
        "out_forward",
        (
            shape((t, fw), F32),
            shape((t, fw), BF16),
            shape((nc, 1, tc), F32),
            shape((8, fw), F32),
            shape((8, fw), F32),
            shape((t, LANES), BF16),
            shape(w_gu.shape, BF16),
            shape((npad, d + LANES), BF16),
        ),
        [VM] * 4 + [ANY, ANY, ANY],
        (VM,) * 6 + (ANY, VM),
        rs_scratch(nl, nc, tc, fw)
        + cs_scratch(nl, d, fw)
        + spread_scratch(ny, nl)
        + row_move_scratch(ny),
        2,
        90,
        (attended, weights, x, magnitude, w_gu, blocks, rows_down),
        flow=(0, 1, 5),
        step=tc,
        aliases={4: 6},
    )


def ffn_forward(cfg, npad, nf, u, stats, w_gu, m_gu, w_down, small, middle, cotangent):
    t, fw, d, nl, nc, tc = cfg

    def kernel(
        io, u_ref, st_ref, wg_ref, mg_ref, wd_ref, m_ref, mid_ref, cin_ref,
        gu_ref, hid_ref, out_ref, gm_ref, rate_ref, gp_ref, sg_ref, qg_ref, sd_ref, qd_ref, lora_ref, cot_ref, am_ref, ad_ref, uf_ref,
        full, own, sd, rd, sc, rc, sb, cb, gb, s1, r1, s2, r2, sa, ss, sr, cpart, cheld, css, csr, keep,
        cs_s, cs_r, cs_l,
    ):
        cm = Comm(nl, nc, tc, fw, out_by_one=0.5, back_by_two=0.5)
        cm.ag_refs(u_ref, full, own, sd, rd, sc, rc)
        cm.rs_refs(sb, cb, gb, s1, r1, s2, r2)
        cm.st_refs(st_ref, sa, ss, sr)
        cm.cs_refs(cpart, cheld, css, csr)
        swap = Swap(cm)
        cm.barrier((), [swap.partner])

        def cot_swap(i):
            rows = cm.rows(i)
            return cin_ref.at[rows], cot_ref.at[rows], (cs_s.at[i], cs_r.at[i], cs_l.at[i])

        cm.st_send(None)
        cm.ag_start()
        io.ready()

        def cot_out(i, carry_on):
            swap.start(*cot_swap(i))
            return carry_on


        def squares(i, total):
            rows = pl.ds(pl.multiple_of(i * fw, fw), fw)
            gain = (
                wg_ref[rows, nf + RANK : nf + RANK + 1].astype(F32)
                + wg_ref[rows, nf + RANK + 1 : nf + RANK + 2].astype(F32)
            )
            value = wg_ref[rows, :].astype(F32) * (1.0 / gain)
            return total + row_sum(value * value)

        square = lax.fori_loop(0, 2 * nl, squares, jnp.zeros((1, 2 * npad), F32))
        column = lax.rem(lax.broadcasted_iota(jnp.int32, (1, 2 * npad), 1), npad)
        square = jnp.where(column < nf, square, 1.0)
        qg_ref[...] = jnp.broadcast_to(square, (8, 2 * npad))
        sg_ref[...] = jnp.broadcast_to(mg_ref[...] * lax.rsqrt(square), (8, 2 * npad))
        cm.ag_ahead()
        gm_ref[...] = jnp.zeros_like(gm_ref)

        def stored(i):
            rows = cm.rows(i)
            return pltpu.make_async_copy(full.at[rows], uf_ref.at[rows], keep.at[i])

        cm.cs_start(wd_ref)
        lax.fori_loop(0, nc, cot_out, 0)

        def body(i, carry_on):
            @pl.when(i < nc)
            def _():
                cm.ag_step(i + 2)
                cm.ag_wait(i)

                @pl.when(i == 0)
                def _():
                    cm.st_wait(None)

                stored(i).start()
                rows = cm.rows(i)
                rate = lax.rsqrt(cm.st_sum(i) / d + EPS)
                rate_ref[rows, :] = jnp.broadcast_to(rate, (tc, LANES))
                out = nn(full[rows, :], wg_ref[...]) * rate * sg_ref[0:1, :]
                gu_ref[rows, :] = out.astype(BF16)
                gate, up = out[:, :npad], out[:, npad:]
                hidden = (gate / (1.0 + jnp.exp(-gate)) * up).astype(BF16)
                hid_ref[rows, :] = hidden
                for role in range(2 * nl):
                    sb[i, role // nl, role % nl] = nn(
                        hidden, wd_ref[:, role * fw : (role + 1) * fw]
                    ).astype(BF16)
                cm.rs_across(i).start()
                lora_ref[rows, :] = nn(hidden, wd_ref[:, d:]).astype(BF16)
                io.store(i, 0, 1, 4, 10)

            @pl.when(i == nc)
            def _():
                off = nf - (npad - LANES)
                for k in range(2):
                    tail = wg_ref[:, (k + 1) * npad - LANES : (k + 1) * npad]
                    _, gain = gain_rows(tail, off + RANK)
                    factor = (tail.astype(F32) / (gain * gain)).astype(BF16)
                    product = tn(factor, wg_ref[:, k * npad : (k + 1) * npad])
                    am_ref[k * RANK : (k + 1) * RANK, :] = product[off : off + RANK, :]
                ad_ref[...] = tn(wd_ref[:, d:], wd_ref[:, :d])[:RANK, :]

            cm.rs_steps(i)

            @pl.when(i == 3)
            def _():
                total = cm.cs_total()
                qd_ref[...] = jnp.broadcast_to(total, (8, fw))
                sd_ref[...] = jnp.broadcast_to(m_ref[4:5, :] * lax.rsqrt(total), (8, fw))

            @pl.when(i >= 3)
            def _():
                rows = cm.rows(i - 3)
                down = cm.rs_total(i - 3) * sd_ref[0:1, :]
                out_ref[rows, :] = (mid_ref[rows, :] + down).astype(BF16)
                swap.wait(*cot_swap(i - 3))
                seed = cot_ref[rows, :].astype(F32)
                gm_ref[0:1, :] += row_sum(seed * down)
                gp_ref[rows, :] = (seed * sd_ref[0:1, :]).astype(BF16)
                io.store(i - 3, 2, 5)

            return carry_on

        lax.fori_loop(0, nc + 3, body, 0)

        def drain(i, carry_on):
            cm.ag_drain(i)
            cm.rs_drain(i)
            stored(i).wait()
            io.stored(i)
            swap.drain(*cot_swap(i))
            return carry_on

        lax.fori_loop(0, nc, drain, 0)
        cm.st_drain(None)
        cm.cs_drain()

    dma = pltpu.SemaphoreType.DMA
    return call(
        kernel,
        "ffn_forward",
        (
            shape((t, 2 * npad), BF16),
            shape((t, npad), BF16),
            shape((t, fw), BF16),
            shape((8, fw), F32),
            shape((t, LANES), F32),
            shape((t, fw), BF16),
            shape((8, 2 * npad), F32),
            shape((8, 2 * npad), F32),
            shape((8, fw), F32),
            shape((8, fw), F32),
            shape((t, LANES), BF16),
            shape((t, fw), BF16),
            shape((2 * RANK, npad), F32),
            shape((RANK, d), F32),
            shape((t, d), BF16),
        ),
        [VM] * 8,
        (VM,) * 14 + (ANY,),
        ag_scratch(nl, nc, t, d)
        + rs_scratch(nl, nc, tc, fw)
        + st_scratch(nl, nc, t)
        + cs_scratch(nl, d, fw)
        + [dma((nc,))] * 4,
        3,
        110,
        (u, stats, w_gu, m_gu, w_down, small, middle, cotangent),
        late=(2, 4, 6),
        flow=(0, 1, 2, 4, 5, 10),
        step=tc,
    )


def ffn_backward(cfg, npad, gp, gu, w_gu, sc_gu, b_gu, w_down, b_down, rate, cotangent, middle, x, sc_out):
    t, fw, d, nl, nc, tc = cfg

    def kernel(
        io, gp_ref, gu_hbm, wg_ref, sg_ref, bg_ref, wd_ref, bd_ref, rate_ref, cot_ref, mid_ref, x_ref, so_ref,
        dm_ref, go_ref, gmo_ref, gm_ref, lg_ref, ld_ref, dp_hbm, gf_ref,
        full, own, sd, rd, sc, rc, sb, cb, gb, s1, r1, s2, r2, sa, ss, sr, st, gu_s, keep, load, save,
    ):
        cm = Comm(nl, nc, tc, fw)
        cm.ag_refs(gp_ref, full, own, sd, rd, sc, rc)
        cm.rs_refs(sb, cb, gb, s1, r1, s2, r2)
        cm.st_refs(st, sa, ss, sr)

        def loaded(i):
            rows = cm.rows(i)
            return pltpu.make_async_copy(gu_hbm.at[rows], gu_s.at[rows], load.at[i])

        def saved(i):
            rows = cm.rows(i)
            return pltpu.make_async_copy(gu_s.at[rows], dp_hbm.at[rows], save.at[i])

        def stored(i):
            rows = cm.rows(i)
            return pltpu.make_async_copy(full.at[rows], gf_ref.at[rows], keep.at[i])

        cm.barrier()
        cm.ag_start()

        def start_loads(i, carry_on):
            loaded(i).start()
            return carry_on

        lax.fori_loop(0, nc, start_loads, 0)
        cm.ag_ahead()
        io.ready()
        gm_ref[...] = jnp.zeros_like(gm_ref)
        gmo_ref[...] = jnp.zeros_like(gmo_ref)

        def body(i, carry_on):
            @pl.when(i < nc)
            def _():
                cm.ag_step(i + 2)
                cm.ag_wait(i)
                stored(i).start()
                loaded(i).wait()
                rows = cm.rows(i)
                block = full[rows, :]
                dh = nt(block, wd_ref[:, :d])
                ld_ref[rows, :] = nt(block, bd_ref[...]).astype(BF16)
                gate = gu_s[rows, :npad].astype(F32)
                up = gu_s[rows, npad:].astype(F32)
                sig = 1.0 / (1.0 + jnp.exp(-gate))
                dgate = dh * up * (sig * (1.0 + gate * (1.0 - sig)))
                dup = dh * (gate * sig)
                pg, pu = dgate * gate, dup * up
                gm_ref[0:1, :npad] += jnp.sum(pg, axis=0, keepdims=True)
                gm_ref[0:1, npad:] += jnp.sum(pu, axis=0, keepdims=True)
                st[i] = ones_rows(pg + pu)[0:1, :]
                cm.st_send(i)
                gu_s[rows, :npad] = (dgate * sg_ref[0:1, :npad]).astype(BF16)
                gu_s[rows, npad:] = (dup * sg_ref[0:1, npad:]).astype(BF16)
                saved(i).start()
                dp = gu_s[rows, :]
                lg_ref[rows, :] = (nt(dp, bg_ref[...].astype(BF16)) * rate_ref[rows, :]).astype(BF16)
                io.store(i, 4, 5)
                for role in range(2 * nl):
                    sb[i, role // nl, role % nl] = nt(
                        dp, wg_ref[role * fw : (role + 1) * fw, :]
                    ).astype(BF16)
                cm.rs_across(i).start()

            cm.rs_steps(i)

            @pl.when(i >= 3)
            def _():
                k = i - 3
                rows = cm.rows(k)
                cm.st_wait(k)
                r = rate_ref[rows, 0:1]
                inner = cm.st_sum(k)
                mid = mid_ref[rows, :]
                dm = (
                    cot_ref[rows, :].astype(F32)
                    + r * cm.rs_total(k)
                    - mid * (r * r * inner / d)
                )
                dm_ref[rows, :] = dm
                go_ref[rows, :] = (dm * so_ref[0:1, :]).astype(BF16)
                io.store(k, 0, 1)
                gmo_ref[0:1, :] += jnp.sum(
                    dm * (mid - x_ref[rows, :].astype(F32)), axis=0, keepdims=True
                )

            return carry_on

        lax.fori_loop(0, nc + 3, body, 0)

        def drain(i, carry_on):
            cm.ag_drain(i)
            cm.rs_drain(i)
            cm.st_drain(i)
            stored(i).wait()
            saved(i).wait()
            io.stored(i)
            return carry_on

        lax.fori_loop(0, nc, drain, 0)

    return call(
        kernel,
        "ffn_backward",
        (
            shape((t, fw), F32),
            shape((t, fw), BF16),
            shape((8, fw), F32),
            shape((8, 2 * npad), F32),
            shape((t, LANES), BF16),
            shape((t, LANES), BF16),
            shape((t, 2 * npad), BF16),
            shape((t, d), BF16),
        ),
        [VM, ANY] + [VM] * 10,
        (VM,) * 6 + (ANY, ANY),
        ag_scratch(nl, nc, t, d)
        + rs_scratch(nl, nc, tc, fw)
        + st_scratch(nl, nc, t)
        + [
            pltpu.VMEM((nc, 1, tc), F32),
            pltpu.VMEM((t, 2 * npad), BF16),
            pltpu.SemaphoreType.DMA((nc,)),
            pltpu.SemaphoreType.DMA((nc,)),
            pltpu.SemaphoreType.DMA((nc,)),
        ],
        4,
        120,
        (gp, gu, w_gu, sc_gu, b_gu, w_down, b_down, rate, cotangent, middle, x, sc_out),
        late=(2, 4, 5, 6, 7, 8, 9, 10),
        flow=(0, 1, 4, 5),
        step=tc,
    )


def gain_rows(tail, at):
    lane = lax.broadcasted_iota(jnp.int32, (8, LANES), 1)
    pick = jnp.where((lane == at) | (lane == at + 1), 1.0, 0.0).astype(BF16)
    column = tail[:, at : at + 1].astype(F32) + tail[:, at + 1 : at + 2].astype(F32)
    return nt(pick, tail)[0:1, :], column


class Stream:
    def __init__(self, sources, slots, sems, step):
        self.sources, self.slots, self.sems, self.step = sources, slots, sems, step

    def copies(self, i):
        rows = pl.ds(pl.multiple_of(i * self.step, self.step), self.step)
        slot = lax.rem(i, 2)
        return [
            pltpu.make_async_copy(src.at[rows, columns], held.at[slot], self.sems.at[k, slot])
            for k, ((src, columns), held) in enumerate(zip(self.sources, self.slots))
        ]

    def start(self, i):
        for copy in self.copies(i):
            copy.start()

    def wait(self, i):
        for copy in self.copies(i):
            copy.wait()
        return [held[lax.rem(i, 2)] for held in self.slots]


def stream_scratch(step, widths):
    return [pltpu.VMEM((2, step, n), BF16) for n in widths] + [pltpu.SemaphoreType.DMA((len(widths), 2))]


def out_backward(
    cfg, npad, nf, go, weights, b_out, sums, w_gu, w_down, up_gu, b_down, gm_gu, square_gu, m_gu,
    u_full, lg_gu, gu, dp_gu, hidden, lg_down, lora_down, gp_full, result, merged_low_gu, merged_low_down,
):
    t, fw, d, nl, nc, tc = cfg
    off = nf - (npad - LANES)
    widths = (d, LANES, LANES, LANES, 2 * npad, npad, LANES, LANES, d)

    def kernel(
        io, go_ref, w_ref, b_ref, s1_ref, s2_ref, s3_ref, s4_ref, wg_ref, wd_ref, up_ref, bd_ref, gm_ref, sq_ref, m_ref,
        uf_hbm, lg_hbm, gu_hbm, dp_hbm, hid_hbm, ld_hbm, lo2_hbm, gp_hbm, res_hbm, am_ref, amd_ref,
        da_ref, lo_ref, qs_ref, sh_ref, lc_ref, gf_ref, moved_ref,
        full, own, sd, rd, sc, rc, keep, qss, qsr, res_sems, acc_a, acc_g, acc_u, acc_d, acc_p, term, term_d, q_ref, *streams,
    ):
        cm = Comm(nl, nc, tc, fw, out_by_one=0.75)
        swap = Swap(cm)
        result_swap = (res_hbm, moved_ref, tuple(res_sems.at[k] for k in range(3)))
        cm.ag_refs(go_ref, full, own, sd, rd, sc, rc)
        every = lambda n: pl.ds(0, n)
        stream = Stream(
            [
                (uf_hbm, every(d)),
                (lg_hbm, every(LANES)),
                (gu_hbm, pl.ds(npad - LANES, LANES)),
                (gu_hbm, pl.ds(2 * npad - LANES, LANES)),
                (dp_hbm, every(2 * npad)),
                (hid_hbm, every(npad)),
                (ld_hbm, every(LANES)),
                (lo2_hbm, every(LANES)),
                (gp_hbm, every(d)),
            ],
            streams[:-1],
            streams[-1],
            tc,
        )
        stream.start(jnp.int32(0))
        cm.barrier((), [swap.partner])

        def ratio_copy(o, m):
            k = o * nl + m
            return cm.copy(
                q_ref, qs_ref.at[:, cm.columns(cm.c, cm.g)], qss.at[k], qsr.at[k], 1 - cm.c if o else cm.c, cm.after(m)
            )

        cm.ag_start()
        q_ref[...] = jnp.zeros_like(q_ref)
        q_ref[0:1, :] = -s1_ref[0:1, :] / s2_ref[0:1, :]
        q_ref[1:2, :] = -s3_ref[0:1, :] / s4_ref[0:1, :]
        for o, m in cm.st_peers():
            ratio_copy(o, m).start()
        qs_ref[:, cm.columns(cm.c, cm.g)] = q_ref[...]
        swap.start(*result_swap)
        for acc in (acc_a, acc_g, acc_u, acc_d, acc_p):
            acc[...] = jnp.zeros_like(acc)
        io.ready()
        ratio = -gm_ref[0:1, :] / sq_ref[0:1, :]
        term[...] = nt((up_ref[...] * ratio).astype(BF16), wg_ref[...])[: 2 * RANK, :]
        cm.ag_ahead()

        def stored(i):
            rows = cm.rows(i)
            return pltpu.make_async_copy(full.at[rows], gf_ref.at[rows], keep.at[i])

        def body(i, carry_on):
            cm.ag_step(i + 2)

            @pl.when(i == min(2, nc - 1))
            def _():
                for o, m in cm.st_peers():
                    ratio_copy(o, m).wait_recv()
                term_d[...] = nt((bd_ref[...].astype(F32) * qs_ref[1:2, :]).astype(BF16), wd_ref[:, :d])[:RANK, :]

            @pl.when(i + 1 < nc)
            def _():
                stream.start(i + 1)

            u, lg, low_g, low_u, dp, hid, ld, low_d, gp = stream.wait(i)
            acc_a[...] += tn(lg, u)
            acc_g[...] += tn(low_g, dp[:, :npad])
            acc_u[...] += tn(low_u, dp[:, npad:])
            acc_d[...] += tn(ld, hid)
            acc_p[...] += tn(low_d, gp)
            cm.ag_wait(i)
            stored(i).start()
            rows = cm.rows(i)
            block = full[rows, :]
            da_ref[rows, :] = nt(block, w_ref[:, :d]).astype(BF16)
            lo_ref[rows, :] = nt(block, b_ref[...]).astype(BF16)
            return carry_on

        lax.fori_loop(0, nc, body, 0)

        gain_row, _ = gain_rows(wg_ref[:, npad - LANES : npad], off + RANK)
        sh_ref[: 2 * RANK, :] = (SCALE * (acc_a[: 2 * RANK, :] * gain_row + term[...] / gain_row)).astype(BF16)
        for k, acc in enumerate((acc_g, acc_u)):
            at, low = slice(k * npad, (k + 1) * npad), slice(k * RANK, (k + 1) * RANK)
            lc_ref[(1 + k) * RANK : (2 + k) * RANK, :] = (
                SCALE * (acc[off : off + RANK, :] + am_ref[low, :] * ratio[:, at])
            ).astype(BF16)
            lc_ref[3 * RANK + k : 3 * RANK + k + 1, :] = (gm_ref[0:1, at] / m_ref[0:1, at]).astype(BF16)
        lc_ref[3 * RANK + 2 :, :] = jnp.zeros((RANK - 2, npad), BF16)
        lc_ref[:RANK, :] = (SCALE * (acc_d[:RANK, :] + term_d[...])).astype(BF16)
        sh_ref[2 * RANK :, :] = (SCALE * (acc_p[:RANK, :] + amd_ref[...] * qs_ref[1:2, :])).astype(BF16)

        def drain(i, carry_on):
            cm.ag_drain(i)
            stored(i).wait()
            return carry_on

        lax.fori_loop(0, nc, drain, 0)
        swap.wait(*result_swap)
        swap.drain(*result_swap)
        for o, m in cm.st_peers():
            ratio_copy(o, m).wait_send()

    dma = pltpu.SemaphoreType.DMA
    return call(
        kernel,
        "out_backward",
        (
            shape((t, fw), BF16),
            shape((t, LANES), BF16),
            shape((8, d), F32),
            shape((3 * RANK, d), BF16),
            shape((4 * RANK, npad), BF16),
            shape((t, d), BF16),
            shape((t, fw), BF16),
        ),
        [VM] * 14 + [ANY] * 9 + [VM] * 2,
        (VM,) * 5 + (ANY, ANY),
        ag_scratch(nl, nc, t, d)
        + [dma((nc,)), dma((2 * nl,)), dma((2 * nl,)), dma((3,))]
        + [pltpu.VMEM((LANES, n), F32) for n in (d, npad, npad, npad, d)]
        + [pltpu.VMEM((2 * RANK, d), F32), pltpu.VMEM((RANK, npad), F32), pltpu.VMEM((8, fw), F32)]
        + stream_scratch(tc, widths),
        5,
        60,
        (
            go, weights, b_out, *sums, w_gu, w_down, up_gu, b_down, gm_gu, square_gu, m_gu,
            u_full, lg_gu, gu, dp_gu, hidden, lg_down, lora_down, gp_full, result, merged_low_gu, merged_low_down,
        ),
        late=(1, 2, 7, 8, 9, 10),
    )


def attention_backward(
    cfg, qkv, attended, grad, lse, seg_column, seg_row, first_block, block, cosine, sine, scale, rate, b_qkv
):
    t, fw = cfg[0], cfg[1]
    heads = fw // HD
    width = 3 * fw

    def kernel(
        io, qkv_ref, att_ref, grad_ref, lse_ref, sc_ref, sr_ref, first_ref, cos_ref, sin_ref, scale_ref, rate_ref, b_ref,
        dp_ref, st_ref, gm_ref, lg_ref, dq, dk, dv,
    ):
        def at(i):
            return pl.ds(pl.multiple_of(i * block, block), block)

        def columns(k, hd):
            return slice(k * fw + hd * HD, k * fw + (hd + 1) * HD)

        gm_ref[...] = jnp.zeros_like(gm_ref)
        dk[...] = jnp.zeros_like(dk)
        dv[...] = jnp.zeros_like(dv)

        def one_query(i, carry_on):
            queries = [qkv_ref[at(i), columns(0, hd)] for hd in range(heads)]
            grads = [grad_ref[at(i), columns(0, hd)] for hd in range(heads)]
            deltas = [
                ones_rows(grads[hd].astype(F32) * att_ref[at(i), columns(0, hd)].astype(F32))[0:1, :]
                for hd in range(heads)
            ]
            query_segment = sr_ref[0:1, at(i)]

            def one_key(j, accs):
                allowed = allowed_of(sc_ref[at(j), 0:1], query_segment, j, i, block)
                out = []
                for hd in range(heads):
                    keys = qkv_ref[at(j), columns(1, hd)]
                    s = nt(keys, queries[hd]) * (HD**-0.5)
                    p = jnp.where(allowed, jnp.exp(s - lse_ref[hd * 8 : hd * 8 + 1, at(i)]), 0.0)
                    ds = (p * (nt(qkv_ref[at(j), columns(2, hd)], grads[hd]) - deltas[hd])).astype(BF16)
                    dv[hd, at(j), :] += nn(p.astype(BF16), grads[hd])
                    dk[hd, at(j), :] += nn(ds, queries[hd])
                    out.append(accs[hd] + tn(ds, keys))
                return tuple(out)

            accs = lax.fori_loop(first_ref[i], i + 1, one_key, (jnp.zeros((block, HD), F32),) * heads)
            for hd in range(heads):
                dq[hd, at(i), :] = accs[hd]
            return carry_on

        lax.fori_loop(0, t // block, one_query, 0)

        def finish(i, carry_on):
            rows = at(i)
            cosine_here, sine_here = cos_ref[rows, :], sin_ref[rows, :]
            inner = jnp.zeros((block, HD), F32)
            for hd in range(heads):
                for n, source in enumerate((dq, dk, dv)):
                    where = columns(n, hd)
                    dout = source[hd, rows, :]
                    value = qkv_ref[rows, where].astype(F32)
                    if n < 2:
                        dout = dout * (HD**-0.5)
                        dout = dout * cosine_here - pltpu.roll(dout, HD // 2, 1) * sine_here
                        value = value * cosine_here - pltpu.roll(value, HD // 2, 1) * sine_here
                    product = dout * value
                    inner = inner + product
                    gm_ref[0:1, where] += row_sum(product)
                    dp_ref[rows, where] = (dout * scale_ref[0:1, where]).astype(BF16)
            st_ref[i] = ones_rows(inner)[0:1, :]
            lg_ref[rows, :] = (nt(dp_ref[rows, :], b_ref[...].astype(BF16)) * rate_ref[rows, :]).astype(BF16)
            return carry_on

        lax.fori_loop(0, t // block, finish, 0)

    return call(
        kernel,
        "attention_backward",
        (
            shape((t, width), BF16),
            shape((t // block, 1, block), F32),
            shape((8, width), F32),
            shape((t, LANES), BF16),
        ),
        [VM] * 6 + [SM] + [VM] * 5,
        (VM,) * 4,
        [pltpu.VMEM((heads, t, HD), F32)] * 3,
        None,
        35,
        (qkv, attended, grad, lse, seg_column, seg_row, first_block, cosine, sine, scale, rate, b_qkv),
    )


def qkv_backward(
    cfg, ny, dp, stats, weights, rate, dm, x, shared, local_gu, w_out, up_qkv, b_out, ratios, gm_qkv, square_qkv,
    gm_out, gm_down, small, x_full, lg_qkv, lora_qkv, attended, lg_out, lora_out, go_full,
):
    t, fw, d, nl, nc, tc = cfg
    width = 3 * fw
    peers = 2 * nl
    step = 2 * tc if nc % 2 == 0 else tc
    parts = t // step
    widths = (d, LANES, LANES, fw, LANES, LANES, d)

    def kernel(
        io, dp_ref, st_ref, w_ref, rate_ref, dm_ref, x_ref, sh_ref, l_ref, wo_ref, up_ref, bo_ref, q_ref,
        gm_ref, sq_ref, gmo_ref, gmd_ref, m_ref, xf_hbm, lg_hbm, lq_hbm, at_hbm, lgo_hbm, lo_hbm, gf_hbm,
        out_ref, as_ref, bs_ref, ls_ref,
        sb, cb, gb, s1, r1, s2, r2, sa, ss, sr,
        stage, gs_s, gs_r, gs_l, group, gsum, gss, gsr, final_a, final_b, final_l, fs, fr, fl,
        a_ref, b_ref, acc_a, acc_b, acc_o, acc_p, *streams,
    ):
        cm = Comm(nl, nc, tc, fw, back_by_two=0.25)
        c, g = cm.c, cm.g
        y, h = lax.axis_index("y"), lax.axis_index("h")
        cm.rs_refs(sb, cb, gb, s1, r1, s2, r2)
        cm.st_refs(st_ref, sa, ss, sr)
        swap = Swap(cm)
        every = lambda n: pl.ds(0, n)
        stream = Stream(
            [
                (xf_hbm, every(d)),
                (lg_hbm, every(LANES)),
                (lq_hbm, every(LANES)),
                (at_hbm, every(fw)),
                (lgo_hbm, every(LANES)),
                (lo_hbm, every(LANES)),
                (gf_hbm, every(d)),
            ],
            streams[:-1],
            streams[-1],
            step,
        )
        stream.start(jnp.int32(0))
        senders = [
            {"y": lax.rem(y + ny - k, ny), "c": h, "h": hh} for k in range(1, ny) for hh in (0, 1)
        ]
        cm.barrier(senders + [{"c": h, "h": 1 - h}], [swap.partner, {"c": h, "h": h}])

        def gather_part(o, m):
            to_c, to_g = 1 - c if o else c, cm.after(m)
            k = o * nl + m
            return cm.copy(
                a_ref.at[:, cm.columns(to_c, to_g)], group.at[k], gss.at[k], gsr.at[k], to_c, to_g
            )

        def sums(k, e):
            device = {"y": lax.rem(y + k, ny), "c": lax.rem(c + e, 2), "h": c}
            slot = k * 2 + h
            return [
                pltpu.make_async_remote_copy(
                    src_ref=src, dst_ref=dst.at[slot], send_sem=fs.at[n, k * 2 + e], recv_sem=fr.at[n, slot],
                    device_id=device, device_id_type=MESH,
                )
                for n, (src, dst) in enumerate(((gsum, final_a), (b_ref, final_b), (l_ref, final_l)))
            ]

        def sums_here():
            return [
                pltpu.make_async_copy(src, dst.at[h], fl.at[n])
                for n, (src, dst) in enumerate(((gsum, final_a), (b_ref, final_b), (l_ref, final_l)))
            ]

        cm.st_send(None)
        for acc in (acc_a, acc_b, acc_o, acc_p):
            acc[...] = jnp.zeros_like(acc)

        def adapters(k):
            @pl.when(k + 1 < parts)
            def _():
                stream.start(k + 1)

            xf, lg, low_q, att, lg_o, low_o, gf = stream.wait(k)
            rows = pl.ds(pl.multiple_of(k * step, step), step)
            acc_a[...] += tn(lg, xf)
            acc_b[...] += tn(low_q, dp_ref[rows, :])
            acc_o[...] += tn(lg_o, att)
            acc_p[...] += tn(low_o, gf)

        def adapters_end():
            ratio = -gm_ref[0:1, :] / sq_ref[0:1, :]
            ratio_out = q_ref[0:1, :]
            tail = w_ref[:, width:]
            gain_row, gain_column = gain_rows(tail, 3 * RANK)
            term = nt((up_ref[...] * ratio).astype(BF16), w_ref[:, :width])
            a_ref[: 3 * RANK, :] = (
                SCALE * (acc_a[: 3 * RANK, :] * gain_row + term[: 3 * RANK, :] / gain_row)
            ).astype(BF16)
            merged = tn(
                (tail.astype(F32) / (gain_column * gain_column)).astype(BF16), w_ref[:, :width]
            )
            for k in range(3):
                at, low = slice(k * fw, (k + 1) * fw), slice(k * RANK, (k + 1) * RANK)
                b_ref[(1 + k) * RANK : (2 + k) * RANK, :] = (
                    SCALE * (acc_b[low, at] + merged[low, at] * ratio[:, at])
                ).astype(BF16)
                b_ref[4 * RANK + k : 4 * RANK + k + 1, :] = (gm_ref[0:1, at] / m_ref[k : k + 1, :]).astype(BF16)
            b_ref[4 * RANK + 3 : 4 * RANK + 4, :] = (gmo_ref[0:1, :] / m_ref[3:4, :]).astype(BF16)
            b_ref[4 * RANK + 4 : 4 * RANK + 5, :] = (gmd_ref[0:1, :] / m_ref[4:5, :]).astype(BF16)
            b_ref[4 * RANK + 5 :, :] = jnp.zeros((RANK - 5, fw), BF16)
            b_ref[:RANK, :] = (
                SCALE
                * (acc_o[:RANK, :] + nt((bo_ref[...].astype(F32) * ratio_out).astype(BF16), wo_ref[:, :d])[:RANK, :])
            ).astype(BF16)
            a_ref[3 * RANK : 4 * RANK, :] = (
                SCALE * (acc_p[:RANK, :] + tn(wo_ref[:, d:], wo_ref[:, :d])[:RANK, :] * ratio_out)
            ).astype(BF16)
            a_ref[4 * RANK :, :] = sh_ref[...]
            for o, m in cm.st_peers():
                gather_part(o, m).start()

        io.ready()

        def grad_swap(i):
            rows = cm.rows(i)
            return stage.at[rows], out_ref.at[rows], (gs_s.at[i], gs_r.at[i], gs_l.at[i])

        def body(i, carry_on):
            @pl.when(i < nc)
            def _():
                block = dp_ref[cm.rows(i), :]
                for role in range(2 * nl):
                    sb[i, role // nl, role % nl] = nt(
                        block, w_ref[role * fw : (role + 1) * fw, :width]
                    ).astype(BF16)
                cm.rs_across(i).start()

            cm.rs_steps(i)

            @pl.when(i < parts)
            def _():
                adapters(i)

            @pl.when(i == parts)
            def _():
                adapters_end()

            @pl.when(i == min(parts + 3, nc + 2))
            def _():
                total = a_ref[:, cm.columns(c, g)].astype(F32)
                for o, m in cm.st_peers():
                    gather_part(o, m).wait_recv()
                    total = total + group[o * nl + m].astype(F32)
                gsum[...] = total.astype(BF16)
                for k in range(ny):
                    for e in (0, 1):
                        if (k, e) == (0, 0):

                            @pl.when(swap.moves)
                            def _():
                                for copy in sums(0, 0):
                                    copy.start()

                            @pl.when(jnp.logical_not(swap.moves))
                            def _():
                                for copy in sums_here():
                                    copy.start()
                        else:
                            for copy in sums(k, e):
                                copy.start()

            @pl.when(i >= 3)
            def _():
                k = i - 3
                rows = cm.rows(k)

                @pl.when(k == 0)
                def _():
                    cm.st_wait(None)

                r = rate_ref[rows, 0:1]
                inner = cm.st_sum(k)
                stage[rows, :] = (
                    dm_ref[rows, :]
                    + r * cm.rs_total(k)
                    - x_ref[rows, :].astype(F32) * (r * r * inner / d)
                ).astype(BF16)
                swap.start(*grad_swap(k))

            return carry_on

        lax.fori_loop(0, nc + 3, body, 0)

        for k in range(ny):
            for hh in (0, 1):
                slot = k * 2 + hh

                def arrived():
                    for n, dst in enumerate((final_a, final_b, final_l)):
                        src = (gsum, b_ref, l_ref)[n]
                        pltpu.make_async_remote_copy(
                            src_ref=src, dst_ref=dst.at[slot], send_sem=fs.at[n, 0], recv_sem=fr.at[n, slot],
                            device_id=swap.partner, device_id_type=MESH,
                        ).wait_recv()

                if k == 0:
                    here = jnp.logical_and(c == h, h == hh)

                    @pl.when(here)
                    def _():
                        for copy in sums_here():
                            copy.wait()

                    @pl.when(jnp.logical_not(here))
                    def _():
                        arrived()
                else:
                    arrived()
        for out, held in ((as_ref, final_a), (bs_ref, final_b), (ls_ref, final_l)):
            total = held[0].astype(F32)
            for slot in range(1, 2 * ny):
                total = total + held[slot].astype(F32)
            out[...] = total

        def drain(i, carry_on):
            swap.wait(*grad_swap(i))
            cm.rs_drain(i)
            swap.drain(*grad_swap(i))
            return carry_on

        lax.fori_loop(0, nc, drain, 0)
        cm.st_drain(None)
        for o, m in cm.st_peers():
            gather_part(o, m).wait_send()
        for k in range(ny):
            for e in (0, 1):
                if (k, e) == (0, 0):

                    @pl.when(swap.moves)
                    def _():
                        for copy in sums(0, 0):
                            copy.wait_send()
                else:
                    for copy in sums(k, e):
                        copy.wait_send()

    dma = pltpu.SemaphoreType.DMA
    na, nb, ng = 7 * RANK, (5 * RANK, fw), local_gu.shape
    return call(
        kernel,
        "qkv_backward",
        (shape((t, fw), BF16), shape((na, fw), F32), shape(nb, F32), shape(ng, F32)),
        [VM] * 17 + [ANY] * 7,
        (VM,) * 4,
        rs_scratch(nl, nc, tc, fw)
        + st_scratch(nl, nc, t)
        + [pltpu.VMEM((t, fw), BF16)]
        + [dma((nc,))] * 3
        + [pltpu.VMEM((peers, na, fw), BF16), pltpu.VMEM((na, fw), BF16), dma((peers,)), dma((peers,))]
        + [
            pltpu.VMEM((2 * ny, na, fw), BF16),
            pltpu.VMEM((2 * ny, *nb), BF16),
            pltpu.VMEM((2 * ny, *ng), BF16),
            dma((3, 2 * ny)),
            dma((3, 2 * ny)),
            dma((3,)),
            pltpu.VMEM((na, d), BF16),
            pltpu.VMEM(nb, BF16),
        ]
        + [pltpu.VMEM((LANES, n), F32) for n in (d, width, fw, d)]
        + stream_scratch(step, widths),
        6,
        70,
        (
            dp, stats, weights, rate, dm, x, shared, local_gu, w_out, up_qkv, b_out, ratios, gm_qkv, square_qkv,
            gm_out, gm_down, small, x_full, lg_qkv, lora_qkv, attended, lg_out, lora_out, go_full,
        ),
        late=(2, 3, 4, 5, 6, 7, 8, 9, 10, 11),
    )


def last_step(fw, nf, grad, result, shared, local, local_gu):
    def kernel(
        io, g_ref, r_ref, s_ref, l_ref, u_ref,
        result_ref, grad_ref, aq_ref, bq_ref, mq_ref, ao_ref, bo_ref, mo_ref,
        ag_ref, bg_ref, mg_ref, ad_ref, bd_ref, md_ref,
    ):
        result_ref[...] = r_ref[...]
        grad_ref[...] = g_ref[...].astype(F32)
        for k in range(3):
            aq_ref[k] = s_ref[k * RANK : (k + 1) * RANK, :]
            bq_ref[k] = l_ref[(1 + k) * RANK : (2 + k) * RANK, :]
        for k in range(2):
            ag_ref[k] = s_ref[(4 + k) * RANK : (5 + k) * RANK, :]
            bg_ref[k] = u_ref[(1 + k) * RANK : (2 + k) * RANK, :nf]
        mq_ref[...] = l_ref[4 * RANK : 4 * RANK + 3, :]
        mg_ref[...] = u_ref[3 * RANK : 3 * RANK + 2, :nf]
        ao_ref[...] = l_ref[:RANK, :]
        bo_ref[...] = s_ref[3 * RANK : 4 * RANK, :]
        mo_ref[...] = l_ref[4 * RANK + 3 : 4 * RANK + 4, :]
        ad_ref[...] = u_ref[:RANK, :nf]
        bd_ref[...] = s_ref[6 * RANK :, :]
        md_ref[...] = l_ref[4 * RANK + 4 : 4 * RANK + 5, :]

    f = [
        (3, RANK, fw), (3, RANK, fw), (3, fw), (RANK, fw), (RANK, fw), (1, fw),
        (2, RANK, fw), (2, RANK, nf), (2, nf), (RANK, nf), (RANK, fw), (1, fw),
    ]
    return call(
        kernel,
        "last_step",
        (shape(result.shape, BF16), shape(grad.shape, F32), *[shape(v, F32) for v in f]),
        [VM] * 5,
        (VM,) * 14,
        [],
        None,
        4,
        (grad, result, shared, local, local_gu),
    )


def turn_constants():
    f = 10000.0 ** (-2.0 * np.arange(HD // 2) / HD)
    out = []
    for scale in (32.0, 1.0):
        angle = scale * np.arange(32)[:, None] * f[None, :]
        table = np.concatenate([np.cos(angle), np.cos(angle), np.sin(angle), np.sin(angle)], axis=1)
        high = table.astype(BF16)
        low = (table - high.astype(np.float64)).astype(BF16)
        out.append(jnp.asarray(np.concatenate([high, low], axis=1)))
    return out


def padded(rows, total):
    return jnp.pad(rows, ((0, 0), (0, total - rows.shape[1])))


def on_device(ny, nl, *operands):
    (
        inputs, segments, gain_attn, gain_ffn, w_qkv, a_qkv, b_qkv, m_qkv, w_out, a_out, b_out, m_out,
        w_gu, a_gu, b_gu, m_gu, w_down, a_down, b_down, m_down, cotangent,
    ) = operands
    t, fw = inputs.shape
    mp = 2 * nl
    d = mp * fw
    nf = m_gu.shape[1]
    npad = -(-(nf + RANK) // LANES) * LANES
    width = 3 * fw
    nc = t // 256 if t % 256 == 0 else 1
    block = t // nc
    cfg = (t, fw, d, nl, nc, block)
    y, c, h, g = (lax.axis_index(name) for name in ("y", "c", "h", "g"))
    role = c * nl + g

    def two_parts(gain):
        high = gain.astype(BF16)
        return [high[:, None], (gain - high.astype(F32)).astype(BF16)[:, None]]

    tail_qkv = padded(
        jnp.concatenate(
            [(a_qkv[k] * gain_attn[:, None]).astype(BF16) for k in range(3)] + two_parts(gain_attn), axis=1
        ),
        LANES,
    )
    tail_gu = jnp.stack(
        [
            jnp.pad(
                jnp.concatenate(
                    [(a_gu[k] * gain_ffn[:, None]).astype(BF16)] + two_parts(gain_ffn), axis=1
                ),
                ((0, 0), (nf, npad - nf - RANK - 2)),
            )
            for k in range(2)
        ]
    )
    gains = padded(jnp.stack([gain_attn, gain_ffn], axis=1), LANES)
    b_gu_padded = jnp.pad(
        b_gu.reshape(2, RANK, mp, nf), ((0, 0), (0, 0), (0, 0), (0, npad - nf))
    ).transpose(0, 2, 1, 3)
    small = jnp.concatenate([m_qkv, m_out[None], m_down[None], jnp.zeros((3, fw), F32)], axis=0)
    small_gu = jnp.broadcast_to(
        jnp.pad(m_gu, ((0, 0), (0, npad - nf)), constant_values=1.0).reshape(1, 2 * npad), (8, 2 * npad)
    )

    def take(whole, n, axis):
        return lax.dynamic_slice_in_dim(whole, role * n, n, axis)

    b_qkv_here = take(b_qkv, fw, 2)
    b_gu_here = take(b_gu, nf, 2)

    def block_up(up, pad):
        k, _, n = up.shape
        wide = jnp.pad(up, ((0, 0), (0, 0), (0, pad - n)))[:, :, None, :]
        same = (jnp.arange(k)[:, None] == jnp.arange(k)[None, :])[:, None, :, None]
        rows = jnp.where(same, wide, 0.0).reshape(k * RANK, k * pad)
        return jnp.pad(rows, ((0, LANES - k * RANK), (0, 0)))

    up_qkv = block_up(b_qkv_here, fw)
    up_gu = block_up(b_gu_here, npad)
    up_out = jnp.pad(b_out, ((0, LANES - RANK), (0, 0))).astype(BF16)
    up_down = jnp.pad(b_down, ((0, LANES - RANK), (0, 0))).astype(BF16)

    (
        x, weights_qkv, weights_out, small, small_gu, scale_qkv, square_qkv, qkv, lora_qkv_in, rate_attn,
        blocks_gu, rows_down, weights_gu, x_full, cosine, sine, seg_column, seg_row,
    ) = qkv_forward(
        cfg, ny, npad, nf, inputs, w_qkv, a_qkv.transpose(0, 2, 1), b_qkv, tail_qkv, gains, w_out, small, small_gu, segments,
        turn_constants(), w_gu, a_gu.transpose(0, 2, 1), b_gu_padded, tail_gu, w_down, a_down, b_down, a_out.T, b_out,
    )
    first_number = seg_row[0, ::block]
    first_block = jnp.sum((seg_row[0][None, :] < first_number[:, None]).astype(jnp.int32), axis=1) // block
    attended, lse = attention_forward(cfg, qkv, seg_column, seg_row, first_block, block)
    middle, u, stats, sc_out, square_out, lora_out, weights_gu, weights_down = out_forward(
        cfg, ny, npad, attended, weights_out, x, small, weights_gu, blocks_gu, rows_down
    )
    (
        gu, hidden, block_out, gm_down, rate_ffn, gp, scale_gu, square_gu, sc_down, square_down,
        lora_down, grad_seed, merged_low_gu, merged_low_down, u_full,
    ) = ffn_forward(
        cfg, npad, nf, u, stats, weights_gu, small_gu[0:1], weights_down, small, middle, cotangent
    )

    dm, go, gm_out, gm_gu, lg_gu, lg_down, dp_gu, gp_full = ffn_backward(
        cfg, npad, gp, gu, weights_gu, scale_gu, up_gu, weights_down, up_down, rate_ffn,
        grad_seed, middle, x, sc_out,
    )
    grad_attended, lg_out, ratios, shared, local_gu, go_full, block_out = out_backward(
        cfg, npad, nf, go, weights_out, up_out, (gm_out, square_out, gm_down, square_down), weights_gu, weights_down, up_gu, up_down, gm_gu, square_gu,
        small_gu, u_full, lg_gu, gu, dp_gu, hidden, lg_down, lora_down, gp_full, block_out,
        merged_low_gu, merged_low_down,
    )
    dp_qkv, inner, gm_qkv, lg_qkv = attention_backward(
        cfg, qkv, attended, grad_attended, lse, seg_column, seg_row, first_block, block, cosine, sine,
        scale_qkv, rate_attn, up_qkv,
    )

    grad_input, shared, local, local_gu = qkv_backward(
        cfg, ny, dp_qkv, inner, weights_qkv, rate_attn, dm, x, shared, local_gu, weights_out, up_qkv, up_out, ratios,
        gm_qkv, square_qkv, gm_out, gm_down, small, x_full, lg_qkv, lora_qkv_in, attended, lg_out, lora_out, go_full,
    )
    out = list(last_step(fw, nf, grad_input, block_out, shared, local, local_gu))
    out[2], out[8] = out[2].transpose(0, 2, 1), out[8].transpose(0, 2, 1)
    out[5], out[11] = out[5].T, out[11].T
    out[7], out[13] = out[7][0], out[13][0]
    return tuple(out)


def solution(mesh):
    dp, mp = mesh.shape["dp"], mesh.shape["mp"]
    ny, nl = dp // 2, mp // 2
    fine = Mesh(mesh.devices.reshape(ny, 2, 2, nl), ("y", "c", "h", "g"))
    rows, cols = ("y", "c"), ("h", "g")
    in_specs = (
        P(rows, cols),
        P(rows, None),
        P(cols),
        P(cols),
        P(None, cols, None),
        P(None, cols, None),
        P(),
        P(None, cols),
        P(cols, None),
        P(cols, None),
        P(),
        P(cols),
        P(None, cols, None),
        P(None, cols, None),
        P(),
        P(None, cols),
        P(cols, None),
        P(cols, None),
        P(),
        P(cols),
        P(rows, cols),
    )
    out_specs = (
        P(rows, cols),
        P(rows, cols),
        P(None, cols, None),
        P(None, None, cols),
        P(None, cols),
        P(cols, None),
        P(None, cols),
        P(cols),
        P(None, cols, None),
        P(None, None, cols),
        P(None, cols),
        P(cols, None),
        P(None, cols),
        P(cols),
    )
    return jax.shard_map(
        lambda *operands: on_device(ny, nl, *operands),
        mesh=fine,
        in_specs=in_specs,
        out_specs=out_specs,
        check_vma=False,
    )
```

```python
import jax
import jax.numpy as jnp
import numpy as np
from jax import lax
from jax.experimental import pallas as pl
from jax.experimental.pallas import tpu as pltpu
from jax.sharding import Mesh
from jax.sharding import PartitionSpec as P

HD = 128
RANK = 16
SCALE = 2.0
EPS = 1e-05
MASKED = -1e30
HIGHEST = lax.Precision.HIGHEST
MESH = pl.DeviceIdType.MESH
F32 = jnp.float32
BF16 = jnp.bfloat16
LANES = 128
SEGMENTS = 8
VMEM_LIMIT = 60 * 1024 * 1024


def nt(a, b, precision=None):
    return lax.dot_general(
        a, b, (((1,), (1,)), ((), ())), precision=precision, preferred_element_type=F32
    )


def tn(a, b, precision=None):
    return lax.dot_general(
        a, b, (((0,), (0,)), ((), ())), precision=precision, preferred_element_type=F32
    )


def nn(a, b, precision=None):
    return lax.dot_general(
        a, b, (((1,), (0,)), ((), ())), precision=precision, preferred_element_type=F32
    )


WINDOW = 2
EARLY = 1


class Comm:
    def __init__(self, nl, nc, tc, fw, out_by_one=0.5, back_by_two=0.5):
        self.nl, self.nc, self.tc, self.fw = nl, nc, tc, fw
        self.square = nl == 4
        self.cut = int(tc * out_by_one) // 16 * 16
        self.back = int(tc * back_by_two) // 16 * 16
        self.c = lax.axis_index("c")
        self.g = lax.axis_index("g")

    def rows(self, i):
        return pl.ds(pl.multiple_of(i * self.tc, self.tc), self.tc)

    def after(self, m):
        return lax.rem(self.g + m, self.nl)

    def before(self, m):
        return lax.rem(self.g + self.nl - m, self.nl)

    def columns(self, c, g):
        return pl.ds(pl.multiple_of((c * self.nl + g) * self.fw, self.fw), self.fw)

    def copy(self, src, dst, send, recv, c, g):
        return pltpu.make_async_remote_copy(
            src_ref=src,
            dst_ref=dst,
            send_sem=send,
            recv_sem=recv,
            device_id={"c": c, "g": g},
            device_id_type=MESH,
        )

    def barrier(self, others=(), one_more=None):
        sem = pltpu.get_barrier_semaphore()
        everyone = [
            {"c": 1 - self.c if other else self.c, "g": self.after(m)}
            for other in (0, 1)
            for m in range(self.nl)
            if (other, m) != (0, 0)
        ] + list(others)
        for device in everyone:
            pl.semaphore_signal(sem, inc=1, device_id=device, device_id_type=MESH)
        if one_more is None:
            pl.semaphore_wait(sem, len(everyone))
        else:
            apart = self.c - lax.axis_index("h")

            @pl.when(apart != 0)
            def _():
                for device in one_more:
                    pl.semaphore_signal(sem, inc=1, device_id=device, device_id_type=MESH)

            pl.semaphore_wait(sem, len(everyone) + len(one_more) * apart * apart)

    def other(self, m):
        if m == 1:
            return self.g + 1 - 2 * lax.rem(self.g, 2)
        return lax.rem(self.g + 2, 4) if m == 2 else 3 - self.g

    def comes_from(self, m):
        if m == 0:
            return self.g
        return self.other(m) if self.square else self.before(m)

    def goes_to(self, m):
        return self.other(m) if self.square else self.after(m)

    def some(self, i, way):
        cut = self.cut
        start, size = (0, cut) if way == 0 else (cut, self.tc - cut)
        return pl.ds(pl.multiple_of(i * self.tc + start, 16), size)

    def ag_refs(self, x, full, own, sd, rd, sc, rc):
        self.x, self.full, self.own = x, full, own
        self.sd, self.rd, self.sc, self.rc = sd, rd, sc, rc

    def ag_steps(self):
        return (1, 2) if self.square else range(1, self.nl)

    def ag_direct(self, i, m):
        rows = self.rows(i)
        return self.copy(
            self.x.at[rows],
            self.full.at[rows, self.columns(self.c, self.g)],
            self.sd.at[i, m],
            self.rd.at[i, m],
            self.c,
            self.goes_to(m),
        )

    def ag_relay(self, i, way):
        rows = self.some(i, way)
        columns = self.columns(self.c, self.other(2 - way))
        return self.copy(
            self.full.at[rows, columns],
            self.full.at[rows, columns],
            self.sd.at[i, 3 * way],
            self.rd.at[i, 3 * way],
            self.c,
            self.other(1 + way),
        )

    def ag_across(self, i, m):
        rows = self.rows(i)
        columns = self.columns(self.c, self.comes_from(m))
        src = self.x.at[rows] if m == 0 else self.full.at[rows, columns]
        return self.copy(
            src,
            self.full.at[rows, columns],
            self.sc.at[i, m],
            self.rc.at[i, m],
            1 - self.c,
            self.g,
        )

    def ag_own(self, i):
        rows = self.rows(i)
        return pltpu.make_async_copy(
            self.x.at[rows],
            self.full.at[rows, self.columns(self.c, self.g)],
            self.own.at[i],
        )

    def ag_send(self, i):
        for m in self.ag_steps():
            self.ag_direct(i, m).start()
        self.ag_across(i, 0).start()
        self.ag_own(i).start()

    def ag_start(self):
        for i in range(min(WINDOW, self.nc)):
            self.ag_send(jnp.int32(i))

    def ag_forward(self, i):
        for m in self.ag_steps():
            self.ag_direct(i, m).wait_recv()
        if self.square:
            for way in (0, 1):
                self.ag_relay(i, way).start()
        for m in self.ag_steps():
            self.ag_across(i, m).start()

    def ag_corner(self, i):
        if self.square:
            for way in (0, 1):
                self.ag_relay(i, way).wait_recv()
            self.ag_across(i, 3).start()

    def ag_step(self, i, more=True):
        @pl.when(i < self.nc)
        def _():
            self.ag_forward(i)

        if more:

            @pl.when(i + WINDOW < self.nc)
            def _():
                self.ag_send(i + WINDOW)

        @pl.when((i >= 1) & (i <= self.nc))
        def _():
            self.ag_corner(i - 1)

    def ag_ahead(self):
        self.ag_step(jnp.int32(0))
        self.ag_step(jnp.int32(1))

    def ag_wait(self, i):
        self.ag_own(i).wait()
        for m in range(self.nl):
            self.ag_across(i, m).wait_recv()

    def ag_drain(self, i):
        for m in self.ag_steps():
            self.ag_direct(i, m).wait_send()
        if self.square:
            for way in (0, 1):
                self.ag_relay(i, way).wait_send()
        for m in range(self.nl):
            self.ag_across(i, m).wait_send()

    def rs_refs(self, sb, cb, gb, s1, r1, s2, r2):
        self.sb, self.cb, self.gb = sb, cb, gb
        self.s1, self.r1, self.s2, self.r2 = s1, r1, s2, r2

    def rs_across(self, i):
        return self.copy(
            self.sb.at[i, 1 - self.c],
            self.cb.at[i],
            self.s1.at[i],
            self.r1.at[i],
            1 - self.c,
            self.g,
        )

    def rs_direct(self, i, m):
        to = self.goes_to(m)
        return self.copy(
            self.sb.at[i, self.c, to],
            self.gb.at[i, m - 1],
            self.s2.at[i, m],
            self.r2.at[i, m],
            self.c,
            to,
        )

    def rs_corner(self, i, way):
        rows = pl.ds(0, self.back) if way == 0 else pl.ds(self.back, self.tc - self.back)
        return self.copy(
            self.sb.at[i, self.c, self.other(3), rows],
            self.gb.at[i, 2, rows],
            self.s2.at[i, 3 * way],
            self.r2.at[i, 3 * way],
            self.c,
            self.other(2 - way),
        )

    def rs_middle(self, i):
        self.rs_across(i).wait_recv()
        for gp in range(self.nl):
            mine = self.sb[i, self.c, gp].astype(F32) + self.cb[i, gp].astype(F32)
            self.sb[i, self.c, gp] = mine.astype(BF16)
        if self.square:
            for way in (0, 1):
                self.rs_corner(i, way).start()
        else:
            for m in range(1, self.nl):
                self.rs_direct(i, m).start()

    def rs_second(self, i):
        if not self.square:
            return
        for way in (0, 1):
            self.rs_corner(i, way).wait_recv()
            rows = pl.ds(0, self.back) if way == 0 else pl.ds(self.back, self.tc - self.back)
            to = self.other(1 + way)
            both = self.sb[i, self.c, to, rows].astype(F32) + self.gb[i, 2, rows].astype(F32)
            self.sb[i, self.c, to, rows] = both.astype(BF16)
        for m in (1, 2):
            self.rs_direct(i, m).start()

    def rs_total(self, i):
        steps = (1, 2) if self.square else range(1, self.nl)
        for m in steps:
            self.rs_direct(i, m).wait_recv()
        total = self.sb[i, self.c, self.g].astype(F32)
        for m in steps:
            total = total + self.gb[i, m - 1].astype(F32)
        return total

    def rs_drain(self, i):
        self.rs_across(i).wait_send()
        if self.square:
            for way in (0, 1):
                self.rs_corner(i, way).wait_send()
        for m in (1, 2) if self.square else range(1, self.nl):
            self.rs_direct(i, m).wait_send()

    def rs_steps(self, i):
        @pl.when((i >= 1) & (i <= self.nc))
        def _():
            self.rs_middle(i - 1)

        @pl.when((i >= 2) & (i <= self.nc + 1))
        def _():
            self.rs_second(i - 2)

    def st_refs(self, st, sa, ss, sr):
        self.st, self.sa, self.ss, self.sr = st, sa, ss, sr

    def st_copy(self, i, other, m):
        mine = self.c * self.nl + self.g
        src, dst = (self.st, self.sa.at[mine]) if i is None else (self.st.at[i], self.sa.at[mine, i])
        i = 0 if i is None else i
        return self.copy(
            src,
            dst,
            self.ss.at[i, other * self.nl + m],
            self.sr.at[i, other * self.nl + m],
            1 - self.c if other else self.c,
            self.after(m),
        )

    def st_peers(self):
        return [(o, m) for o in (0, 1) for m in range(self.nl) if (o, m) != (0, 0)]

    def st_send(self, i):
        for o, m in self.st_peers():
            self.st_copy(i, o, m).start()
        mine = self.c * self.nl + self.g
        if i is None:
            self.sa[mine] = self.st[...]
        else:
            self.sa[mine, i] = self.st[i]

    def st_wait(self, i):
        for o, m in self.st_peers():
            self.st_copy(i, o, m).wait_recv()

    def st_sum(self, i):
        total = self.sa[0, i]
        for role in range(1, 2 * self.nl):
            total = total + self.sa[role, i]
        return jnp.broadcast_to(total, (8, self.tc)).T[:, 0:1]

    def st_drain(self, i):
        for o, m in self.st_peers():
            self.st_copy(i, o, m).wait_send()

    def cs_refs(self, part, held, ss, sr):
        self.part, self.held, self.cs, self.cr = part, held, ss, sr

    def cs_copy(self, other, m):
        c, g = 1 - self.c if other else self.c, self.after(m)
        place = pl.ds(pl.multiple_of((self.c * self.nl + self.g) * 8, 8), 8)
        k = other * self.nl + m
        return self.copy(
            self.part.at[:, self.columns(c, g)], self.held.at[place], self.cs.at[k], self.cr.at[k], c, g
        )

    def cs_start(self, w_ref):
        for role in range(2 * self.nl):
            at = slice(role * self.fw, (role + 1) * self.fw)
            value = w_ref[:, at].astype(F32)
            self.part[:, at] = jnp.broadcast_to(row_sum(value * value), (8, self.fw))
        for o, m in self.st_peers():
            self.cs_copy(o, m).start()
        place = pl.ds(pl.multiple_of((self.c * self.nl + self.g) * 8, 8), 8)
        self.held[place, :] = self.part[:, self.columns(self.c, self.g)]

    def cs_total(self):
        for o, m in self.st_peers():
            self.cs_copy(o, m).wait_recv()
        return row_sum(self.held[...]) * 0.125

    def cs_drain(self):
        for o, m in self.st_peers():
            self.cs_copy(o, m).wait_send()


class Swap:
    def __init__(self, cm):
        self.cm = cm
        self.h = lax.axis_index("h")
        self.moves = cm.c != self.h
        self.partner = {"c": self.h, "h": cm.c}

    def far(self, src, dst, send, recv):
        return pltpu.make_async_remote_copy(
            src_ref=src, dst_ref=dst, send_sem=send, recv_sem=recv, device_id=self.partner, device_id_type=MESH
        )

    def start(self, src, dst, sems):
        @pl.when(self.moves)
        def _():
            self.far(src, dst, sems[0], sems[1]).start()

        @pl.when(jnp.logical_not(self.moves))
        def _():
            pltpu.make_async_copy(src, dst, sems[2]).start()

    def wait(self, src, dst, sems):
        @pl.when(self.moves)
        def _():
            self.far(src, dst, sems[0], sems[1]).wait_recv()

        @pl.when(jnp.logical_not(self.moves))
        def _():
            pltpu.make_async_copy(src, dst, sems[2]).wait()

    def drain(self, src, dst, sems):
        @pl.when(self.moves)
        def _():
            self.far(src, dst, sems[0], sems[1]).wait_send()


PIECES = 2


class RowMove:
    def __init__(self, swap, ny, part, e_ref, w_ref, ws, wr, wl, ys, yr):
        self.swap, self.ny, self.part, self.size = swap, ny, part, part // PIECES
        self.e, self.w = e_ref, w_ref
        self.ws, self.wr, self.wl, self.ys, self.yr = ws, wr, wl, ys, yr
        self.y = lax.axis_index("y")

    def rows(self, y, p):
        return pl.ds(pl.multiple_of(y * self.part + p * self.size, 16), self.size)

    def far(self, p):
        mine = self.rows(self.y, p)
        return self.swap.far(self.e.at[mine], self.w.at[mine], self.ws.at[p], self.wr.at[p])

    def near(self):
        every = pl.ds(0, self.part * self.ny)
        return pltpu.make_async_copy(self.e.at[every], self.w.at[every], self.wl)

    def shared(self, k, p, y):
        where = self.rows(y, p)
        return pltpu.make_async_remote_copy(
            src_ref=self.w.at[where], dst_ref=self.w.at[where],
            send_sem=self.ys.at[k - 1, p], recv_sem=self.yr.at[k - 1, p],
            device_id={"y": lax.rem(self.y + k, self.ny)}, device_id_type=MESH,
        )

    def start(self):
        @pl.when(self.swap.moves)
        def _():
            for p in range(PIECES):
                self.far(p).start()

        @pl.when(jnp.logical_not(self.swap.moves))
        def _():
            self.near().start()

    def pass_on(self):
        @pl.when(self.swap.moves)
        def _():
            for p in range(PIECES):
                self.far(p).wait_recv()
                for k in range(1, self.ny):
                    self.shared(k, p, self.y).start()

    def wait(self):
        @pl.when(self.swap.moves)
        def _():
            for k in range(1, self.ny):
                for p in range(PIECES):
                    self.shared(k, p, lax.rem(self.y + self.ny - k, self.ny)).wait_recv()

        @pl.when(jnp.logical_not(self.swap.moves))
        def _():
            self.near().wait()

    def drain(self):
        @pl.when(self.swap.moves)
        def _():
            for p in range(PIECES):
                self.far(p).wait_send()
                for k in range(1, self.ny):
                    self.shared(k, p, self.y).wait_send()


def row_move_scratch(ny):
    dma = pltpu.SemaphoreType.DMA
    between = dma((max(ny - 1, 1), PIECES))
    return [dma((PIECES,)), dma((PIECES,)), dma, between, between]


class Spread:
    def __init__(self, cm, ny, e_ref, w_ref, hs, hr, ps, pr, pn, ys, yr):
        self.cm, self.ny, self.e, self.w = cm, ny, e_ref, w_ref
        self.hs, self.hr, self.ps, self.pr, self.pn, self.ys, self.yr = hs, hr, ps, pr, pn, ys, yr
        self.y, self.h = lax.axis_index("y"), lax.axis_index("h")
        self.part = cm.fw // ny

    def place(self, hh, gg, yy):
        return self.w.at[
            pl.ds(pl.multiple_of((hh * self.cm.nl + gg) * self.cm.fw + yy * self.part, self.part), self.part)
        ]

    def piece(self, m):
        cm, to = self.cm, self.cm.after(m)
        return cm.copy(
            self.e.at[to], self.place(self.h, cm.g, self.y), self.ps.at[m], self.pr.at[m], cm.c, to
        )

    def here(self):
        return pltpu.make_async_copy(
            self.e.at[self.cm.g], self.place(self.h, self.cm.g, self.y), self.pn
        )

    def crossed(self, m, hh):
        where = self.place(hh, self.cm.before(m), self.y)
        return pltpu.make_async_remote_copy(
            src_ref=where, dst_ref=where, send_sem=self.hs.at[m], recv_sem=self.hr.at[m],
            device_id={"h": 1 - self.h}, device_id_type=MESH,
        )

    def shared(self, side, m, k, yy):
        where = self.place(self.h if side == 0 else 1 - self.h, self.cm.before(m), yy)
        return pltpu.make_async_remote_copy(
            src_ref=where, dst_ref=where,
            send_sem=self.ys.at[side, m, k - 1], recv_sem=self.yr.at[side, m, k - 1],
            device_id={"y": lax.rem(self.y + k, self.ny)}, device_id_type=MESH,
        )

    def start(self, steps):
        for m in steps:
            if m == 0:
                self.here().start()
            else:
                self.piece(m).start()

    def own(self, m):
        if m == 0:
            self.here().wait()
        else:
            self.piece(m).wait_recv()

    def start_crossing(self, m):
        self.crossed(m, self.h).start()

    def wait_crossing(self, m):
        self.crossed(m, 1 - self.h).wait_recv()

    def share(self, side, m):
        for k in range(1, self.ny):
            self.shared(side, m, k, self.y).start()

    def pass_own(self, m, cross=True):
        self.own(m)
        if cross:
            self.start_crossing(m)
        self.share(0, m)

    def pass_crossed(self, m, following=None):
        self.wait_crossing(m)
        if following is not None and following < self.cm.nl:
            self.start_crossing(following)
        self.share(1, m)

    def wait(self, side, steps):
        for m in steps:
            for k in range(1, self.ny):
                self.shared(side, m, k, lax.rem(self.y + self.ny - k, self.ny)).wait_recv()

    def drain_own(self, steps):
        for m in steps:
            if m > 0:
                self.piece(m).wait_send()

    def drain_crossing(self, steps):
        for m in steps:
            self.crossed(m, self.h).wait_send()

    def drain_shared(self, side, steps):
        for m in steps:
            for k in range(1, self.ny):
                self.shared(side, m, k, self.y).wait_send()


def spread_scratch(ny, nl):
    dma = pltpu.SemaphoreType.DMA
    return [
        dma((nl,)),
        dma((nl,)),
        dma((nl,)),
        dma((nl,)),
        dma,
        dma((2, nl, max(ny - 1, 1))),
        dma((2, nl, max(ny - 1, 1))),
    ]


def movers(ny):
    y, h = lax.axis_index("y"), lax.axis_index("h")
    return [{"y": lax.rem(y + k, ny)} for k in range(1, ny)] + [{"h": 1 - h}]


def ag_scratch(nl, nc, t, d):
    return [
        pltpu.VMEM((t, d), BF16),
        pltpu.SemaphoreType.DMA((nc,)),
        pltpu.SemaphoreType.DMA((nc, nl)),
        pltpu.SemaphoreType.DMA((nc, nl)),
        pltpu.SemaphoreType.DMA((nc, nl)),
        pltpu.SemaphoreType.DMA((nc, nl)),
    ]


def rs_scratch(nl, nc, tc, fw):
    return [
        pltpu.VMEM((nc, 2, nl, tc, fw), BF16),
        pltpu.VMEM((nc, nl, tc, fw), BF16),
        pltpu.VMEM((nc, nl - 1, tc, fw), BF16),
        pltpu.SemaphoreType.DMA((nc,)),
        pltpu.SemaphoreType.DMA((nc,)),
        pltpu.SemaphoreType.DMA((nc, nl)),
        pltpu.SemaphoreType.DMA((nc, nl)),
    ]


def st_scratch(nl, nc, t):
    return [
        pltpu.VMEM((2 * nl, nc, 1, t // nc), F32),
        pltpu.SemaphoreType.DMA((nc, 2 * nl)),
        pltpu.SemaphoreType.DMA((nc, 2 * nl)),
    ]


def cs_scratch(nl, d, fw):
    return [
        pltpu.VMEM((8, d), F32),
        pltpu.VMEM((2 * nl * 8, fw), F32),
        pltpu.SemaphoreType.DMA((2 * nl,)),
        pltpu.SemaphoreType.DMA((2 * nl,)),
    ]


VM = pl.BlockSpec(memory_space=pltpu.VMEM)
SM = pl.BlockSpec(memory_space=pltpu.SMEM)
ANY = pl.BlockSpec(memory_space=pl.ANY)


class Background:
    def __init__(self, loads, stores, step):
        self.loads, self.stores, self.step = loads, stores, step
        for copy in loads:
            copy.start()

    def ready(self):
        for copy in self.loads:
            copy.wait()

    def copy(self, k, i):
        held, out, sems = self.stores[k]
        rows = pl.ds(pl.multiple_of(i * self.step, self.step), self.step)
        return pltpu.make_async_copy(held.at[rows], out.at[rows], sems.at[i])

    def store(self, i, *which):
        for k in which:
            self.copy(k, i).start()

    def stored(self, i):
        for k in self.stores:
            self.copy(k, i).wait()


def call(kernel, name, outs, in_specs, out_specs, scratch, collective, us, args, late=(), flow=(), step=1, aliases=None):
    extra = {}
    if collective is not None:
        extra = {"collective_id": collective, "has_side_effects": True}
    single = not isinstance(outs, tuple)
    results = (outs,) if single else outs
    in_specs, out_specs = list(in_specs), [out_specs] if single else list(out_specs)
    n_in, n_out, n_scratch = len(args), len(results), len(scratch)
    dma = pltpu.SemaphoreType.DMA
    more = []
    for k in late:
        in_specs[k] = ANY
        more += [pltpu.VMEM(args[k].shape, args[k].dtype), dma]
    for k in flow:
        out_specs[k] = ANY
        more += [pltpu.VMEM(results[k].shape, results[k].dtype), dma((results[k].shape[0] // step,))]

    def whole(*refs):
        ins, results_here = list(refs[:n_in]), list(refs[n_in : n_in + n_out])
        own = refs[n_in + n_out : n_in + n_out + n_scratch]
        extras = list(refs[n_in + n_out + n_scratch :])
        loads, stores = [], {}
        for k in late:
            held, sem = extras.pop(0), extras.pop(0)
            loads.append(pltpu.make_async_copy(ins[k], held, sem))
            ins[k] = held
        for k in flow:
            held, sems = extras.pop(0), extras.pop(0)
            stores[k] = (held, results_here[k], sems)
            results_here[k] = held
        kernel(Background(loads, stores, step), *ins, *results_here, *own)

    return pl.pallas_call(
        whole,
        name=name,
        out_shape=outs,
        in_specs=in_specs,
        out_specs=out_specs[0] if single else tuple(out_specs),
        scratch_shapes=scratch + more,
        input_output_aliases=aliases or {},
        compiler_params=pltpu.CompilerParams(vmem_limit_bytes=VMEM_LIMIT, **extra),
        cost_estimate=pl.CostEstimate(
            flops=int(us * 5e8), bytes_accessed=int(us * 3e6), transcendentals=0
        ),
    )(*args)


def shape(s, dtype):
    return jax.ShapeDtypeStruct(s, dtype)


def ones_rows(values):
    folded = values[:, :LANES]
    for k in range(1, values.shape[1] // LANES):
        folded = folded + values[:, k * LANES : (k + 1) * LANES]
    return nt(jnp.ones((8, LANES), F32), folded, HIGHEST)


def row_sum(values):
    return jnp.sum(values, axis=0, keepdims=True)


def down_part(nf, ny):
    return -(-(-(-nf // ny)) // (16 * PIECES)) * 16 * PIECES


def merged_tile(frozen, down, up):
    down_high, up_high = down.astype(BF16), up.astype(BF16)
    down_low = (down - down_high.astype(F32)).astype(BF16)
    up_low = (up - up_high.astype(F32)).astype(BF16)
    low = nn(down_high, up_high) + (nn(down_high, up_low) + nn(down_low, up_high))
    return frozen.astype(F32) + SCALE * low


def qkv_forward(
    cfg, ny, npad, nf, x_in, w_qkv, a_qkv, b_qkv, tail_qkv, gains, w_out, small, small_gu, segments, turns,
    w_gu, a_gu, b_gu, tail_gu, w_down, a_down, b_down, a_out, b_out,
):
    t, fw, d, nl, nc, tc = cfg
    width = 3 * fw
    wide = width + LANES
    part = fw // ny
    down_rows = down_part(nf, ny) * ny
    ff_half = w_gu.shape[2] // 2

    def kernel(
        io, x_ref, wq_hbm, aq_ref, bq_ref, tq_ref, gain_ref, wout_ref, m_ref, mg_ref, seg_ref, ta_ref, tb_ref,
        wg_hbm, ag_ref, bg_ref, tg_ref, wdown_ref, ad_ref, bd_ref, ao_ref, bo_ref,
        xs_ref, w_ref, wo_ref, ms_ref, mgs_ref, sc_ref, sq_ref, qkv_ref, lora_ref, rate_ref, eg_ref, ed_ref, wgs_ref, out_ref, cos_ref, sin_ref, sgc_ref, sgr_ref,
        full, own, sd, rd, sc, rc, keep, xs_s, xs_r, xs_l, small_sems,
        hs, hr, ps, pr, pn, ys, yr, os, orr, ol, oys, oyr,
        e_ref, wq, wg, wload, eo_ref, sg, place, aq_t, ag_t, ao_t, ghs, ghr, gps, gpr, gpn, gys, gyr,
    ):
        cm = Comm(nl, nc, tc, fw, out_by_one=0.9375)
        cm.ag_refs(xs_ref, full, own, sd, rd, sc, rc)
        swap = Swap(cm)
        weights = Spread(cm, ny, e_ref, w_ref, hs, hr, ps, pr, pn, ys, yr)
        mine = pl.ds(pl.multiple_of(weights.y * part, part), part)
        load_q = pltpu.make_async_copy(
            wq_hbm.at[:, mine, pl.ds(pl.multiple_of(cm.c * (d // 2), LANES), d // 2)], wq, wload.at[0]
        )
        load_g = pltpu.make_async_copy(
            wg_hbm.at[:, mine, pl.ds(pl.multiple_of(cm.c * ff_half, LANES), ff_half)], wg, wload.at[1]
        )
        load_q.start()
        load_g.start()
        later = Spread(cm, ny, eg_ref, wgs_ref, ghs, ghr, gps, gpr, gpn, gys, gyr)
        output = RowMove(swap, ny, fw // ny, eo_ref, wo_ref, os, orr, ol, oys, oyr)
        cm.barrier(movers(ny), [swap.partner])

        def token_swap(i):
            rows = cm.rows(i)
            return x_ref.at[rows], xs_ref.at[rows], (xs_s.at[i], xs_r.at[i], xs_l.at[i])

        m_swap = (m_ref, ms_ref, tuple(small_sems.at[k] for k in range(3)))
        mg_swap = (mg_ref, mgs_ref, tuple(small_sems.at[k] for k in range(3, 6)))

        seg_swap = (seg_ref, sg, tuple(small_sems.at[k] for k in range(6, 9)))

        def start_swap(i, carry_on):
            swap.start(*token_swap(i))
            return carry_on

        lax.fori_loop(0, min(WINDOW, nc), start_swap, 0)
        swap.start(*m_swap)
        swap.start(*mg_swap)
        swap.start(*seg_swap)
        for k in range(3):
            aq_t[k] = aq_ref[k].T
        load_q.wait()
        gain_attn, gain_ffn = gain_ref[mine, 0:1], gain_ref[mine, 1:2]
        for gg in range(nl):
            columns = pl.ds(pl.multiple_of((cm.c * nl + gg) * fw, fw), fw)
            for k in range(3):
                tile = merged_tile(wq[k, :, gg * fw : (gg + 1) * fw], aq_t[k, mine, :], bq_ref[k, :, columns])
                e_ref[gg, :, k * fw : (k + 1) * fw] = (tile * gain_attn).astype(BF16)
            e_ref[gg, :, width:] = tq_ref[mine, :]
        weights.start(range(nl))

        def gate_up(gg):
            off = gg * nf % LANES
            window = -(-(off + nf) // LANES) * LANES
            for k in range(2):
                raw = wg[k, :, gg * nf - off : gg * nf - off + window].astype(F32)
                if off:
                    raw = pltpu.roll(raw, window - off, 1)
                tile = merged_tile(raw[:, :npad], ag_t[k, mine, :], bg_ref[k, cm.c * nl + gg]) * gain_ffn
                lane = lax.broadcasted_iota(jnp.int32, tile.shape, 1)
                eg_ref[gg, :, k * npad : (k + 1) * npad] = jnp.where(
                    lane < nf, tile, tg_ref[k, mine, :].astype(F32)
                ).astype(BF16)

        def merged_rows(k):
            if k == 0:
                if down_rows > nf:
                    ed_ref[nf:, :] = jnp.zeros((down_rows - nf, ed_ref.shape[1]), BF16)
                ed_ref[:nf, d:] = jnp.zeros((nf, LANES), BF16)
                ed_ref[:nf, d : d + RANK] = ad_ref[...].astype(BF16)
                eo_ref[:, d:] = jnp.zeros((fw, LANES), BF16)
                eo_ref[:, d : d + RANK] = ao_t[...].astype(BF16)
            for n in (2 * k, 2 * k + 1):
                at = slice(n * fw, (n + 1) * fw)
                eo_ref[:, at] = merged_tile(wout_ref[:, at], ao_t[...], bo_ref[:, at]).astype(BF16)
                ed_ref[:nf, at] = merged_tile(wdown_ref[:, at], ad_ref[...], bd_ref[:, at]).astype(BF16)

        def gather(i, carry_on):
            swap.wait(*token_swap(i))

            @pl.when(i + WINDOW < nc)
            def _():
                swap.start(*token_swap(i + WINDOW))

            cm.ag_send(i)
            return carry_on

        def forward(i, carry_on):
            cm.ag_step(i, more=False)
            return carry_on

        weights.pass_own(0)
        half = nc // 2
        lax.fori_loop(0, half, gather, 0)
        weights.pass_own(1)
        lax.fori_loop(half, nc, gather, 0)
        for m in range(2, nl):
            weights.pass_own(m, cross=False)
        load_g.wait()
        io.ready()
        for k in range(2):
            ag_t[k] = ag_ref[k].T
        ao_t[...] = ao_ref[...].T
        for m in range(nl):
            lax.fori_loop(nc * m // nl, nc * (m + 1) // nl, forward, 0)
            gate_up(m)
            weights.pass_crossed(m, m + 2)
            merged_rows(m)
        output.start()
        later.start(range(EARLY + 1))
        for m in range(EARLY):
            later.own(m)
            later.start_crossing(m)
        cm.ag_step(jnp.int32(nc), more=False)

        def stored(i):
            rows = cm.rows(i)
            return pltpu.make_async_copy(full.at[rows], out_ref.at[rows], keep.at[i])

        swap.wait(*seg_swap)
        number = sg[...]
        begin = jnp.zeros((1, t), F32)
        for n in range(1, SEGMENTS):
            before = jnp.sum(jnp.where(number < n, 1.0, 0.0), axis=1, keepdims=True)
            begin = jnp.where(number == n, before, begin)
        standing = lax.broadcasted_iota(jnp.int32, (1, t), 1).astype(F32) - begin
        high = jnp.floor(standing * (1.0 / 32.0))
        place[0:1, :] = high.astype(jnp.int32)
        place[1:2, :] = (standing - 32.0 * high).astype(jnp.int32)
        sgr_ref[...] = jnp.broadcast_to(number, (8, t))

        def turn_tables(rows):
            def chosen(row, count):
                return jnp.where(lax.broadcasted_iota(jnp.int32, (count, tc), 0) == row, 1.0, 0.0)

            def looked_up(row, table):
                parts = tn(chosen(row, 32).astype(BF16), table)
                both = parts[:, : 2 * HD] + parts[:, 2 * HD :]
                return both[:, :HD], both[:, HD:]

            ca, sa = looked_up(place[0:1, rows], ta_ref[...])
            cb, sb = looked_up(place[1:2, rows], tb_ref[...])
            sign = jnp.where(lax.broadcasted_iota(jnp.int32, (tc, HD), 1) < HD // 2, -1.0, 1.0)
            cos_ref[rows, :] = ca * cb - sa * sb
            sin_ref[rows, :] = (sa * cb + ca * sb) * sign
            numbers = lax.broadcasted_iota(jnp.int32, (SEGMENTS, LANES), 0).astype(F32)
            sgc_ref[rows, :] = tn(chosen(sgr_ref[0:1, rows], SEGMENTS), numbers).astype(jnp.int32)

        def rates(i, carry_on):
            turn_tables(cm.rows(i))
            cm.ag_wait(i)
            stored(i).start()
            wide_block = full[cm.rows(i), :].astype(F32)
            rate = lax.rsqrt(jnp.sum(wide_block * wide_block, axis=1, keepdims=True) / d + EPS)
            rate_ref[cm.rows(i), :] = jnp.broadcast_to(rate, (tc, LANES))
            return carry_on

        lax.fori_loop(0, nc, rates, 0)
        for side in (0, 1):
            weights.wait(side, range(nl))

        def squares(i, total):
            rows = pl.ds(pl.multiple_of(i * fw, fw), fw)
            tail = w_ref[rows, width:].astype(F32)
            gain = tail[:, 3 * RANK : 3 * RANK + 1] + tail[:, 3 * RANK + 1 : 3 * RANK + 2]
            value = w_ref[rows, :width].astype(F32) * (1.0 / gain)
            return total + row_sum(value * value)

        square = lax.fori_loop(0, 2 * nl, squares, jnp.zeros((1, width), F32))
        swap.wait(*m_swap)
        sq_ref[...] = jnp.broadcast_to(square, (8, width))
        for k in range(3):
            at = slice(k * fw, (k + 1) * fw)
            sc_ref[:, at] = jnp.broadcast_to(ms_ref[k : k + 1, :] * lax.rsqrt(square[:, at]), (8, fw))
        sc_ref[:, width:] = jnp.ones((8, LANES), F32)

        big = 2 * tc if nc % 2 == 0 else tc

        def body(i, carry_on):
            rows = pl.ds(pl.multiple_of(i * big, big), big)
            out = nn(full[rows, :], w_ref[...]) * rate_ref[rows, 0:1] * sc_ref[0:1, :]
            cosine_here, sine_here = cos_ref[rows, :], sin_ref[rows, :]
            for k in range(3):
                for hd in range(fw // HD):
                    at = k * fw + hd * HD
                    value = out[:, at : at + HD]
                    if k < 2:
                        value = value * cosine_here + pltpu.roll(value, HD // 2, 1) * sine_here
                    qkv_ref[rows, at : at + HD] = value.astype(BF16)
            lora_ref[rows, :] = out[:, width:].astype(BF16)
            for k in range(big // tc):
                io.store(i * (big // tc) + k, 7, 8, 9, 14, 15, 16)
            return carry_on

        lax.fori_loop(0, t // big, body, 0)
        output.pass_on()
        for m in range(EARLY):
            later.wait_crossing(m)
        later.own(EARLY)
        output.wait()
        swap.wait(*mg_swap)

        def drain(i, carry_on):
            cm.ag_drain(i)
            stored(i).wait()
            io.stored(i)
            swap.drain(*token_swap(i))
            return carry_on

        lax.fori_loop(0, nc, drain, 0)
        swap.drain(*m_swap)
        swap.drain(*mg_swap)
        swap.drain(*seg_swap)
        weights.drain_own(range(nl))
        weights.drain_crossing(range(nl))
        for side in (0, 1):
            weights.drain_shared(side, range(nl))
        later.drain_own(range(EARLY + 1))
        later.drain_crossing(range(EARLY))
        output.drain()

    dma = pltpu.SemaphoreType.DMA
    return call(
        kernel,
        "qkv_forward",
        (
            shape((t, fw), BF16),
            shape((d, wide), BF16),
            shape((fw, d + LANES), BF16),
            shape(small.shape, F32),
            shape(small_gu.shape, F32),
            shape((8, wide), F32),
            shape((8, width), F32),
            shape((t, width), BF16),
            shape((t, LANES), BF16),
            shape((t, LANES), F32),
            shape((nl, part, 2 * npad), BF16),
            shape((down_rows, d + LANES), BF16),
            shape((d, 2 * npad), BF16),
            shape((t, d), BF16),
            shape((t, HD), F32),
            shape((t, HD), F32),
            shape((t, LANES), jnp.int32),
            shape((8, t), jnp.int32),
        ),
        [VM, ANY] + [VM] * 10 + [ANY] + [VM] * 8,
        (VM,) * 12 + (ANY, ANY) + (VM,) * 4,
        ag_scratch(nl, nc, t, d)
        + [dma((nc,))] * 4
        + [dma((9,))]
        + spread_scratch(ny, nl)
        + row_move_scratch(ny)
        + [
            pltpu.VMEM((nl, part, wide), BF16),
            pltpu.VMEM((3, part, d // 2), BF16),
            pltpu.VMEM((2, part, ff_half), BF16),
            dma((2,)),
            pltpu.VMEM((fw, d + LANES), BF16),
            pltpu.VMEM((1, t), jnp.int32),
            pltpu.VMEM((8, t), jnp.int32),
            pltpu.VMEM((3, fw, RANK), F32),
            pltpu.VMEM((2, fw, RANK), F32),
            pltpu.VMEM((fw, RANK), F32),
        ]
        + spread_scratch(ny, nl),
        1,
        90,
        (
            x_in, w_qkv, a_qkv, b_qkv, tail_qkv, gains, w_out, small, small_gu, segments, *turns,
            w_gu, a_gu, b_gu, tail_gu, w_down, a_down, b_down, a_out, b_out,
        ),
        late=(6, 10, 11, *range(13, 21)),
        flow=(7, 8, 9, 14, 15, 16),
        step=tc,
    )


def allowed_of(key_segment, query_segment, j, i, block):
    key_at = j * block + lax.broadcasted_iota(jnp.int32, (block, block), 0)
    query_at = i * block + lax.broadcasted_iota(jnp.int32, (block, block), 1)
    return (key_segment == query_segment) & (key_at <= query_at)


def attention_forward(cfg, qkv, seg_column, seg_row, first_block, block):
    t, fw = cfg[0], cfg[1]
    heads = fw // HD

    def kernel(io, qkv_ref, sc_ref, sr_ref, first_ref, out_ref, lse_ref):
        def at(i):
            return pl.ds(pl.multiple_of(i * block, block), block)

        def columns(k, hd):
            return slice(k * fw + hd * HD, k * fw + (hd + 1) * HD)

        def one_query(i, carry_on):
            queries = [qkv_ref[at(i), columns(0, hd)] for hd in range(heads)]
            query_segment = sr_ref[0:1, at(i)]

            def one_key(j, carry):
                allowed = allowed_of(sc_ref[at(j), 0:1], query_segment, j, i, block)
                out = []
                for hd in range(heads):
                    top, total, acc = carry[hd]
                    s = nt(qkv_ref[at(j), columns(1, hd)], queries[hd]) * (HD**-0.5)
                    s = jnp.where(allowed, s, MASKED)
                    new = jnp.maximum(top, jnp.max(s, axis=0, keepdims=True))
                    p = jnp.exp(s - new)
                    shrink = jnp.exp(top - new)
                    total = total * shrink + jnp.sum(p, axis=0, keepdims=True)
                    acc = acc * shrink + tn(qkv_ref[at(j), columns(2, hd)], p.astype(BF16))
                    out.append((new, total, acc))
                return tuple(out)

            first = (
                jnp.full((1, block), MASKED, F32),
                jnp.zeros((1, block), F32),
                jnp.zeros((HD, block), F32),
            )
            out = lax.fori_loop(first_ref[i], i + 1, one_key, (first,) * heads)
            for hd in range(heads):
                top, total, acc = out[hd]
                out_ref[at(i), hd * HD : (hd + 1) * HD] = (acc / total).T.astype(BF16)
                lse_ref[hd * 8 : hd * 8 + 8, at(i)] = jnp.broadcast_to(
                    top + jnp.log(total), (8, block)
                )
            return carry_on

        lax.fori_loop(0, t // block, one_query, 0)

    return call(
        kernel,
        "attention_forward",
        (shape((t, fw), BF16), shape((heads * 8, t), F32)),
        [VM, VM, VM, SM],
        (VM, VM),
        [],
        None,
        15,
        (qkv, seg_column, seg_row, first_block),
    )


def out_forward(cfg, ny, npad, attended, weights, x, magnitude, w_gu, blocks, rows_down):
    t, fw, d, nl, nc, tc = cfg
    part = rows_down.shape[0] // ny

    def kernel(
        io, a_ref, w_ref, x_ref, m_ref, w_in, e_ref, ed_ref,
        mid_ref, u_ref, st_ref, sc_ref, sq_ref, lora_ref, wg_ref, wd_ref,
        sb, cb, gb, s1, r1, s2, r2, cpart, cheld, css, csr,
        hs, hr, ps, pr, pn, ys, yr, dws, dwr, dwl, dys, dyr,
    ):
        cm = Comm(nl, nc, tc, fw, back_by_two=0.0625)
        cm.rs_refs(sb, cb, gb, s1, r1, s2, r2)
        cm.cs_refs(cpart, cheld, css, csr)
        columns = Spread(cm, ny, e_ref, wg_ref, hs, hr, ps, pr, pn, ys, yr)
        swap = Swap(cm)
        down_rows = RowMove(swap, ny, part, ed_ref, wd_ref, dws, dwr, dwl, dys, dyr)
        cm.barrier(movers(ny), [swap.partner])
        down_rows.start()
        columns.start_crossing(EARLY)
        columns.start(range(EARLY + 1, nl))
        for m in range(EARLY):
            columns.share(0, m)
            columns.share(1, m)
        columns.share(0, EARLY)
        cm.cs_start(w_ref)
        if part * ny < npad:
            wd_ref[part * ny :, :] = jnp.zeros((npad - part * ny, wd_ref.shape[1]), BF16)
        def body(i, carry_on):
            @pl.when(i < nc)
            def _():
                block = a_ref[cm.rows(i), :]
                for role in range(2 * nl):
                    sb[i, role // nl, role % nl] = nn(
                        block, w_ref[:, role * fw : (role + 1) * fw]
                    ).astype(BF16)
                cm.rs_across(i).start()
                lora_ref[cm.rows(i), :] = nn(block, w_ref[:, d:]).astype(BF16)
                io.store(i, 5)

            cm.rs_steps(i)

            @pl.when(i == 3)
            def _():
                total = cm.cs_total()
                sq_ref[...] = jnp.broadcast_to(total, (8, fw))
                sc_ref[...] = jnp.broadcast_to(m_ref[3:4, :] * lax.rsqrt(total), (8, fw))

            @pl.when(i == 5)
            def _():
                down_rows.pass_on()

            @pl.when(i == 1)
            def _():
                columns.pass_own(EARLY + 1, cross=False)

            @pl.when(i == 3)
            def _():
                for m in range(EARLY + 2, nl):
                    columns.pass_own(m, cross=False)

            @pl.when(i == min(4, nc + 2))
            def _():
                columns.pass_crossed(EARLY, EARLY + 1)

            @pl.when(i == min(7, nc + 2))
            def _():
                columns.pass_crossed(EARLY + 1, EARLY + 2)

            @pl.when((i >= 3) & (i <= nc + 2))
            def _():
                rows = cm.rows(i - 3)
                middle = x_ref[rows, :].astype(F32) + cm.rs_total(i - 3) * sc_ref[0:1, :]
                mid_ref[rows, :] = middle
                u_ref[rows, :] = middle.astype(BF16)
                st_ref[i - 3] = ones_rows(middle * middle)[0:1, :]
                io.store(i - 3, 0, 1)

            return carry_on

        lax.fori_loop(0, nc + 3, body, 0)

        def drain(i, carry_on):
            cm.rs_drain(i)
            io.stored(i)
            return carry_on

        for m in range(EARLY + 2, nl):
            columns.pass_crossed(m, m + 1)
        for side in (0, 1):
            columns.wait(side, range(nl))
        down_rows.wait()
        lax.fori_loop(0, nc, drain, 0)
        cm.cs_drain()
        columns.drain_own(range(EARLY + 1, nl))
        columns.drain_crossing(range(EARLY, nl))
        for side in (0, 1):
            columns.drain_shared(side, range(nl))
        down_rows.drain()

    return call(
        kernel,
        "out_forward",
        (
            shape((t, fw), F32),
            shape((t, fw), BF16),
            shape((nc, 1, tc), F32),
            shape((8, fw), F32),
            shape((8, fw), F32),
            shape((t, LANES), BF16),
            shape(w_gu.shape, BF16),
            shape((npad, d + LANES), BF16),
        ),
        [VM] * 4 + [ANY, ANY, ANY],
        (VM,) * 6 + (ANY, VM),
        rs_scratch(nl, nc, tc, fw)
        + cs_scratch(nl, d, fw)
        + spread_scratch(ny, nl)
        + row_move_scratch(ny),
        2,
        90,
        (attended, weights, x, magnitude, w_gu, blocks, rows_down),
        flow=(0, 1, 5),
        step=tc,
        aliases={4: 6},
    )


def ffn_forward(cfg, npad, nf, u, stats, w_gu, m_gu, w_down, small, middle, cotangent):
    t, fw, d, nl, nc, tc = cfg

    def kernel(
        io, u_ref, st_ref, wg_ref, mg_ref, wd_ref, m_ref, mid_ref, cin_ref,
        gu_ref, hid_ref, out_ref, gm_ref, rate_ref, gp_ref, sg_ref, qg_ref, sd_ref, qd_ref, lora_ref, cot_ref, am_ref, ad_ref, uf_ref,
        full, own, sd, rd, sc, rc, sb, cb, gb, s1, r1, s2, r2, sa, ss, sr, cpart, cheld, css, csr, keep,
        cs_s, cs_r, cs_l,
    ):
        cm = Comm(nl, nc, tc, fw, out_by_one=0.5, back_by_two=0.5)
        cm.ag_refs(u_ref, full, own, sd, rd, sc, rc)
        cm.rs_refs(sb, cb, gb, s1, r1, s2, r2)
        cm.st_refs(st_ref, sa, ss, sr)
        cm.cs_refs(cpart, cheld, css, csr)
        swap = Swap(cm)
        cm.barrier((), [swap.partner])

        def cot_swap(i):
            rows = cm.rows(i)
            return cin_ref.at[rows], cot_ref.at[rows], (cs_s.at[i], cs_r.at[i], cs_l.at[i])

        cm.st_send(None)
        cm.ag_start()
        io.ready()

        def cot_out(i, carry_on):
            swap.start(*cot_swap(i))
            return carry_on


        def squares(i, total):
            rows = pl.ds(pl.multiple_of(i * fw, fw), fw)
            gain = (
                wg_ref[rows, nf + RANK : nf + RANK + 1].astype(F32)
                + wg_ref[rows, nf + RANK + 1 : nf + RANK + 2].astype(F32)
            )
            value = wg_ref[rows, :].astype(F32) * (1.0 / gain)
            return total + row_sum(value * value)

        square = lax.fori_loop(0, 2 * nl, squares, jnp.zeros((1, 2 * npad), F32))
        column = lax.rem(lax.broadcasted_iota(jnp.int32, (1, 2 * npad), 1), npad)
        square = jnp.where(column < nf, square, 1.0)
        qg_ref[...] = jnp.broadcast_to(square, (8, 2 * npad))
        sg_ref[...] = jnp.broadcast_to(mg_ref[...] * lax.rsqrt(square), (8, 2 * npad))
        cm.ag_ahead()
        gm_ref[...] = jnp.zeros_like(gm_ref)

        def stored(i):
            rows = cm.rows(i)
            return pltpu.make_async_copy(full.at[rows], uf_ref.at[rows], keep.at[i])

        cm.cs_start(wd_ref)
        lax.fori_loop(0, nc, cot_out, 0)

        def body(i, carry_on):
            @pl.when(i < nc)
            def _():
                cm.ag_step(i + 2)
                cm.ag_wait(i)

                @pl.when(i == 0)
                def _():
                    cm.st_wait(None)

                stored(i).start()
                rows = cm.rows(i)
                rate = lax.rsqrt(cm.st_sum(i) / d + EPS)
                rate_ref[rows, :] = jnp.broadcast_to(rate, (tc, LANES))
                out = nn(full[rows, :], wg_ref[...]) * rate * sg_ref[0:1, :]
                gu_ref[rows, :] = out.astype(BF16)
                gate, up = out[:, :npad], out[:, npad:]
                hidden = (gate / (1.0 + jnp.exp(-gate)) * up).astype(BF16)
                hid_ref[rows, :] = hidden
                for role in range(2 * nl):
                    sb[i, role // nl, role % nl] = nn(
                        hidden, wd_ref[:, role * fw : (role + 1) * fw]
                    ).astype(BF16)
                cm.rs_across(i).start()
                lora_ref[rows, :] = nn(hidden, wd_ref[:, d:]).astype(BF16)
                io.store(i, 0, 1, 4, 10)

            @pl.when(i == nc)
            def _():
                off = nf - (npad - LANES)
                for k in range(2):
                    tail = wg_ref[:, (k + 1) * npad - LANES : (k + 1) * npad]
                    _, gain = gain_rows(tail, off + RANK)
                    factor = (tail.astype(F32) / (gain * gain)).astype(BF16)
                    product = tn(factor, wg_ref[:, k * npad : (k + 1) * npad])
                    am_ref[k * RANK : (k + 1) * RANK, :] = product[off : off + RANK, :]
                ad_ref[...] = tn(wd_ref[:, d:], wd_ref[:, :d])[:RANK, :]

            cm.rs_steps(i)

            @pl.when(i == 3)
            def _():
                total = cm.cs_total()
                qd_ref[...] = jnp.broadcast_to(total, (8, fw))
                sd_ref[...] = jnp.broadcast_to(m_ref[4:5, :] * lax.rsqrt(total), (8, fw))

            @pl.when(i >= 3)
            def _():
                rows = cm.rows(i - 3)
                down = cm.rs_total(i - 3) * sd_ref[0:1, :]
                out_ref[rows, :] = (mid_ref[rows, :] + down).astype(BF16)
                swap.wait(*cot_swap(i - 3))
                seed = cot_ref[rows, :].astype(F32)
                gm_ref[0:1, :] += row_sum(seed * down)
                gp_ref[rows, :] = (seed * sd_ref[0:1, :]).astype(BF16)
                io.store(i - 3, 2, 5)

            return carry_on

        lax.fori_loop(0, nc + 3, body, 0)

        def drain(i, carry_on):
            cm.ag_drain(i)
            cm.rs_drain(i)
            stored(i).wait()
            io.stored(i)
            swap.drain(*cot_swap(i))
            return carry_on

        lax.fori_loop(0, nc, drain, 0)
        cm.st_drain(None)
        cm.cs_drain()

    dma = pltpu.SemaphoreType.DMA
    return call(
        kernel,
        "ffn_forward",
        (
            shape((t, 2 * npad), BF16),
            shape((t, npad), BF16),
            shape((t, fw), BF16),
            shape((8, fw), F32),
            shape((t, LANES), F32),
            shape((t, fw), BF16),
            shape((8, 2 * npad), F32),
            shape((8, 2 * npad), F32),
            shape((8, fw), F32),
            shape((8, fw), F32),
            shape((t, LANES), BF16),
            shape((t, fw), BF16),
            shape((2 * RANK, npad), F32),
            shape((RANK, d), F32),
            shape((t, d), BF16),
        ),
        [VM] * 8,
        (VM,) * 14 + (ANY,),
        ag_scratch(nl, nc, t, d)
        + rs_scratch(nl, nc, tc, fw)
        + st_scratch(nl, nc, t)
        + cs_scratch(nl, d, fw)
        + [dma((nc,))] * 4,
        3,
        110,
        (u, stats, w_gu, m_gu, w_down, small, middle, cotangent),
        late=(2, 4, 6),
        flow=(0, 1, 2, 4, 5, 10),
        step=tc,
    )


def ffn_backward(cfg, npad, gp, gu, w_gu, sc_gu, b_gu, w_down, b_down, rate, cotangent, middle, x, sc_out):
    t, fw, d, nl, nc, tc = cfg

    def kernel(
        io, gp_ref, gu_hbm, wg_ref, sg_ref, bg_ref, wd_ref, bd_ref, rate_ref, cot_ref, mid_ref, x_ref, so_ref,
        dm_ref, go_ref, gmo_ref, gm_ref, lg_ref, ld_ref, dp_hbm, gf_ref,
        full, own, sd, rd, sc, rc, sb, cb, gb, s1, r1, s2, r2, sa, ss, sr, st, gu_s, keep, load, save,
    ):
        cm = Comm(nl, nc, tc, fw)
        cm.ag_refs(gp_ref, full, own, sd, rd, sc, rc)
        cm.rs_refs(sb, cb, gb, s1, r1, s2, r2)
        cm.st_refs(st, sa, ss, sr)

        def loaded(i):
            rows = cm.rows(i)
            return pltpu.make_async_copy(gu_hbm.at[rows], gu_s.at[rows], load.at[i])

        def saved(i):
            rows = cm.rows(i)
            return pltpu.make_async_copy(gu_s.at[rows], dp_hbm.at[rows], save.at[i])

        def stored(i):
            rows = cm.rows(i)
            return pltpu.make_async_copy(full.at[rows], gf_ref.at[rows], keep.at[i])

        cm.barrier()
        cm.ag_start()

        def start_loads(i, carry_on):
            loaded(i).start()
            return carry_on

        lax.fori_loop(0, nc, start_loads, 0)
        cm.ag_ahead()
        io.ready()
        gm_ref[...] = jnp.zeros_like(gm_ref)
        gmo_ref[...] = jnp.zeros_like(gmo_ref)

        def body(i, carry_on):
            @pl.when(i < nc)
            def _():
                cm.ag_step(i + 2)
                cm.ag_wait(i)
                stored(i).start()
                loaded(i).wait()
                rows = cm.rows(i)
                block = full[rows, :]
                dh = nt(block, wd_ref[:, :d])
                ld_ref[rows, :] = nt(block, bd_ref[...]).astype(BF16)
                gate = gu_s[rows, :npad].astype(F32)
                up = gu_s[rows, npad:].astype(F32)
                sig = 1.0 / (1.0 + jnp.exp(-gate))
                dgate = dh * up * (sig * (1.0 + gate * (1.0 - sig)))
                dup = dh * (gate * sig)
                pg, pu = dgate * gate, dup * up
                gm_ref[0:1, :npad] += jnp.sum(pg, axis=0, keepdims=True)
                gm_ref[0:1, npad:] += jnp.sum(pu, axis=0, keepdims=True)
                st[i] = ones_rows(pg + pu)[0:1, :]
                cm.st_send(i)
                gu_s[rows, :npad] = (dgate * sg_ref[0:1, :npad]).astype(BF16)
                gu_s[rows, npad:] = (dup * sg_ref[0:1, npad:]).astype(BF16)
                saved(i).start()
                dp = gu_s[rows, :]
                lg_ref[rows, :] = (nt(dp, bg_ref[...].astype(BF16)) * rate_ref[rows, :]).astype(BF16)
                io.store(i, 4, 5)
                for role in range(2 * nl):
                    sb[i, role // nl, role % nl] = nt(
                        dp, wg_ref[role * fw : (role + 1) * fw, :]
                    ).astype(BF16)
                cm.rs_across(i).start()

            cm.rs_steps(i)

            @pl.when(i >= 3)
            def _():
                k = i - 3
                rows = cm.rows(k)
                cm.st_wait(k)
                r = rate_ref[rows, 0:1]
                inner = cm.st_sum(k)
                mid = mid_ref[rows, :]
                dm = (
                    cot_ref[rows, :].astype(F32)
                    + r * cm.rs_total(k)
                    - mid * (r * r * inner / d)
                )
                dm_ref[rows, :] = dm
                go_ref[rows, :] = (dm * so_ref[0:1, :]).astype(BF16)
                io.store(k, 0, 1)
                gmo_ref[0:1, :] += jnp.sum(
                    dm * (mid - x_ref[rows, :].astype(F32)), axis=0, keepdims=True
                )

            return carry_on

        lax.fori_loop(0, nc + 3, body, 0)

        def drain(i, carry_on):
            cm.ag_drain(i)
            cm.rs_drain(i)
            cm.st_drain(i)
            stored(i).wait()
            saved(i).wait()
            io.stored(i)
            return carry_on

        lax.fori_loop(0, nc, drain, 0)

    return call(
        kernel,
        "ffn_backward",
        (
            shape((t, fw), F32),
            shape((t, fw), BF16),
            shape((8, fw), F32),
            shape((8, 2 * npad), F32),
            shape((t, LANES), BF16),
            shape((t, LANES), BF16),
            shape((t, 2 * npad), BF16),
            shape((t, d), BF16),
        ),
        [VM, ANY] + [VM] * 10,
        (VM,) * 6 + (ANY, ANY),
        ag_scratch(nl, nc, t, d)
        + rs_scratch(nl, nc, tc, fw)
        + st_scratch(nl, nc, t)
        + [
            pltpu.VMEM((nc, 1, tc), F32),
            pltpu.VMEM((t, 2 * npad), BF16),
            pltpu.SemaphoreType.DMA((nc,)),
            pltpu.SemaphoreType.DMA((nc,)),
            pltpu.SemaphoreType.DMA((nc,)),
        ],
        4,
        120,
        (gp, gu, w_gu, sc_gu, b_gu, w_down, b_down, rate, cotangent, middle, x, sc_out),
        late=(2, 4, 5, 6, 7, 8, 9, 10),
        flow=(0, 1, 4, 5),
        step=tc,
    )


def gain_rows(tail, at):
    lane = lax.broadcasted_iota(jnp.int32, (8, LANES), 1)
    pick = jnp.where((lane == at) | (lane == at + 1), 1.0, 0.0).astype(BF16)
    column = tail[:, at : at + 1].astype(F32) + tail[:, at + 1 : at + 2].astype(F32)
    return nt(pick, tail)[0:1, :], column


class Stream:
    def __init__(self, sources, slots, sems, step):
        self.sources, self.slots, self.sems, self.step = sources, slots, sems, step

    def copies(self, i):
        rows = pl.ds(pl.multiple_of(i * self.step, self.step), self.step)
        slot = lax.rem(i, 2)
        return [
            pltpu.make_async_copy(src.at[rows, columns], held.at[slot], self.sems.at[k, slot])
            for k, ((src, columns), held) in enumerate(zip(self.sources, self.slots))
        ]

    def start(self, i):
        for copy in self.copies(i):
            copy.start()

    def wait(self, i):
        for copy in self.copies(i):
            copy.wait()
        return [held[lax.rem(i, 2)] for held in self.slots]


def stream_scratch(step, widths):
    return [pltpu.VMEM((2, step, n), BF16) for n in widths] + [pltpu.SemaphoreType.DMA((len(widths), 2))]


def out_backward(
    cfg, npad, nf, go, weights, b_out, sums, w_gu, w_down, up_gu, b_down, gm_gu, square_gu, m_gu,
    u_full, lg_gu, gu, dp_gu, hidden, lg_down, lora_down, gp_full, result, merged_low_gu, merged_low_down,
):
    t, fw, d, nl, nc, tc = cfg
    off = nf - (npad - LANES)
    widths = (d, LANES, LANES, LANES, 2 * npad, npad, LANES, LANES, d)

    def kernel(
        io, go_ref, w_ref, b_ref, s1_ref, s2_ref, s3_ref, s4_ref, wg_ref, wd_ref, up_ref, bd_ref, gm_ref, sq_ref, m_ref,
        uf_hbm, lg_hbm, gu_hbm, dp_hbm, hid_hbm, ld_hbm, lo2_hbm, gp_hbm, res_hbm, am_ref, amd_ref,
        da_ref, lo_ref, qs_ref, sh_ref, lc_ref, gf_ref, moved_ref,
        full, own, sd, rd, sc, rc, keep, qss, qsr, res_sems, acc_a, acc_g, acc_u, acc_d, acc_p, term, term_d, q_ref, *streams,
    ):
        cm = Comm(nl, nc, tc, fw, out_by_one=0.75)
        swap = Swap(cm)
        result_swap = (res_hbm, moved_ref, tuple(res_sems.at[k] for k in range(3)))
        cm.ag_refs(go_ref, full, own, sd, rd, sc, rc)
        every = lambda n: pl.ds(0, n)
        stream = Stream(
            [
                (uf_hbm, every(d)),
                (lg_hbm, every(LANES)),
                (gu_hbm, pl.ds(npad - LANES, LANES)),
                (gu_hbm, pl.ds(2 * npad - LANES, LANES)),
                (dp_hbm, every(2 * npad)),
                (hid_hbm, every(npad)),
                (ld_hbm, every(LANES)),
                (lo2_hbm, every(LANES)),
                (gp_hbm, every(d)),
            ],
            streams[:-1],
            streams[-1],
            tc,
        )
        stream.start(jnp.int32(0))
        cm.barrier((), [swap.partner])

        def ratio_copy(o, m):
            k = o * nl + m
            return cm.copy(
                q_ref, qs_ref.at[:, cm.columns(cm.c, cm.g)], qss.at[k], qsr.at[k], 1 - cm.c if o else cm.c, cm.after(m)
            )

        cm.ag_start()
        q_ref[...] = jnp.zeros_like(q_ref)
        q_ref[0:1, :] = -s1_ref[0:1, :] / s2_ref[0:1, :]
        q_ref[1:2, :] = -s3_ref[0:1, :] / s4_ref[0:1, :]
        for o, m in cm.st_peers():
            ratio_copy(o, m).start()
        qs_ref[:, cm.columns(cm.c, cm.g)] = q_ref[...]
        swap.start(*result_swap)
        for acc in (acc_a, acc_g, acc_u, acc_d, acc_p):
            acc[...] = jnp.zeros_like(acc)
        io.ready()
        ratio = -gm_ref[0:1, :] / sq_ref[0:1, :]
        term[...] = nt((up_ref[...] * ratio).astype(BF16), wg_ref[...])[: 2 * RANK, :]
        cm.ag_ahead()

        def stored(i):
            rows = cm.rows(i)
            return pltpu.make_async_copy(full.at[rows], gf_ref.at[rows], keep.at[i])

        def body(i, carry_on):
            cm.ag_step(i + 2)

            @pl.when(i == min(2, nc - 1))
            def _():
                for o, m in cm.st_peers():
                    ratio_copy(o, m).wait_recv()
                term_d[...] = nt((bd_ref[...].astype(F32) * qs_ref[1:2, :]).astype(BF16), wd_ref[:, :d])[:RANK, :]

            @pl.when(i + 1 < nc)
            def _():
                stream.start(i + 1)

            u, lg, low_g, low_u, dp, hid, ld, low_d, gp = stream.wait(i)
            acc_a[...] += tn(lg, u)
            acc_g[...] += tn(low_g, dp[:, :npad])
            acc_u[...] += tn(low_u, dp[:, npad:])
            acc_d[...] += tn(ld, hid)
            acc_p[...] += tn(low_d, gp)
            cm.ag_wait(i)
            stored(i).start()
            rows = cm.rows(i)
            block = full[rows, :]
            da_ref[rows, :] = nt(block, w_ref[:, :d]).astype(BF16)
            lo_ref[rows, :] = nt(block, b_ref[...]).astype(BF16)
            return carry_on

        lax.fori_loop(0, nc, body, 0)

        gain_row, _ = gain_rows(wg_ref[:, npad - LANES : npad], off + RANK)
        sh_ref[: 2 * RANK, :] = (SCALE * (acc_a[: 2 * RANK, :] * gain_row + term[...] / gain_row)).astype(BF16)
        for k, acc in enumerate((acc_g, acc_u)):
            at, low = slice(k * npad, (k + 1) * npad), slice(k * RANK, (k + 1) * RANK)
            lc_ref[(1 + k) * RANK : (2 + k) * RANK, :] = (
                SCALE * (acc[off : off + RANK, :] + am_ref[low, :] * ratio[:, at])
            ).astype(BF16)
            lc_ref[3 * RANK + k : 3 * RANK + k + 1, :] = (gm_ref[0:1, at] / m_ref[0:1, at]).astype(BF16)
        lc_ref[3 * RANK + 2 :, :] = jnp.zeros((RANK - 2, npad), BF16)
        lc_ref[:RANK, :] = (SCALE * (acc_d[:RANK, :] + term_d[...])).astype(BF16)
        sh_ref[2 * RANK :, :] = (SCALE * (acc_p[:RANK, :] + amd_ref[...] * qs_ref[1:2, :])).astype(BF16)

        def drain(i, carry_on):
            cm.ag_drain(i)
            stored(i).wait()
            return carry_on

        lax.fori_loop(0, nc, drain, 0)
        swap.wait(*result_swap)
        swap.drain(*result_swap)
        for o, m in cm.st_peers():
            ratio_copy(o, m).wait_send()

    dma = pltpu.SemaphoreType.DMA
    return call(
        kernel,
        "out_backward",
        (
            shape((t, fw), BF16),
            shape((t, LANES), BF16),
            shape((8, d), F32),
            shape((3 * RANK, d), BF16),
            shape((4 * RANK, npad), BF16),
            shape((t, d), BF16),
            shape((t, fw), BF16),
        ),
        [VM] * 14 + [ANY] * 9 + [VM] * 2,
        (VM,) * 5 + (ANY, ANY),
        ag_scratch(nl, nc, t, d)
        + [dma((nc,)), dma((2 * nl,)), dma((2 * nl,)), dma((3,))]
        + [pltpu.VMEM((LANES, n), F32) for n in (d, npad, npad, npad, d)]
        + [pltpu.VMEM((2 * RANK, d), F32), pltpu.VMEM((RANK, npad), F32), pltpu.VMEM((8, fw), F32)]
        + stream_scratch(tc, widths),
        5,
        60,
        (
            go, weights, b_out, *sums, w_gu, w_down, up_gu, b_down, gm_gu, square_gu, m_gu,
            u_full, lg_gu, gu, dp_gu, hidden, lg_down, lora_down, gp_full, result, merged_low_gu, merged_low_down,
        ),
        late=(1, 2, 7, 8, 9, 10),
    )


def attention_backward(
    cfg, qkv, attended, grad, lse, seg_column, seg_row, first_block, block, cosine, sine, scale, rate, b_qkv
):
    t, fw = cfg[0], cfg[1]
    heads = fw // HD
    width = 3 * fw

    def kernel(
        io, qkv_ref, att_ref, grad_ref, lse_ref, sc_ref, sr_ref, first_ref, cos_ref, sin_ref, scale_ref, rate_ref, b_ref,
        dp_ref, st_ref, gm_ref, lg_ref, dq, dk, dv,
    ):
        def at(i):
            return pl.ds(pl.multiple_of(i * block, block), block)

        def columns(k, hd):
            return slice(k * fw + hd * HD, k * fw + (hd + 1) * HD)

        gm_ref[...] = jnp.zeros_like(gm_ref)
        dk[...] = jnp.zeros_like(dk)
        dv[...] = jnp.zeros_like(dv)

        def one_query(i, carry_on):
            queries = [qkv_ref[at(i), columns(0, hd)] for hd in range(heads)]
            grads = [grad_ref[at(i), columns(0, hd)] for hd in range(heads)]
            deltas = [
                ones_rows(grads[hd].astype(F32) * att_ref[at(i), columns(0, hd)].astype(F32))[0:1, :]
                for hd in range(heads)
            ]
            query_segment = sr_ref[0:1, at(i)]

            def one_key(j, accs):
                allowed = allowed_of(sc_ref[at(j), 0:1], query_segment, j, i, block)
                out = []
                for hd in range(heads):
                    keys = qkv_ref[at(j), columns(1, hd)]
                    s = nt(keys, queries[hd]) * (HD**-0.5)
                    p = jnp.where(allowed, jnp.exp(s - lse_ref[hd * 8 : hd * 8 + 1, at(i)]), 0.0)
                    ds = (p * (nt(qkv_ref[at(j), columns(2, hd)], grads[hd]) - deltas[hd])).astype(BF16)
                    dv[hd, at(j), :] += nn(p.astype(BF16), grads[hd])
                    dk[hd, at(j), :] += nn(ds, queries[hd])
                    out.append(accs[hd] + tn(ds, keys))
                return tuple(out)

            accs = lax.fori_loop(first_ref[i], i + 1, one_key, (jnp.zeros((block, HD), F32),) * heads)
            for hd in range(heads):
                dq[hd, at(i), :] = accs[hd]
            return carry_on

        lax.fori_loop(0, t // block, one_query, 0)

        def finish(i, carry_on):
            rows = at(i)
            cosine_here, sine_here = cos_ref[rows, :], sin_ref[rows, :]
            inner = jnp.zeros((block, HD), F32)
            for hd in range(heads):
                for n, source in enumerate((dq, dk, dv)):
                    where = columns(n, hd)
                    dout = source[hd, rows, :]
                    value = qkv_ref[rows, where].astype(F32)
                    if n < 2:
                        dout = dout * (HD**-0.5)
                        dout = dout * cosine_here - pltpu.roll(dout, HD // 2, 1) * sine_here
                        value = value * cosine_here - pltpu.roll(value, HD // 2, 1) * sine_here
                    product = dout * value
                    inner = inner + product
                    gm_ref[0:1, where] += row_sum(product)
                    dp_ref[rows, where] = (dout * scale_ref[0:1, where]).astype(BF16)
            st_ref[i] = ones_rows(inner)[0:1, :]
            lg_ref[rows, :] = (nt(dp_ref[rows, :], b_ref[...].astype(BF16)) * rate_ref[rows, :]).astype(BF16)
            return carry_on

        lax.fori_loop(0, t // block, finish, 0)

    return call(
        kernel,
        "attention_backward",
        (
            shape((t, width), BF16),
            shape((t // block, 1, block), F32),
            shape((8, width), F32),
            shape((t, LANES), BF16),
        ),
        [VM] * 6 + [SM] + [VM] * 5,
        (VM,) * 4,
        [pltpu.VMEM((heads, t, HD), F32)] * 3,
        None,
        35,
        (qkv, attended, grad, lse, seg_column, seg_row, first_block, cosine, sine, scale, rate, b_qkv),
    )


def qkv_backward(
    cfg, ny, dp, stats, weights, rate, dm, x, shared, local_gu, w_out, up_qkv, b_out, ratios, gm_qkv, square_qkv,
    gm_out, gm_down, small, x_full, lg_qkv, lora_qkv, attended, lg_out, lora_out, go_full,
):
    t, fw, d, nl, nc, tc = cfg
    width = 3 * fw
    peers = 2 * nl
    step = 2 * tc if nc % 2 == 0 else tc
    parts = t // step
    widths = (d, LANES, LANES, fw, LANES, LANES, d)

    def kernel(
        io, dp_ref, st_ref, w_ref, rate_ref, dm_ref, x_ref, sh_ref, l_ref, wo_ref, up_ref, bo_ref, q_ref,
        gm_ref, sq_ref, gmo_ref, gmd_ref, m_ref, xf_hbm, lg_hbm, lq_hbm, at_hbm, lgo_hbm, lo_hbm, gf_hbm,
        out_ref, as_ref, bs_ref, ls_ref,
        sb, cb, gb, s1, r1, s2, r2, sa, ss, sr,
        stage, gs_s, gs_r, gs_l, group, gsum, gss, gsr, final_a, final_b, final_l, fs, fr, fl,
        a_ref, b_ref, acc_a, acc_b, acc_o, acc_p, *streams,
    ):
        cm = Comm(nl, nc, tc, fw, back_by_two=0.25)
        c, g = cm.c, cm.g
        y, h = lax.axis_index("y"), lax.axis_index("h")
        cm.rs_refs(sb, cb, gb, s1, r1, s2, r2)
        cm.st_refs(st_ref, sa, ss, sr)
        swap = Swap(cm)
        every = lambda n: pl.ds(0, n)
        stream = Stream(
            [
                (xf_hbm, every(d)),
                (lg_hbm, every(LANES)),
                (lq_hbm, every(LANES)),
                (at_hbm, every(fw)),
                (lgo_hbm, every(LANES)),
                (lo_hbm, every(LANES)),
                (gf_hbm, every(d)),
            ],
            streams[:-1],
            streams[-1],
            step,
        )
        stream.start(jnp.int32(0))
        senders = [
            {"y": lax.rem(y + ny - k, ny), "c": h, "h": hh} for k in range(1, ny) for hh in (0, 1)
        ]
        cm.barrier(senders + [{"c": h, "h": 1 - h}], [swap.partner, {"c": h, "h": h}])

        def gather_part(o, m):
            to_c, to_g = 1 - c if o else c, cm.after(m)
            k = o * nl + m
            return cm.copy(
                a_ref.at[:, cm.columns(to_c, to_g)], group.at[k], gss.at[k], gsr.at[k], to_c, to_g
            )

        def sums(k, e):
            device = {"y": lax.rem(y + k, ny), "c": lax.rem(c + e, 2), "h": c}
            slot = k * 2 + h
            return [
                pltpu.make_async_remote_copy(
                    src_ref=src, dst_ref=dst.at[slot], send_sem=fs.at[n, k * 2 + e], recv_sem=fr.at[n, slot],
                    device_id=device, device_id_type=MESH,
                )
                for n, (src, dst) in enumerate(((gsum, final_a), (b_ref, final_b), (l_ref, final_l)))
            ]

        def sums_here():
            return [
                pltpu.make_async_copy(src, dst.at[h], fl.at[n])
                for n, (src, dst) in enumerate(((gsum, final_a), (b_ref, final_b), (l_ref, final_l)))
            ]

        cm.st_send(None)
        for acc in (acc_a, acc_b, acc_o, acc_p):
            acc[...] = jnp.zeros_like(acc)

        def adapters(k):
            @pl.when(k + 1 < parts)
            def _():
                stream.start(k + 1)

            xf, lg, low_q, att, lg_o, low_o, gf = stream.wait(k)
            rows = pl.ds(pl.multiple_of(k * step, step), step)
            acc_a[...] += tn(lg, xf)
            acc_b[...] += tn(low_q, dp_ref[rows, :])
            acc_o[...] += tn(lg_o, att)
            acc_p[...] += tn(low_o, gf)

        def adapters_end():
            ratio = -gm_ref[0:1, :] / sq_ref[0:1, :]
            ratio_out = q_ref[0:1, :]
            tail = w_ref[:, width:]
            gain_row, gain_column = gain_rows(tail, 3 * RANK)
            term = nt((up_ref[...] * ratio).astype(BF16), w_ref[:, :width])
            a_ref[: 3 * RANK, :] = (
                SCALE * (acc_a[: 3 * RANK, :] * gain_row + term[: 3 * RANK, :] / gain_row)
            ).astype(BF16)
            merged = tn(
                (tail.astype(F32) / (gain_column * gain_column)).astype(BF16), w_ref[:, :width]
            )
            for k in range(3):
                at, low = slice(k * fw, (k + 1) * fw), slice(k * RANK, (k + 1) * RANK)
                b_ref[(1 + k) * RANK : (2 + k) * RANK, :] = (
                    SCALE * (acc_b[low, at] + merged[low, at] * ratio[:, at])
                ).astype(BF16)
                b_ref[4 * RANK + k : 4 * RANK + k + 1, :] = (gm_ref[0:1, at] / m_ref[k : k + 1, :]).astype(BF16)
            b_ref[4 * RANK + 3 : 4 * RANK + 4, :] = (gmo_ref[0:1, :] / m_ref[3:4, :]).astype(BF16)
            b_ref[4 * RANK + 4 : 4 * RANK + 5, :] = (gmd_ref[0:1, :] / m_ref[4:5, :]).astype(BF16)
            b_ref[4 * RANK + 5 :, :] = jnp.zeros((RANK - 5, fw), BF16)
            b_ref[:RANK, :] = (
                SCALE
                * (acc_o[:RANK, :] + nt((bo_ref[...].astype(F32) * ratio_out).astype(BF16), wo_ref[:, :d])[:RANK, :])
            ).astype(BF16)
            a_ref[3 * RANK : 4 * RANK, :] = (
                SCALE * (acc_p[:RANK, :] + tn(wo_ref[:, d:], wo_ref[:, :d])[:RANK, :] * ratio_out)
            ).astype(BF16)
            a_ref[4 * RANK :, :] = sh_ref[...]
            for o, m in cm.st_peers():
                gather_part(o, m).start()

        io.ready()

        def grad_swap(i):
            rows = cm.rows(i)
            return stage.at[rows], out_ref.at[rows], (gs_s.at[i], gs_r.at[i], gs_l.at[i])

        def body(i, carry_on):
            @pl.when(i < nc)
            def _():
                block = dp_ref[cm.rows(i), :]
                for role in range(2 * nl):
                    sb[i, role // nl, role % nl] = nt(
                        block, w_ref[role * fw : (role + 1) * fw, :width]
                    ).astype(BF16)
                cm.rs_across(i).start()

            cm.rs_steps(i)

            @pl.when(i < parts)
            def _():
                adapters(i)

            @pl.when(i == parts)
            def _():
                adapters_end()

            @pl.when(i == min(parts + 3, nc + 2))
            def _():
                total = a_ref[:, cm.columns(c, g)].astype(F32)
                for o, m in cm.st_peers():
                    gather_part(o, m).wait_recv()
                    total = total + group[o * nl + m].astype(F32)
                gsum[...] = total.astype(BF16)
                for k in range(ny):
                    for e in (0, 1):
                        if (k, e) == (0, 0):

                            @pl.when(swap.moves)
                            def _():
                                for copy in sums(0, 0):
                                    copy.start()

                            @pl.when(jnp.logical_not(swap.moves))
                            def _():
                                for copy in sums_here():
                                    copy.start()
                        else:
                            for copy in sums(k, e):
                                copy.start()

            @pl.when(i >= 3)
            def _():
                k = i - 3
                rows = cm.rows(k)

                @pl.when(k == 0)
                def _():
                    cm.st_wait(None)

                r = rate_ref[rows, 0:1]
                inner = cm.st_sum(k)
                stage[rows, :] = (
                    dm_ref[rows, :]
                    + r * cm.rs_total(k)
                    - x_ref[rows, :].astype(F32) * (r * r * inner / d)
                ).astype(BF16)
                swap.start(*grad_swap(k))

            return carry_on

        lax.fori_loop(0, nc + 3, body, 0)

        for k in range(ny):
            for hh in (0, 1):
                slot = k * 2 + hh

                def arrived():
                    for n, dst in enumerate((final_a, final_b, final_l)):
                        src = (gsum, b_ref, l_ref)[n]
                        pltpu.make_async_remote_copy(
                            src_ref=src, dst_ref=dst.at[slot], send_sem=fs.at[n, 0], recv_sem=fr.at[n, slot],
                            device_id=swap.partner, device_id_type=MESH,
                        ).wait_recv()

                if k == 0:
                    here = jnp.logical_and(c == h, h == hh)

                    @pl.when(here)
                    def _():
                        for copy in sums_here():
                            copy.wait()

                    @pl.when(jnp.logical_not(here))
                    def _():
                        arrived()
                else:
                    arrived()
        for out, held in ((as_ref, final_a), (bs_ref, final_b), (ls_ref, final_l)):
            total = held[0].astype(F32)
            for slot in range(1, 2 * ny):
                total = total + held[slot].astype(F32)
            out[...] = total

        def drain(i, carry_on):
            swap.wait(*grad_swap(i))
            cm.rs_drain(i)
            swap.drain(*grad_swap(i))
            return carry_on

        lax.fori_loop(0, nc, drain, 0)
        cm.st_drain(None)
        for o, m in cm.st_peers():
            gather_part(o, m).wait_send()
        for k in range(ny):
            for e in (0, 1):
                if (k, e) == (0, 0):

                    @pl.when(swap.moves)
                    def _():
                        for copy in sums(0, 0):
                            copy.wait_send()
                else:
                    for copy in sums(k, e):
                        copy.wait_send()

    dma = pltpu.SemaphoreType.DMA
    na, nb, ng = 7 * RANK, (5 * RANK, fw), local_gu.shape
    return call(
        kernel,
        "qkv_backward",
        (shape((t, fw), BF16), shape((na, fw), F32), shape(nb, F32), shape(ng, F32)),
        [VM] * 17 + [ANY] * 7,
        (VM,) * 4,
        rs_scratch(nl, nc, tc, fw)
        + st_scratch(nl, nc, t)
        + [pltpu.VMEM((t, fw), BF16)]
        + [dma((nc,))] * 3
        + [pltpu.VMEM((peers, na, fw), BF16), pltpu.VMEM((na, fw), BF16), dma((peers,)), dma((peers,))]
        + [
            pltpu.VMEM((2 * ny, na, fw), BF16),
            pltpu.VMEM((2 * ny, *nb), BF16),
            pltpu.VMEM((2 * ny, *ng), BF16),
            dma((3, 2 * ny)),
            dma((3, 2 * ny)),
            dma((3,)),
            pltpu.VMEM((na, d), BF16),
            pltpu.VMEM(nb, BF16),
        ]
        + [pltpu.VMEM((LANES, n), F32) for n in (d, width, fw, d)]
        + stream_scratch(step, widths),
        6,
        70,
        (
            dp, stats, weights, rate, dm, x, shared, local_gu, w_out, up_qkv, b_out, ratios, gm_qkv, square_qkv,
            gm_out, gm_down, small, x_full, lg_qkv, lora_qkv, attended, lg_out, lora_out, go_full,
        ),
        late=(2, 3, 4, 5, 6, 7, 8, 9, 10, 11),
    )


def last_step(fw, nf, grad, result, shared, local, local_gu):
    def kernel(
        io, g_ref, r_ref, s_ref, l_ref, u_ref,
        result_ref, grad_ref, aq_ref, bq_ref, mq_ref, ao_ref, bo_ref, mo_ref,
        ag_ref, bg_ref, mg_ref, ad_ref, bd_ref, md_ref,
    ):
        result_ref[...] = r_ref[...]
        grad_ref[...] = g_ref[...].astype(F32)
        for k in range(3):
            aq_ref[k] = s_ref[k * RANK : (k + 1) * RANK, :]
            bq_ref[k] = l_ref[(1 + k) * RANK : (2 + k) * RANK, :]
        for k in range(2):
            ag_ref[k] = s_ref[(4 + k) * RANK : (5 + k) * RANK, :]
            bg_ref[k] = u_ref[(1 + k) * RANK : (2 + k) * RANK, :nf]
        mq_ref[...] = l_ref[4 * RANK : 4 * RANK + 3, :]
        mg_ref[...] = u_ref[3 * RANK : 3 * RANK + 2, :nf]
        ao_ref[...] = l_ref[:RANK, :]
        bo_ref[...] = s_ref[3 * RANK : 4 * RANK, :]
        mo_ref[...] = l_ref[4 * RANK + 3 : 4 * RANK + 4, :]
        ad_ref[...] = u_ref[:RANK, :nf]
        bd_ref[...] = s_ref[6 * RANK :, :]
        md_ref[...] = l_ref[4 * RANK + 4 : 4 * RANK + 5, :]

    f = [
        (3, RANK, fw), (3, RANK, fw), (3, fw), (RANK, fw), (RANK, fw), (1, fw),
        (2, RANK, fw), (2, RANK, nf), (2, nf), (RANK, nf), (RANK, fw), (1, fw),
    ]
    return call(
        kernel,
        "last_step",
        (shape(result.shape, BF16), shape(grad.shape, F32), *[shape(v, F32) for v in f]),
        [VM] * 5,
        (VM,) * 14,
        [],
        None,
        4,
        (grad, result, shared, local, local_gu),
    )


def turn_constants():
    f = 10000.0 ** (-2.0 * np.arange(HD // 2) / HD)
    out = []
    for scale in (32.0, 1.0):
        angle = scale * np.arange(32)[:, None] * f[None, :]
        table = np.concatenate([np.cos(angle), np.cos(angle), np.sin(angle), np.sin(angle)], axis=1)
        high = table.astype(BF16)
        low = (table - high.astype(np.float64)).astype(BF16)
        out.append(jnp.asarray(np.concatenate([high, low], axis=1)))
    return out


def padded(rows, total):
    return jnp.pad(rows, ((0, 0), (0, total - rows.shape[1])))


def on_device(ny, nl, *operands):
    (
        inputs, segments, gain_attn, gain_ffn, w_qkv, a_qkv, b_qkv, m_qkv, w_out, a_out, b_out, m_out,
        w_gu, a_gu, b_gu, m_gu, w_down, a_down, b_down, m_down, cotangent,
    ) = operands
    t, fw = inputs.shape
    mp = 2 * nl
    d = mp * fw
    nf = m_gu.shape[1]
    npad = -(-(nf + RANK) // LANES) * LANES
    width = 3 * fw
    nc = t // 256 if t % 256 == 0 else 1
    block = t // nc
    cfg = (t, fw, d, nl, nc, block)
    y, c, h, g = (lax.axis_index(name) for name in ("y", "c", "h", "g"))
    role = c * nl + g

    def two_parts(gain):
        high = gain.astype(BF16)
        return [high[:, None], (gain - high.astype(F32)).astype(BF16)[:, None]]

    tail_qkv = padded(
        jnp.concatenate(
            [(a_qkv[k] * gain_attn[:, None]).astype(BF16) for k in range(3)] + two_parts(gain_attn), axis=1
        ),
        LANES,
    )
    tail_gu = jnp.stack(
        [
            jnp.pad(
                jnp.concatenate(
                    [(a_gu[k] * gain_ffn[:, None]).astype(BF16)] + two_parts(gain_ffn), axis=1
                ),
                ((0, 0), (nf, npad - nf - RANK - 2)),
            )
            for k in range(2)
        ]
    )
    gains = padded(jnp.stack([gain_attn, gain_ffn], axis=1), LANES)
    b_gu_padded = jnp.pad(
        b_gu.reshape(2, RANK, mp, nf), ((0, 0), (0, 0), (0, 0), (0, npad - nf))
    ).transpose(0, 2, 1, 3)
    small = jnp.concatenate([m_qkv, m_out[None], m_down[None], jnp.zeros((3, fw), F32)], axis=0)
    small_gu = jnp.broadcast_to(
        jnp.pad(m_gu, ((0, 0), (0, npad - nf)), constant_values=1.0).reshape(1, 2 * npad), (8, 2 * npad)
    )

    def take(whole, n, axis):
        return lax.dynamic_slice_in_dim(whole, role * n, n, axis)

    b_qkv_here = take(b_qkv, fw, 2)
    b_gu_here = take(b_gu, nf, 2)

    def block_up(up, pad):
        k, _, n = up.shape
        wide = jnp.pad(up, ((0, 0), (0, 0), (0, pad - n)))[:, :, None, :]
        same = (jnp.arange(k)[:, None] == jnp.arange(k)[None, :])[:, None, :, None]
        rows = jnp.where(same, wide, 0.0).reshape(k * RANK, k * pad)
        return jnp.pad(rows, ((0, LANES - k * RANK), (0, 0)))

    up_qkv = block_up(b_qkv_here, fw)
    up_gu = block_up(b_gu_here, npad)
    up_out = jnp.pad(b_out, ((0, LANES - RANK), (0, 0))).astype(BF16)
    up_down = jnp.pad(b_down, ((0, LANES - RANK), (0, 0))).astype(BF16)

    (
        x, weights_qkv, weights_out, small, small_gu, scale_qkv, square_qkv, qkv, lora_qkv_in, rate_attn,
        blocks_gu, rows_down, weights_gu, x_full, cosine, sine, seg_column, seg_row,
    ) = qkv_forward(
        cfg, ny, npad, nf, inputs, w_qkv, a_qkv.transpose(0, 2, 1), b_qkv, tail_qkv, gains, w_out, small, small_gu, segments,
        turn_constants(), w_gu, a_gu.transpose(0, 2, 1), b_gu_padded, tail_gu, w_down, a_down, b_down, a_out.T, b_out,
    )
    first_number = seg_row[0, ::block]
    first_block = jnp.sum((seg_row[0][None, :] < first_number[:, None]).astype(jnp.int32), axis=1) // block
    attended, lse = attention_forward(cfg, qkv, seg_column, seg_row, first_block, block)
    middle, u, stats, sc_out, square_out, lora_out, weights_gu, weights_down = out_forward(
        cfg, ny, npad, attended, weights_out, x, small, weights_gu, blocks_gu, rows_down
    )
    (
        gu, hidden, block_out, gm_down, rate_ffn, gp, scale_gu, square_gu, sc_down, square_down,
        lora_down, grad_seed, merged_low_gu, merged_low_down, u_full,
    ) = ffn_forward(
        cfg, npad, nf, u, stats, weights_gu, small_gu[0:1], weights_down, small, middle, cotangent
    )

    dm, go, gm_out, gm_gu, lg_gu, lg_down, dp_gu, gp_full = ffn_backward(
        cfg, npad, gp, gu, weights_gu, scale_gu, up_gu, weights_down, up_down, rate_ffn,
        grad_seed, middle, x, sc_out,
    )
    grad_attended, lg_out, ratios, shared, local_gu, go_full, block_out = out_backward(
        cfg, npad, nf, go, weights_out, up_out, (gm_out, square_out, gm_down, square_down), weights_gu, weights_down, up_gu, up_down, gm_gu, square_gu,
        small_gu, u_full, lg_gu, gu, dp_gu, hidden, lg_down, lora_down, gp_full, block_out,
        merged_low_gu, merged_low_down,
    )
    dp_qkv, inner, gm_qkv, lg_qkv = attention_backward(
        cfg, qkv, attended, grad_attended, lse, seg_column, seg_row, first_block, block, cosine, sine,
        scale_qkv, rate_attn, up_qkv,
    )

    grad_input, shared, local, local_gu = qkv_backward(
        cfg, ny, dp_qkv, inner, weights_qkv, rate_attn, dm, x, shared, local_gu, weights_out, up_qkv, up_out, ratios,
        gm_qkv, square_qkv, gm_out, gm_down, small, x_full, lg_qkv, lora_qkv_in, attended, lg_out, lora_out, go_full,
    )
    out = list(last_step(fw, nf, grad_input, block_out, shared, local, local_gu))
    out[2], out[8] = out[2].transpose(0, 2, 1), out[8].transpose(0, 2, 1)
    out[5], out[11] = out[5].T, out[11].T
    out[7], out[13] = out[7][0], out[13][0]
    return tuple(out)


def solution(mesh):
    dp, mp = mesh.shape["dp"], mesh.shape["mp"]
    ny, nl = dp // 2, mp // 2
    fine = Mesh(mesh.devices.reshape(ny, 2, 2, nl), ("y", "c", "h", "g"))
    rows, cols = ("y", "c"), ("h", "g")
    in_specs = (
        P(rows, cols),
        P(rows, None),
        P(cols),
        P(cols),
        P(None, cols, None),
        P(None, cols, None),
        P(),
        P(None, cols),
        P(cols, None),
        P(cols, None),
        P(),
        P(cols),
        P(None, cols, None),
        P(None, cols, None),
        P(),
        P(None, cols),
        P(cols, None),
        P(cols, None),
        P(),
        P(cols),
        P(rows, cols),
    )
    out_specs = (
        P(rows, cols),
        P(rows, cols),
        P(None, cols, None),
        P(None, None, cols),
        P(None, cols),
        P(cols, None),
        P(None, cols),
        P(cols),
        P(None, cols, None),
        P(None, None, cols),
        P(None, cols),
        P(cols, None),
        P(None, cols),
        P(cols),
    )
    return jax.shard_map(
        lambda *operands: on_device(ny, nl, *operands),
        mesh=fine,
        in_specs=in_specs,
        out_specs=out_specs,
        check_vma=False,
    )
```
